128 devices in a mesh: dp: 16 (over y, x), mp: 8 (over z, core).
Axes of the slice: x: 4, y: 4, z: 4, core: 2. Of those that a mesh axis runs over, the one named last changes fastest.
Arguments:
- inputs: bfloat16 [32768, 768], P(('dp', 'mp')), may hold values from -6 to 6
- segment: int32 [32768], P('dp'), may hold values from -1 to 7, as said below
- w_query: bfloat16 [768, 768], P(None, 'mp'), may hold values from -0.21875 to 0.21875
- w_key: bfloat16 [768, 768], P(None, 'mp'), may hold values from -0.21875 to 0.21875
- w_value: bfloat16 [768, 768], P(None, 'mp'), may hold values from -0.21875 to 0.21875
- planes: float32 [32, 64], replicated, may hold values from -6 to 6
- conv_taps: float32 [65, 12], replicated, may hold values from -0.3 to 0.3
- w_out: bfloat16 [768, 768], P('mp'), may hold values from -0.625 to 0.625
- ln1_gain: float32 [768], replicated, may hold values from 0.5 to 1.5
- ln1_bias: float32 [768], replicated, may hold values from -1.5 to 1.5
- w_up: bfloat16 [768, 3072], P(None, 'mp'), may hold values from -0.21875 to 0.21875
- w_down: bfloat16 [3072, 768], P('mp'), may hold values from -0.109375 to 0.109375
- ln2_gain: float32 [768], replicated, may hold values from 0.5 to 1.5
- ln2_bias: float32 [768], replicated, may hold values from -1.5 to 1.5
- cotangent: bfloat16 [32768, 768], P(('dp', 'mp')), may hold values from -6 to 6
Outputs:
- outputs: bfloat16 [32768, 768], P(('dp', 'mp'))
- inputs_grad: float32 [32768, 768], P(('dp', 'mp'))
- w_query_grad: float32 [768, 768], P(None, 'mp')
- w_key_grad: float32 [768, 768], P(None, 'mp')
- w_value_grad: float32 [768, 768], P(None, 'mp')
- conv_taps_grad: float32 [65, 12], replicated
- w_out_grad: float32 [768, 768], P('mp')
- ln1_gain_grad: float32 [768], replicated
- ln1_bias_grad: float32 [768], replicated
- w_up_grad: float32 [768, 3072], P(None, 'mp')
- w_down_grad: float32 [3072, 768], P('mp')
- ln2_gain_grad: float32 [768], replicated
- ln2_bias_grad: float32 [768], replicated
The draws below stay inside these ranges and needn't reach their ends.
Inputs may be any that keep to these rules, and one draw needn't show every extreme that they name: `segment`: in each aligned block of 2048 slots the used slots come first and hold whole sequences numbered 0, 1, 2 and so on in order; padding slots (-1) fill the block's end; a block holds 1 to 8 sequences, some block exactly 8, and some block a single sequence of all 2048 slots.
All inputs are finite; a program needn't handle non-finite values.
Results may differ from the reference program's by a relative error of at most 0.024.
Values may be sent and summed in bfloat16 or wider, within the bound.
A program may use at most 384 MiB of HBM per device.

```python
import math
import jax
import jax.numpy as jnp
from jax import lax

D = 768
HEADS = 12
HD = 64
FF = 3072
TABLES = 4
BITS = 8
KW = 65
MAXSEG = 8
CAP = 2048
TOKENS = 32768


def draw_segment(key, part):
    blocks = TOKENS // CAP
    keys = jax.random.split(key, 5)
    block_ids = jnp.arange(blocks, dtype=jnp.int32)
    counts = jax.random.randint(keys[0], (blocks,), 1, MAXSEG + 1)
    busiest = jax.random.randint(keys[1], (), 0, blocks)
    filled = (busiest + 1 + jax.random.randint(keys[2], (), 0, max(blocks - 1, 1))) % blocks
    counts = jnp.where(block_ids == busiest, MAXSEG, counts)
    counts = jnp.where(block_ids == filled, 1, counts)
    used = CAP - jax.random.randint(keys[3], (blocks,), 0, CAP // 2 + 1)
    used = jnp.where(block_ids == filled, CAP, used)
    weights = jax.random.randint(keys[4], (blocks, MAXSEG), 1, 9)
    weights = jnp.where(jnp.arange(MAXSEG, dtype=jnp.int32)[None, :] < counts[:, None], weights, 0)
    cumulative = jnp.cumsum(weights, axis=1)
    ends = used[:, None] * cumulative // cumulative[:, -1:]
    position = jnp.arange(CAP, dtype=jnp.int32)
    numbers = jnp.sum((position[None, :, None] >= ends[:, None, :]).astype(jnp.int32), axis=2)
    numbers = jnp.where(position[None, :] < used[:, None], numbers, -1)
    return numbers.reshape(-1).astype(jnp.int32)


def shard_levels(stream_key, extent, shards, smallest, top_value):
    factor_of = 1.0
    for dim, blocks in shards:
        steps = jax.random.uniform(jax.random.fold_in(jax.random.fold_in(stream_key, 6), dim), (blocks,), jnp.float32, smallest / len(shards), top_value / len(shards))
        factor_of = factor_of * jnp.repeat(jnp.exp(steps), extent[dim] // blocks).reshape((-1,) + (1,) * (len(extent) - 1 - dim))
    return factor_of


def bell_draw(key, shape, width, reach, shards=(), kind=jnp.bfloat16):
    result = width * jax.random.normal(key, shape, jnp.float32)
    if shards:
        result = result * shard_levels(key, shape, shards, -0.22, 0.18)
    return jnp.clip(result, -reach, reach).astype(kind)


def setup_inputs(seed: int = 0) -> dict:
    arg_keys = jax.random.split(jax.random.key(seed), 16)
    inputs = bell_draw(arg_keys[0], (TOKENS, D), 1.0, 6.0, ((0, 128),))
    segment = draw_segment(jax.random.fold_in(arg_keys[15], 71), 0)
    w_query = bell_draw(arg_keys[2], (D, D), D ** -0.5, 0.21875, ((1, 8),))
    w_key = bell_draw(arg_keys[3], (D, D), D ** -0.5, 0.21875, ((1, 8),))
    w_value = bell_draw(arg_keys[4], (D, D), D ** -0.5, 0.21875, ((1, 8),))
    planes = bell_draw(arg_keys[5], (TABLES * BITS, HD), 1.0, 6.0, (), jnp.float32)
    conv_taps = bell_draw(arg_keys[6], (KW, HEADS), 0.05, 0.3, (), jnp.float32)
    w_out = bell_draw(arg_keys[7], (D, D), (D // 8) ** -0.5, 0.625, ((0, 8),))
    ln1_gain = jnp.clip(1.0 + 0.1 * jax.random.normal(arg_keys[8], (D,), jnp.float32), 0.5, 1.5)
    ln1_bias = bell_draw(arg_keys[9], (D,), 0.3, 1.5, (), jnp.float32)
    w_up = bell_draw(arg_keys[10], (D, FF), D ** -0.5, 0.21875, ((1, 8),))
    w_down = bell_draw(arg_keys[11], (FF, D), FF ** -0.5, 0.109375, ((0, 8),))
    ln2_gain = jnp.clip(1.0 + 0.1 * jax.random.normal(arg_keys[12], (D,), jnp.float32), 0.5, 1.5)
    ln2_bias = bell_draw(arg_keys[13], (D,), 0.3, 1.5, (), jnp.float32)
    cotangent = bell_draw(arg_keys[14], (TOKENS, D), 1.0, 6.0, ((0, 128),))
    return dict(inputs=inputs, segment=segment, w_query=w_query, w_key=w_key, w_value=w_value, planes=planes, conv_taps=conv_taps, w_out=w_out, ln1_gain=ln1_gain, ln1_bias=ln1_bias, w_up=w_up, w_down=w_down, ln2_gain=ln2_gain, ln2_bias=ln2_bias, cotangent=cotangent)


HIGHEST_PREC = lax.Precision.HIGHEST

@jax.custom_vjp
def low(v):
    return lax.optimization_barrier(v.astype(jnp.bfloat16)).astype(jnp.float32)

@jax.custom_vjp
def low_back(v):
    return v

def low_keep(v):
    return (low(v), None)

def low_pass(kept, grad):
    return (grad,)

def back_keep(v):
    return (v, None)

def back_low(kept, grad):
    return (low(grad),)
low.defvjp(low_keep, low_pass)
low_back.defvjp(back_keep, back_low)

def matmul(left_arr, right_arr):
    return jnp.dot(left_arr, right_arr, precision=HIGHEST_PREC, preferred_element_type=jnp.float32)

def layer_norm(values, gain_vec, shift_vec):
    center = values - lax.optimization_barrier(jnp.mean(values, axis=-1, keepdims=True))
    inv_std = lax.rsqrt(lax.optimization_barrier(jnp.mean(center * center, axis=-1, keepdims=True)) + 1e-05)
    return center * inv_std * gain_vec + shift_vec

def normal_planes(planes):
    grouped = planes.reshape(TABLES, BITS, HD)
    return grouped * lax.rsqrt(lax.optimization_barrier(jnp.sum(grouped * grouped, axis=-1, keepdims=True)) + 1e-06)

def bucket_probs(vectors, planes_unit):
    unit_vec = vectors * lax.rsqrt(lax.optimization_barrier(jnp.sum(vectors * vectors, axis=-1, keepdims=True)) + 1e-06)
    signs = jnp.tanh(math.sqrt(HD) * jnp.einsum('ld,tbd->tlb', unit_vec, planes_unit, precision=HIGHEST_PREC))
    chances = jnp.ones(signs.shape[:2] + (1,), jnp.float32)
    for bit_index in range(BITS):
        bit_sign = signs[:, :, bit_index]
        bit_pair = jnp.stack(((1.0 + bit_sign) * 0.5, (1.0 - bit_sign) * 0.5), axis=-1)
        chances = (chances[:, :, :, None] * bit_pair[:, :, None, :]).reshape(signs.shape[0], signs.shape[1], -1)
    return chances

def segment_conv(values, tap_rows, segment):
    length = values.shape[0]
    margin = (KW - 1) // 2
    padded = jnp.pad(values, ((margin, margin), (0, 0)))
    seg_pad = jnp.pad(segment, (margin, margin), constant_values=-1)
    summed = jnp.zeros(values.shape, jnp.float32)
    for offset in range(KW):
        matches = jnp.logical_and(seg_pad[offset:offset + length] == segment, segment >= 0)
        summed = summed + tap_rows[offset] * padded[offset:offset + length] * matches[:, None].astype(jnp.float32)
    return summed

def head_mix(query_h, key_h, value_h, tap_rows, planes_unit, onehot, segment):
    query_p = low(bucket_probs(query_h, planes_unit))
    key_p = low(bucket_probs(key_h, planes_unit))
    length = query_h.shape[0]
    query_x = (onehot[None, :, :, None] * query_p[:, :, None, :]).reshape(TABLES, length, -1)
    key_x = (onehot[None, :, :, None] * key_p[:, :, None, :]).reshape(TABLES, length, -1)
    bucket_sums = low_back(low(jnp.einsum('ld,tlc->tdc', value_h, key_x, precision=HIGHEST_PREC)))
    key_mass = jnp.einsum('ls,tlc->tsc', onehot, key_p, precision=HIGHEST_PREC)
    spread_mass = jnp.einsum('ls,tsc->tlc', onehot, key_mass, precision=HIGHEST_PREC)
    density = lax.optimization_barrier(jnp.sum(query_p * spread_mass, axis=-1))
    numerator = low_back(jnp.einsum('tlc,tdc->tld', query_x, bucket_sums, precision=HIGHEST_PREC))
    estimate = numerator / jnp.maximum(density, 1.0)[:, :, None]
    return lax.optimization_barrier(jnp.sum(estimate, axis=0)) / TABLES + segment_conv(value_h, tap_rows, segment)

def block_forward(x_block, seg_block, w_query, w_key, w_value, conv_taps, w_out, ln1_gain, ln1_bias, w_up, w_down, ln2_gain, ln2_bias, planes_unit):
    queries = low_back(low(matmul(x_block, w_query)))
    key_rows = low_back(low(matmul(x_block, w_key)))
    val_rows = low_back(low(matmul(x_block, w_value)))
    onehot = (seg_block[:, None] == jnp.arange(MAXSEG, dtype=jnp.int32)[None, :]).astype(jnp.float32)
    length = x_block.shape[0]

    def one_head(head_index):
        first_col = head_index * HD
        query_h = lax.dynamic_slice_in_dim(queries, first_col, HD, 1)
        key_h = lax.dynamic_slice_in_dim(key_rows, first_col, HD, 1)
        value_h = lax.dynamic_slice_in_dim(val_rows, first_col, HD, 1)
        tap_rows = jnp.broadcast_to(lax.dynamic_slice_in_dim(conv_taps, head_index, 1, 1), (KW, HD))
        return head_mix(query_h, key_h, value_h, tap_rows, planes_unit, onehot, seg_block)
    head_out = lax.map(jax.checkpoint(one_head), jnp.arange(HEADS, dtype=jnp.int32))
    attended = low_back(low(jnp.transpose(head_out, (1, 0, 2)).reshape(length, HEADS * HD)))
    residual_one = x_block + low_back(matmul(attended, w_out))
    hidden_one = layer_norm(residual_one, ln1_gain, ln1_bias)
    preact = low_back(matmul(low(hidden_one), w_up))
    activated = low(jax.nn.gelu(preact, approximate=False))
    residual_two = hidden_one + low_back(matmul(activated, w_down))
    return layer_norm(residual_two, ln2_gain, ln2_bias)

def reference(inputs, segment, w_query, w_key, w_value, planes, conv_taps, w_out, ln1_gain, ln1_bias, w_up, w_down, ln2_gain, ln2_bias, cotangent):
    planes_unit = normal_planes(planes)
    seg_blocks = segment.reshape(-1, CAP)

    def forward(inputs_f, w_query_f, w_key_f, w_value_f, conv_f, w_out_f, gain_one, bias_one, w_up_f, w_down_f, gain_two, bias_two):

        def block_call(x_block, seg_block):
            return block_forward(x_block, seg_block, w_query_f, w_key_f, w_value_f, conv_f, w_out_f, gain_one, bias_one, w_up_f, w_down_f, gain_two, bias_two, planes_unit)
        checked = jax.checkpoint(block_call)

        def scan_step(carried, block_pair):
            return (carried, checked(block_pair[0], block_pair[1]))
        carried, results = lax.scan(scan_step, jnp.zeros((), jnp.float32), (inputs_f.reshape(-1, CAP, D), seg_blocks))
        return results.reshape(-1, D)
    results, back_fn = jax.vjp(forward, inputs.astype(jnp.float32), w_query.astype(jnp.float32), w_key.astype(jnp.float32), w_value.astype(jnp.float32), conv_taps, w_out.astype(jnp.float32), ln1_gain, ln1_bias, w_up.astype(jnp.float32), w_down.astype(jnp.float32), ln2_gain, ln2_bias)
    grads = back_fn(cotangent.astype(jnp.float32))
    return (results.astype(jnp.bfloat16), grads[0], grads[1], grads[2], grads[3], grads[4], grads[5], grads[6], grads[7], grads[8], grads[9], grads[10], grads[11])
```

```python
from functools import partial
import math
import jax
import jax.numpy as jnp
from jax import lax
from jax.experimental import pallas as pl
from jax.experimental.pallas import tpu as pltpu
from jax.sharding import PartitionSpec as P

HEADS = 12
HD = 64
TABLES = 4
BITS = 8
KW = 65
MAXSEG = 8
CODES = 256
UNITS = 6
SOLO = 4
SPREAD = MAXSEG * HD
EXT = SPREAD + 128
LANES = 128
TILE = 256
F32 = jnp.float32
BF16 = jnp.bfloat16
VMEM_BYTES = 56 * 1024 * 1024


def nt_dot(left, right):
    return lax.dot_general(left, right, (((1,), (1,)), ((), ())), preferred_element_type=F32)


def tn_dot(left, right):
    return lax.dot_general(left, right, (((0,), (0,)), ((), ())), preferred_element_type=F32)


def nn_dot(left, right):
    return lax.dot_general(left, right, (((1,), (0,)), ((), ())), preferred_element_type=F32)


def half_sign(bit):
    rows = lax.broadcasted_iota(jnp.int32, (8, LANES), 0)
    return jnp.where((rows >> bit) & 1 == 0, 0.5, -0.5).astype(F32)


def code_factors(signs):
    pos0, neg0 = 0.5 + 0.5 * signs[0:1], 0.5 - 0.5 * signs[0:1]
    pos1, neg1 = 0.5 + 0.5 * signs[1:2], 0.5 - 0.5 * signs[1:2]
    tops = (pos0 * pos1, pos0 * neg1, neg0 * pos1, neg0 * neg1)
    picks = [half_sign(2), half_sign(1), half_sign(0)]
    mids = [0.5 + picks[n] * signs[2 + n : 3 + n] for n in range(3)]
    lows = [0.5 + picks[n] * signs[5 + n : 6 + n] for n in range(3)]
    return tops, mids, lows, picks


def code_probs(signs, out_ref, lane):
    tops, mids, lows, _ = code_factors(signs)
    mid = mids[0] * mids[1] * mids[2]
    low = lows[0] * lows[1] * lows[2]
    for top_index in range(4):
        low_top = low * tops[top_index]
        for pair in range(4):
            rows = jnp.concatenate(
                (
                    low_top * mid[2 * pair : 2 * pair + 1],
                    low_top * mid[2 * pair + 1 : 2 * pair + 2],
                ),
                axis=0,
            )
            first = top_index * 64 + pair * 16
            out_ref[first : first + 16, lane] = rows.astype(BF16)


def signs_back(signs, grads):
    tops, mids, lows, picks = code_factors(signs)
    mid = mids[0] * mids[1] * mids[2]
    low = lows[0] * lows[1] * lows[2]
    mid_rows = [jnp.broadcast_to(mid[m : m + 1], (8, LANES)) for m in range(8)]
    top_rows = [jnp.broadcast_to(tops[t], (8, LANES)) for t in range(4)]
    by_top = [None] * 4
    by_mid = [None] * 8
    for t in range(4):
        for m in range(8):
            piece = grads[t * 64 + m * 8 : t * 64 + m * 8 + 8]
            a = piece * mid_rows[m]
            b = piece * top_rows[t]
            by_top[t] = a if by_top[t] is None else by_top[t] + a
            by_mid[m] = b if by_mid[m] is None else by_mid[m] + b
    low_grad = by_top[0] * top_rows[0]
    for t in range(1, 4):
        low_grad = low_grad + by_top[t] * top_rows[t]
    top_grad = [jnp.sum(low * by_top[t], axis=0, keepdims=True) for t in range(4)]
    mid_grad = jnp.concatenate(
        [jnp.sum(low * by_mid[m], axis=0, keepdims=True) for m in range(8)], axis=0
    )
    pos0, neg0 = 0.5 + 0.5 * signs[0:1], 0.5 - 0.5 * signs[0:1]
    pos1, neg1 = 0.5 + 0.5 * signs[1:2], 0.5 - 0.5 * signs[1:2]
    out = [
        0.5 * ((top_grad[0] - top_grad[2]) * pos1 + (top_grad[1] - top_grad[3]) * neg1),
        0.5 * ((top_grad[0] - top_grad[1]) * pos0 + (top_grad[2] - top_grad[3]) * neg0),
    ]
    for grad, parts in ((mid_grad, mids), (low_grad, lows)):
        for n in range(3):
            others = parts[(n + 1) % 3] * parts[(n + 2) % 3] * picks[n]
            out.append(jnp.sum(grad * others, axis=0, keepdims=True))
    return jnp.concatenate(out, axis=0)


def split_two(value):
    high = value.astype(BF16).astype(F32)
    return high, value - high


def unit_planes(planes):
    return planes * lax.rsqrt(jnp.sum(planes * planes, axis=1, keepdims=True) + 1e-06)


def fill_spread(values, seg_row, spread_ref, lane):
    for s in range(MAXSEG):
        spread_ref[s * HD : (s + 1) * HD, lane] = jnp.where(
            seg_row == s, values, jnp.zeros_like(values)
        )


def fill_member(seg_row, spread_ref, lane):
    width = seg_row.shape[1]
    rows = lax.broadcasted_iota(jnp.int32, (128, width), 0)
    hit = jnp.logical_and(rows < 16, (rows & 7) == seg_row)
    spread_ref[SPREAD:EXT, lane] = jnp.where(hit, 1.0, 0.0).astype(BF16)


def lanes_of(index, width):
    return pl.ds(pl.multiple_of(index * width, width), width)


def masked_fold(product, seg_row):
    total = None
    for s in range(MAXSEG):
        piece = jnp.where(seg_row == s, product[s * HD : (s + 1) * HD], 0.0)
        total = piece if total is None else total + piece
    return total


def attend_kernel(
    qkv_ref, planes_ref, seg_ref,
    est_ref, numer_ref, dens_ref, sign_ref, bucket_ref,
    spread, norm, qprob, kprob, total, table,
):
    unit = pl.program_id(0)
    slot = unit // SOLO
    length = qkv_ref.shape[1]
    tiles = length // TILE
    q_rows = pl.ds(pl.multiple_of(slot * HD, HD), HD)
    k_rows = pl.ds(pl.multiple_of(2 * HD + slot * HD, HD), HD)
    v_rows = pl.ds(pl.multiple_of(4 * HD + slot * HD, HD), HD)

    @pl.when(jnp.logical_or(unit == 0, unit == SOLO))
    def _():
        def step(i, carry):
            lane = lanes_of(i, TILE)
            seg_row = seg_ref[:, lane]
            fill_spread(qkv_ref[v_rows, lane], seg_row, spread, lane)
            fill_member(seg_row, spread, lane)
            query = qkv_ref[q_rows, lane].astype(F32)
            key = qkv_ref[k_rows, lane].astype(F32)
            scale = math.sqrt(HD)
            norm[0:1, lane] = scale * lax.rsqrt(
                jnp.sum(query * query, axis=0, keepdims=True) + 1e-06
            )
            norm[1:2, lane] = scale * lax.rsqrt(jnp.sum(key * key, axis=0, keepdims=True) + 1e-06)
            est_ref[q_rows, lane] = jnp.zeros((HD, TILE), F32)
            return carry

        lax.fori_loop(0, tiles, step, 0)

    planes = unit_planes(planes_ref[pl.ds(pl.multiple_of(unit * BITS, BITS), BITS), :])
    high, rest = split_two(planes)
    middle, low = split_two(rest)
    stack = jnp.concatenate((high, middle, low), axis=0).astype(BF16)
    total[...] = jnp.zeros_like(total)

    def collect(i, carry):
        lane = lanes_of(i, TILE)
        flat_q = nn_dot(stack, qkv_ref[q_rows, lane])
        flat_k = nn_dot(stack, qkv_ref[k_rows, lane])
        sign_q = jnp.tanh((flat_q[0:8] + flat_q[8:16] + flat_q[16:24]) * norm[0:1, lane])
        sign_k = jnp.tanh((flat_k[0:8] + flat_k[8:16] + flat_k[16:24]) * norm[1:2, lane])
        sign_ref[0, 0:8, lane] = sign_q
        sign_ref[0, 8:16, lane] = sign_k
        for part in range(TILE // LANES):
            inner = slice(part * LANES, (part + 1) * LANES)
            code_probs(sign_k[:, inner], kprob, inner)
            code_probs(
                sign_q[:, inner], qprob, pl.ds(pl.multiple_of(i * TILE + part * LANES, LANES), LANES)
            )
        total[...] += nt_dot(spread[0 : SPREAD + 16, lane], kprob[...])
        return carry

    lax.fori_loop(0, tiles, collect, 0)
    mass = total[SPREAD : SPREAD + 8, :]
    mass_high, mass_low = split_two(mass)
    extra = jnp.concatenate(
        (mass_high, mass_high, mass_low, jnp.zeros((104, CODES), F32)), axis=0
    )
    table[0:SPREAD, :] = total[0:SPREAD, :].astype(BF16)
    table[SPREAD:EXT, :] = extra.astype(BF16)
    bucket_ref[0, :, 0:SPREAD] = jnp.transpose(total[0:SPREAD, :]).astype(BF16)
    bucket_ref[0, :, SPREAD:EXT] = jnp.transpose(extra).astype(BF16)

    def spend(i, carry):
        lane = lanes_of(i, TILE)
        seg_row = seg_ref[:, lane]
        product = nn_dot(table[0 : SPREAD + 32, :], qprob[:, lane])
        numer = masked_fold(product, seg_row)
        both = product[SPREAD : SPREAD + 8] + product[SPREAD + 16 : SPREAD + 24]
        which = lax.broadcasted_iota(jnp.int32, (8, TILE), 0)
        density = jnp.sum(jnp.where(which == seg_row, both, 0.0), axis=0, keepdims=True)
        numer_ref[0, :, lane] = numer
        dens_ref[0, :, lane] = density
        est_ref[q_rows, lane] += numer * (1.0 / jnp.maximum(density, 1.0))
        return carry

    lax.fori_loop(0, tiles, spend, 0)


def attend(qkv, planes, seg_row):
    length = qkv.shape[1]
    per_unit = lambda u: (u, 0, 0)
    fixed = lambda u: (0, 0)
    return pl.pallas_call(
        attend_kernel,
        grid=(UNITS,),
        in_specs=[
            pl.BlockSpec(qkv.shape, fixed),
            pl.BlockSpec(planes.shape, fixed),
            pl.BlockSpec(seg_row.shape, fixed),
        ],
        out_specs=[
            pl.BlockSpec((2 * HD, length), fixed),
            pl.BlockSpec((1, HD, length), per_unit),
            pl.BlockSpec((1, 1, length), per_unit),
            pl.BlockSpec((1, 16, length), per_unit),
            pl.BlockSpec((1, CODES, EXT), per_unit),
        ],
        out_shape=[
            jax.ShapeDtypeStruct((2 * HD, length), F32),
            jax.ShapeDtypeStruct((UNITS, HD, length), F32),
            jax.ShapeDtypeStruct((UNITS, 1, length), F32),
            jax.ShapeDtypeStruct((UNITS, 16, length), F32),
            jax.ShapeDtypeStruct((UNITS, CODES, EXT), BF16),
        ],
        scratch_shapes=[
            pltpu.VMEM((EXT, length), BF16),
            pltpu.VMEM((8, length), F32),
            pltpu.VMEM((CODES, length), BF16),
            pltpu.VMEM((CODES, TILE), BF16),
            pltpu.VMEM((SPREAD + 16, CODES), F32),
            pltpu.VMEM((EXT, CODES), BF16),
        ],
        compiler_params=pltpu.CompilerParams(vmem_limit_bytes=VMEM_BYTES),
        cost_estimate=pl.CostEstimate(
            flops=UNITS * 4 * length * CODES * SPREAD, bytes_accessed=16_000_000, transcendentals=0
        ),
        name="attend",
    )(qkv, planes, seg_row)


def attend_back_kernel(
    qkv_ref, planes_ref, seg_ref, grad_ref, numer_ref, dens_ref, sign_ref, bucket_ref,
    out_ref,
    spread, qprob, kprob, gspread, total, table, turned, gsign, proj,
):
    unit = pl.program_id(0)
    slot = unit // SOLO
    length = qkv_ref.shape[1]
    tiles = length // TILE
    q_rows = pl.ds(pl.multiple_of(slot * HD, HD), HD)
    k_rows = pl.ds(pl.multiple_of(2 * HD + slot * HD, HD), HD)
    v_rows = pl.ds(pl.multiple_of(4 * HD + slot * HD, HD), HD)

    @pl.when(jnp.logical_or(unit == 0, unit == SOLO))
    def _():
        def step(i, carry):
            lane = lanes_of(i, TILE)
            seg_row = seg_ref[:, lane]
            fill_spread(qkv_ref[v_rows, lane], seg_row, spread, lane)
            fill_member(seg_row, spread, lane)
            proj[:, lane] = jnp.zeros((2 * HD, TILE), F32)
            out_ref[v_rows, lane] = jnp.zeros((HD, TILE), F32)
            return carry

        lax.fori_loop(0, tiles, step, 0)
        gspread[SPREAD:EXT, :] = jnp.zeros((128, TILE), BF16)

    total[...] = jnp.zeros_like(total)

    def first(i, carry):
        lane = lanes_of(i, TILE)
        seg_row = seg_ref[:, lane]
        density = dens_ref[0, :, lane]
        inverse = 1.0 / jnp.maximum(density, 1.0)
        est_grad = grad_ref[q_rows, lane].astype(F32) * (1.0 / TABLES)
        num_grad = (est_grad * inverse).astype(BF16)
        fill_spread(num_grad, seg_row, gspread, slice(0, TILE))
        inner_sum = jnp.sum(est_grad * numer_ref[0, :, lane], axis=0, keepdims=True)
        dens_grad = jnp.where(density > 1.0, -inner_sum * inverse * inverse, 0.0)
        which = lax.broadcasted_iota(jnp.int32, (8, TILE), 0)
        high, low = split_two(jnp.where(which == seg_row, dens_grad, 0.0))
        gspread[SPREAD : SPREAD + 32, :] = jnp.concatenate(
            (high, low, high, jnp.zeros_like(high)), axis=0
        ).astype(BF16)
        collected = nn_dot(bucket_ref[0], gspread[...])
        for part in range(TILE // LANES):
            inner = slice(part * LANES, (part + 1) * LANES)
            outer = pl.ds(pl.multiple_of(i * TILE + part * LANES, LANES), LANES)
            sign_q = sign_ref[0, 0:8, outer]
            code_probs(sign_q, qprob, inner)
            gsign[0:8, outer] = signs_back(sign_q, collected[:, inner])
        total[...] += nt_dot(gspread[0 : SPREAD + 16, :], qprob[...])
        return carry

    lax.fori_loop(0, tiles, first, 0)
    mass_grad = total[SPREAD : SPREAD + 8, :] + total[SPREAD + 8 : SPREAD + 16, :]
    high, low = split_two(mass_grad)
    extra = jnp.concatenate((high, low, jnp.zeros((112, CODES), F32)), axis=0)
    table[...] = total[0:SPREAD, :].astype(BF16)
    turned[:, 0:SPREAD] = jnp.transpose(total[0:SPREAD, :]).astype(BF16)
    turned[:, SPREAD:EXT] = jnp.transpose(extra).astype(BF16)

    planes = unit_planes(planes_ref[pl.ds(pl.multiple_of(unit * BITS, BITS), BITS), :])
    plane_high, plane_low = split_two(planes)
    stack = jnp.concatenate((plane_high, plane_low, plane_high, jnp.zeros_like(plane_high)), axis=0)
    stack = stack.astype(BF16)

    def second(i, carry):
        lane = lanes_of(i, TILE)
        seg_row = seg_ref[:, lane]
        for part in range(TILE // LANES):
            inner = slice(part * LANES, (part + 1) * LANES)
            outer = pl.ds(pl.multiple_of(i * TILE + part * LANES, LANES), LANES)
            code_probs(sign_ref[0, 8:16, outer], kprob, inner)
        out_ref[v_rows, lane] += masked_fold(nn_dot(table[...], kprob[...]), seg_row)
        collected = nn_dot(turned[...], spread[:, lane])
        for part in range(TILE // LANES):
            inner = slice(part * LANES, (part + 1) * LANES)
            outer = pl.ds(pl.multiple_of(i * TILE + part * LANES, LANES), LANES)
            gsign[8:16, outer] = signs_back(sign_ref[0, 8:16, outer], collected[:, inner])
        signs = sign_ref[0, :, lane]
        flat = gsign[:, lane] * (1.0 - signs * signs)
        high, low = split_two(flat)
        for side in range(2):
            rows = slice(8 * side, 8 * side + 8)
            pieces = jnp.concatenate(
                (high[rows], high[rows], low[rows], jnp.zeros((8, TILE), F32)), axis=0
            ).astype(BF16)
            proj[side * HD : (side + 1) * HD, lane] += tn_dot(stack, pieces)
        return carry

    lax.fori_loop(0, tiles, second, 0)

    @pl.when(jnp.logical_or(unit == SOLO - 1, unit == UNITS - 1))
    def _():
        def step(i, carry):
            lane = lanes_of(i, TILE)
            for side, rows in ((0, q_rows), (1, k_rows)):
                vec = qkv_ref[rows, lane].astype(F32)
                inverse = lax.rsqrt(jnp.sum(vec * vec, axis=0, keepdims=True) + 1e-06)
                unit_vec = vec * inverse
                grad = proj[side * HD : (side + 1) * HD, lane]
                along = jnp.sum(unit_vec * grad, axis=0, keepdims=True)
                out_ref[rows, lane] = math.sqrt(HD) * inverse * (grad - unit_vec * along)
            return carry

        lax.fori_loop(0, tiles, step, 0)


def attend_back(qkv, planes, seg_row, grad, numer, dens, sign, bucket):
    length = qkv.shape[1]
    per_unit = lambda u: (u, 0, 0)
    fixed = lambda u: (0, 0)
    return pl.pallas_call(
        attend_back_kernel,
        grid=(UNITS,),
        in_specs=[
            pl.BlockSpec(qkv.shape, fixed),
            pl.BlockSpec(planes.shape, fixed),
            pl.BlockSpec(seg_row.shape, fixed),
            pl.BlockSpec(grad.shape, fixed),
            pl.BlockSpec((1, HD, length), per_unit),
            pl.BlockSpec((1, 1, length), per_unit),
            pl.BlockSpec((1, 16, length), per_unit),
            pl.BlockSpec((1, CODES, EXT), per_unit),
        ],
        out_specs=pl.BlockSpec((6 * HD, length), fixed),
        out_shape=jax.ShapeDtypeStruct((6 * HD, length), F32),
        scratch_shapes=[
            pltpu.VMEM((EXT, length), BF16),
            pltpu.VMEM((CODES, TILE), BF16),
            pltpu.VMEM((CODES, TILE), BF16),
            pltpu.VMEM((EXT, TILE), BF16),
            pltpu.VMEM((SPREAD + 16, CODES), F32),
            pltpu.VMEM((SPREAD, CODES), BF16),
            pltpu.VMEM((CODES, EXT), BF16),
            pltpu.VMEM((16, length), F32),
            pltpu.VMEM((2 * HD, length), F32),
        ],
        compiler_params=pltpu.CompilerParams(vmem_limit_bytes=VMEM_BYTES),
        cost_estimate=pl.CostEstimate(
            flops=UNITS * 8 * length * CODES * SPREAD, bytes_accessed=16_000_000, transcendentals=0
        ),
        name="attend_back",
    )(qkv, planes, seg_row, grad, numer, dens, sign, bucket)


SPAN = 192
OWN = 96
BLOCKS = ((0, HD), (HD, OWN))


def toeplitz(taps):
    row = jnp.pad(taps, ((0, 0), (0, SPAN + 1 - KW)))
    flat = jnp.tile(row, (1, LANES))[:, : LANES * SPAN]
    return jnp.swapaxes(flat.reshape(2, LANES, SPAN), 1, 2)


def band_product(pad_ref, band_ref, lane_wide, mask, out_ref, lane):
    for h, (low_row, high_row) in enumerate(BLOCKS):
        band = jnp.where(mask, band_ref[h], 0.0)
        high, low = split_two(band)
        rows = pad_ref[low_row:high_row, lane_wide]
        out_ref[low_row:high_row, lane] = nn_dot(rows, high.astype(BF16)) + nn_dot(
            rows, low.astype(BF16)
        )


def conv_kernel(pad_ref, band_ref, col_ref, seg_ref, out_ref):
    tiles = out_ref.shape[1] // LANES

    def step(i, carry):
        lane = lanes_of(i, LANES)
        start = pl.multiple_of(i * LANES, LANES)
        wide = pl.ds(start, SPAN)
        mask = col_ref[wide, :] == seg_ref[:, lane]
        band_product(pad_ref, band_ref, wide, mask, out_ref, lane)
        return carry

    lax.fori_loop(0, tiles, step, 0)


def segment_conv(padded, band, seg_col, seg_own):
    length = seg_own.shape[1]
    return pl.pallas_call(
        conv_kernel,
        out_shape=jax.ShapeDtypeStruct((OWN, length), F32),
        compiler_params=pltpu.CompilerParams(vmem_limit_bytes=VMEM_BYTES),
        cost_estimate=pl.CostEstimate(
            flops=8 * length * SPAN * HD, bytes_accessed=3_000_000, transcendentals=0
        ),
        name="segment_conv",
    )(padded, band, seg_col, seg_own)


def conv_back_kernel(gpad_ref, grad_ref, vpad_ref, band_ref, col_ref, seg_ref, segt_ref, colt_ref,
                     out_ref, tap_ref, corr):
    tiles = out_ref.shape[1] // LANES
    corr[...] = jnp.zeros_like(corr)

    def step(i, carry):
        lane = lanes_of(i, LANES)
        start = pl.multiple_of(i * LANES, LANES)
        wide = pl.ds(start, SPAN)
        twice = pl.ds(start, 2 * LANES)
        mask = col_ref[wide, :] == seg_ref[:, lane]
        band_product(gpad_ref, band_ref, wide, mask, out_ref, lane)
        mask_turned = colt_ref[lane, :] == segt_ref[:, twice]
        for h, (low_row, high_row) in enumerate(BLOCKS):
            match = tn_dot(grad_ref[low_row:high_row, lane], vpad_ref[low_row:high_row, twice])
            corr[h] += jnp.where(mask_turned, match, 0.0)
        return carry

    lax.fori_loop(0, tiles, step, 0)
    row = lax.broadcasted_iota(jnp.int32, (LANES, 2 * LANES), 0)
    for h in range(2):
        skew = corr[h]
        for bit in range(7):
            moved = pltpu.roll(skew, 2 * LANES - (1 << bit), 1)
            skew = jnp.where((row >> bit) & 1 == 1, moved, skew)
        tap_ref[h] = jnp.sum(skew, axis=0, keepdims=True)


def conv_back(gpad, grad, vpad, band, seg_col, seg_own, seg_wide, col_own):
    length = seg_own.shape[1]
    return pl.pallas_call(
        conv_back_kernel,
        out_shape=(
            jax.ShapeDtypeStruct((OWN, length), F32),
            jax.ShapeDtypeStruct((2, 1, 2 * LANES), F32),
        ),
        scratch_shapes=[pltpu.VMEM((2, LANES, 2 * LANES), F32)],
        compiler_params=pltpu.CompilerParams(vmem_limit_bytes=VMEM_BYTES),
        cost_estimate=pl.CostEstimate(
            flops=16 * length * SPAN * HD, bytes_accessed=4_000_000, transcendentals=0
        ),
        name="conv_back",
    )(gpad, grad, vpad, band, seg_col, seg_own, seg_wide, col_own)


def layer_norm_rows(values, gain_vec, shift_vec):
    center = values - jnp.mean(values, axis=-1, keepdims=True)
    inv_std = lax.rsqrt(jnp.mean(center * center, axis=-1, keepdims=True) + 1e-05)
    normed = center * inv_std
    return (normed * gain_vec + shift_vec, normed, inv_std)


def layer_norm_back(upstream, normed, inv_std, gain_vec):
    scaled = upstream * gain_vec
    inner = (
        scaled
        - jnp.mean(scaled, axis=-1, keepdims=True)
        - normed * jnp.mean(scaled * normed, axis=-1, keepdims=True)
    )
    return (inner * inv_std, jnp.sum(upstream * normed, axis=0), jnp.sum(upstream, axis=0))


def from_partner(block):
    count = lax.axis_size("mp")
    route = [(n, n ^ 1) for n in range(count)]
    return lax.ppermute(block, "mp", route)


def gather_rows(rows):
    return lax.all_gather(rows, "mp", axis=0, tiled=True)


def scatter_rows(rows):
    return lax.psum_scatter(
        rows.astype(BF16), "mp", scatter_dimension=0, tiled=True
    ).astype(F32)


def on_device(
    inputs, segment, w_query, w_key, w_value, planes, conv_taps, w_out,
    ln1_gain, ln1_bias, w_up, w_down, ln2_gain, ln2_bias, cotangent,
):
    position = lax.axis_index("mp")
    side = position % 2
    first_side = side == 0
    half = OWN - HD

    def solo_first(block, axis):
        return jnp.where(first_side, block, jnp.roll(block, -half, axis))

    def own_order(block, axis):
        return jnp.where(first_side, block, jnp.roll(block, half, axis))

    def join(own_half, peer_half, axis):
        return jnp.where(
            first_side,
            jnp.concatenate((own_half, peer_half), axis),
            jnp.concatenate((peer_half, own_half), axis),
        )

    def half_of(block, which):
        return lax.dynamic_slice_in_dim(block, which * half, half, 0)

    query_w, key_w, value_w = (solo_first(w, 1) for w in (w_query, w_key, w_value))
    out_w = solo_first(w_out, 0)
    halves = jnp.concatenate((query_w[:, HD:], key_w[:, HD:], value_w[:, HD:]), 1)
    peer_halves, peer_out = from_partner((halves, out_w[HD:]))
    wide = []
    for n, w in enumerate((query_w, key_w, value_w)):
        wide += [w[:, :HD], join(w[:, HD:], peer_halves[:, n * half : (n + 1) * half], 1)]
    wide_w = jnp.concatenate(wide, 1)
    out_group = jnp.concatenate((out_w[:HD], join(out_w[HD:], peer_out, 0)), 0)

    unit_rows = jnp.concatenate(
        (planes, lax.dynamic_slice_in_dim(planes, side * 2 * BITS, 2 * BITS, 0)), 0
    )
    seg_row = segment[None, :]
    seg_wide = jnp.pad(segment, (32, 96), constant_values=-2)
    seg_own = jnp.where(segment < 0, -3, segment)
    group = position // 2
    heads = jnp.stack((3 * group + 2 * side, 3 * group + 1))
    selector = (heads[:, None] == jnp.arange(HEADS, dtype=jnp.int32)[None, :]).astype(F32)
    taps = jnp.dot(selector, conv_taps.T, precision=lax.Precision.HIGHEST)

    gathered = gather_rows(inputs)
    qkv = lax.dot_general(
        wide_w, gathered, (((0,), (1,)), ((), ())), preferred_element_type=F32
    ).astype(BF16)
    est, numer, dens, sign, bucket = attend(qkv, unit_rows, seg_row)
    received = from_partner(half_of(est[HD:], 1 - side).astype(BF16)).astype(F32)
    value_own = jnp.concatenate((qkv[4 * HD : 5 * HD], half_of(qkv[5 * HD :], side)), 0)
    value_pad = jnp.pad(value_own, ((0, 0), (32, 96)))
    conv = segment_conv(value_pad, toeplitz(taps), seg_wide[:, None], seg_own[None, :])
    table_sum = jnp.concatenate((est[:HD], half_of(est[HD:], side) + received), 0)
    attended = (table_sum / TABLES + conv).astype(BF16)
    out_part = scatter_rows(
        lax.dot_general(attended, out_w, (((0,), (0,)), ((), ())), preferred_element_type=F32)
    )
    residual_one = inputs.astype(F32) + out_part
    hidden_one, normed_one, inv_std_one = layer_norm_rows(residual_one, ln1_gain, ln1_bias)
    hidden_full = gather_rows(hidden_one.astype(BF16))
    preact = jnp.dot(hidden_full, w_up, preferred_element_type=F32)
    activated = jax.nn.gelu(preact, approximate=False).astype(BF16)
    ffn_part = scatter_rows(jnp.dot(activated, w_down, preferred_element_type=F32))
    residual_two = hidden_one + ffn_part
    result_rows, normed_two, inv_std_two = layer_norm_rows(residual_two, ln2_gain, ln2_bias)
    outputs = result_rows.astype(BF16)
    two_grad, ln2_gain_part, ln2_bias_part = layer_norm_back(
        cotangent.astype(F32), normed_two, inv_std_two, ln2_gain
    )
    gelu_back = jax.vjp(partial(jax.nn.gelu, approximate=False), preact)[1]
    ffn_full = gather_rows(two_grad.astype(BF16))
    act_grad = jnp.dot(ffn_full, w_down.T, preferred_element_type=F32)
    pre_grad = gelu_back(act_grad)[0].astype(BF16)
    w_down_grad = jnp.dot(activated.T, ffn_full, preferred_element_type=F32)
    w_up_grad = jnp.dot(hidden_full.T, pre_grad, preferred_element_type=F32)
    hidden_ffn = scatter_rows(jnp.dot(pre_grad, w_up.T, preferred_element_type=F32))
    one_grad, ln1_gain_part, ln1_bias_part = layer_norm_back(
        two_grad + hidden_ffn, normed_one, inv_std_one, ln1_gain
    )
    out_full = gather_rows(one_grad.astype(BF16))
    w_out_grad = own_order(jnp.dot(attended, out_full, preferred_element_type=F32), 0)
    attn_grad = lax.dot_general(
        out_group, out_full, (((1,), (1,)), ((), ())), preferred_element_type=F32
    ).astype(BF16)
    grad_own = jnp.concatenate((attn_grad[:HD], half_of(attn_grad[HD:], side)), 0)
    back = attend_back(qkv, unit_rows, seg_row, attn_grad, numer, dens, sign, bucket)
    shared = jnp.concatenate(
        [half_of(back[(2 * n + 1) * HD : (2 * n + 2) * HD], 1 - side) for n in range(3)], 0
    )
    peer_shared = from_partner(shared.astype(BF16)).astype(F32)
    grad_pad = jnp.pad(grad_own, ((0, 0), (32, 96)))
    value_conv, tap_part = conv_back(
        grad_pad, grad_own, value_pad, toeplitz(taps[:, ::-1]),
        seg_wide[:, None], seg_own[None, :], seg_wide[None, :], seg_own[:, None],
    )
    conv_part = jnp.dot(
        tap_part[:, 0, :KW].T, selector, precision=lax.Precision.HIGHEST
    )
    sums = []
    for n in range(3):
        solo = back[2 * n * HD : (2 * n + 1) * HD]
        mixed = half_of(back[(2 * n + 1) * HD : (2 * n + 2) * HD], side)
        mixed = mixed + peer_shared[n * half : (n + 1) * half]
        sums.append(jnp.concatenate((solo, mixed), 0))
    sums[2] = sums[2] + value_conv
    lows = jnp.concatenate([s.astype(BF16) for s in sums], 0)
    weight_grads = lax.dot_general(
        gathered, lows, (((0,), (1,)), ((), ())), preferred_element_type=F32
    )
    w_query_grad, w_key_grad, w_value_grad = (
        own_order(weight_grads[:, n * OWN : (n + 1) * OWN], 1) for n in range(3)
    )
    inputs_grad = one_grad + scatter_rows(
        lax.dot_general(
            lows,
            jnp.concatenate((query_w, key_w, value_w), 1),
            (((0,), (1,)), ((), ())),
            preferred_element_type=F32,
        )
    )
    w_query_grad, w_key_grad, w_value_grad, w_out_grad, w_up_grad, w_down_grad = (
        lax.psum(g.astype(BF16), "dp").astype(F32)
        for g in (w_query_grad, w_key_grad, w_value_grad, w_out_grad, w_up_grad, w_down_grad)
    )
    ln1_gain_grad, ln1_bias_grad, ln2_gain_grad, ln2_bias_grad, conv_taps_grad = lax.psum(
        (ln1_gain_part, ln1_bias_part, ln2_gain_part, ln2_bias_part, conv_part), ("dp", "mp")
    )
    return (
        outputs, inputs_grad, w_query_grad, w_key_grad, w_value_grad, conv_taps_grad, w_out_grad,
        ln1_gain_grad, ln1_bias_grad, w_up_grad, w_down_grad, ln2_gain_grad, ln2_bias_grad,
    )


def solution(mesh):
    rows = P(("dp", "mp"), None)
    cols = P(None, "mp")
    return jax.shard_map(
        on_device,
        mesh=mesh,
        in_specs=(
            rows, P("dp"), cols, cols, cols, P(), P(), P("mp", None), P(), P(),
            cols, P("mp", None), P(), P(), rows,
        ),
        out_specs=(
            rows, rows, cols, cols, cols, P(), P("mp", None), P(), P(),
            cols, P("mp", None), P(), P(),
        ),
        check_vma=False,
    )
```

```python
import math
import jax
import jax.numpy as jnp
from jax import lax
from jax.experimental import pallas as pl
from jax.experimental.pallas import tpu as pltpu
from jax.sharding import PartitionSpec as P

HEADS = 12
HD = 64
TABLES = 4
BITS = 8
KW = 65
MAXSEG = 8
CODES = 256
UNITS = 6
SOLO = 4
SPREAD = MAXSEG * HD
EXT = SPREAD + 128
LANES = 128
TILE = 256
F32 = jnp.float32
BF16 = jnp.bfloat16
VMEM_BYTES = 56 * 1024 * 1024


def nt_dot(left, right):
    return lax.dot_general(left, right, (((1,), (1,)), ((), ())), preferred_element_type=F32)


def tn_dot(left, right):
    return lax.dot_general(left, right, (((0,), (0,)), ((), ())), preferred_element_type=F32)


def nn_dot(left, right):
    return lax.dot_general(left, right, (((1,), (0,)), ((), ())), preferred_element_type=F32)


def half_sign(bit):
    rows = lax.broadcasted_iota(jnp.int32, (8, LANES), 0)
    return jnp.where((rows >> bit) & 1 == 0, 0.5, -0.5).astype(F32)


def code_factors(signs):
    pos0, neg0 = 0.5 + 0.5 * signs[0:1], 0.5 - 0.5 * signs[0:1]
    pos1, neg1 = 0.5 + 0.5 * signs[1:2], 0.5 - 0.5 * signs[1:2]
    tops = (pos0 * pos1, pos0 * neg1, neg0 * pos1, neg0 * neg1)
    picks = [half_sign(2), half_sign(1), half_sign(0)]
    mids = [0.5 + picks[n] * signs[2 + n : 3 + n] for n in range(3)]
    lows = [0.5 + picks[n] * signs[5 + n : 6 + n] for n in range(3)]
    return tops, mids, lows, picks


def code_probs(signs, out_ref, lane):
    tops, mids, lows, _ = code_factors(signs)
    mid = mids[0] * mids[1] * mids[2]
    low = lows[0] * lows[1] * lows[2]
    for top_index in range(4):
        low_top = low * tops[top_index]
        for pair in range(4):
            rows = jnp.concatenate(
                (
                    low_top * mid[2 * pair : 2 * pair + 1],
                    low_top * mid[2 * pair + 1 : 2 * pair + 2],
                ),
                axis=0,
            )
            first = top_index * 64 + pair * 16
            out_ref[first : first + 16, lane] = rows.astype(BF16)


def signs_back(signs, grads):
    tops, mids, lows, picks = code_factors(signs)
    mid = mids[0] * mids[1] * mids[2]
    low = lows[0] * lows[1] * lows[2]
    mid_rows = [jnp.broadcast_to(mid[m : m + 1], (8, LANES)) for m in range(8)]
    top_rows = [jnp.broadcast_to(tops[t], (8, LANES)) for t in range(4)]
    by_top = [None] * 4
    by_mid = [None] * 8
    for t in range(4):
        for m in range(8):
            piece = grads[t * 64 + m * 8 : t * 64 + m * 8 + 8]
            a = piece * mid_rows[m]
            b = piece * top_rows[t]
            by_top[t] = a if by_top[t] is None else by_top[t] + a
            by_mid[m] = b if by_mid[m] is None else by_mid[m] + b
    low_grad = by_top[0] * top_rows[0]
    for t in range(1, 4):
        low_grad = low_grad + by_top[t] * top_rows[t]
    top_grad = [jnp.sum(low * by_top[t], axis=0, keepdims=True) for t in range(4)]
    mid_grad = jnp.concatenate(
        [jnp.sum(low * by_mid[m], axis=0, keepdims=True) for m in range(8)], axis=0
    )
    pos0, neg0 = 0.5 + 0.5 * signs[0:1], 0.5 - 0.5 * signs[0:1]
    pos1, neg1 = 0.5 + 0.5 * signs[1:2], 0.5 - 0.5 * signs[1:2]
    out = [
        0.5 * ((top_grad[0] - top_grad[2]) * pos1 + (top_grad[1] - top_grad[3]) * neg1),
        0.5 * ((top_grad[0] - top_grad[1]) * pos0 + (top_grad[2] - top_grad[3]) * neg0),
    ]
    for grad, parts in ((mid_grad, mids), (low_grad, lows)):
        for n in range(3):
            others = parts[(n + 1) % 3] * parts[(n + 2) % 3] * picks[n]
            out.append(jnp.sum(grad * others, axis=0, keepdims=True))
    return jnp.concatenate(out, axis=0)


def split_two(value):
    high = value.astype(BF16).astype(F32)
    return high, value - high


def unit_planes(planes):
    return planes * lax.rsqrt(jnp.sum(planes * planes, axis=1, keepdims=True) + 1e-06)


def fill_spread(values, seg_row, spread_ref, lane):
    for s in range(MAXSEG):
        spread_ref[s * HD : (s + 1) * HD, lane] = jnp.where(
            seg_row == s, values, jnp.zeros_like(values)
        )


def fill_member(seg_row, spread_ref, lane):
    width = seg_row.shape[1]
    rows = lax.broadcasted_iota(jnp.int32, (128, width), 0)
    hit = jnp.logical_and(rows < 16, (rows & 7) == seg_row)
    spread_ref[SPREAD:EXT, lane] = jnp.where(hit, 1.0, 0.0).astype(BF16)


def lanes_of(index, width):
    return pl.ds(pl.multiple_of(index * width, width), width)


def masked_fold(product, seg_row):
    total = None
    for s in range(MAXSEG):
        piece = jnp.where(seg_row == s, product[s * HD : (s + 1) * HD], 0.0)
        total = piece if total is None else total + piece
    return total


def attend_kernel(
    qkv_ref, planes_ref, seg_ref,
    est_ref, numer_ref, dens_ref, sign_ref, bucket_ref,
    spread, norm, qprob, kprob, total, table,
):
    unit = pl.program_id(0)
    slot = unit // SOLO
    length = qkv_ref.shape[1]
    tiles = length // TILE
    q_rows = pl.ds(pl.multiple_of(slot * HD, HD), HD)
    k_rows = pl.ds(pl.multiple_of(2 * HD + slot * HD, HD), HD)
    v_rows = pl.ds(pl.multiple_of(4 * HD + slot * HD, HD), HD)

    @pl.when(jnp.logical_or(unit == 0, unit == SOLO))
    def _():
        def step(i, carry):
            lane = lanes_of(i, TILE)
            seg_row = seg_ref[:, lane]
            fill_spread(qkv_ref[v_rows, lane], seg_row, spread, lane)
            fill_member(seg_row, spread, lane)
            query = qkv_ref[q_rows, lane].astype(F32)
            key = qkv_ref[k_rows, lane].astype(F32)
            scale = math.sqrt(HD)
            norm[0:1, lane] = scale * lax.rsqrt(
                jnp.sum(query * query, axis=0, keepdims=True) + 1e-06
            )
            norm[1:2, lane] = scale * lax.rsqrt(jnp.sum(key * key, axis=0, keepdims=True) + 1e-06)
            est_ref[q_rows, lane] = jnp.zeros((HD, TILE), F32)
            return carry

        lax.fori_loop(0, tiles, step, 0)

    planes = unit_planes(planes_ref[pl.ds(pl.multiple_of(unit * BITS, BITS), BITS), :])
    high, rest = split_two(planes)
    middle, low = split_two(rest)
    stack = jnp.concatenate((high, middle, low), axis=0).astype(BF16)
    total[...] = jnp.zeros_like(total)

    def collect(i, carry):
        lane = lanes_of(i, TILE)
        flat_q = nn_dot(stack, qkv_ref[q_rows, lane])
        flat_k = nn_dot(stack, qkv_ref[k_rows, lane])
        sign_q = jnp.tanh((flat_q[0:8] + flat_q[8:16] + flat_q[16:24]) * norm[0:1, lane])
        sign_k = jnp.tanh((flat_k[0:8] + flat_k[8:16] + flat_k[16:24]) * norm[1:2, lane])
        sign_ref[0, 0:8, lane] = sign_q
        sign_ref[0, 8:16, lane] = sign_k
        for part in range(TILE // LANES):
            inner = slice(part * LANES, (part + 1) * LANES)
            code_probs(sign_k[:, inner], kprob, inner)
            code_probs(
                sign_q[:, inner], qprob, pl.ds(pl.multiple_of(i * TILE + part * LANES, LANES), LANES)
            )
        total[...] += nt_dot(spread[0 : SPREAD + 16, lane], kprob[...])
        return carry

    lax.fori_loop(0, tiles, collect, 0)
    mass = total[SPREAD : SPREAD + 8, :]
    mass_high, mass_low = split_two(mass)
    extra = jnp.concatenate(
        (mass_high, mass_high, mass_low, jnp.zeros((104, CODES), F32)), axis=0
    )
    table[0:SPREAD, :] = total[0:SPREAD, :].astype(BF16)
    table[SPREAD:EXT, :] = extra.astype(BF16)
    bucket_ref[0, :, 0:SPREAD] = jnp.transpose(total[0:SPREAD, :]).astype(BF16)
    bucket_ref[0, :, SPREAD:EXT] = jnp.transpose(extra).astype(BF16)

    def spend(i, carry):
        lane = lanes_of(i, TILE)
        seg_row = seg_ref[:, lane]
        product = nn_dot(table[0 : SPREAD + 32, :], qprob[:, lane])
        numer = masked_fold(product, seg_row)
        both = product[SPREAD : SPREAD + 8] + product[SPREAD + 16 : SPREAD + 24]
        which = lax.broadcasted_iota(jnp.int32, (8, TILE), 0)
        density = jnp.sum(jnp.where(which == seg_row, both, 0.0), axis=0, keepdims=True)
        numer_ref[0, :, lane] = numer
        dens_ref[0, :, lane] = density
        est_ref[q_rows, lane] += numer * (1.0 / jnp.maximum(density, 1.0))
        return carry

    lax.fori_loop(0, tiles, spend, 0)


def attend(qkv, planes, seg_row):
    length = qkv.shape[1]
    per_unit = lambda u: (u, 0, 0)
    fixed = lambda u: (0, 0)
    return pl.pallas_call(
        attend_kernel,
        grid=(UNITS,),
        in_specs=[
            pl.BlockSpec(qkv.shape, fixed),
            pl.BlockSpec(planes.shape, fixed),
            pl.BlockSpec(seg_row.shape, fixed),
        ],
        out_specs=[
            pl.BlockSpec((2 * HD, length), fixed),
            pl.BlockSpec((1, HD, length), per_unit),
            pl.BlockSpec((1, 1, length), per_unit),
            pl.BlockSpec((1, 16, length), per_unit),
            pl.BlockSpec((1, CODES, EXT), per_unit),
        ],
        out_shape=[
            jax.ShapeDtypeStruct((2 * HD, length), F32),
            jax.ShapeDtypeStruct((UNITS, HD, length), F32),
            jax.ShapeDtypeStruct((UNITS, 1, length), F32),
            jax.ShapeDtypeStruct((UNITS, 16, length), F32),
            jax.ShapeDtypeStruct((UNITS, CODES, EXT), BF16),
        ],
        scratch_shapes=[
            pltpu.VMEM((EXT, length), BF16),
            pltpu.VMEM((8, length), F32),
            pltpu.VMEM((CODES, length), BF16),
            pltpu.VMEM((CODES, TILE), BF16),
            pltpu.VMEM((SPREAD + 16, CODES), F32),
            pltpu.VMEM((EXT, CODES), BF16),
        ],
        compiler_params=pltpu.CompilerParams(vmem_limit_bytes=VMEM_BYTES),
        cost_estimate=pl.CostEstimate(
            flops=UNITS * 4 * length * CODES * SPREAD, bytes_accessed=16_000_000, transcendentals=0
        ),
        name="attend",
    )(qkv, planes, seg_row)


def attend_back_kernel(
    qkv_ref, planes_ref, seg_ref, grad_ref, numer_ref, dens_ref, sign_ref, bucket_ref,
    out_ref,
    spread, qprob, kprob, gspread, total, table, turned, gsign, proj,
):
    unit = pl.program_id(0)
    slot = unit // SOLO
    length = qkv_ref.shape[1]
    tiles = length // TILE
    q_rows = pl.ds(pl.multiple_of(slot * HD, HD), HD)
    k_rows = pl.ds(pl.multiple_of(2 * HD + slot * HD, HD), HD)
    v_rows = pl.ds(pl.multiple_of(4 * HD + slot * HD, HD), HD)

    @pl.when(jnp.logical_or(unit == 0, unit == SOLO))
    def _():
        def step(i, carry):
            lane = lanes_of(i, TILE)
            seg_row = seg_ref[:, lane]
            fill_spread(qkv_ref[v_rows, lane], seg_row, spread, lane)
            fill_member(seg_row, spread, lane)
            proj[:, lane] = jnp.zeros((2 * HD, TILE), F32)
            out_ref[v_rows, lane] = jnp.zeros((HD, TILE), F32)
            return carry

        lax.fori_loop(0, tiles, step, 0)
        gspread[SPREAD:EXT, :] = jnp.zeros((128, TILE), BF16)

    total[...] = jnp.zeros_like(total)

    def first(i, carry):
        lane = lanes_of(i, TILE)
        seg_row = seg_ref[:, lane]
        density = dens_ref[0, :, lane]
        inverse = 1.0 / jnp.maximum(density, 1.0)
        est_grad = grad_ref[q_rows, lane].astype(F32) * (1.0 / TABLES)
        num_grad = (est_grad * inverse).astype(BF16)
        fill_spread(num_grad, seg_row, gspread, slice(0, TILE))
        inner_sum = jnp.sum(est_grad * numer_ref[0, :, lane], axis=0, keepdims=True)
        dens_grad = jnp.where(density > 1.0, -inner_sum * inverse * inverse, 0.0)
        which = lax.broadcasted_iota(jnp.int32, (8, TILE), 0)
        high, low = split_two(jnp.where(which == seg_row, dens_grad, 0.0))
        gspread[SPREAD : SPREAD + 32, :] = jnp.concatenate(
            (high, low, high, jnp.zeros_like(high)), axis=0
        ).astype(BF16)
        collected = nn_dot(bucket_ref[0], gspread[...])
        for part in range(TILE // LANES):
            inner = slice(part * LANES, (part + 1) * LANES)
            outer = pl.ds(pl.multiple_of(i * TILE + part * LANES, LANES), LANES)
            sign_q = sign_ref[0, 0:8, outer]
            code_probs(sign_q, qprob, inner)
            gsign[0:8, outer] = signs_back(sign_q, collected[:, inner])
        total[...] += nt_dot(gspread[0 : SPREAD + 16, :], qprob[...])
        return carry

    lax.fori_loop(0, tiles, first, 0)
    mass_grad = total[SPREAD : SPREAD + 8, :] + total[SPREAD + 8 : SPREAD + 16, :]
    high, low = split_two(mass_grad)
    extra = jnp.concatenate((high, low, jnp.zeros((112, CODES), F32)), axis=0)
    table[...] = total[0:SPREAD, :].astype(BF16)
    turned[:, 0:SPREAD] = jnp.transpose(total[0:SPREAD, :]).astype(BF16)
    turned[:, SPREAD:EXT] = jnp.transpose(extra).astype(BF16)

    planes = unit_planes(planes_ref[pl.ds(pl.multiple_of(unit * BITS, BITS), BITS), :])
    plane_high, plane_low = split_two(planes)
    stack = jnp.concatenate((plane_high, plane_low, plane_high, jnp.zeros_like(plane_high)), axis=0)
    stack = stack.astype(BF16)

    def second(i, carry):
        lane = lanes_of(i, TILE)
        seg_row = seg_ref[:, lane]
        for part in range(TILE // LANES):
            inner = slice(part * LANES, (part + 1) * LANES)
            outer = pl.ds(pl.multiple_of(i * TILE + part * LANES, LANES), LANES)
            code_probs(sign_ref[0, 8:16, outer], kprob, inner)
        out_ref[v_rows, lane] += masked_fold(nn_dot(table[...], kprob[...]), seg_row)
        collected = nn_dot(turned[...], spread[:, lane])
        for part in range(TILE // LANES):
            inner = slice(part * LANES, (part + 1) * LANES)
            outer = pl.ds(pl.multiple_of(i * TILE + part * LANES, LANES), LANES)
            gsign[8:16, outer] = signs_back(sign_ref[0, 8:16, outer], collected[:, inner])
        signs = sign_ref[0, :, lane]
        flat = gsign[:, lane] * (1.0 - signs * signs)
        high, low = split_two(flat)
        for side in range(2):
            rows = slice(8 * side, 8 * side + 8)
            pieces = jnp.concatenate(
                (high[rows], high[rows], low[rows], jnp.zeros((8, TILE), F32)), axis=0
            ).astype(BF16)
            proj[side * HD : (side + 1) * HD, lane] += tn_dot(stack, pieces)
        return carry

    lax.fori_loop(0, tiles, second, 0)

    @pl.when(jnp.logical_or(unit == SOLO - 1, unit == UNITS - 1))
    def _():
        def step(i, carry):
            lane = lanes_of(i, TILE)
            for side, rows in ((0, q_rows), (1, k_rows)):
                vec = qkv_ref[rows, lane].astype(F32)
                inverse = lax.rsqrt(jnp.sum(vec * vec, axis=0, keepdims=True) + 1e-06)
                unit_vec = vec * inverse
                grad = proj[side * HD : (side + 1) * HD, lane]
                along = jnp.sum(unit_vec * grad, axis=0, keepdims=True)
                out_ref[rows, lane] = math.sqrt(HD) * inverse * (grad - unit_vec * along)
            return carry

        lax.fori_loop(0, tiles, step, 0)


def attend_back(qkv, planes, seg_row, grad, numer, dens, sign, bucket):
    length = qkv.shape[1]
    per_unit = lambda u: (u, 0, 0)
    fixed = lambda u: (0, 0)
    return pl.pallas_call(
        attend_back_kernel,
        grid=(UNITS,),
        in_specs=[
            pl.BlockSpec(qkv.shape, fixed),
            pl.BlockSpec(planes.shape, fixed),
            pl.BlockSpec(seg_row.shape, fixed),
            pl.BlockSpec(grad.shape, fixed),
            pl.BlockSpec((1, HD, length), per_unit),
            pl.BlockSpec((1, 1, length), per_unit),
            pl.BlockSpec((1, 16, length), per_unit),
            pl.BlockSpec((1, CODES, EXT), per_unit),
        ],
        out_specs=pl.BlockSpec((6 * HD, length), fixed),
        out_shape=jax.ShapeDtypeStruct((6 * HD, length), F32),
        scratch_shapes=[
            pltpu.VMEM((EXT, length), BF16),
            pltpu.VMEM((CODES, TILE), BF16),
            pltpu.VMEM((CODES, TILE), BF16),
            pltpu.VMEM((EXT, TILE), BF16),
            pltpu.VMEM((SPREAD + 16, CODES), F32),
            pltpu.VMEM((SPREAD, CODES), BF16),
            pltpu.VMEM((CODES, EXT), BF16),
            pltpu.VMEM((16, length), F32),
            pltpu.VMEM((2 * HD, length), F32),
        ],
        compiler_params=pltpu.CompilerParams(vmem_limit_bytes=VMEM_BYTES),
        cost_estimate=pl.CostEstimate(
            flops=UNITS * 8 * length * CODES * SPREAD, bytes_accessed=16_000_000, transcendentals=0
        ),
        name="attend_back",
    )(qkv, planes, seg_row, grad, numer, dens, sign, bucket)


SPAN = 192
OWN = 96
BLOCKS = ((0, HD), (HD, OWN))


def toeplitz(taps):
    row = jnp.pad(taps, ((0, 0), (0, SPAN + 1 - KW)))
    flat = jnp.tile(row, (1, LANES))[:, : LANES * SPAN]
    return jnp.swapaxes(flat.reshape(2, LANES, SPAN), 1, 2)


def band_product(pad_ref, band_ref, lane_wide, mask, out_ref, lane):
    for h, (low_row, high_row) in enumerate(BLOCKS):
        band = jnp.where(mask, band_ref[h], 0.0)
        high, low = split_two(band)
        rows = pad_ref[low_row:high_row, lane_wide]
        out_ref[low_row:high_row, lane] = nn_dot(rows, high.astype(BF16)) + nn_dot(
            rows, low.astype(BF16)
        )


def conv_kernel(pad_ref, band_ref, col_ref, seg_ref, out_ref):
    tiles = out_ref.shape[1] // LANES

    def step(i, carry):
        lane = lanes_of(i, LANES)
        start = pl.multiple_of(i * LANES, LANES)
        wide = pl.ds(start, SPAN)
        mask = col_ref[wide, :] == seg_ref[:, lane]
        band_product(pad_ref, band_ref, wide, mask, out_ref, lane)
        return carry

    lax.fori_loop(0, tiles, step, 0)


def segment_conv(padded, band, seg_col, seg_own):
    length = seg_own.shape[1]
    return pl.pallas_call(
        conv_kernel,
        out_shape=jax.ShapeDtypeStruct((OWN, length), F32),
        compiler_params=pltpu.CompilerParams(vmem_limit_bytes=VMEM_BYTES),
        cost_estimate=pl.CostEstimate(
            flops=8 * length * SPAN * HD, bytes_accessed=3_000_000, transcendentals=0
        ),
        name="segment_conv",
    )(padded, band, seg_col, seg_own)


def conv_back_kernel(gpad_ref, grad_ref, vpad_ref, band_ref, col_ref, seg_ref, segt_ref, colt_ref,
                     out_ref, tap_ref, corr):
    tiles = out_ref.shape[1] // LANES
    corr[...] = jnp.zeros_like(corr)

    def step(i, carry):
        lane = lanes_of(i, LANES)
        start = pl.multiple_of(i * LANES, LANES)
        wide = pl.ds(start, SPAN)
        twice = pl.ds(start, 2 * LANES)
        mask = col_ref[wide, :] == seg_ref[:, lane]
        band_product(gpad_ref, band_ref, wide, mask, out_ref, lane)
        mask_turned = colt_ref[lane, :] == segt_ref[:, twice]
        for h, (low_row, high_row) in enumerate(BLOCKS):
            match = tn_dot(grad_ref[low_row:high_row, lane], vpad_ref[low_row:high_row, twice])
            corr[h] += jnp.where(mask_turned, match, 0.0)
        return carry

    lax.fori_loop(0, tiles, step, 0)
    row = lax.broadcasted_iota(jnp.int32, (LANES, 2 * LANES), 0)
    for h in range(2):
        skew = corr[h]
        for bit in range(7):
            moved = pltpu.roll(skew, 2 * LANES - (1 << bit), 1)
            skew = jnp.where((row >> bit) & 1 == 1, moved, skew)
        tap_ref[h] = jnp.sum(skew, axis=0, keepdims=True)


def conv_back(gpad, grad, vpad, band, seg_col, seg_own, seg_wide, col_own):
    length = seg_own.shape[1]
    return pl.pallas_call(
        conv_back_kernel,
        out_shape=(
            jax.ShapeDtypeStruct((OWN, length), F32),
            jax.ShapeDtypeStruct((2, 1, 2 * LANES), F32),
        ),
        scratch_shapes=[pltpu.VMEM((2, LANES, 2 * LANES), F32)],
        compiler_params=pltpu.CompilerParams(vmem_limit_bytes=VMEM_BYTES),
        cost_estimate=pl.CostEstimate(
            flops=16 * length * SPAN * HD, bytes_accessed=4_000_000, transcendentals=0
        ),
        name="conv_back",
    )(gpad, grad, vpad, band, seg_col, seg_own, seg_wide, col_own)


def norm_rows(values):
    center = values - jnp.mean(values, axis=1, keepdims=True)
    inverse = lax.rsqrt(jnp.mean(center * center, axis=1, keepdims=True) + 1e-05)
    return center * inverse, inverse


def norm_back(upstream, normed, inverse, gain):
    scaled = upstream * gain
    inner = (
        scaled
        - jnp.mean(scaled, axis=1, keepdims=True)
        - normed * jnp.mean(scaled * normed, axis=1, keepdims=True)
    )
    return inner * inverse


def gelu_pair(value):
    cdf = 0.5 + 0.5 * lax.erf(value * math.sqrt(0.5))
    pdf = jnp.exp(-0.5 * value * value) * (1.0 / math.sqrt(2.0 * math.pi))
    return value * cdf, cdf + value * pdf


def column_sum(values):
    return jnp.sum(values, axis=0, keepdims=True)


def middle_kernel(
    att_ref, x_ref, cot_ref, out_w_ref, up_ref, down_ref, scale_ref,
    result_ref, hidden_low_ref, ffn_low_ref, out_low_ref, one_ref, attn_ref, part_ref,
    hidden, normed, inverse, acc, slope, two,
):
    step = pl.program_id(0)
    parts = pl.num_programs(0) // 2
    block = step % parts

    @pl.when(step == 0)
    def _():
        projected = tn_dot(att_ref[...], out_w_ref[...])
        unit, inv = norm_rows(x_ref[...].astype(F32) + projected)
        value = unit * scale_ref[0:1] + scale_ref[1:2]
        normed[...] = unit
        inverse[...] = inv
        hidden[...] = value
        hidden_low_ref[...] = value.astype(BF16)
        acc[...] = jnp.zeros_like(acc)

    @pl.when(step < parts)
    def _():
        active, lean = gelu_pair(nn_dot(hidden_low_ref[...], up_ref[0]))
        slope[block] = lean
        acc[...] += nn_dot(active.astype(BF16), down_ref[0])

    @pl.when(step == parts - 1)
    def _():
        unit, inv = norm_rows(hidden[...] + acc[...])
        result_ref[...] = (unit * scale_ref[2:3] + scale_ref[3:4]).astype(BF16)
        upstream = cot_ref[...].astype(F32)
        part_ref[2:3] = column_sum(upstream * unit)
        part_ref[3:4] = column_sum(upstream)
        grad = norm_back(upstream, unit, inv, scale_ref[2:3])
        two[...] = grad
        ffn_low_ref[...] = grad.astype(BF16)
        acc[...] = jnp.zeros_like(acc)

    @pl.when(step >= parts)
    def _():
        pre_grad = (nt_dot(ffn_low_ref[...], down_ref[0]) * slope[block]).astype(BF16)
        acc[...] += nt_dot(pre_grad, up_ref[0])

    @pl.when(step == 2 * parts - 1)
    def _():
        upstream = two[...] + acc[...]
        unit = normed[...]
        part_ref[0:1] = column_sum(upstream * unit)
        part_ref[1:2] = column_sum(upstream)
        part_ref[4:8] = jnp.zeros((4, part_ref.shape[1]), F32)
        grad = norm_back(upstream, unit, inverse[...], scale_ref[0:1])
        one_ref[...] = grad
        out_low_ref[...] = grad.astype(BF16)
        attn_ref[...] = nt_dot(out_w_ref[...], grad.astype(BF16)).astype(BF16)


def middle(att, x, cot, out_w, up, down, scale):
    rows, width = x.shape
    parts, _, hidden_units = up.shape
    fixed = lambda i: (0, 0)
    each = lambda i: (i % parts, 0, 0)
    full = lambda array: pl.BlockSpec(array.shape, fixed)
    row_low = jax.ShapeDtypeStruct((rows, width), BF16)
    outs = (
        row_low, row_low, row_low, row_low,
        jax.ShapeDtypeStruct((rows, width), F32),
        jax.ShapeDtypeStruct(att.shape, BF16),
        jax.ShapeDtypeStruct((8, width), F32),
    )
    return pl.pallas_call(
        middle_kernel,
        grid=(2 * parts,),
        in_specs=[
            full(att), full(x), full(cot), full(out_w),
            pl.BlockSpec((1,) + up.shape[1:], each),
            pl.BlockSpec((1,) + down.shape[1:], each),
            full(scale),
        ],
        out_specs=[full(o) for o in outs],
        out_shape=outs,
        scratch_shapes=[
            pltpu.VMEM((rows, width), F32),
            pltpu.VMEM((rows, width), F32),
            pltpu.VMEM((rows, 1), F32),
            pltpu.VMEM((rows, width), F32),
            pltpu.VMEM((parts, rows, hidden_units), F32),
            pltpu.VMEM((rows, width), F32),
        ],
        compiler_params=pltpu.CompilerParams(vmem_limit_bytes=VMEM_BYTES),
        cost_estimate=pl.CostEstimate(
            flops=8 * rows * width * parts * hidden_units, bytes_accessed=26_000_000,
            transcendentals=0,
        ),
        name="middle",
    )(att, x, cot, out_w, up, down, scale)


def ffn_grad_kernel(hidden_ref, ffn_ref, out_ref, att_ref, up_ref, down_ref, grad_ref, acc):
    step = pl.program_id(0)
    units = up_ref.shape[1]

    @pl.when(step == 0)
    def _():
        acc[...] = jnp.zeros_like(acc)

    active, lean = gelu_pair(nn_dot(hidden_ref[...], up_ref[...]))
    pre_grad = (nt_dot(ffn_ref[...], down_ref[...]) * lean).astype(BF16)
    acc[0:units, :] += tn_dot(pre_grad, hidden_ref[...])
    acc[units : 2 * units, :] += tn_dot(active.astype(BF16), ffn_ref[...])
    acc[2 * units : 2 * units + OWN, :] += nn_dot(att_ref[...], out_ref[...])

    @pl.when(step == pl.num_programs(0) - 1)
    def _():
        grad_ref[...] = acc[...].astype(BF16)


def ffn_grad(hidden_full, ffn_full, out_full, attended, up, down):
    length, width = hidden_full.shape
    units = up.shape[1]
    total = 2 * units + OWN
    tile = 256
    rows = lambda i: (i, 0)
    fixed = lambda i: (0, 0)
    return pl.pallas_call(
        ffn_grad_kernel,
        grid=(length // tile,),
        in_specs=[
            pl.BlockSpec((tile, width), rows),
            pl.BlockSpec((tile, width), rows),
            pl.BlockSpec((tile, width), rows),
            pl.BlockSpec((OWN, tile), lambda i: (0, i)),
            pl.BlockSpec(up.shape, fixed),
            pl.BlockSpec(down.shape, fixed),
        ],
        out_specs=pl.BlockSpec((total, width), fixed),
        out_shape=jax.ShapeDtypeStruct((total, width), BF16),
        scratch_shapes=[pltpu.VMEM((total, width), F32)],
        compiler_params=pltpu.CompilerParams(vmem_limit_bytes=VMEM_BYTES),
        cost_estimate=pl.CostEstimate(
            flops=8 * length * width * units, bytes_accessed=12_000_000, transcendentals=0
        ),
        name="ffn_grad",
    )(hidden_full, ffn_full, out_full, attended, up, down)


def from_partner(block):
    count = lax.axis_size("mp")
    route = [(n, n ^ 1) for n in range(count)]
    return lax.ppermute(block, "mp", route)


def gather_rows(rows):
    return lax.all_gather(rows, "mp", axis=0, tiled=True)


def sum_blocks(grads):
    rows = grads.shape[0]
    step = 8 * lax.axis_size("dp")
    padded = jnp.pad(grads, ((0, -rows % step), (0, 0)))
    part = lax.psum_scatter(padded, "dp", scatter_dimension=0, tiled=True)
    return lax.all_gather(part, "dp", axis=0, tiled=True)[:rows]


def on_device(
    inputs, segment, w_query, w_key, w_value, planes, conv_taps, w_out,
    ln1_gain, ln1_bias, w_up, w_down, ln2_gain, ln2_bias, cotangent,
):
    position = lax.axis_index("mp")
    count = lax.axis_size("mp")
    side = position % 2
    first_side = side == 0
    half = OWN - HD
    rows = inputs.shape[0]

    def solo_first(block, axis):
        return jnp.where(first_side, block, jnp.roll(block, -half, axis))

    def own_order(block, axis):
        return jnp.where(first_side, block, jnp.roll(block, half, axis))

    def join(own_half, peer_half, axis):
        return jnp.where(
            first_side,
            jnp.concatenate((own_half, peer_half), axis),
            jnp.concatenate((peer_half, own_half), axis),
        )

    def half_of(block, which):
        return lax.dynamic_slice_in_dim(block, which * half, half, 0)

    query_w, key_w, value_w = (solo_first(w, 1) for w in (w_query, w_key, w_value))
    out_w = solo_first(w_out, 0)
    halves = jnp.concatenate((query_w[:, HD:], key_w[:, HD:], value_w[:, HD:]), 1)
    peer_halves, peer_out = from_partner((halves, out_w[HD:]))
    wide = []
    for n, w in enumerate((query_w, key_w, value_w)):
        wide += [w[:, :HD], join(w[:, HD:], peer_halves[:, n * half : (n + 1) * half], 1)]
    wide_w = jnp.concatenate(wide, 1)
    out_group = jnp.concatenate((out_w[:HD], join(out_w[HD:], peer_out, 0)), 0)

    unit_rows = jnp.concatenate(
        (planes, lax.dynamic_slice_in_dim(planes, side * 2 * BITS, 2 * BITS, 0)), 0
    )
    seg_row = segment[None, :]
    seg_wide = jnp.pad(segment, (32, 96), constant_values=-2)
    seg_own = jnp.where(segment < 0, -3, segment)
    group = position // 2
    heads = jnp.stack((3 * group + 2 * side, 3 * group + 1))
    selector = (heads[:, None] == jnp.arange(HEADS, dtype=jnp.int32)[None, :]).astype(F32)
    taps = jnp.dot(selector, conv_taps.T, precision=lax.Precision.HIGHEST)

    gathered = gather_rows(inputs)
    out_all = gather_rows(out_group)
    up_all = gather_rows(w_up[None])
    down_all = gather_rows(w_down[None])
    qkv = lax.dot_general(
        wide_w, gathered, (((0,), (1,)), ((), ())), preferred_element_type=F32
    ).astype(BF16)
    value_own = jnp.concatenate((qkv[4 * HD : 5 * HD], half_of(qkv[5 * HD :], side)), 0)
    value_pad = jnp.pad(value_own, ((0, 0), (32, 96)))
    conv = segment_conv(value_pad, toeplitz(taps), seg_wide[:, None], seg_own[None, :])
    est, numer, dens, sign, bucket = attend(qkv, unit_rows, seg_row)
    conv_wide = jnp.concatenate(
        (conv[:HD], join(conv[HD:], jnp.zeros_like(conv[HD:]), 0)), 0
    )
    sent = (est / TABLES + conv_wide).astype(BF16)
    att = lax.all_to_all(
        jnp.swapaxes(sent.reshape(2 * HD, count, rows), 0, 1), "mp", 0, 0
    ).reshape(2 * HD * count, rows)
    scale = jnp.stack((ln1_gain, ln1_bias, ln2_gain, ln2_bias) * 2)
    outputs, hidden_low, ffn_low, out_low, one_grad, attn_part, norm_part = middle(
        att, inputs, cotangent, out_all, up_all, down_all, scale
    )
    attn_all = lax.all_to_all(attn_part.reshape(count, 2 * HD, rows), "mp", 0, 0)
    attn_grad = jnp.swapaxes(attn_all, 0, 1).reshape(2 * HD, rows * count)
    received = from_partner(half_of(sent[HD:], 1 - side)).astype(F32)
    mixed = (half_of(sent[HD:], side).astype(F32) + received).astype(BF16)
    attended = jnp.concatenate((sent[:HD], mixed), 0)
    hidden_full = gather_rows(hidden_low)
    ffn_full = gather_rows(ffn_low)
    out_full = gather_rows(out_low)

    grad_own = jnp.concatenate((attn_grad[:HD], half_of(attn_grad[HD:], side)), 0)
    grad_pad = jnp.pad(grad_own, ((0, 0), (32, 96)))
    value_conv, tap_part = conv_back(
        grad_pad, grad_own, value_pad, toeplitz(taps[:, ::-1]),
        seg_wide[:, None], seg_own[None, :], seg_wide[None, :], seg_own[:, None],
    )
    conv_part = jnp.dot(
        tap_part[:, 0, :KW].T, selector, precision=lax.Precision.HIGHEST
    )
    back = attend_back(qkv, unit_rows, seg_row, attn_grad, numer, dens, sign, bucket)
    ffn_sums = sum_blocks(ffn_grad(hidden_full, ffn_full, out_full, attended, w_up, w_down))
    shared = jnp.concatenate(
        [half_of(back[(2 * n + 1) * HD : (2 * n + 2) * HD], 1 - side) for n in range(3)], 0
    )
    peer_shared = from_partner(shared.astype(BF16)).astype(F32)
    sums = []
    for n in range(3):
        solo = back[2 * n * HD : (2 * n + 1) * HD]
        mixed = half_of(back[(2 * n + 1) * HD : (2 * n + 2) * HD], side)
        mixed = mixed + peer_shared[n * half : (n + 1) * half]
        sums.append(jnp.concatenate((solo, mixed), 0))
    sums[2] = sums[2] + value_conv
    lows = jnp.concatenate([s.astype(BF16) for s in sums], 0)
    weight_grads = sum_blocks(
        lax.dot_general(
            lows, gathered, (((1,), (0,)), ((), ())), preferred_element_type=F32
        ).astype(BF16)
    ).astype(F32).T
    w_query_grad, w_key_grad, w_value_grad = (
        own_order(weight_grads[:, n * OWN : (n + 1) * OWN], 1) for n in range(3)
    )
    inputs_part = lax.dot_general(
        lows,
        jnp.concatenate((query_w, key_w, value_w), 1),
        (((0,), (1,)), ((), ())),
        preferred_element_type=F32,
    ).astype(BF16)
    inputs_grad = one_grad + lax.psum_scatter(
        inputs_part, "mp", scatter_dimension=0, tiled=True
    ).astype(F32)
    units = w_up.shape[1]
    w_up_grad = ffn_sums[:units].astype(F32).T
    w_down_grad = ffn_sums[units : 2 * units].astype(F32)
    w_out_grad = own_order(ffn_sums[2 * units :].astype(F32), 0)
    norm_grads, conv_taps_grad = lax.psum((norm_part, conv_part), ("dp", "mp"))
    return (
        outputs, inputs_grad, w_query_grad, w_key_grad, w_value_grad, conv_taps_grad, w_out_grad,
        norm_grads[0], norm_grads[1], w_up_grad, w_down_grad, norm_grads[2], norm_grads[3],
    )


def solution(mesh):
    rows = P(("dp", "mp"), None)
    cols = P(None, "mp")
    return jax.shard_map(
        on_device,
        mesh=mesh,
        in_specs=(
            rows, P("dp"), cols, cols, cols, P(), P(), P("mp", None), P(), P(),
            cols, P("mp", None), P(), P(), rows,
        ),
        out_specs=(
            rows, rows, cols, cols, cols, P(), P("mp", None), P(), P(),
            cols, P("mp", None), P(), P(),
        ),
        check_vma=False,
    )
```

```python
import math
import jax
import jax.numpy as jnp
from jax import lax
from jax.experimental import pallas as pl
from jax.experimental.pallas import tpu as pltpu
from jax.sharding import PartitionSpec as P

HEADS = 12
HD = 64
TABLES = 4
BITS = 8
KW = 65
MAXSEG = 8
CODES = 256
UNITS = 6
SOLO = 4
SPREAD = MAXSEG * HD
EXT = SPREAD + 128
LANES = 128
TILE = 256
F32 = jnp.float32
BF16 = jnp.bfloat16
VMEM_BYTES = 56 * 1024 * 1024


def nt_dot(left, right):
    return lax.dot_general(left, right, (((1,), (1,)), ((), ())), preferred_element_type=F32)


def tn_dot(left, right):
    return lax.dot_general(left, right, (((0,), (0,)), ((), ())), preferred_element_type=F32)


def nn_dot(left, right):
    return lax.dot_general(left, right, (((1,), (0,)), ((), ())), preferred_element_type=F32)


def half_sign(bit):
    rows = lax.broadcasted_iota(jnp.int32, (8, LANES), 0)
    return jnp.where((rows >> bit) & 1 == 0, 0.5, -0.5).astype(F32)


def code_factors(signs):
    pos0, neg0 = 0.5 + 0.5 * signs[0:1], 0.5 - 0.5 * signs[0:1]
    pos1, neg1 = 0.5 + 0.5 * signs[1:2], 0.5 - 0.5 * signs[1:2]
    tops = (pos0 * pos1, pos0 * neg1, neg0 * pos1, neg0 * neg1)
    picks = [half_sign(2), half_sign(1), half_sign(0)]
    mids = [0.5 + picks[n] * signs[2 + n : 3 + n] for n in range(3)]
    lows = [0.5 + picks[n] * signs[5 + n : 6 + n] for n in range(3)]
    return tops, mids, lows, picks


def code_probs(signs, out_ref, lane):
    tops, mids, lows, _ = code_factors(signs)
    mid = mids[0] * mids[1] * mids[2]
    low = lows[0] * lows[1] * lows[2]
    for top_index in range(4):
        low_top = low * tops[top_index]
        for pair in range(4):
            rows = jnp.concatenate(
                (
                    low_top * mid[2 * pair : 2 * pair + 1],
                    low_top * mid[2 * pair + 1 : 2 * pair + 2],
                ),
                axis=0,
            )
            first = top_index * 64 + pair * 16
            out_ref[first : first + 16, lane] = rows.astype(BF16)


def signs_back(signs, grads):
    tops, mids, lows, picks = code_factors(signs)
    mid = mids[0] * mids[1] * mids[2]
    low = lows[0] * lows[1] * lows[2]
    mid_rows = [jnp.broadcast_to(mid[m : m + 1], (8, LANES)) for m in range(8)]
    top_rows = [jnp.broadcast_to(tops[t], (8, LANES)) for t in range(4)]
    by_top = [None] * 4
    by_mid = [None] * 8
    for t in range(4):
        for m in range(8):
            piece = grads[t * 64 + m * 8 : t * 64 + m * 8 + 8]
            a = piece * mid_rows[m]
            b = piece * top_rows[t]
            by_top[t] = a if by_top[t] is None else by_top[t] + a
            by_mid[m] = b if by_mid[m] is None else by_mid[m] + b
    low_grad = by_top[0] * top_rows[0]
    for t in range(1, 4):
        low_grad = low_grad + by_top[t] * top_rows[t]
    top_grad = [jnp.sum(low * by_top[t], axis=0, keepdims=True) for t in range(4)]
    mid_grad = jnp.concatenate(
        [jnp.sum(low * by_mid[m], axis=0, keepdims=True) for m in range(8)], axis=0
    )
    pos0, neg0 = 0.5 + 0.5 * signs[0:1], 0.5 - 0.5 * signs[0:1]
    pos1, neg1 = 0.5 + 0.5 * signs[1:2], 0.5 - 0.5 * signs[1:2]
    out = [
        0.5 * ((top_grad[0] - top_grad[2]) * pos1 + (top_grad[1] - top_grad[3]) * neg1),
        0.5 * ((top_grad[0] - top_grad[1]) * pos0 + (top_grad[2] - top_grad[3]) * neg0),
    ]
    for grad, parts in ((mid_grad, mids), (low_grad, lows)):
        for n in range(3):
            others = parts[(n + 1) % 3] * parts[(n + 2) % 3] * picks[n]
            out.append(jnp.sum(grad * others, axis=0, keepdims=True))
    return jnp.concatenate(out, axis=0)


def split_two(value):
    high = value.astype(BF16).astype(F32)
    return high, value - high


def unit_planes(planes):
    return planes * lax.rsqrt(jnp.sum(planes * planes, axis=1, keepdims=True) + 1e-06)


def fill_spread(values, seg_row, spread_ref, lane):
    for s in range(MAXSEG):
        spread_ref[s * HD : (s + 1) * HD, lane] = jnp.where(
            seg_row == s, values, jnp.zeros_like(values)
        )


def fill_member(seg_row, spread_ref, lane):
    width = seg_row.shape[1]
    rows = lax.broadcasted_iota(jnp.int32, (128, width), 0)
    hit = jnp.logical_and(rows < 16, (rows & 7) == seg_row)
    spread_ref[SPREAD:EXT, lane] = jnp.where(hit, 1.0, 0.0).astype(BF16)


def lanes_of(index, width):
    return pl.ds(pl.multiple_of(index * width, width), width)


def masked_fold(product, seg_row):
    total = None
    for s in range(MAXSEG):
        piece = jnp.where(seg_row == s, product[s * HD : (s + 1) * HD], 0.0)
        total = piece if total is None else total + piece
    return total


def attend_kernel(
    qkv_ref, planes_ref, seg_ref,
    est_ref, numer_ref, dens_ref, sign_ref, bucket_ref,
    spread, norm, qprob, kprob, total, table,
):
    unit = pl.program_id(0)
    slot = unit // SOLO
    length = qkv_ref.shape[1]
    tiles = length // TILE
    q_rows = pl.ds(pl.multiple_of(slot * HD, HD), HD)
    k_rows = pl.ds(pl.multiple_of(2 * HD + slot * HD, HD), HD)
    v_rows = pl.ds(pl.multiple_of(4 * HD + slot * HD, HD), HD)

    @pl.when(jnp.logical_or(unit == 0, unit == SOLO))
    def _():
        def step(i, carry):
            lane = lanes_of(i, TILE)
            seg_row = seg_ref[:, lane]
            fill_spread(qkv_ref[v_rows, lane], seg_row, spread, lane)
            fill_member(seg_row, spread, lane)
            query = qkv_ref[q_rows, lane].astype(F32)
            key = qkv_ref[k_rows, lane].astype(F32)
            scale = math.sqrt(HD)
            norm[0:1, lane] = scale * lax.rsqrt(
                jnp.sum(query * query, axis=0, keepdims=True) + 1e-06
            )
            norm[1:2, lane] = scale * lax.rsqrt(jnp.sum(key * key, axis=0, keepdims=True) + 1e-06)
            est_ref[q_rows, lane] = jnp.zeros((HD, TILE), F32)
            return carry

        lax.fori_loop(0, tiles, step, 0)

    planes = unit_planes(planes_ref[pl.ds(pl.multiple_of(unit * BITS, BITS), BITS), :])
    high, rest = split_two(planes)
    middle, low = split_two(rest)
    stack = jnp.concatenate((high, middle, low), axis=0).astype(BF16)
    total[...] = jnp.zeros_like(total)

    def collect(i, carry):
        lane = lanes_of(i, TILE)
        flat_q = nn_dot(stack, qkv_ref[q_rows, lane])
        flat_k = nn_dot(stack, qkv_ref[k_rows, lane])
        sign_q = jnp.tanh((flat_q[0:8] + flat_q[8:16] + flat_q[16:24]) * norm[0:1, lane])
        sign_k = jnp.tanh((flat_k[0:8] + flat_k[8:16] + flat_k[16:24]) * norm[1:2, lane])
        sign_ref[0, 0:8, lane] = sign_q
        sign_ref[0, 8:16, lane] = sign_k
        for part in range(TILE // LANES):
            inner = slice(part * LANES, (part + 1) * LANES)
            code_probs(sign_k[:, inner], kprob, inner)
            code_probs(
                sign_q[:, inner], qprob, pl.ds(pl.multiple_of(i * TILE + part * LANES, LANES), LANES)
            )
        total[...] += nt_dot(spread[0 : SPREAD + 16, lane], kprob[...])
        return carry

    lax.fori_loop(0, tiles, collect, 0)
    mass = total[SPREAD : SPREAD + 8, :]
    mass_high, mass_low = split_two(mass)
    extra = jnp.concatenate(
        (mass_high, mass_high, mass_low, jnp.zeros((104, CODES), F32)), axis=0
    )
    table[0:SPREAD, :] = total[0:SPREAD, :].astype(BF16)
    table[SPREAD:EXT, :] = extra.astype(BF16)
    bucket_ref[0, :, 0:SPREAD] = jnp.transpose(total[0:SPREAD, :]).astype(BF16)
    bucket_ref[0, :, SPREAD:EXT] = jnp.transpose(extra).astype(BF16)

    def spend(i, carry):
        lane = lanes_of(i, TILE)
        seg_row = seg_ref[:, lane]
        product = nn_dot(table[0 : SPREAD + 32, :], qprob[:, lane])
        numer = masked_fold(product, seg_row)
        both = product[SPREAD : SPREAD + 8] + product[SPREAD + 16 : SPREAD + 24]
        which = lax.broadcasted_iota(jnp.int32, (8, TILE), 0)
        density = jnp.sum(jnp.where(which == seg_row, both, 0.0), axis=0, keepdims=True)
        numer_ref[0, :, lane] = numer
        dens_ref[0, :, lane] = density
        est_ref[q_rows, lane] += numer * (1.0 / jnp.maximum(density, 1.0))
        return carry

    lax.fori_loop(0, tiles, spend, 0)


def attend(qkv, planes, seg_row):
    length = qkv.shape[1]
    per_unit = lambda u: (u, 0, 0)
    fixed = lambda u: (0, 0)
    return pl.pallas_call(
        attend_kernel,
        grid=(UNITS,),
        in_specs=[
            pl.BlockSpec(qkv.shape, fixed),
            pl.BlockSpec(planes.shape, fixed),
            pl.BlockSpec(seg_row.shape, fixed),
        ],
        out_specs=[
            pl.BlockSpec((2 * HD, length), fixed),
            pl.BlockSpec((1, HD, length), per_unit),
            pl.BlockSpec((1, 1, length), per_unit),
            pl.BlockSpec((1, 16, length), per_unit),
            pl.BlockSpec((1, CODES, EXT), per_unit),
        ],
        out_shape=[
            jax.ShapeDtypeStruct((2 * HD, length), F32),
            jax.ShapeDtypeStruct((UNITS, HD, length), F32),
            jax.ShapeDtypeStruct((UNITS, 1, length), F32),
            jax.ShapeDtypeStruct((UNITS, 16, length), F32),
            jax.ShapeDtypeStruct((UNITS, CODES, EXT), BF16),
        ],
        scratch_shapes=[
            pltpu.VMEM((EXT, length), BF16),
            pltpu.VMEM((8, length), F32),
            pltpu.VMEM((CODES, length), BF16),
            pltpu.VMEM((CODES, TILE), BF16),
            pltpu.VMEM((SPREAD + 16, CODES), F32),
            pltpu.VMEM((EXT, CODES), BF16),
        ],
        compiler_params=pltpu.CompilerParams(vmem_limit_bytes=VMEM_BYTES),
        cost_estimate=pl.CostEstimate(
            flops=UNITS * 4 * length * CODES * SPREAD, bytes_accessed=16_000_000, transcendentals=0
        ),
        name="attend",
    )(qkv, planes, seg_row)


def attend_back_kernel(
    qkv_ref, planes_ref, seg_ref, grad_ref, numer_ref, dens_ref, sign_ref, bucket_ref,
    out_ref,
    spread, qprob, kprob, gspread, total, table, turned, gsign, proj,
):
    unit = pl.program_id(0)
    slot = unit // SOLO
    length = qkv_ref.shape[1]
    tiles = length // TILE
    q_rows = pl.ds(pl.multiple_of(slot * HD, HD), HD)
    k_rows = pl.ds(pl.multiple_of(2 * HD + slot * HD, HD), HD)
    v_rows = pl.ds(pl.multiple_of(4 * HD + slot * HD, HD), HD)

    @pl.when(jnp.logical_or(unit == 0, unit == SOLO))
    def _():
        def step(i, carry):
            lane = lanes_of(i, TILE)
            seg_row = seg_ref[:, lane]
            fill_spread(qkv_ref[v_rows, lane], seg_row, spread, lane)
            fill_member(seg_row, spread, lane)
            proj[:, lane] = jnp.zeros((2 * HD, TILE), F32)
            out_ref[v_rows, lane] = jnp.zeros((HD, TILE), F32)
            return carry

        lax.fori_loop(0, tiles, step, 0)
        gspread[SPREAD:EXT, :] = jnp.zeros((128, TILE), BF16)

    total[...] = jnp.zeros_like(total)

    def first(i, carry):
        lane = lanes_of(i, TILE)
        seg_row = seg_ref[:, lane]
        density = dens_ref[0, :, lane]
        inverse = 1.0 / jnp.maximum(density, 1.0)
        est_grad = grad_ref[q_rows, lane].astype(F32) * (1.0 / TABLES)
        num_grad = (est_grad * inverse).astype(BF16)
        fill_spread(num_grad, seg_row, gspread, slice(0, TILE))
        inner_sum = jnp.sum(est_grad * numer_ref[0, :, lane], axis=0, keepdims=True)
        dens_grad = jnp.where(density > 1.0, -inner_sum * inverse * inverse, 0.0)
        which = lax.broadcasted_iota(jnp.int32, (8, TILE), 0)
        high, low = split_two(jnp.where(which == seg_row, dens_grad, 0.0))
        gspread[SPREAD : SPREAD + 32, :] = jnp.concatenate(
            (high, low, high, jnp.zeros_like(high)), axis=0
        ).astype(BF16)
        collected = nn_dot(bucket_ref[0], gspread[...])
        for part in range(TILE // LANES):
            inner = slice(part * LANES, (part + 1) * LANES)
            outer = pl.ds(pl.multiple_of(i * TILE + part * LANES, LANES), LANES)
            sign_q = sign_ref[0, 0:8, outer]
            code_probs(sign_q, qprob, inner)
            gsign[0:8, outer] = signs_back(sign_q, collected[:, inner])
        total[...] += nt_dot(gspread[0 : SPREAD + 16, :], qprob[...])
        return carry

    lax.fori_loop(0, tiles, first, 0)
    mass_grad = total[SPREAD : SPREAD + 8, :] + total[SPREAD + 8 : SPREAD + 16, :]
    high, low = split_two(mass_grad)
    extra = jnp.concatenate((high, low, jnp.zeros((112, CODES), F32)), axis=0)
    table[...] = total[0:SPREAD, :].astype(BF16)
    turned[:, 0:SPREAD] = jnp.transpose(total[0:SPREAD, :]).astype(BF16)
    turned[:, SPREAD:EXT] = jnp.transpose(extra).astype(BF16)

    planes = unit_planes(planes_ref[pl.ds(pl.multiple_of(unit * BITS, BITS), BITS), :])
    plane_high, plane_low = split_two(planes)
    stack = jnp.concatenate((plane_high, plane_low, plane_high, jnp.zeros_like(plane_high)), axis=0)
    stack = stack.astype(BF16)

    def second(i, carry):
        lane = lanes_of(i, TILE)
        seg_row = seg_ref[:, lane]
        for part in range(TILE // LANES):
            inner = slice(part * LANES, (part + 1) * LANES)
            outer = pl.ds(pl.multiple_of(i * TILE + part * LANES, LANES), LANES)
            code_probs(sign_ref[0, 8:16, outer], kprob, inner)
        out_ref[v_rows, lane] += masked_fold(nn_dot(table[...], kprob[...]), seg_row)
        collected = nn_dot(turned[...], spread[:, lane])
        for part in range(TILE // LANES):
            inner = slice(part * LANES, (part + 1) * LANES)
            outer = pl.ds(pl.multiple_of(i * TILE + part * LANES, LANES), LANES)
            gsign[8:16, outer] = signs_back(sign_ref[0, 8:16, outer], collected[:, inner])
        signs = sign_ref[0, :, lane]
        flat = gsign[:, lane] * (1.0 - signs * signs)
        high, low = split_two(flat)
        for side in range(2):
            rows = slice(8 * side, 8 * side + 8)
            pieces = jnp.concatenate(
                (high[rows], high[rows], low[rows], jnp.zeros((8, TILE), F32)), axis=0
            ).astype(BF16)
            proj[side * HD : (side + 1) * HD, lane] += tn_dot(stack, pieces)
        return carry

    lax.fori_loop(0, tiles, second, 0)

    @pl.when(jnp.logical_or(unit == SOLO - 1, unit == UNITS - 1))
    def _():
        def step(i, carry):
            lane = lanes_of(i, TILE)
            for side, rows in ((0, q_rows), (1, k_rows)):
                vec = qkv_ref[rows, lane].astype(F32)
                inverse = lax.rsqrt(jnp.sum(vec * vec, axis=0, keepdims=True) + 1e-06)
                unit_vec = vec * inverse
                grad = proj[side * HD : (side + 1) * HD, lane]
                along = jnp.sum(unit_vec * grad, axis=0, keepdims=True)
                out_ref[rows, lane] = math.sqrt(HD) * inverse * (grad - unit_vec * along)
            return carry

        lax.fori_loop(0, tiles, step, 0)


def attend_back(qkv, planes, seg_row, grad, numer, dens, sign, bucket):
    length = qkv.shape[1]
    per_unit = lambda u: (u, 0, 0)
    fixed = lambda u: (0, 0)
    return pl.pallas_call(
        attend_back_kernel,
        grid=(UNITS,),
        in_specs=[
            pl.BlockSpec(qkv.shape, fixed),
            pl.BlockSpec(planes.shape, fixed),
            pl.BlockSpec(seg_row.shape, fixed),
            pl.BlockSpec(grad.shape, fixed),
            pl.BlockSpec((1, HD, length), per_unit),
            pl.BlockSpec((1, 1, length), per_unit),
            pl.BlockSpec((1, 16, length), per_unit),
            pl.BlockSpec((1, CODES, EXT), per_unit),
        ],
        out_specs=pl.BlockSpec((6 * HD, length), fixed),
        out_shape=jax.ShapeDtypeStruct((6 * HD, length), F32),
        scratch_shapes=[
            pltpu.VMEM((EXT, length), BF16),
            pltpu.VMEM((CODES, TILE), BF16),
            pltpu.VMEM((CODES, TILE), BF16),
            pltpu.VMEM((EXT, TILE), BF16),
            pltpu.VMEM((SPREAD + 16, CODES), F32),
            pltpu.VMEM((SPREAD, CODES), BF16),
            pltpu.VMEM((CODES, EXT), BF16),
            pltpu.VMEM((16, length), F32),
            pltpu.VMEM((2 * HD, length), F32),
        ],
        compiler_params=pltpu.CompilerParams(vmem_limit_bytes=VMEM_BYTES),
        cost_estimate=pl.CostEstimate(
            flops=UNITS * 8 * length * CODES * SPREAD, bytes_accessed=16_000_000, transcendentals=0
        ),
        name="attend_back",
    )(qkv, planes, seg_row, grad, numer, dens, sign, bucket)


SPAN = 192
OWN = 96
BLOCKS = ((0, HD), (HD, OWN))


def toeplitz(taps):
    row = jnp.pad(taps, ((0, 0), (0, SPAN + 1 - KW)))
    flat = jnp.tile(row, (1, LANES))[:, : LANES * SPAN]
    return jnp.swapaxes(flat.reshape(2, LANES, SPAN), 1, 2)


def band_product(pad_ref, band_ref, lane_wide, mask, out_ref, lane):
    for h, (low_row, high_row) in enumerate(BLOCKS):
        band = jnp.where(mask, band_ref[h], 0.0)
        high, low = split_two(band)
        rows = pad_ref[low_row:high_row, lane_wide]
        out_ref[low_row:high_row, lane] = nn_dot(rows, high.astype(BF16)) + nn_dot(
            rows, low.astype(BF16)
        )


def conv_kernel(pad_ref, band_ref, col_ref, seg_ref, out_ref):
    tiles = out_ref.shape[1] // LANES

    def step(i, carry):
        lane = lanes_of(i, LANES)
        start = pl.multiple_of(i * LANES, LANES)
        wide = pl.ds(start, SPAN)
        mask = col_ref[wide, :] == seg_ref[:, lane]
        band_product(pad_ref, band_ref, wide, mask, out_ref, lane)
        return carry

    lax.fori_loop(0, tiles, step, 0)


def segment_conv(padded, band, seg_col, seg_own):
    length = seg_own.shape[1]
    return pl.pallas_call(
        conv_kernel,
        out_shape=jax.ShapeDtypeStruct((OWN, length), F32),
        compiler_params=pltpu.CompilerParams(vmem_limit_bytes=VMEM_BYTES),
        cost_estimate=pl.CostEstimate(
            flops=8 * length * SPAN * HD, bytes_accessed=3_000_000, transcendentals=0
        ),
        name="segment_conv",
    )(padded, band, seg_col, seg_own)


def conv_back_kernel(gpad_ref, grad_ref, vpad_ref, band_ref, col_ref, seg_ref, segt_ref, colt_ref,
                     out_ref, tap_ref, corr):
    tiles = out_ref.shape[1] // LANES
    corr[...] = jnp.zeros_like(corr)

    def step(i, carry):
        lane = lanes_of(i, LANES)
        start = pl.multiple_of(i * LANES, LANES)
        wide = pl.ds(start, SPAN)
        twice = pl.ds(start, 2 * LANES)
        mask = col_ref[wide, :] == seg_ref[:, lane]
        band_product(gpad_ref, band_ref, wide, mask, out_ref, lane)
        mask_turned = colt_ref[lane, :] == segt_ref[:, twice]
        for h, (low_row, high_row) in enumerate(BLOCKS):
            match = tn_dot(grad_ref[low_row:high_row, lane], vpad_ref[low_row:high_row, twice])
            corr[h] += jnp.where(mask_turned, match, 0.0)
        return carry

    lax.fori_loop(0, tiles, step, 0)
    row = lax.broadcasted_iota(jnp.int32, (LANES, 2 * LANES), 0)
    for h in range(2):
        skew = corr[h]
        for bit in range(7):
            moved = pltpu.roll(skew, 2 * LANES - (1 << bit), 1)
            skew = jnp.where((row >> bit) & 1 == 1, moved, skew)
        tap_ref[h] = jnp.sum(skew, axis=0, keepdims=True)


def conv_back(gpad, grad, vpad, band, seg_col, seg_own, seg_wide, col_own):
    length = seg_own.shape[1]
    return pl.pallas_call(
        conv_back_kernel,
        out_shape=(
            jax.ShapeDtypeStruct((OWN, length), F32),
            jax.ShapeDtypeStruct((2, 1, 2 * LANES), F32),
        ),
        scratch_shapes=[pltpu.VMEM((2, LANES, 2 * LANES), F32)],
        compiler_params=pltpu.CompilerParams(vmem_limit_bytes=VMEM_BYTES),
        cost_estimate=pl.CostEstimate(
            flops=16 * length * SPAN * HD, bytes_accessed=4_000_000, transcendentals=0
        ),
        name="conv_back",
    )(gpad, grad, vpad, band, seg_col, seg_own, seg_wide, col_own)


def norm_rows(values):
    center = values - jnp.mean(values, axis=1, keepdims=True)
    inverse = lax.rsqrt(jnp.mean(center * center, axis=1, keepdims=True) + 1e-05)
    return center * inverse, inverse


def norm_back(upstream, normed, inverse, gain):
    scaled = upstream * gain
    inner = (
        scaled
        - jnp.mean(scaled, axis=1, keepdims=True)
        - normed * jnp.mean(scaled * normed, axis=1, keepdims=True)
    )
    return inner * inverse


def gelu_pair(value):
    cdf = 0.5 + 0.5 * lax.erf(value * math.sqrt(0.5))
    pdf = jnp.exp(-0.5 * value * value) * (1.0 / math.sqrt(2.0 * math.pi))
    return value * cdf, cdf + value * pdf


def column_sum(values):
    return jnp.sum(values, axis=0, keepdims=True)


def middle_kernel(
    att_ref, x_ref, cot_ref, out_w_ref, up_ref, down_ref, scale_ref,
    result_ref, hidden_low_ref, ffn_low_ref, out_low_ref, one_ref, attn_ref, part_ref,
    hidden, normed, inverse, acc, slope, two,
):
    step = pl.program_id(0)
    parts = pl.num_programs(0) // 2
    block = step % parts

    @pl.when(step == 0)
    def _():
        projected = tn_dot(att_ref[...], out_w_ref[...])
        unit, inv = norm_rows(x_ref[...].astype(F32) + projected)
        value = unit * scale_ref[0:1] + scale_ref[1:2]
        normed[...] = unit
        inverse[...] = inv
        hidden[...] = value
        hidden_low_ref[...] = value.astype(BF16)
        acc[...] = jnp.zeros_like(acc)

    @pl.when(step < parts)
    def _():
        active, lean = gelu_pair(nn_dot(hidden_low_ref[...], up_ref[0]))
        slope[block] = lean
        acc[...] += nn_dot(active.astype(BF16), down_ref[0])

    @pl.when(step == parts - 1)
    def _():
        unit, inv = norm_rows(hidden[...] + acc[...])
        result_ref[...] = (unit * scale_ref[2:3] + scale_ref[3:4]).astype(BF16)
        upstream = cot_ref[...].astype(F32)
        part_ref[2:3] = column_sum(upstream * unit)
        part_ref[3:4] = column_sum(upstream)
        grad = norm_back(upstream, unit, inv, scale_ref[2:3])
        two[...] = grad
        ffn_low_ref[...] = grad.astype(BF16)
        acc[...] = jnp.zeros_like(acc)

    @pl.when(step >= parts)
    def _():
        pre_grad = (nt_dot(ffn_low_ref[...], down_ref[0]) * slope[block]).astype(BF16)
        acc[...] += nt_dot(pre_grad, up_ref[0])

    @pl.when(step == 2 * parts - 1)
    def _():
        upstream = two[...] + acc[...]
        unit = normed[...]
        part_ref[0:1] = column_sum(upstream * unit)
        part_ref[1:2] = column_sum(upstream)
        part_ref[4:8] = jnp.zeros((4, part_ref.shape[1]), F32)
        grad = norm_back(upstream, unit, inverse[...], scale_ref[0:1])
        one_ref[...] = grad
        out_low_ref[...] = grad.astype(BF16)
        attn_ref[...] = nt_dot(out_w_ref[...], grad.astype(BF16)).astype(BF16)


def middle(att, x, cot, out_w, up, down, scale):
    rows, width = x.shape
    parts, _, hidden_units = up.shape
    fixed = lambda i: (0, 0)
    each = lambda i: (i % parts, 0, 0)
    full = lambda array: pl.BlockSpec(array.shape, fixed)
    row_low = jax.ShapeDtypeStruct((rows, width), BF16)
    outs = (
        row_low, row_low, row_low, row_low,
        jax.ShapeDtypeStruct((rows, width), F32),
        jax.ShapeDtypeStruct(att.shape, BF16),
        jax.ShapeDtypeStruct((8, width), F32),
    )
    return pl.pallas_call(
        middle_kernel,
        grid=(2 * parts,),
        in_specs=[
            full(att), full(x), full(cot), full(out_w),
            pl.BlockSpec((1,) + up.shape[1:], each),
            pl.BlockSpec((1,) + down.shape[1:], each),
            full(scale),
        ],
        out_specs=[full(o) for o in outs],
        out_shape=outs,
        scratch_shapes=[
            pltpu.VMEM((rows, width), F32),
            pltpu.VMEM((rows, width), F32),
            pltpu.VMEM((rows, 1), F32),
            pltpu.VMEM((rows, width), F32),
            pltpu.VMEM((parts, rows, hidden_units), F32),
            pltpu.VMEM((rows, width), F32),
        ],
        compiler_params=pltpu.CompilerParams(vmem_limit_bytes=VMEM_BYTES),
        cost_estimate=pl.CostEstimate(
            flops=8 * rows * width * parts * hidden_units, bytes_accessed=26_000_000,
            transcendentals=0,
        ),
        name="middle",
    )(att, x, cot, out_w, up, down, scale)


def ffn_grad_kernel(hidden_ref, ffn_ref, out_ref, att_ref, up_ref, down_ref, grad_ref, acc):
    step = pl.program_id(0)
    units = up_ref.shape[1]

    @pl.when(step == 0)
    def _():
        acc[...] = jnp.zeros_like(acc)

    active, lean = gelu_pair(nn_dot(hidden_ref[...], up_ref[...]))
    pre_grad = (nt_dot(ffn_ref[...], down_ref[...]) * lean).astype(BF16)
    acc[0:units, :] += tn_dot(pre_grad, hidden_ref[...])
    acc[units : 2 * units, :] += tn_dot(active.astype(BF16), ffn_ref[...])
    acc[2 * units : 2 * units + OWN, :] += nn_dot(att_ref[...], out_ref[...])

    @pl.when(step == pl.num_programs(0) - 1)
    def _():
        grad_ref[...] = acc[...].astype(BF16)


def ffn_grad(hidden_full, ffn_full, out_full, attended, up, down):
    length, width = hidden_full.shape
    units = up.shape[1]
    total = 2 * units + OWN
    tile = 256
    rows = lambda i: (i, 0)
    fixed = lambda i: (0, 0)
    return pl.pallas_call(
        ffn_grad_kernel,
        grid=(length // tile,),
        in_specs=[
            pl.BlockSpec((tile, width), rows),
            pl.BlockSpec((tile, width), rows),
            pl.BlockSpec((tile, width), rows),
            pl.BlockSpec((OWN, tile), lambda i: (0, i)),
            pl.BlockSpec(up.shape, fixed),
            pl.BlockSpec(down.shape, fixed),
        ],
        out_specs=pl.BlockSpec((total, width), fixed),
        out_shape=jax.ShapeDtypeStruct((total, width), BF16),
        scratch_shapes=[pltpu.VMEM((total, width), F32)],
        compiler_params=pltpu.CompilerParams(vmem_limit_bytes=VMEM_BYTES),
        cost_estimate=pl.CostEstimate(
            flops=8 * length * width * units, bytes_accessed=12_000_000, transcendentals=0
        ),
        name="ffn_grad",
    )(hidden_full, ffn_full, out_full, attended, up, down)


MESH = pl.DeviceIdType.MESH


def finish_kernel(
    part_ref, one_ref, grads_ref, small_ref,
    out_ref, sums_ref, tiny_ref,
    pair_in, stage, line_in, slice_in, near_in, far_in,
    pair_send, pair_recv, line_send, line_recv, slice_send, slice_recv,
    whole_send, whole_recv, near_send, near_recv, far_send, far_recv,
):
    blocks = grads_ref.shape[0]
    count = part_ref.shape[0]
    chips = count // 2
    d = lax.axis_index("dp")
    m = lax.axis_index("mp")
    core = m % 2
    chip = m // 2
    sibling = m + 1 - 2 * core

    barrier = pltpu.get_barrier_semaphore()

    def greet_block(r, carry):
        pl.semaphore_signal(
            barrier, inc=1, device_id={"dp": (d + r) % blocks}, device_id_type=MESH
        )
        return carry

    def greet_model(r, carry):
        pl.semaphore_signal(barrier, inc=1, device_id={"mp": (m + r) % count}, device_id_type=MESH)
        return carry

    lax.fori_loop(1, blocks, greet_block, 0)
    lax.fori_loop(1, count, greet_model, 0)
    pl.semaphore_wait(barrier, blocks + count - 2)

    def pair_copy(target):
        return pltpu.make_async_remote_copy(
            src_ref=part_ref.at[2 * target + 1 - core],
            dst_ref=pair_in.at[target],
            send_sem=pair_send.at[target],
            recv_sem=pair_recv.at[target],
            device_id={"mp": sibling},
            device_id_type=MESH,
        )

    def line_copy(k):
        return pltpu.make_async_remote_copy(
            src_ref=stage.at[k],
            dst_ref=line_in.at[k],
            send_sem=line_send.at[k],
            recv_sem=line_recv.at[k],
            device_id={"mp": (m + 2 * k) % count},
            device_id_type=MESH,
        )

    def slice_copy(r):
        peer = (d + r) % blocks
        return pltpu.make_async_remote_copy(
            src_ref=grads_ref.at[peer],
            dst_ref=slice_in.at[r],
            send_sem=slice_send.at[r],
            recv_sem=slice_recv.at[r],
            device_id={"dp": peer},
            device_id_type=MESH,
        )

    def whole_copy(r, owner):
        return pltpu.make_async_remote_copy(
            src_ref=sums_ref.at[d],
            dst_ref=sums_ref.at[owner],
            send_sem=whole_send.at[r],
            recv_sem=whole_recv.at[r],
            device_id={"dp": (d + r) % blocks},
            device_id_type=MESH,
        )

    def near_copy(r, owner):
        return pltpu.make_async_remote_copy(
            src_ref=small_ref,
            dst_ref=near_in.at[owner],
            send_sem=near_send.at[r],
            recv_sem=near_recv.at[r],
            device_id={"mp": (m + r) % count},
            device_id_type=MESH,
        )

    def far_copy(r, owner):
        return pltpu.make_async_remote_copy(
            src_ref=far_in.at[d],
            dst_ref=far_in.at[owner],
            send_sem=far_send.at[r],
            recv_sem=far_recv.at[r],
            device_id={"dp": (d + r) % blocks},
            device_id_type=MESH,
        )

    def repeat(start, stop, action):
        def body(r, carry):
            action(r)
            return carry

        lax.fori_loop(start, stop, body, 0)

    order = [2, 1, 3, 0]
    for k in order:
        pair_copy((chip + k) % chips).start()
    repeat(1, count, lambda r: near_copy(r, m).start())
    repeat(1, blocks, lambda r: slice_copy(r).start())

    for k in order[:3]:
        target = (chip + k) % chips
        pair_copy(target).wait_recv()
        both = part_ref[2 * target + core].astype(F32) + pair_in[target].astype(F32)
        stage[k] = both.astype(BF16)
        line_copy(k).start()

    near_in[m] = small_ref[...]
    repeat(1, count, lambda r: near_copy(r, (m + count - r) % count).wait_recv())
    total = near_in[0]
    for r in range(1, count):
        total = total + near_in[r]
    far_in[d] = total
    repeat(1, blocks, lambda r: far_copy(r, d).start())

    repeat(1, blocks, lambda r: slice_copy(r).wait_recv())
    depth = grads_ref.shape[1]
    for low in range(0, depth, 16):
        rows = slice(low, min(low + 16, depth))
        total = grads_ref[d, rows].astype(F32)
        for r in range(1, blocks):
            total = total + slice_in[r, rows].astype(F32)
        sums_ref[d, rows] = total.astype(BF16)
    repeat(1, blocks, lambda r: whole_copy(r, d).start())

    pair_copy(chip).wait_recv()
    total = part_ref[m].astype(F32) + pair_in[chip].astype(F32)
    for k in range(1, chips):
        line_copy(k).wait_recv()
        total = total + line_in[k].astype(F32)
    out_ref[...] = one_ref[...] + total

    repeat(1, blocks, lambda r: far_copy(r, (d + blocks - r) % blocks).wait_recv())
    total = far_in[0]
    for r in range(1, blocks):
        total = total + far_in[r]
    tiny_ref[...] = total
    repeat(1, blocks, lambda r: whole_copy(r, (d + blocks - r) % blocks).wait_recv())

    for k in range(chips):
        pair_copy((chip + k) % chips).wait_send()
    for k in range(1, chips):
        line_copy(k).wait_send()
    repeat(1, count, lambda r: near_copy(r, m).wait_send())
    repeat(1, blocks, lambda r: slice_copy(r).wait_send())
    repeat(1, blocks, lambda r: far_copy(r, d).wait_send())
    repeat(1, blocks, lambda r: whole_copy(r, d).wait_send())


def finish(part, one_grad, grads, small, blocks):
    count = part.shape[0]
    chips = count // 2
    rows, width = one_grad.shape
    sems = lambda n: pltpu.SemaphoreType.DMA((n,))
    vmem = pl.BlockSpec(memory_space=pltpu.VMEM)
    return pl.pallas_call(
        finish_kernel,
        in_specs=[vmem] * 4,
        out_specs=[vmem] * 3,
        out_shape=(
            jax.ShapeDtypeStruct(one_grad.shape, F32),
            jax.ShapeDtypeStruct(grads.shape, BF16),
            jax.ShapeDtypeStruct(small.shape, F32),
        ),
        scratch_shapes=[
            pltpu.VMEM((chips, rows, width), BF16),
            pltpu.VMEM((chips, rows, width), BF16),
            pltpu.VMEM((chips, rows, width), BF16),
            pltpu.VMEM(grads.shape, BF16),
            pltpu.VMEM((count,) + small.shape, F32),
            pltpu.VMEM((blocks,) + small.shape, F32),
            sems(chips), sems(chips), sems(chips), sems(chips), sems(blocks), sems(blocks),
            sems(blocks), sems(blocks), sems(count), sems(count), sems(blocks), sems(blocks),
        ],
        compiler_params=pltpu.CompilerParams(
            vmem_limit_bytes=VMEM_BYTES, collective_id=0, has_side_effects=True
        ),
        cost_estimate=pl.CostEstimate(flops=0, bytes_accessed=30_000_000, transcendentals=0),
        name="finish",
    )(part, one_grad, grads, small)


def from_partner(block):
    count = lax.axis_size("mp")
    route = [(n, n ^ 1) for n in range(count)]
    return lax.ppermute(block, "mp", route)


def gather_rows(rows):
    return lax.all_gather(rows, "mp", axis=0, tiled=True)


def on_device(
    inputs, segment, w_query, w_key, w_value, planes, conv_taps, w_out,
    ln1_gain, ln1_bias, w_up, w_down, ln2_gain, ln2_bias, cotangent,
):
    position = lax.axis_index("mp")
    count = lax.axis_size("mp")
    side = position % 2
    first_side = side == 0
    half = OWN - HD
    rows = inputs.shape[0]

    def solo_first(block, axis):
        return jnp.where(first_side, block, jnp.roll(block, -half, axis))

    def own_order(block, axis):
        return jnp.where(first_side, block, jnp.roll(block, half, axis))

    def join(own_half, peer_half, axis):
        return jnp.where(
            first_side,
            jnp.concatenate((own_half, peer_half), axis),
            jnp.concatenate((peer_half, own_half), axis),
        )

    def half_of(block, which):
        return lax.dynamic_slice_in_dim(block, which * half, half, 0)

    query_w, key_w, value_w = (solo_first(w, 1) for w in (w_query, w_key, w_value))
    out_w = solo_first(w_out, 0)
    halves = jnp.concatenate((query_w[:, HD:], key_w[:, HD:], value_w[:, HD:]), 1)
    peer_halves, peer_out = from_partner((halves, out_w[HD:]))
    wide = []
    for n, w in enumerate((query_w, key_w, value_w)):
        wide += [w[:, :HD], join(w[:, HD:], peer_halves[:, n * half : (n + 1) * half], 1)]
    wide_w = jnp.concatenate(wide, 1)
    out_group = jnp.concatenate((out_w[:HD], join(out_w[HD:], peer_out, 0)), 0)

    unit_rows = jnp.concatenate(
        (planes, lax.dynamic_slice_in_dim(planes, side * 2 * BITS, 2 * BITS, 0)), 0
    )
    seg_row = segment[None, :]
    seg_wide = jnp.pad(segment, (32, 96), constant_values=-2)
    seg_own = jnp.where(segment < 0, -3, segment)
    group = position // 2
    heads = jnp.stack((3 * group + 2 * side, 3 * group + 1))
    selector = (heads[:, None] == jnp.arange(HEADS, dtype=jnp.int32)[None, :]).astype(F32)
    taps = jnp.dot(selector, conv_taps.T, precision=lax.Precision.HIGHEST)

    gathered = gather_rows(inputs)
    out_all = gather_rows(out_group)
    up_all = gather_rows(w_up[None])
    down_all = gather_rows(w_down[None])
    qkv = lax.dot_general(
        wide_w, gathered, (((0,), (1,)), ((), ())), preferred_element_type=F32
    ).astype(BF16)
    value_own = jnp.concatenate((qkv[4 * HD : 5 * HD], half_of(qkv[5 * HD :], side)), 0)
    value_pad = jnp.pad(value_own, ((0, 0), (32, 96)))
    conv = segment_conv(value_pad, toeplitz(taps), seg_wide[:, None], seg_own[None, :])
    est, numer, dens, sign, bucket = attend(qkv, unit_rows, seg_row)
    conv_wide = jnp.concatenate(
        (conv[:HD], join(conv[HD:], jnp.zeros_like(conv[HD:]), 0)), 0
    )
    sent = (est / TABLES + conv_wide).astype(BF16)
    att = lax.all_to_all(
        jnp.swapaxes(sent.reshape(2 * HD, count, rows), 0, 1), "mp", 0, 0
    ).reshape(2 * HD * count, rows)
    scale = jnp.stack((ln1_gain, ln1_bias, ln2_gain, ln2_bias) * 2)
    outputs, hidden_low, ffn_low, out_low, one_grad, attn_part, norm_part = middle(
        att, inputs, cotangent, out_all, up_all, down_all, scale
    )
    attn_all = lax.all_to_all(attn_part.reshape(count, 2 * HD, rows), "mp", 0, 0)
    attn_grad = jnp.swapaxes(attn_all, 0, 1).reshape(2 * HD, rows * count)
    received = from_partner(half_of(sent[HD:], 1 - side)).astype(F32)
    mixed = (half_of(sent[HD:], side).astype(F32) + received).astype(BF16)
    attended = jnp.concatenate((sent[:HD], mixed), 0)
    hidden_full = gather_rows(hidden_low)
    ffn_full = gather_rows(ffn_low)
    out_full = gather_rows(out_low)

    grad_own = jnp.concatenate((attn_grad[:HD], half_of(attn_grad[HD:], side)), 0)
    grad_pad = jnp.pad(grad_own, ((0, 0), (32, 96)))
    value_conv, tap_part = conv_back(
        grad_pad, grad_own, value_pad, toeplitz(taps[:, ::-1]),
        seg_wide[:, None], seg_own[None, :], seg_wide[None, :], seg_own[:, None],
    )
    conv_part = jnp.dot(
        tap_part[:, 0, :KW].T, selector, precision=lax.Precision.HIGHEST
    )
    back = attend_back(qkv, unit_rows, seg_row, attn_grad, numer, dens, sign, bucket)
    ffn_part = ffn_grad(hidden_full, ffn_full, out_full, attended, w_up, w_down)
    shared = jnp.concatenate(
        [half_of(back[(2 * n + 1) * HD : (2 * n + 2) * HD], 1 - side) for n in range(3)], 0
    )
    peer_shared = from_partner(shared.astype(BF16)).astype(F32)
    sums = []
    for n in range(3):
        solo = back[2 * n * HD : (2 * n + 1) * HD]
        mixed = half_of(back[(2 * n + 1) * HD : (2 * n + 2) * HD], side)
        mixed = mixed + peer_shared[n * half : (n + 1) * half]
        sums.append(jnp.concatenate((solo, mixed), 0))
    sums[2] = sums[2] + value_conv
    lows = jnp.concatenate([s.astype(BF16) for s in sums], 0)
    weight_part = lax.dot_general(
        lows, gathered, (((1,), (0,)), ((), ())), preferred_element_type=F32
    ).astype(BF16)
    inputs_part = lax.dot_general(
        lows,
        jnp.concatenate((query_w, key_w, value_w), 1),
        (((0,), (1,)), ((), ())),
        preferred_element_type=F32,
    ).astype(BF16)
    blocks = lax.axis_size("dp")
    width = inputs.shape[1]
    conv_flat = jnp.pad(conv_part.reshape(-1), (0, -KW * HEADS % width)).reshape(-1, width)
    small = jnp.concatenate((norm_part[:4], conv_flat), 0)
    small = jnp.pad(small, ((0, -small.shape[0] % 8), (0, 0)))
    inputs_grad, sums, tiny = finish(
        inputs_part.reshape(count, rows, width),
        one_grad,
        jnp.concatenate((ffn_part, weight_part), 0).reshape(blocks, -1, width),
        small,
        blocks,
    )
    sums = sums.reshape(-1, width).astype(F32)
    units = w_up.shape[1]
    w_up_grad = sums[:units].T
    w_down_grad = sums[units : 2 * units]
    w_out_grad = own_order(sums[2 * units : 2 * units + OWN], 0)
    weight_grads = sums[2 * units + OWN :].T
    w_query_grad, w_key_grad, w_value_grad = (
        own_order(weight_grads[:, n * OWN : (n + 1) * OWN], 1) for n in range(3)
    )
    conv_taps_grad = tiny[4:].reshape(-1)[: KW * HEADS].reshape(KW, HEADS)
    norm_grads = tiny
    return (
        outputs, inputs_grad, w_query_grad, w_key_grad, w_value_grad, conv_taps_grad, w_out_grad,
        norm_grads[0], norm_grads[1], w_up_grad, w_down_grad, norm_grads[2], norm_grads[3],
    )


def solution(mesh):
    rows = P(("dp", "mp"), None)
    cols = P(None, "mp")
    return jax.shard_map(
        on_device,
        mesh=mesh,
        in_specs=(
            rows, P("dp"), cols, cols, cols, P(), P(), P("mp", None), P(), P(),
            cols, P("mp", None), P(), P(), rows,
        ),
        out_specs=(
            rows, rows, cols, cols, cols, P(), P("mp", None), P(), P(),
            cols, P("mp", None), P(), P(),
        ),
        check_vma=False,
    )
```

```python
import math
import jax
import jax.numpy as jnp
from jax import lax
from jax.experimental import pallas as pl
from jax.experimental.pallas import tpu as pltpu
from jax.sharding import PartitionSpec as P

HEADS = 12
HD = 64
TABLES = 4
BITS = 8
KW = 65
MAXSEG = 8
CODES = 256
UNITS = 6
SOLO = 4
SPREAD = MAXSEG * HD
EXT = SPREAD + 128
LANES = 128
TILE = 2048
F32 = jnp.float32
BF16 = jnp.bfloat16
VMEM_BYTES = 56 * 1024 * 1024


def nt_dot(left, right):
    return lax.dot_general(left, right, (((1,), (1,)), ((), ())), preferred_element_type=F32)


def tn_dot(left, right):
    return lax.dot_general(left, right, (((0,), (0,)), ((), ())), preferred_element_type=F32)


def nn_dot(left, right):
    return lax.dot_general(left, right, (((1,), (0,)), ((), ())), preferred_element_type=F32)


def half_sign(bit):
    rows = lax.broadcasted_iota(jnp.int32, (8, LANES), 0)
    return jnp.where((rows >> bit) & 1 == 0, 0.5, -0.5).astype(F32)


def code_factors(signs):
    pos0, neg0 = 0.5 + 0.5 * signs[0:1], 0.5 - 0.5 * signs[0:1]
    pos1, neg1 = 0.5 + 0.5 * signs[1:2], 0.5 - 0.5 * signs[1:2]
    tops = (pos0 * pos1, pos0 * neg1, neg0 * pos1, neg0 * neg1)
    picks = [half_sign(2), half_sign(1), half_sign(0)]
    mids = [0.5 + picks[n] * signs[2 + n : 3 + n] for n in range(3)]
    lows = [0.5 + picks[n] * signs[5 + n : 6 + n] for n in range(3)]
    return tops, mids, lows, picks


def code_probs(signs, out_ref, lane):
    tops, mids, lows, _ = code_factors(signs)
    mid = mids[0] * mids[1] * mids[2]
    low = lows[0] * lows[1] * lows[2]
    for top_index in range(4):
        low_top = low * tops[top_index]
        for pair in range(4):
            rows = jnp.concatenate(
                (
                    low_top * mid[2 * pair : 2 * pair + 1],
                    low_top * mid[2 * pair + 1 : 2 * pair + 2],
                ),
                axis=0,
            )
            first = top_index * 64 + pair * 16
            out_ref[first : first + 16, lane] = rows.astype(BF16)


def signs_back(signs, grads):
    tops, mids, lows, picks = code_factors(signs)
    mid = mids[0] * mids[1] * mids[2]
    low = lows[0] * lows[1] * lows[2]
    mid_rows = [jnp.broadcast_to(mid[m : m + 1], (8, LANES)) for m in range(8)]
    top_rows = [jnp.broadcast_to(tops[t], (8, LANES)) for t in range(4)]
    by_top = [None] * 4
    by_mid = [None] * 8
    for t in range(4):
        for m in range(8):
            piece = grads[t * 64 + m * 8 : t * 64 + m * 8 + 8]
            a = piece * mid_rows[m]
            b = piece * top_rows[t]
            by_top[t] = a if by_top[t] is None else by_top[t] + a
            by_mid[m] = b if by_mid[m] is None else by_mid[m] + b
    low_grad = by_top[0] * top_rows[0]
    for t in range(1, 4):
        low_grad = low_grad + by_top[t] * top_rows[t]
    top_grad = [jnp.sum(low * by_top[t], axis=0, keepdims=True) for t in range(4)]
    mid_grad = jnp.concatenate(
        [jnp.sum(low * by_mid[m], axis=0, keepdims=True) for m in range(8)], axis=0
    )
    pos0, neg0 = 0.5 + 0.5 * signs[0:1], 0.5 - 0.5 * signs[0:1]
    pos1, neg1 = 0.5 + 0.5 * signs[1:2], 0.5 - 0.5 * signs[1:2]
    out = [
        0.5 * ((top_grad[0] - top_grad[2]) * pos1 + (top_grad[1] - top_grad[3]) * neg1),
        0.5 * ((top_grad[0] - top_grad[1]) * pos0 + (top_grad[2] - top_grad[3]) * neg0),
    ]
    for grad, parts in ((mid_grad, mids), (low_grad, lows)):
        for n in range(3):
            others = parts[(n + 1) % 3] * parts[(n + 2) % 3] * picks[n]
            out.append(jnp.sum(grad * others, axis=0, keepdims=True))
    return jnp.concatenate(out, axis=0)


def split_two(value):
    high = value.astype(BF16).astype(F32)
    return high, value - high


def unit_planes(planes):
    return planes * lax.rsqrt(jnp.sum(planes * planes, axis=1, keepdims=True) + 1e-06)


def fill_spread(values, seg_row, spread_ref, lane):
    for s in range(MAXSEG):
        spread_ref[s * HD : (s + 1) * HD, lane] = jnp.where(
            seg_row == s, values, jnp.zeros_like(values)
        )


def fill_member(seg_row, spread_ref, lane):
    width = seg_row.shape[1]
    rows = lax.broadcasted_iota(jnp.int32, (128, width), 0)
    hit = jnp.logical_and(rows < 16, (rows & 7) == seg_row)
    spread_ref[SPREAD:EXT, lane] = jnp.where(hit, 1.0, 0.0).astype(BF16)


def lanes_of(index, width):
    return pl.ds(pl.multiple_of(index * width, width), width)


def masked_fold(product, seg_row):
    total = None
    for s in range(MAXSEG):
        piece = jnp.where(seg_row == s, product[s * HD : (s + 1) * HD], 0.0)
        total = piece if total is None else total + piece
    return total


def attend_kernel(
    qkv_ref, planes_ref, seg_ref, conv_ref,
    sent_ref, numer_ref, dens_ref, sign_ref, bucket_ref,
    spread, norm, qprob, kprob, total, table, est,
):
    unit = pl.program_id(0)
    slot = unit // SOLO
    length = qkv_ref.shape[1]
    tiles = length // TILE
    q_rows = pl.ds(pl.multiple_of(slot * HD, HD), HD)
    k_rows = pl.ds(pl.multiple_of(2 * HD + slot * HD, HD), HD)
    v_rows = pl.ds(pl.multiple_of(4 * HD + slot * HD, HD), HD)

    @pl.when(jnp.logical_or(unit == 0, unit == SOLO))
    def _():
        def step(i, carry):
            lane = lanes_of(i, TILE)
            seg_row = seg_ref[:, lane]
            fill_spread(qkv_ref[v_rows, lane], seg_row, spread, lane)
            fill_member(seg_row, spread, lane)
            query = qkv_ref[q_rows, lane].astype(F32)
            key = qkv_ref[k_rows, lane].astype(F32)
            scale = math.sqrt(HD)
            norm[0:1, lane] = scale * lax.rsqrt(
                jnp.sum(query * query, axis=0, keepdims=True) + 1e-06
            )
            norm[1:2, lane] = scale * lax.rsqrt(jnp.sum(key * key, axis=0, keepdims=True) + 1e-06)
            est[:, lane] = jnp.zeros((HD, TILE), F32)
            return carry

        lax.fori_loop(0, tiles, step, 0)

    planes = unit_planes(planes_ref[pl.ds(pl.multiple_of(unit * BITS, BITS), BITS), :])
    high, rest = split_two(planes)
    middle, low = split_two(rest)
    stack = jnp.concatenate((high, middle, low), axis=0).astype(BF16)
    total[...] = jnp.zeros_like(total)

    def collect(i, carry):
        lane = lanes_of(i, TILE)
        flat_q = nn_dot(stack, qkv_ref[q_rows, lane])
        flat_k = nn_dot(stack, qkv_ref[k_rows, lane])
        sign_q = jnp.tanh((flat_q[0:8] + flat_q[8:16] + flat_q[16:24]) * norm[0:1, lane])
        sign_k = jnp.tanh((flat_k[0:8] + flat_k[8:16] + flat_k[16:24]) * norm[1:2, lane])
        sign_ref[0, 0:8, lane] = sign_q
        sign_ref[0, 8:16, lane] = sign_k
        for part in range(TILE // LANES):
            inner = slice(part * LANES, (part + 1) * LANES)
            code_probs(sign_k[:, inner], kprob, inner)
            code_probs(
                sign_q[:, inner], qprob, pl.ds(pl.multiple_of(i * TILE + part * LANES, LANES), LANES)
            )
        total[...] += nt_dot(spread[0 : SPREAD + 16, lane], kprob[...])
        return carry

    lax.fori_loop(0, tiles, collect, 0)
    mass = total[SPREAD : SPREAD + 8, :]
    mass_high, mass_low = split_two(mass)
    extra = jnp.concatenate(
        (mass_high, mass_high, mass_low, jnp.zeros((104, CODES), F32)), axis=0
    )
    table[0:SPREAD, :] = total[0:SPREAD, :].astype(BF16)
    table[SPREAD:EXT, :] = extra.astype(BF16)
    bucket_ref[0, :, 0:SPREAD] = jnp.transpose(total[0:SPREAD, :]).astype(BF16)
    bucket_ref[0, :, SPREAD:EXT] = jnp.transpose(extra).astype(BF16)

    def spend(i, carry):
        lane = lanes_of(i, TILE)
        seg_row = seg_ref[:, lane]
        product = nn_dot(table[0 : SPREAD + 32, :], qprob[:, lane])
        numer = masked_fold(product, seg_row)
        both = product[SPREAD : SPREAD + 8] + product[SPREAD + 16 : SPREAD + 24]
        which = lax.broadcasted_iota(jnp.int32, (8, TILE), 0)
        density = jnp.sum(jnp.where(which == seg_row, both, 0.0), axis=0, keepdims=True)
        numer_ref[0, :, lane] = numer
        dens_ref[0, :, lane] = density
        est[:, lane] += numer * (1.0 / jnp.maximum(density, 1.0))
        return carry

    lax.fori_loop(0, tiles, spend, 0)

    @pl.when(jnp.logical_or(unit == SOLO - 1, unit == UNITS - 1))
    def _():
        sent_ref[q_rows, :] = (est[...] * (1.0 / TABLES) + conv_ref[q_rows, :]).astype(BF16)


def attend(qkv, planes, seg_row, conv):
    length = qkv.shape[1]
    per_unit = lambda u: (u, 0, 0)
    fixed = lambda u: (0, 0)
    return pl.pallas_call(
        attend_kernel,
        grid=(UNITS,),
        in_specs=[
            pl.BlockSpec(qkv.shape, fixed),
            pl.BlockSpec(planes.shape, fixed),
            pl.BlockSpec(seg_row.shape, fixed),
            pl.BlockSpec(conv.shape, fixed),
        ],
        out_specs=[
            pl.BlockSpec((2 * HD, length), fixed),
            pl.BlockSpec((1, HD, length), per_unit),
            pl.BlockSpec((1, 1, length), per_unit),
            pl.BlockSpec((1, 16, length), per_unit),
            pl.BlockSpec((1, CODES, EXT), per_unit),
        ],
        out_shape=[
            jax.ShapeDtypeStruct((2 * HD, length), BF16),
            jax.ShapeDtypeStruct((UNITS, HD, length), F32),
            jax.ShapeDtypeStruct((UNITS, 1, length), F32),
            jax.ShapeDtypeStruct((UNITS, 16, length), F32),
            jax.ShapeDtypeStruct((UNITS, CODES, EXT), BF16),
        ],
        scratch_shapes=[
            pltpu.VMEM((EXT, length), BF16),
            pltpu.VMEM((8, length), F32),
            pltpu.VMEM((CODES, length), BF16),
            pltpu.VMEM((CODES, TILE), BF16),
            pltpu.VMEM((SPREAD + 16, CODES), F32),
            pltpu.VMEM((EXT, CODES), BF16),
            pltpu.VMEM((HD, length), F32),
        ],
        compiler_params=pltpu.CompilerParams(vmem_limit_bytes=VMEM_BYTES),
        cost_estimate=pl.CostEstimate(flops=0, bytes_accessed=1_000_000, transcendentals=0),
        name="attend",
    )(qkv, planes, seg_row, conv)


def attend_back_kernel(
    qkv_ref, planes_ref, seg_ref, grad_ref, numer_ref, dens_ref, sign_ref, bucket_ref,
    out_ref,
    spread, qprob, kprob, gspread, total, table, turned, gsign, proj,
):
    unit = pl.program_id(0)
    slot = unit // SOLO
    length = qkv_ref.shape[1]
    tiles = length // TILE
    q_rows = pl.ds(pl.multiple_of(slot * HD, HD), HD)
    k_rows = pl.ds(pl.multiple_of(2 * HD + slot * HD, HD), HD)
    v_rows = pl.ds(pl.multiple_of(4 * HD + slot * HD, HD), HD)

    @pl.when(jnp.logical_or(unit == 0, unit == SOLO))
    def _():
        def step(i, carry):
            lane = lanes_of(i, TILE)
            seg_row = seg_ref[:, lane]
            fill_spread(qkv_ref[v_rows, lane], seg_row, spread, lane)
            fill_member(seg_row, spread, lane)
            proj[:, lane] = jnp.zeros((2 * HD, TILE), F32)
            out_ref[v_rows, lane] = jnp.zeros((HD, TILE), F32)
            return carry

        lax.fori_loop(0, tiles, step, 0)
        gspread[SPREAD:EXT, :] = jnp.zeros((128, TILE), BF16)

    total[...] = jnp.zeros_like(total)

    def first(i, carry):
        lane = lanes_of(i, TILE)
        seg_row = seg_ref[:, lane]
        density = dens_ref[0, :, lane]
        inverse = 1.0 / jnp.maximum(density, 1.0)
        est_grad = grad_ref[q_rows, lane].astype(F32) * (1.0 / TABLES)
        num_grad = (est_grad * inverse).astype(BF16)
        fill_spread(num_grad, seg_row, gspread, slice(0, TILE))
        inner_sum = jnp.sum(est_grad * numer_ref[0, :, lane], axis=0, keepdims=True)
        dens_grad = jnp.where(density > 1.0, -inner_sum * inverse * inverse, 0.0)
        which = lax.broadcasted_iota(jnp.int32, (8, TILE), 0)
        high, low = split_two(jnp.where(which == seg_row, dens_grad, 0.0))
        gspread[SPREAD : SPREAD + 32, :] = jnp.concatenate(
            (high, low, high, jnp.zeros_like(high)), axis=0
        ).astype(BF16)
        collected = nn_dot(bucket_ref[0], gspread[...])
        for part in range(TILE // LANES):
            inner = slice(part * LANES, (part + 1) * LANES)
            outer = pl.ds(pl.multiple_of(i * TILE + part * LANES, LANES), LANES)
            sign_q = sign_ref[0, 0:8, outer]
            code_probs(sign_q, qprob, inner)
            gsign[0:8, outer] = signs_back(sign_q, collected[:, inner])
        total[...] += nt_dot(gspread[0 : SPREAD + 16, :], qprob[...])
        return carry

    lax.fori_loop(0, tiles, first, 0)
    mass_grad = total[SPREAD : SPREAD + 8, :] + total[SPREAD + 8 : SPREAD + 16, :]
    high, low = split_two(mass_grad)
    extra = jnp.concatenate((high, low, jnp.zeros((112, CODES), F32)), axis=0)
    table[...] = total[0:SPREAD, :].astype(BF16)
    turned[:, 0:SPREAD] = jnp.transpose(total[0:SPREAD, :]).astype(BF16)
    turned[:, SPREAD:EXT] = jnp.transpose(extra).astype(BF16)

    planes = unit_planes(planes_ref[pl.ds(pl.multiple_of(unit * BITS, BITS), BITS), :])
    plane_high, plane_low = split_two(planes)
    stack = jnp.concatenate((plane_high, plane_low, plane_high, jnp.zeros_like(plane_high)), axis=0)
    stack = stack.astype(BF16)

    def second(i, carry):
        lane = lanes_of(i, TILE)
        seg_row = seg_ref[:, lane]
        for part in range(TILE // LANES):
            inner = slice(part * LANES, (part + 1) * LANES)
            outer = pl.ds(pl.multiple_of(i * TILE + part * LANES, LANES), LANES)
            code_probs(sign_ref[0, 8:16, outer], kprob, inner)
        out_ref[v_rows, lane] += masked_fold(nn_dot(table[...], kprob[...]), seg_row)
        collected = nn_dot(turned[...], spread[:, lane])
        for part in range(TILE // LANES):
            inner = slice(part * LANES, (part + 1) * LANES)
            outer = pl.ds(pl.multiple_of(i * TILE + part * LANES, LANES), LANES)
            gsign[8:16, outer] = signs_back(sign_ref[0, 8:16, outer], collected[:, inner])
        signs = sign_ref[0, :, lane]
        flat = gsign[:, lane] * (1.0 - signs * signs)
        high, low = split_two(flat)
        for side in range(2):
            rows = slice(8 * side, 8 * side + 8)
            pieces = jnp.concatenate(
                (high[rows], high[rows], low[rows], jnp.zeros((8, TILE), F32)), axis=0
            ).astype(BF16)
            proj[side * HD : (side + 1) * HD, lane] += tn_dot(stack, pieces)
        return carry

    lax.fori_loop(0, tiles, second, 0)

    @pl.when(jnp.logical_or(unit == SOLO - 1, unit == UNITS - 1))
    def _():
        def step(i, carry):
            lane = lanes_of(i, TILE)
            for side, rows in ((0, q_rows), (1, k_rows)):
                vec = qkv_ref[rows, lane].astype(F32)
                inverse = lax.rsqrt(jnp.sum(vec * vec, axis=0, keepdims=True) + 1e-06)
                unit_vec = vec * inverse
                grad = proj[side * HD : (side + 1) * HD, lane]
                along = jnp.sum(unit_vec * grad, axis=0, keepdims=True)
                out_ref[rows, lane] = math.sqrt(HD) * inverse * (grad - unit_vec * along)
            return carry

        lax.fori_loop(0, tiles, step, 0)


def attend_back(qkv, planes, seg_row, grad, numer, dens, sign, bucket):
    length = qkv.shape[1]
    per_unit = lambda u: (u, 0, 0)
    fixed = lambda u: (0, 0)
    return pl.pallas_call(
        attend_back_kernel,
        grid=(UNITS,),
        in_specs=[
            pl.BlockSpec(qkv.shape, fixed),
            pl.BlockSpec(planes.shape, fixed),
            pl.BlockSpec(seg_row.shape, fixed),
            pl.BlockSpec(grad.shape, fixed),
            pl.BlockSpec((1, HD, length), per_unit),
            pl.BlockSpec((1, 1, length), per_unit),
            pl.BlockSpec((1, 16, length), per_unit),
            pl.BlockSpec((1, CODES, EXT), per_unit),
        ],
        out_specs=pl.BlockSpec((6 * HD, length), fixed),
        out_shape=jax.ShapeDtypeStruct((6 * HD, length), F32),
        scratch_shapes=[
            pltpu.VMEM((EXT, length), BF16),
            pltpu.VMEM((CODES, TILE), BF16),
            pltpu.VMEM((CODES, TILE), BF16),
            pltpu.VMEM((EXT, TILE), BF16),
            pltpu.VMEM((SPREAD + 16, CODES), F32),
            pltpu.VMEM((SPREAD, CODES), BF16),
            pltpu.VMEM((CODES, EXT), BF16),
            pltpu.VMEM((16, length), F32),
            pltpu.VMEM((2 * HD, length), F32),
        ],
        compiler_params=pltpu.CompilerParams(vmem_limit_bytes=VMEM_BYTES),
        cost_estimate=pl.CostEstimate(flops=0, bytes_accessed=1_000_000, transcendentals=0),
        name="attend_back",
    )(qkv, planes, seg_row, grad, numer, dens, sign, bucket)


SPAN = 192
OWN = 96
BLOCKS = ((0, HD), (HD, OWN))


def toeplitz(taps):
    row = jnp.pad(taps, ((0, 0), (0, SPAN + 1 - KW)))
    flat = jnp.tile(row, (1, LANES))[:, : LANES * SPAN]
    return jnp.swapaxes(flat.reshape(2, LANES, SPAN), 1, 2)


def band_product(pad_ref, band_ref, lane_wide, mask, h):
    low_row, high_row = BLOCKS[h]
    high, low = split_two(jnp.where(mask, band_ref[h], 0.0))
    rows = pad_ref[low_row:high_row, lane_wide]
    return nn_dot(rows, high.astype(BF16)) + nn_dot(rows, low.astype(BF16))


def conv_kernel(pad_ref, band_ref, col_ref, seg_ref, out_ref):
    tiles = out_ref.shape[1] // LANES
    side = lax.axis_index("mp") % 2
    half = OWN - HD
    own = pl.ds(pl.multiple_of(HD + side * half, half), half)
    other = pl.ds(pl.multiple_of(HD + (1 - side) * half, half), half)

    def step(i, carry):
        lane = lanes_of(i, LANES)
        start = pl.multiple_of(i * LANES, LANES)
        wide = pl.ds(start, SPAN)
        mask = col_ref[wide, :] == seg_ref[:, lane]
        out_ref[0:HD, lane] = band_product(pad_ref, band_ref, wide, mask, 0)
        out_ref[own, lane] = band_product(pad_ref, band_ref, wide, mask, 1)
        out_ref[other, lane] = jnp.zeros((half, LANES), F32)
        return carry

    lax.fori_loop(0, tiles, step, 0, unroll=16)


def segment_conv(padded, band, seg_col, seg_own):
    length = seg_own.shape[1]
    return pl.pallas_call(
        conv_kernel,
        out_shape=jax.ShapeDtypeStruct((2 * HD, length), F32),
        compiler_params=pltpu.CompilerParams(vmem_limit_bytes=VMEM_BYTES),
        cost_estimate=pl.CostEstimate(flops=0, bytes_accessed=1_000_000, transcendentals=0),
        name="segment_conv",
    )(padded, band, seg_col, seg_own)


def conv_back_kernel(gpad_ref, grad_ref, vpad_ref, band_ref, col_ref, seg_ref, segt_ref, colt_ref,
                     out_ref, tap_ref, corr):
    tiles = out_ref.shape[1] // LANES
    corr[...] = jnp.zeros_like(corr)

    def step(i, carry):
        lane = lanes_of(i, LANES)
        start = pl.multiple_of(i * LANES, LANES)
        wide = pl.ds(start, SPAN)
        twice = pl.ds(start, 2 * LANES)
        mask = col_ref[wide, :] == seg_ref[:, lane]
        for h, (low_row, high_row) in enumerate(BLOCKS):
            out_ref[low_row:high_row, lane] = band_product(gpad_ref, band_ref, wide, mask, h)
        mask_turned = colt_ref[lane, :] == segt_ref[:, twice]
        for h, (low_row, high_row) in enumerate(BLOCKS):
            match = tn_dot(grad_ref[low_row:high_row, lane], vpad_ref[low_row:high_row, twice])
            corr[h] += jnp.where(mask_turned, match, 0.0)
        return carry

    lax.fori_loop(0, tiles, step, 0, unroll=16)
    row = lax.broadcasted_iota(jnp.int32, (LANES, 2 * LANES), 0)
    for h in range(2):
        skew = corr[h]
        for bit in range(7):
            moved = pltpu.roll(skew, 2 * LANES - (1 << bit), 1)
            skew = jnp.where((row >> bit) & 1 == 1, moved, skew)
        tap_ref[h] = jnp.sum(skew, axis=0, keepdims=True)


def conv_back(gpad, grad, vpad, band, seg_col, seg_own, seg_wide, col_own):
    length = seg_own.shape[1]
    return pl.pallas_call(
        conv_back_kernel,
        out_shape=(
            jax.ShapeDtypeStruct((OWN, length), F32),
            jax.ShapeDtypeStruct((2, 1, 2 * LANES), F32),
        ),
        scratch_shapes=[pltpu.VMEM((2, LANES, 2 * LANES), F32)],
        compiler_params=pltpu.CompilerParams(vmem_limit_bytes=VMEM_BYTES),
        cost_estimate=pl.CostEstimate(flops=0, bytes_accessed=1_000_000, transcendentals=0),
        name="conv_back",
    )(gpad, grad, vpad, band, seg_col, seg_own, seg_wide, col_own)


def norm_rows(values):
    center = values - jnp.mean(values, axis=1, keepdims=True)
    inverse = lax.rsqrt(jnp.mean(center * center, axis=1, keepdims=True) + 1e-05)
    return center * inverse, inverse


def norm_back(upstream, normed, inverse, gain):
    scaled = upstream * gain
    inner = (
        scaled
        - jnp.mean(scaled, axis=1, keepdims=True)
        - normed * jnp.mean(scaled * normed, axis=1, keepdims=True)
    )
    return inner * inverse


def gelu_pair(value):
    cdf = 0.5 + 0.5 * lax.erf(value * math.sqrt(0.5))
    pdf = jnp.exp(-0.5 * value * value) * (1.0 / math.sqrt(2.0 * math.pi))
    return value * cdf, cdf + value * pdf


def column_sum(values):
    return jnp.sum(values, axis=0, keepdims=True)


MESH = pl.DeviceIdType.MESH
OFFSETS = (0, -2, 2, 4)
INVERSE = (0, 2, 1, 3, 4, 6, 5, 7)


def repeat(start, stop, action):
    def body(r, carry):
        action(r)
        return carry

    lax.fori_loop(start, stop, body, 0)


def remote(src, dst, send, recv, target):
    return pltpu.make_async_remote_copy(
        src_ref=src, dst_ref=dst, send_sem=send, recv_sem=recv,
        device_id={"mp": target}, device_id_type=MESH,
    )


def greet(targets):
    barrier = pltpu.get_barrier_semaphore()
    for target in targets:
        pl.semaphore_signal(barrier, inc=1, device_id={"mp": target}, device_id_type=MESH)
    pl.semaphore_wait(barrier, len(targets))


def gather_kernel(x_ref, w_ref, all_ref, qkv_ref, wide, send, recv):
    count, rows, _ = all_ref.shape
    m = lax.axis_index("mp")
    side = m % 2
    sibling = m + 1 - 2 * side
    left = (m + count - 2) % count
    right = (m + 2) % count
    far = (m + 4) % count
    half = OWN - HD
    cut = rows // 2
    greet((left, right, sibling))

    def copy(n, src, dst, target):
        return remote(src, dst, send.at[n], recv.at[n], target)

    def piece(n, which):
        return pl.ds(pl.multiple_of(n * 2 * HD + HD + which * half, half), half)

    def weight_copy(n, which):
        source = w_ref.at[pl.ds(pl.multiple_of(n * OWN + (1 - side) * HD, half), half), :]
        return copy(8 + n, source, wide.at[piece(n, which), :], sibling)

    for n in range(3):
        weight_copy(n, side).start()
    to_right = copy(0, x_ref, all_ref.at[m], right)
    to_left = copy(1, x_ref, all_ref.at[m], left)
    to_sibling = copy(2, x_ref, all_ref.at[m], sibling)
    to_right.start()
    to_left.start()
    to_sibling.start()
    all_ref[m] = x_ref[...]
    for n in range(3):
        solo = pl.ds(pl.multiple_of(n * OWN + side * half, half), HD)
        own = pl.ds(pl.multiple_of(n * OWN + (1 - side) * HD, half), half)
        wide[n * 2 * HD : n * 2 * HD + HD, :] = w_ref[solo, :]
        wide[piece(n, side), :] = w_ref[own, :]
    for n in range(3):
        weight_copy(n, 1 - side).wait_recv()

    def project(block):
        lane = pl.ds(pl.multiple_of(block * rows, rows), rows)
        qkv_ref[:, lane] = nt_dot(wide[...], all_ref[block]).astype(BF16)

    project(m)
    copy(2, x_ref, all_ref.at[sibling], sibling).wait_recv()
    project(sibling)
    copy(0, x_ref, all_ref.at[left], left).wait_recv()
    on_right = copy(3, all_ref.at[left, 0:cut], all_ref.at[left, 0:cut], right)
    on_right.start()
    over_left = copy(5, all_ref.at[left], all_ref.at[left], sibling)
    over_left.start()
    copy(1, x_ref, all_ref.at[right], right).wait_recv()
    on_left = copy(4, all_ref.at[right, cut:rows], all_ref.at[right, cut:rows], left)
    on_left.start()
    over_right = copy(6, all_ref.at[right], all_ref.at[right], sibling)
    over_right.start()
    project(left)
    project(right)
    other_left = (sibling + count - 2) % count
    other_right = (sibling + 2) % count
    other_far = (sibling + 4) % count
    copy(5, x_ref, all_ref.at[other_left], sibling).wait_recv()
    project(other_left)
    copy(6, x_ref, all_ref.at[other_right], sibling).wait_recv()
    project(other_right)
    copy(3, x_ref.at[0:cut], all_ref.at[far, 0:cut], left).wait_recv()
    copy(4, x_ref.at[cut:rows], all_ref.at[far, cut:rows], right).wait_recv()
    over_far = copy(7, all_ref.at[far], all_ref.at[far], sibling)
    over_far.start()
    project(far)
    copy(7, x_ref, all_ref.at[other_far], sibling).wait_recv()
    project(other_far)
    for n in range(3):
        weight_copy(n, side).wait_send()
    for sent in (
        to_right, to_left, to_sibling, on_right, on_left, over_left, over_right, over_far
    ):
        sent.wait_send()


def gather_qkv(x, w_rows, count):
    rows, width = x.shape
    vmem = pl.BlockSpec(memory_space=pltpu.VMEM)
    return pl.pallas_call(
        gather_kernel,
        in_specs=[vmem] * 2,
        out_specs=[vmem] * 2,
        out_shape=(
            jax.ShapeDtypeStruct((count, rows, width), BF16),
            jax.ShapeDtypeStruct((6 * HD, count * rows), BF16),
        ),
        scratch_shapes=[
            pltpu.VMEM((6 * HD, width), BF16),
            pltpu.SemaphoreType.DMA((11,)),
            pltpu.SemaphoreType.DMA((11,)),
        ],
        compiler_params=pltpu.CompilerParams(
            vmem_limit_bytes=VMEM_BYTES, collective_id=2, has_side_effects=True
        ),
        cost_estimate=pl.CostEstimate(
            flops=12 * HD * count * rows * width, bytes_accessed=30_000_000, transcendentals=0
        ),
        name="gather_qkv",
    )(x, w_rows)


def around(m, count):
    sibling = m + 1 - 2 * (m % 2)
    return [(base + count + off) % count for base in (m, sibling) for off in OFFSETS]


def middle_kernel(
    sent_ref, x_ref, cot_ref, own_w, left_w, right_w, far_w, scale_ref,
    result_ref, lows_ref, one_ref, attn_ref, part_ref,
    wall, att_in, attn_out, slope, keep, acc,
    load, give_send, give_recv, rest_send, rest_recv, in_send, in_recv, out_send, out_recv,
):
    rows = x_ref.shape[0]
    count = att_in.shape[0]
    units = slope.shape[2]
    both = 2 * units
    m = lax.axis_index("mp")
    devices = around(m, count)
    sibling = devices[4]
    greet(devices[1:])

    def tokens(index):
        return pl.ds(pl.multiple_of(index * rows, rows), rows)

    blocks = (own_w, left_w, right_w, far_w)
    out_rows = slice(both, both + 2 * HD)
    ffn_rows = slice(0, both)

    def give(n):
        return remote(
            blocks[n].at[out_rows], wall.at[4 + n, out_rows], give_send.at[n], give_recv.at[n],
            sibling,
        )

    def rest(n):
        return remote(
            blocks[n].at[ffn_rows], wall.at[4 + n, ffn_rows], rest_send.at[n], rest_recv.at[n],
            sibling,
        )

    def att_copy(n, slot, sem):
        return remote(
            sent_ref.at[:, tokens(devices[n])], att_in.at[slot], in_send.at[n], in_recv.at[sem],
            devices[n],
        )

    def attn_copy(n, lane, sem):
        return remote(
            attn_out.at[n], attn_ref.at[:, tokens(lane)], out_send.at[n], out_recv.at[sem],
            devices[n],
        )

    for n in range(1, count):
        att_copy(n, INVERSE[n], INVERSE[n]).start()
    for n in range(4):
        give(n).start()
    for n in range(4):
        pltpu.make_async_copy(blocks[n], wall.at[n], load.at[n]).start()
    for n in range(4):
        rest(n).start()
    att_in[0] = sent_ref[:, tokens(m)]
    for n in range(4):
        pltpu.make_async_copy(blocks[n], wall.at[n], load.at[n]).wait()
        give(n).wait_recv()
    for n in range(1, count):
        att_copy(n, n, n).wait_recv()
    projected = tn_dot(att_in[0], wall[0, out_rows])
    for n in range(1, count):
        projected = projected + tn_dot(att_in[n], wall[n, out_rows])
    unit, inverse = norm_rows(x_ref[...].astype(F32) + projected)
    hidden = unit * scale_ref[0:1] + scale_ref[1:2]
    keep[0] = unit
    keep[1] = hidden
    lows_ref[0] = hidden.astype(BF16)
    acc[...] = jnp.zeros_like(acc)

    def forward(i, carry):
        low = lows_ref[0]
        total = acc[...]
        for n in range(2):
            active, lean = gelu_pair(nt_dot(low, wall[2 * i + n, 0:units]))
            slope[2 * i + n] = lean
            total = total + nn_dot(active.astype(BF16), wall[2 * i + n, units:both])
        acc[...] = total
        return carry

    lax.fori_loop(0, 2, forward, 0)
    for n in range(4):
        rest(n).wait_recv()
    lax.fori_loop(2, 4, forward, 0)
    unit, inv = norm_rows(keep[1] + acc[...])
    result_ref[...] = (unit * scale_ref[2:3] + scale_ref[3:4]).astype(BF16)
    upstream = cot_ref[...].astype(F32)
    part_ref[2:3] = column_sum(upstream * unit)
    part_ref[3:4] = column_sum(upstream)
    grad = norm_back(upstream, unit, inv, scale_ref[2:3])
    keep[1] = grad
    lows_ref[1] = grad.astype(BF16)
    acc[...] = jnp.zeros_like(acc)

    def backward(i, carry):
        low = lows_ref[1]
        total = acc[...]
        for n in range(2):
            pre_grad = nt_dot(low, wall[2 * i + n, units:both]) * slope[2 * i + n]
            total = total + nn_dot(pre_grad.astype(BF16), wall[2 * i + n, 0:units])
        acc[...] = total
        return carry

    lax.fori_loop(0, 4, backward, 0)
    upstream = keep[1] + acc[...]
    unit = keep[0]
    part_ref[0:1] = column_sum(upstream * unit)
    part_ref[1:2] = column_sum(upstream)
    part_ref[4:8] = jnp.zeros((4, part_ref.shape[1]), F32)
    grad = norm_back(upstream, unit, inverse, scale_ref[0:1])
    one_ref[...] = grad
    low = grad.astype(BF16)
    lows_ref[2] = low
    for n in range(1, count):
        attn_out[n] = nt_dot(wall[n, out_rows], low).astype(BF16)
        attn_copy(n, m, INVERSE[n]).start()
    attn_ref[:, tokens(m)] = nt_dot(wall[0, out_rows], low).astype(BF16)
    for n in range(1, count):
        attn_copy(n, devices[n], n).wait_recv()
    for n in range(4):
        give(n).wait_send()
        rest(n).wait_send()
    for n in range(1, count):
        att_copy(n, INVERSE[n], INVERSE[n]).wait_send()
        attn_copy(n, m, INVERSE[n]).wait_send()


def middle(sent, x, cot, blocks, scale, count):
    rows, width = x.shape
    depth = sent.shape[0]
    units = (blocks[0].shape[0] - depth) // 2
    vmem = pl.BlockSpec(memory_space=pltpu.VMEM)
    sems = lambda n: pltpu.SemaphoreType.DMA((n,))
    return pl.pallas_call(
        middle_kernel,
        in_specs=[vmem] * 3 + [pl.BlockSpec(memory_space=pl.ANY)] * 4 + [vmem],
        out_specs=[vmem] * 5,
        out_shape=(
            jax.ShapeDtypeStruct((rows, width), BF16),
            jax.ShapeDtypeStruct((3, rows, width), BF16),
            jax.ShapeDtypeStruct((rows, width), F32),
            jax.ShapeDtypeStruct(sent.shape, BF16),
            jax.ShapeDtypeStruct((8, width), F32),
        ),
        scratch_shapes=[
            pltpu.VMEM((count,) + blocks[0].shape, BF16),
            pltpu.VMEM((count, depth, rows), BF16),
            pltpu.VMEM((count, depth, rows), BF16),
            pltpu.VMEM((count, rows, units), F32),
            pltpu.VMEM((2, rows, width), F32),
            pltpu.VMEM((rows, width), F32),
            sems(4), sems(4), sems(4), sems(4), sems(4),
            sems(count), sems(count), sems(count), sems(count),
        ],
        compiler_params=pltpu.CompilerParams(
            vmem_limit_bytes=VMEM_BYTES, collective_id=1, has_side_effects=True
        ),
        cost_estimate=pl.CostEstimate(
            flops=16 * rows * width * count * units, bytes_accessed=26_000_000,
            transcendentals=0,
        ),
        name="middle",
    )(sent, x, cot, *blocks, scale)


def ffn_grad_kernel(
    own_x, left_x, right_x, far_x, att_ref, w_ref, grad_ref, wall, acc, load, give_send, give_recv
):
    count, _, rows, _ = wall.shape
    units = (w_ref.shape[0] - 2 * HD) // 2
    m = lax.axis_index("mp")
    sibling = m + 1 - 2 * (m % 2)
    greet((sibling,))
    blocks = (own_x, left_x, right_x, far_x)

    def give(n):
        return remote(blocks[n], wall.at[4 + n], give_send.at[n], give_recv.at[n], sibling)

    for n in range(4):
        pltpu.make_async_copy(blocks[n], wall.at[n], load.at[n]).start()
    for n in range(4):
        give(n).start()
    acc[...] = jnp.zeros_like(acc)
    for n in range(4):
        pltpu.make_async_copy(blocks[n], wall.at[n], load.at[n]).wait()

    def lane_of(slot):
        base = jnp.where(slot < 4, m, sibling)
        place = slot % 4
        offset = jnp.where(place == 0, 0, jnp.where(place == 1, count - 2, 2 * place - 2))
        device = (base + offset) % count
        return pl.ds(pl.multiple_of(device * rows, rows), rows)

    def step(i, carry):
        sums = [None] * 3
        for n in range(2):
            slot = 2 * i + n
            hidden, ffn, out = wall[slot, 0], wall[slot, 1], wall[slot, 2]
            active, lean = gelu_pair(nt_dot(hidden, w_ref[0:units]))
            pre_grad = (nt_dot(ffn, w_ref[units : 2 * units]) * lean).astype(BF16)
            parts = (
                tn_dot(pre_grad, hidden),
                tn_dot(active.astype(BF16), ffn),
                nn_dot(att_ref[:, lane_of(slot)], out),
            )
            sums = [p if t is None else t + p for t, p in zip(sums, parts)]
        acc[0:units, :] += sums[0]
        acc[units : 2 * units, :] += sums[1]
        acc[2 * units : 2 * units + OWN, :] += sums[2]
        return carry

    lax.fori_loop(0, 2, step, 0)
    for n in range(4):
        give(n).wait_recv()
    lax.fori_loop(2, 4, step, 0)
    grad_ref[...] = acc[...].astype(BF16)
    for n in range(4):
        give(n).wait_send()


def ffn_grad(blocks, attended, weights, count):
    _, rows, width = blocks[0].shape
    units = (weights.shape[0] - 2 * HD) // 2
    total = 2 * units + OWN
    vmem = pl.BlockSpec(memory_space=pltpu.VMEM)
    sems = pltpu.SemaphoreType.DMA((4,))
    return pl.pallas_call(
        ffn_grad_kernel,
        in_specs=[pl.BlockSpec(memory_space=pl.ANY)] * 4 + [vmem] * 2,
        out_specs=vmem,
        out_shape=jax.ShapeDtypeStruct((total, width), BF16),
        scratch_shapes=[
            pltpu.VMEM((count,) + blocks[0].shape, BF16),
            pltpu.VMEM((total, width), F32),
            sems, sems, sems,
        ],
        compiler_params=pltpu.CompilerParams(
            vmem_limit_bytes=VMEM_BYTES, collective_id=3, has_side_effects=True
        ),
        cost_estimate=pl.CostEstimate(
            flops=8 * count * rows * width * units, bytes_accessed=12_000_000, transcendentals=0
        ),
        name="ffn_grad",
    )(*blocks, attended, weights)


def finish_kernel(
    part_ref, one_ref, grads_ref, small_ref,
    out_ref, sums_ref, tiny_ref,
    pair_in, stage, line_in, slice_in, near_in, far_in,
    pair_send, pair_recv, line_send, line_recv, slice_send, slice_recv,
    whole_send, whole_recv, near_send, near_recv, far_send, far_recv,
):
    blocks = grads_ref.shape[0]
    count = part_ref.shape[0]
    chips = count // 2
    d = lax.axis_index("dp")
    m = lax.axis_index("mp")
    core = m % 2
    chip = m // 2
    sibling = m + 1 - 2 * core

    barrier = pltpu.get_barrier_semaphore()

    def greet_block(r, carry):
        pl.semaphore_signal(
            barrier, inc=1, device_id={"dp": (d + r) % blocks}, device_id_type=MESH
        )
        return carry

    def greet_model(r, carry):
        pl.semaphore_signal(barrier, inc=1, device_id={"mp": (m + r) % count}, device_id_type=MESH)
        return carry

    lax.fori_loop(1, blocks, greet_block, 0)
    lax.fori_loop(1, count, greet_model, 0)
    pl.semaphore_wait(barrier, blocks + count - 2)

    def pair_copy(target):
        return pltpu.make_async_remote_copy(
            src_ref=part_ref.at[2 * target + 1 - core],
            dst_ref=pair_in.at[target],
            send_sem=pair_send.at[target],
            recv_sem=pair_recv.at[target],
            device_id={"mp": sibling},
            device_id_type=MESH,
        )

    def line_copy(k):
        return pltpu.make_async_remote_copy(
            src_ref=stage.at[k],
            dst_ref=line_in.at[k],
            send_sem=line_send.at[k],
            recv_sem=line_recv.at[k],
            device_id={"mp": (m + 2 * k) % count},
            device_id_type=MESH,
        )

    def slice_copy(r):
        peer = (d + r) % blocks
        return pltpu.make_async_remote_copy(
            src_ref=grads_ref.at[peer],
            dst_ref=slice_in.at[r],
            send_sem=slice_send.at[r],
            recv_sem=slice_recv.at[r],
            device_id={"dp": peer},
            device_id_type=MESH,
        )

    def whole_copy(r, owner):
        return pltpu.make_async_remote_copy(
            src_ref=sums_ref.at[d],
            dst_ref=sums_ref.at[owner],
            send_sem=whole_send.at[r],
            recv_sem=whole_recv.at[r],
            device_id={"dp": (d + r) % blocks},
            device_id_type=MESH,
        )

    def near_copy(r, owner):
        return pltpu.make_async_remote_copy(
            src_ref=small_ref,
            dst_ref=near_in.at[owner],
            send_sem=near_send.at[r],
            recv_sem=near_recv.at[r],
            device_id={"mp": (m + r) % count},
            device_id_type=MESH,
        )

    def far_copy(r, owner):
        return pltpu.make_async_remote_copy(
            src_ref=far_in.at[d],
            dst_ref=far_in.at[owner],
            send_sem=far_send.at[r],
            recv_sem=far_recv.at[r],
            device_id={"dp": (d + r) % blocks},
            device_id_type=MESH,
        )

    order = [2, 1, 3, 0]
    for k in order:
        pair_copy((chip + k) % chips).start()
    repeat(1, count, lambda r: near_copy(r, m).start())
    repeat(1, blocks, lambda r: slice_copy(r).start())

    for k in order[:3]:
        target = (chip + k) % chips
        pair_copy(target).wait_recv()
        both = part_ref[2 * target + core].astype(F32) + pair_in[target].astype(F32)
        stage[k] = both.astype(BF16)
        line_copy(k).start()

    near_in[m] = small_ref[...]
    repeat(1, count, lambda r: near_copy(r, (m + count - r) % count).wait_recv())
    total = near_in[0]
    for r in range(1, count):
        total = total + near_in[r]
    far_in[d] = total
    repeat(1, blocks, lambda r: far_copy(r, d).start())

    repeat(1, blocks, lambda r: slice_copy(r).wait_recv())
    depth = grads_ref.shape[1]
    for low in range(0, depth, 16):
        rows = slice(low, min(low + 16, depth))
        total = grads_ref[d, rows].astype(F32)
        for r in range(1, blocks):
            total = total + slice_in[r, rows].astype(F32)
        sums_ref[d, rows] = total.astype(BF16)
    repeat(1, blocks, lambda r: whole_copy(r, d).start())

    pair_copy(chip).wait_recv()
    total = part_ref[m].astype(F32) + pair_in[chip].astype(F32)
    for k in range(1, chips):
        line_copy(k).wait_recv()
        total = total + line_in[k].astype(F32)
    out_ref[...] = one_ref[...] + total

    repeat(1, blocks, lambda r: far_copy(r, (d + blocks - r) % blocks).wait_recv())
    total = far_in[0]
    for r in range(1, blocks):
        total = total + far_in[r]
    tiny_ref[...] = total
    repeat(1, blocks, lambda r: whole_copy(r, (d + blocks - r) % blocks).wait_recv())

    for k in range(chips):
        pair_copy((chip + k) % chips).wait_send()
    for k in range(1, chips):
        line_copy(k).wait_send()
    repeat(1, count, lambda r: near_copy(r, m).wait_send())
    repeat(1, blocks, lambda r: slice_copy(r).wait_send())
    repeat(1, blocks, lambda r: far_copy(r, d).wait_send())
    repeat(1, blocks, lambda r: whole_copy(r, d).wait_send())


def finish(part, one_grad, grads, small, blocks):
    count = part.shape[0]
    chips = count // 2
    rows, width = one_grad.shape
    sems = lambda n: pltpu.SemaphoreType.DMA((n,))
    vmem = pl.BlockSpec(memory_space=pltpu.VMEM)
    return pl.pallas_call(
        finish_kernel,
        in_specs=[vmem] * 4,
        out_specs=[vmem] * 3,
        out_shape=(
            jax.ShapeDtypeStruct(one_grad.shape, F32),
            jax.ShapeDtypeStruct(grads.shape, BF16),
            jax.ShapeDtypeStruct(small.shape, F32),
        ),
        scratch_shapes=[
            pltpu.VMEM((chips, rows, width), BF16),
            pltpu.VMEM((chips, rows, width), BF16),
            pltpu.VMEM((chips, rows, width), BF16),
            pltpu.VMEM(grads.shape, BF16),
            pltpu.VMEM((count,) + small.shape, F32),
            pltpu.VMEM((blocks,) + small.shape, F32),
            sems(chips), sems(chips), sems(chips), sems(chips), sems(blocks), sems(blocks),
            sems(blocks), sems(blocks), sems(count), sems(count), sems(blocks), sems(blocks),
        ],
        compiler_params=pltpu.CompilerParams(
            vmem_limit_bytes=VMEM_BYTES, collective_id=0, has_side_effects=True
        ),
        cost_estimate=pl.CostEstimate(flops=0, bytes_accessed=30_000_000, transcendentals=0),
        name="finish",
    )(part, one_grad, grads, small)


def from_partner(block):
    count = lax.axis_size("mp")
    route = [(n, n ^ 1) for n in range(count)]
    return lax.ppermute(block, "mp", route)


def from_chips(block):
    count = lax.axis_size("mp")
    return tuple(
        lax.ppermute(block, "mp", [(n, (n - off) % count) for n in range(count)])
        for off in OFFSETS[1:]
    )


def on_device(
    inputs, segment, w_query, w_key, w_value, planes, conv_taps, w_out,
    ln1_gain, ln1_bias, w_up, w_down, ln2_gain, ln2_bias, cotangent,
):
    position = lax.axis_index("mp")
    count = lax.axis_size("mp")
    side = position % 2
    first_side = side == 0
    half = OWN - HD
    rows = inputs.shape[0]

    def solo_first(block, axis):
        return jnp.where(first_side, block, jnp.roll(block, -half, axis))

    def own_order(block, axis):
        return jnp.where(first_side, block, jnp.roll(block, half, axis))

    def join(own_half, peer_half, axis):
        return jnp.where(
            first_side,
            jnp.concatenate((own_half, peer_half), axis),
            jnp.concatenate((peer_half, own_half), axis),
        )

    def half_of(block, which):
        return lax.dynamic_slice_in_dim(block, which * half, half, 0)

    query_w, key_w, value_w = (solo_first(w, 1) for w in (w_query, w_key, w_value))
    out_w = solo_first(w_out, 0)
    out_group = jnp.concatenate((out_w[:HD], join(out_w[HD:], from_partner(out_w[HD:]), 0)), 0)
    block_w = jnp.concatenate((w_up.T, w_down, out_group), 0)
    gathered, qkv = gather_qkv(
        inputs, jnp.concatenate((w_query, w_key, w_value), 1).T, count
    )
    block_w, qkv = lax.optimization_barrier((block_w, qkv))
    blocks_w = (block_w,) + from_chips(block_w)
    gathered = gathered.reshape(rows * count, -1)

    unit_rows = jnp.concatenate(
        (planes, lax.dynamic_slice_in_dim(planes, side * 2 * BITS, 2 * BITS, 0)), 0
    )
    seg_row = segment[None, :]
    seg_wide = jnp.pad(segment, (32, 96), constant_values=-2)
    seg_own = jnp.where(segment < 0, -3, segment)
    group = position // 2
    heads = jnp.stack((3 * group + 2 * side, 3 * group + 1))
    selector = (heads[:, None] == jnp.arange(HEADS, dtype=jnp.int32)[None, :]).astype(F32)
    taps = jnp.dot(selector, conv_taps.T, precision=lax.Precision.HIGHEST)

    value_own = jnp.concatenate((qkv[4 * HD : 5 * HD], half_of(qkv[5 * HD :], side)), 0)
    value_pad = jnp.pad(value_own, ((0, 0), (32, 96)))
    conv = segment_conv(value_pad, toeplitz(taps), seg_wide[:, None], seg_own[None, :])
    sent, numer, dens, sign, bucket = attend(qkv, unit_rows, seg_row, conv)
    scale = jnp.stack((ln1_gain, ln1_bias, ln2_gain, ln2_bias) * 2)
    outputs, lows, one_grad, attn_grad, norm_part = middle(
        sent, inputs, cotangent, blocks_w, scale, count
    )
    blocks_x = (lows,) + from_chips(lows)
    received = from_partner(half_of(sent[HD:], 1 - side)).astype(F32)
    mixed = (half_of(sent[HD:], side).astype(F32) + received).astype(BF16)
    attended = jnp.concatenate((sent[:HD], mixed), 0)
    grad_own = jnp.concatenate((attn_grad[:HD], half_of(attn_grad[HD:], side)), 0)
    grad_pad = jnp.pad(grad_own, ((0, 0), (32, 96)))
    value_conv, tap_part = conv_back(
        grad_pad, grad_own, value_pad, toeplitz(taps[:, ::-1]),
        seg_wide[:, None], seg_own[None, :], seg_wide[None, :], seg_own[:, None],
    )
    conv_part = jnp.dot(
        tap_part[:, 0, :KW].T, selector, precision=lax.Precision.HIGHEST
    )
    back = attend_back(qkv, unit_rows, seg_row, attn_grad, numer, dens, sign, bucket)
    back, *blocks_x = lax.optimization_barrier((back,) + blocks_x)
    ffn_part = ffn_grad(blocks_x, attended, block_w, count)
    shared = jnp.concatenate(
        [half_of(back[(2 * n + 1) * HD : (2 * n + 2) * HD], 1 - side) for n in range(3)], 0
    )
    peer_shared = from_partner(shared.astype(BF16)).astype(F32)
    sums = []
    for n in range(3):
        solo = back[2 * n * HD : (2 * n + 1) * HD]
        mixed = half_of(back[(2 * n + 1) * HD : (2 * n + 2) * HD], side)
        mixed = mixed + peer_shared[n * half : (n + 1) * half]
        sums.append(jnp.concatenate((solo, mixed), 0))
    sums[2] = sums[2] + value_conv
    lows = jnp.concatenate([s.astype(BF16) for s in sums], 0)
    weight_part = lax.dot_general(
        lows, gathered, (((1,), (0,)), ((), ())), preferred_element_type=F32
    ).astype(BF16)
    inputs_part = lax.dot_general(
        lows,
        jnp.concatenate((query_w, key_w, value_w), 1),
        (((0,), (1,)), ((), ())),
        preferred_element_type=F32,
    ).astype(BF16)
    blocks = lax.axis_size("dp")
    width = inputs.shape[1]
    conv_flat = jnp.pad(conv_part.reshape(-1), (0, -KW * HEADS % width)).reshape(-1, width)
    small = jnp.concatenate((norm_part[:4], conv_flat), 0)
    small = jnp.pad(small, ((0, -small.shape[0] % 8), (0, 0)))
    inputs_grad, sums, tiny = finish(
        inputs_part.reshape(count, rows, width),
        one_grad,
        jnp.concatenate((ffn_part, weight_part), 0).reshape(blocks, -1, width),
        small,
        blocks,
    )
    sums = sums.reshape(-1, width).astype(F32)
    units = w_up.shape[1]
    w_up_grad = sums[:units].T
    w_down_grad = sums[units : 2 * units]
    w_out_grad = own_order(sums[2 * units : 2 * units + OWN], 0)
    weight_grads = sums[2 * units + OWN :].T
    w_query_grad, w_key_grad, w_value_grad = (
        own_order(weight_grads[:, n * OWN : (n + 1) * OWN], 1) for n in range(3)
    )
    conv_taps_grad = tiny[4:].reshape(-1)[: KW * HEADS].reshape(KW, HEADS)
    norm_grads = tiny
    return (
        outputs, inputs_grad, w_query_grad, w_key_grad, w_value_grad, conv_taps_grad, w_out_grad,
        norm_grads[0], norm_grads[1], w_up_grad, w_down_grad, norm_grads[2], norm_grads[3],
    )


def solution(mesh):
    rows = P(("dp", "mp"), None)
    cols = P(None, "mp")
    return jax.shard_map(
        on_device,
        mesh=mesh,
        in_specs=(
            rows, P("dp"), cols, cols, cols, P(), P(), P("mp", None), P(), P(),
            cols, P("mp", None), P(), P(), rows,
        ),
        out_specs=(
            rows, rows, cols, cols, cols, P(), P("mp", None), P(), P(),
            cols, P("mp", None), P(), P(),
        ),
        check_vma=False,
    )
```

```python
from functools import partial
import math
import jax
import jax.numpy as jnp
from jax import lax
from jax.experimental import pallas as pl
from jax.experimental.pallas import tpu as pltpu
from jax.sharding import PartitionSpec as P

HEADS = 12
HD = 64
TABLES = 4
BITS = 8
KW = 65
MAXSEG = 8
CODES = 256
UNITS = 6
SOLO = 4
SPREAD = MAXSEG * HD
EXT = SPREAD + 128
LANES = 128
TILE = 2048
F32 = jnp.float32
BF16 = jnp.bfloat16
VMEM_BYTES = 56 * 1024 * 1024


def nt_dot(left, right):
    return lax.dot_general(left, right, (((1,), (1,)), ((), ())), preferred_element_type=F32)


def tn_dot(left, right):
    return lax.dot_general(left, right, (((0,), (0,)), ((), ())), preferred_element_type=F32)


def nn_dot(left, right):
    return lax.dot_general(left, right, (((1,), (0,)), ((), ())), preferred_element_type=F32)


def half_sign(bit):
    rows = lax.broadcasted_iota(jnp.int32, (8, LANES), 0)
    return jnp.where((rows >> bit) & 1 == 0, 0.5, -0.5).astype(F32)


def code_factors(signs):
    pos0, neg0 = 0.5 + 0.5 * signs[0:1], 0.5 - 0.5 * signs[0:1]
    pos1, neg1 = 0.5 + 0.5 * signs[1:2], 0.5 - 0.5 * signs[1:2]
    tops = (pos0 * pos1, pos0 * neg1, neg0 * pos1, neg0 * neg1)
    picks = [half_sign(2), half_sign(1), half_sign(0)]
    mids = [0.5 + picks[n] * signs[2 + n : 3 + n] for n in range(3)]
    lows = [0.5 + picks[n] * signs[5 + n : 6 + n] for n in range(3)]
    return tops, mids, lows, picks


def code_probs(signs, out_ref, lane):
    tops, mids, lows, _ = code_factors(signs)
    mid = mids[0] * mids[1] * mids[2]
    low = lows[0] * lows[1] * lows[2]
    for top_index in range(4):
        low_top = low * tops[top_index]
        for pair in range(4):
            rows = jnp.concatenate(
                (
                    low_top * mid[2 * pair : 2 * pair + 1],
                    low_top * mid[2 * pair + 1 : 2 * pair + 2],
                ),
                axis=0,
            )
            first = top_index * 64 + pair * 16
            out_ref[first : first + 16, lane] = rows.astype(BF16)


def signs_back(signs, grads):
    tops, mids, lows, picks = code_factors(signs)
    mid = mids[0] * mids[1] * mids[2]
    low = lows[0] * lows[1] * lows[2]
    mid_rows = [jnp.broadcast_to(mid[m : m + 1], (8, LANES)) for m in range(8)]
    top_rows = [jnp.broadcast_to(tops[t], (8, LANES)) for t in range(4)]
    by_top = [None] * 4
    by_mid = [None] * 8
    for t in range(4):
        for m in range(8):
            piece = grads[t * 64 + m * 8 : t * 64 + m * 8 + 8]
            a = piece * mid_rows[m]
            b = piece * top_rows[t]
            by_top[t] = a if by_top[t] is None else by_top[t] + a
            by_mid[m] = b if by_mid[m] is None else by_mid[m] + b
    low_grad = by_top[0] * top_rows[0]
    for t in range(1, 4):
        low_grad = low_grad + by_top[t] * top_rows[t]
    top_grad = [jnp.sum(low * by_top[t], axis=0, keepdims=True) for t in range(4)]
    mid_grad = jnp.concatenate(
        [jnp.sum(low * by_mid[m], axis=0, keepdims=True) for m in range(8)], axis=0
    )
    pos0, neg0 = 0.5 + 0.5 * signs[0:1], 0.5 - 0.5 * signs[0:1]
    pos1, neg1 = 0.5 + 0.5 * signs[1:2], 0.5 - 0.5 * signs[1:2]
    out = [
        0.5 * ((top_grad[0] - top_grad[2]) * pos1 + (top_grad[1] - top_grad[3]) * neg1),
        0.5 * ((top_grad[0] - top_grad[1]) * pos0 + (top_grad[2] - top_grad[3]) * neg0),
    ]
    for grad, parts in ((mid_grad, mids), (low_grad, lows)):
        for n in range(3):
            others = parts[(n + 1) % 3] * parts[(n + 2) % 3] * picks[n]
            out.append(jnp.sum(grad * others, axis=0, keepdims=True))
    return jnp.concatenate(out, axis=0)


def split_two(value):
    high = value.astype(BF16).astype(F32)
    return high, value - high


def unit_planes(planes):
    return planes * lax.rsqrt(jnp.sum(planes * planes, axis=1, keepdims=True) + 1e-06)


def fill_spread(values, seg_row, spread_ref, lane):
    for s in range(MAXSEG):
        spread_ref[s * HD : (s + 1) * HD, lane] = jnp.where(
            seg_row == s, values, jnp.zeros_like(values)
        )


def fill_member(seg_row, spread_ref, lane):
    width = seg_row.shape[1]
    rows = lax.broadcasted_iota(jnp.int32, (128, width), 0)
    hit = jnp.logical_and(rows < 16, (rows & 7) == seg_row)
    spread_ref[SPREAD:EXT, lane] = jnp.where(hit, 1.0, 0.0).astype(BF16)


def plane_rows(unit):
    side = lax.axis_index("mp") % 2
    row = jnp.where(unit < SOLO, unit, 2 * side + unit - SOLO)
    return pl.ds(pl.multiple_of(row * BITS, BITS), BITS)


def lanes_of(index, width):
    return pl.ds(pl.multiple_of(index * width, width), width)


def masked_fold(product, seg_row):
    total = None
    for s in range(MAXSEG):
        piece = jnp.where(seg_row == s, product[s * HD : (s + 1) * HD], 0.0)
        total = piece if total is None else total + piece
    return total


def attend_kernel(
    qkv_ref, planes_ref, seg_ref, conv_ref,
    sent_ref, numer_ref, dens_ref, sign_ref, bucket_ref,
    spread, norm, qprob, kprob, total, table, est,
):
    unit = pl.program_id(0)
    slot = unit // SOLO
    length = qkv_ref.shape[1]
    tiles = length // TILE
    q_rows = pl.ds(pl.multiple_of(slot * HD, HD), HD)
    k_rows = pl.ds(pl.multiple_of(2 * HD + slot * HD, HD), HD)
    v_rows = pl.ds(pl.multiple_of(4 * HD + slot * HD, HD), HD)

    @pl.when(jnp.logical_or(unit == 0, unit == SOLO))
    def _():
        def step(i, carry):
            lane = lanes_of(i, TILE)
            seg_row = seg_ref[:, lane]
            fill_spread(qkv_ref[v_rows, lane], seg_row, spread, lane)
            fill_member(seg_row, spread, lane)
            query = qkv_ref[q_rows, lane].astype(F32)
            key = qkv_ref[k_rows, lane].astype(F32)
            scale = math.sqrt(HD)
            norm[0:1, lane] = scale * lax.rsqrt(
                jnp.sum(query * query, axis=0, keepdims=True) + 1e-06
            )
            norm[1:2, lane] = scale * lax.rsqrt(jnp.sum(key * key, axis=0, keepdims=True) + 1e-06)
            est[:, lane] = jnp.zeros((HD, TILE), F32)
            return carry

        lax.fori_loop(0, tiles, step, 0)

    planes = unit_planes(planes_ref[plane_rows(unit), :])
    high, rest = split_two(planes)
    middle, low = split_two(rest)
    stack = jnp.concatenate((high, middle, low), axis=0).astype(BF16)
    total[...] = jnp.zeros_like(total)

    def collect(i, carry):
        lane = lanes_of(i, TILE)
        flat_q = nn_dot(stack, qkv_ref[q_rows, lane])
        flat_k = nn_dot(stack, qkv_ref[k_rows, lane])
        sign_q = jnp.tanh((flat_q[0:8] + flat_q[8:16] + flat_q[16:24]) * norm[0:1, lane])
        sign_k = jnp.tanh((flat_k[0:8] + flat_k[8:16] + flat_k[16:24]) * norm[1:2, lane])
        sign_ref[0, 0:8, lane] = sign_q
        sign_ref[0, 8:16, lane] = sign_k
        for part in range(TILE // LANES):
            inner = slice(part * LANES, (part + 1) * LANES)
            code_probs(sign_k[:, inner], kprob, inner)
            code_probs(
                sign_q[:, inner], qprob, pl.ds(pl.multiple_of(i * TILE + part * LANES, LANES), LANES)
            )
        total[...] += nt_dot(spread[0 : SPREAD + 16, lane], kprob[...])
        return carry

    lax.fori_loop(0, tiles, collect, 0)
    mass = total[SPREAD : SPREAD + 8, :]
    mass_high, mass_low = split_two(mass)
    extra = jnp.concatenate(
        (mass_high, mass_high, mass_low, jnp.zeros((104, CODES), F32)), axis=0
    )
    table[0:SPREAD, :] = total[0:SPREAD, :].astype(BF16)
    table[SPREAD:EXT, :] = extra.astype(BF16)
    bucket_ref[0, :, 0:SPREAD] = jnp.transpose(total[0:SPREAD, :]).astype(BF16)
    bucket_ref[0, :, SPREAD:EXT] = jnp.transpose(extra).astype(BF16)

    def spend(i, carry):
        lane = lanes_of(i, TILE)
        seg_row = seg_ref[:, lane]
        product = nn_dot(table[0 : SPREAD + 32, :], qprob[:, lane])
        numer = masked_fold(product, seg_row)
        both = product[SPREAD : SPREAD + 8] + product[SPREAD + 16 : SPREAD + 24]
        which = lax.broadcasted_iota(jnp.int32, (8, TILE), 0)
        density = jnp.sum(jnp.where(which == seg_row, both, 0.0), axis=0, keepdims=True)
        numer_ref[0, :, lane] = numer
        dens_ref[0, :, lane] = density
        est[:, lane] += numer * (1.0 / jnp.maximum(density, 1.0))
        return carry

    lax.fori_loop(0, tiles, spend, 0)

    @pl.when(jnp.logical_or(unit == SOLO - 1, unit == UNITS - 1))
    def _():
        sent_ref[q_rows, :] = (est[...] * (1.0 / TABLES) + conv_ref[q_rows, :]).astype(BF16)


def attend(qkv, planes, seg_row, conv):
    length = qkv.shape[1]
    per_unit = lambda u: (u, 0, 0)
    fixed = lambda u: (0, 0)
    return pl.pallas_call(
        attend_kernel,
        grid=(UNITS,),
        in_specs=[
            pl.BlockSpec(qkv.shape, fixed),
            pl.BlockSpec(planes.shape, fixed),
            pl.BlockSpec(seg_row.shape, fixed),
            pl.BlockSpec(conv.shape, fixed),
        ],
        out_specs=[
            pl.BlockSpec((2 * HD, length), fixed),
            pl.BlockSpec((1, HD, length), per_unit),
            pl.BlockSpec((1, 1, length), per_unit),
            pl.BlockSpec((1, 16, length), per_unit),
            pl.BlockSpec((1, CODES, EXT), per_unit),
        ],
        out_shape=[
            jax.ShapeDtypeStruct((2 * HD, length), BF16),
            jax.ShapeDtypeStruct((UNITS, HD, length), F32),
            jax.ShapeDtypeStruct((UNITS, 1, length), F32),
            jax.ShapeDtypeStruct((UNITS, 16, length), F32),
            jax.ShapeDtypeStruct((UNITS, CODES, EXT), BF16),
        ],
        scratch_shapes=[
            pltpu.VMEM((EXT, length), BF16),
            pltpu.VMEM((8, length), F32),
            pltpu.VMEM((CODES, length), BF16),
            pltpu.VMEM((CODES, TILE), BF16),
            pltpu.VMEM((SPREAD + 16, CODES), F32),
            pltpu.VMEM((EXT, CODES), BF16),
            pltpu.VMEM((HD, length), F32),
        ],
        compiler_params=pltpu.CompilerParams(vmem_limit_bytes=VMEM_BYTES),
        cost_estimate=pl.CostEstimate(flops=0, bytes_accessed=1_000_000, transcendentals=0),
        name="attend",
    )(qkv, planes, seg_row, conv)


def attend_back_kernel(
    slot, first_unit, units,
    qkv_ref, planes_ref, seg_ref, grad_ref, numer_ref, dens_ref, sign_ref, bucket_ref,
    out_ref,
    spread, qprob, kprob, gspread, total, table, turned, gsign, proj,
):
    step_unit = pl.program_id(0)
    unit = first_unit + step_unit
    length = qkv_ref.shape[1]
    tiles = length // TILE
    q_rows = slice(slot * HD, slot * HD + HD)
    k_rows = slice(2 * HD + slot * HD, 3 * HD + slot * HD)
    v_rows = slice(4 * HD + slot * HD, 5 * HD + slot * HD)
    v_out = slice(2 * HD, 3 * HD)

    @pl.when(step_unit == 0)
    def _():
        def step(i, carry):
            lane = lanes_of(i, TILE)
            seg_row = seg_ref[:, lane]
            fill_spread(qkv_ref[v_rows, lane], seg_row, spread, lane)
            fill_member(seg_row, spread, lane)
            proj[:, lane] = jnp.zeros((2 * HD, TILE), F32)
            out_ref[v_out, lane] = jnp.zeros((HD, TILE), F32)
            return carry

        lax.fori_loop(0, tiles, step, 0)
        gspread[SPREAD:EXT, :] = jnp.zeros((128, TILE), BF16)

    total[...] = jnp.zeros_like(total)

    def first(i, carry):
        lane = lanes_of(i, TILE)
        seg_row = seg_ref[:, lane]
        density = dens_ref[0, :, lane]
        inverse = 1.0 / jnp.maximum(density, 1.0)
        est_grad = grad_ref[q_rows, lane].astype(F32) * (1.0 / TABLES)
        num_grad = (est_grad * inverse).astype(BF16)
        fill_spread(num_grad, seg_row, gspread, slice(0, TILE))
        inner_sum = jnp.sum(est_grad * numer_ref[0, :, lane], axis=0, keepdims=True)
        dens_grad = jnp.where(density > 1.0, -inner_sum * inverse * inverse, 0.0)
        which = lax.broadcasted_iota(jnp.int32, (8, TILE), 0)
        high, low = split_two(jnp.where(which == seg_row, dens_grad, 0.0))
        gspread[SPREAD : SPREAD + 32, :] = jnp.concatenate(
            (high, low, high, jnp.zeros_like(high)), axis=0
        ).astype(BF16)
        collected = nn_dot(bucket_ref[0], gspread[...])
        for part in range(TILE // LANES):
            inner = slice(part * LANES, (part + 1) * LANES)
            outer = pl.ds(pl.multiple_of(i * TILE + part * LANES, LANES), LANES)
            sign_q = sign_ref[0, 0:8, outer]
            code_probs(sign_q, qprob, inner)
            gsign[0:8, outer] = signs_back(sign_q, collected[:, inner])
        total[...] += nt_dot(gspread[0 : SPREAD + 16, :], qprob[...])
        return carry

    lax.fori_loop(0, tiles, first, 0)
    mass_grad = total[SPREAD : SPREAD + 8, :] + total[SPREAD + 8 : SPREAD + 16, :]
    high, low = split_two(mass_grad)
    extra = jnp.concatenate((high, low, jnp.zeros((112, CODES), F32)), axis=0)
    table[...] = total[0:SPREAD, :].astype(BF16)
    turned[:, 0:SPREAD] = jnp.transpose(total[0:SPREAD, :]).astype(BF16)
    turned[:, SPREAD:EXT] = jnp.transpose(extra).astype(BF16)

    planes = unit_planes(planes_ref[plane_rows(unit), :])
    plane_high, plane_low = split_two(planes)
    stack = jnp.concatenate((plane_high, plane_low, plane_high, jnp.zeros_like(plane_high)), axis=0)
    stack = stack.astype(BF16)

    def second(i, carry):
        lane = lanes_of(i, TILE)
        seg_row = seg_ref[:, lane]
        for part in range(TILE // LANES):
            inner = slice(part * LANES, (part + 1) * LANES)
            outer = pl.ds(pl.multiple_of(i * TILE + part * LANES, LANES), LANES)
            code_probs(sign_ref[0, 8:16, outer], kprob, inner)
        out_ref[v_out, lane] += masked_fold(nn_dot(table[...], kprob[...]), seg_row)
        collected = nn_dot(turned[...], spread[:, lane])
        for part in range(TILE // LANES):
            inner = slice(part * LANES, (part + 1) * LANES)
            outer = pl.ds(pl.multiple_of(i * TILE + part * LANES, LANES), LANES)
            gsign[8:16, outer] = signs_back(sign_ref[0, 8:16, outer], collected[:, inner])
        signs = sign_ref[0, :, lane]
        flat = gsign[:, lane] * (1.0 - signs * signs)
        high, low = split_two(flat)
        for side in range(2):
            rows = slice(8 * side, 8 * side + 8)
            pieces = jnp.concatenate(
                (high[rows], high[rows], low[rows], jnp.zeros((8, TILE), F32)), axis=0
            ).astype(BF16)
            proj[side * HD : (side + 1) * HD, lane] += tn_dot(stack, pieces)
        return carry

    lax.fori_loop(0, tiles, second, 0)

    @pl.when(step_unit == units - 1)
    def _():
        def step(i, carry):
            lane = lanes_of(i, TILE)
            for side, rows in ((0, q_rows), (1, k_rows)):
                vec = qkv_ref[rows, lane].astype(F32)
                inverse = lax.rsqrt(jnp.sum(vec * vec, axis=0, keepdims=True) + 1e-06)
                unit_vec = vec * inverse
                grad = proj[side * HD : (side + 1) * HD, lane]
                along = jnp.sum(unit_vec * grad, axis=0, keepdims=True)
                out_ref[side * HD : (side + 1) * HD, lane] = math.sqrt(HD) * inverse * (grad - unit_vec * along)
            return carry

        lax.fori_loop(0, tiles, step, 0)


def attend_back(slot, qkv, planes, seg_row, grad, numer, dens, sign, bucket):
    length = qkv.shape[1]
    first_unit = slot * SOLO
    units = SOLO if slot == 0 else UNITS - SOLO
    per_unit = lambda u: (u + first_unit, 0, 0)
    fixed = lambda u: (0, 0)
    return pl.pallas_call(
        partial(attend_back_kernel, slot, first_unit, units),
        grid=(units,),
        in_specs=[
            pl.BlockSpec(qkv.shape, fixed),
            pl.BlockSpec(planes.shape, fixed),
            pl.BlockSpec(seg_row.shape, fixed),
            pl.BlockSpec(grad.shape, fixed),
            pl.BlockSpec((1, HD, length), per_unit),
            pl.BlockSpec((1, 1, length), per_unit),
            pl.BlockSpec((1, 16, length), per_unit),
            pl.BlockSpec((1, CODES, EXT), per_unit),
        ],
        out_specs=pl.BlockSpec((3 * HD, length), fixed),
        out_shape=jax.ShapeDtypeStruct((3 * HD, length), F32),
        scratch_shapes=[
            pltpu.VMEM((EXT, length), BF16),
            pltpu.VMEM((CODES, TILE), BF16),
            pltpu.VMEM((CODES, TILE), BF16),
            pltpu.VMEM((EXT, TILE), BF16),
            pltpu.VMEM((SPREAD + 16, CODES), F32),
            pltpu.VMEM((SPREAD, CODES), BF16),
            pltpu.VMEM((CODES, EXT), BF16),
            pltpu.VMEM((16, length), F32),
            pltpu.VMEM((2 * HD, length), F32),
        ],
        compiler_params=pltpu.CompilerParams(vmem_limit_bytes=VMEM_BYTES),
        cost_estimate=pl.CostEstimate(flops=0, bytes_accessed=1_000_000, transcendentals=0),
        name="attend_back",
    )(qkv, planes, seg_row, grad, numer, dens, sign, bucket)


SPAN = 192
SHIFT = (KW - 1) // 2
OWN = 96
BLOCKS = ((0, HD), (HD, OWN))


def own_heads():
    m = lax.axis_index("mp")
    group = m // 2
    return (3 * group + 2 * (m % 2), 3 * group + 1)


def own_half():
    side = lax.axis_index("mp") % 2
    half = OWN - HD
    return side, half


def band_of(row):
    turned = jnp.broadcast_to(row, (LANES, 2 * LANES))
    index = lax.broadcasted_iota(jnp.int32, turned.shape, 0)
    for bit in range(7):
        moved = pltpu.roll(turned, 1 << bit, 1)
        turned = jnp.where((index >> bit) & 1 == 1, moved, turned)
    return jnp.transpose(turned)[0:SPAN]


def fill_hot(seg_ref, hot, hot_pad):
    length = seg_ref.shape[1]
    rows = lax.broadcasted_iota(jnp.int32, (16, length), 0)
    value = jnp.where(rows == seg_ref[...], 1.0, 0.0)
    value = jnp.where(rows < MAXSEG, value, 0.0).astype(BF16)
    hot[...] = value
    hot_pad[...] = jnp.zeros_like(hot_pad)
    hot_pad[:, SHIFT : SHIFT + length] = value


def band_product(rows, band):
    high, low = split_two(band)
    return nn_dot(rows, high.astype(BF16)) + nn_dot(rows, low.astype(BF16))


def conv_kernel(qkv_ref, taps_ref, seg_ref, out_ref, hot, hot_pad, pad, band):
    length = out_ref.shape[1]
    side, half = own_half()
    own = pl.ds(pl.multiple_of(HD + side * half, half), half)
    other = pl.ds(pl.multiple_of(HD + (1 - side) * half, half), half)
    fill_hot(seg_ref, hot, hot_pad)
    pad[...] = jnp.zeros_like(pad)
    pad[0:HD, SHIFT : SHIFT + length] = qkv_ref[4 * HD : 5 * HD, :]
    value_half = pl.ds(pl.multiple_of(5 * HD + side * half, half), half)
    pad[HD:OWN, SHIFT : SHIFT + length] = qkv_ref[value_half, :]
    for h, head in enumerate(own_heads()):
        band[h] = band_of(taps_ref[pl.ds(head, 1), :])
    out_ref[other, :] = jnp.zeros((half, length), F32)
    for i in range(length // LANES):
        lane = slice(i * LANES, (i + 1) * LANES)
        wide = slice(i * LANES, i * LANES + SPAN)
        mask = tn_dot(hot_pad[:, wide], hot[:, lane])
        out_ref[0:HD, lane] = band_product(pad[0:HD, wide], band[0] * mask)
        out_ref[own, lane] = band_product(pad[HD:OWN, wide], band[1] * mask)


def segment_conv(qkv, taps, seg_row):
    length = seg_row.shape[1]
    return pl.pallas_call(
        conv_kernel,
        out_shape=jax.ShapeDtypeStruct((2 * HD, length), F32),
        scratch_shapes=[
            pltpu.VMEM((16, length), BF16),
            pltpu.VMEM((16, length + LANES), BF16),
            pltpu.VMEM((OWN, length + LANES), BF16),
            pltpu.VMEM((2, SPAN, LANES), F32),
        ],
        compiler_params=pltpu.CompilerParams(vmem_limit_bytes=VMEM_BYTES),
        cost_estimate=pl.CostEstimate(flops=0, bytes_accessed=1_000_000, transcendentals=0),
        name="segment_conv",
    )(qkv, taps, seg_row)


def conv_back_kernel(
    qkv_ref, grad_ref, taps_ref, seg_ref, out_ref, tap_ref, hot, hot_pad, pad, gpad, band, corr
):
    length = seg_ref.shape[1]
    side, half = own_half()
    fill_hot(seg_ref, hot, hot_pad)
    pad[...] = jnp.zeros_like(pad)
    gpad[...] = jnp.zeros_like(gpad)
    inside = slice(SHIFT, SHIFT + length)
    value_half = pl.ds(pl.multiple_of(5 * HD + side * half, half), half)
    grad_half = pl.ds(pl.multiple_of(HD + side * half, half), half)
    pad[0:HD, inside] = qkv_ref[4 * HD : 5 * HD, :]
    pad[HD:OWN, inside] = qkv_ref[value_half, :]
    gpad[0:HD, inside] = grad_ref[0:HD, :]
    gpad[HD:OWN, inside] = grad_ref[grad_half, :]
    heads = own_heads()
    for h, head in enumerate(heads):
        band[h] = band_of(taps_ref[pl.ds(16 + head, 1), :])
    corr[...] = jnp.zeros_like(corr)
    for i in range(length // LANES):
        lane = slice(i * LANES, (i + 1) * LANES)
        wide = slice(i * LANES, i * LANES + SPAN)
        twice = slice(i * LANES, (i + 2) * LANES)
        mask = tn_dot(hot_pad[:, wide], hot[:, lane])
        turned = tn_dot(hot[:, lane], hot_pad[:, twice])
        grads = (grad_ref[0:HD, lane], grad_ref[grad_half, lane])
        for h, (low_row, high_row) in enumerate(BLOCKS):
            out_ref[low_row:high_row, lane] = band_product(
                gpad[low_row:high_row, wide], band[h] * mask
            )
            corr[h] += turned * tn_dot(grads[h], pad[low_row:high_row, twice])
    row = lax.broadcasted_iota(jnp.int32, (LANES, 2 * LANES), 0)
    place = lax.broadcasted_iota(jnp.int32, (8, LANES), 0)
    low_heads = jnp.zeros((8, LANES), F32)
    high_heads = jnp.zeros((8, LANES), F32)
    for h, head in enumerate(heads):
        skew = corr[h]
        for bit in range(7):
            moved = pltpu.roll(skew, 2 * LANES - (1 << bit), 1)
            skew = jnp.where((row >> bit) & 1 == 1, moved, skew)
        taps = jnp.sum(skew, axis=0, keepdims=True)[:, 0:LANES]
        low_heads = low_heads + jnp.where(place == head, taps, 0.0)
        high_heads = high_heads + jnp.where(place + 8 == head, taps, 0.0)
    tap_ref[:, 0:LANES] = low_heads
    tap_ref[:, LANES : 2 * LANES] = high_heads


def conv_back(qkv, grad, taps, seg_row):
    length = seg_row.shape[1]
    return pl.pallas_call(
        conv_back_kernel,
        out_shape=(
            jax.ShapeDtypeStruct((OWN, length), F32),
            jax.ShapeDtypeStruct((8, 2 * LANES), F32),
        ),
        scratch_shapes=[
            pltpu.VMEM((16, length), BF16),
            pltpu.VMEM((16, length + LANES), BF16),
            pltpu.VMEM((OWN, length + LANES), BF16),
            pltpu.VMEM((OWN, length + LANES), BF16),
            pltpu.VMEM((2, SPAN, LANES), F32),
            pltpu.VMEM((2, LANES, 2 * LANES), F32),
        ],
        compiler_params=pltpu.CompilerParams(vmem_limit_bytes=VMEM_BYTES),
        cost_estimate=pl.CostEstimate(flops=0, bytes_accessed=1_000_000, transcendentals=0),
        name="conv_back",
    )(qkv, grad, taps, seg_row)


def norm_rows(values):
    center = values - jnp.mean(values, axis=1, keepdims=True)
    inverse = lax.rsqrt(jnp.mean(center * center, axis=1, keepdims=True) + 1e-05)
    return center * inverse, inverse


def norm_back(upstream, normed, inverse, gain):
    scaled = upstream * gain
    inner = (
        scaled
        - jnp.mean(scaled, axis=1, keepdims=True)
        - normed * jnp.mean(scaled * normed, axis=1, keepdims=True)
    )
    return inner * inverse


def gelu_pair(value):
    cdf = 0.5 + 0.5 * lax.erf(value * math.sqrt(0.5))
    pdf = jnp.exp(-0.5 * value * value) * (1.0 / math.sqrt(2.0 * math.pi))
    return value * cdf, cdf + value * pdf


def column_sum(values):
    return jnp.sum(values, axis=0, keepdims=True)


MESH = pl.DeviceIdType.MESH
OFFSETS = (0, -2, 2, 4)
INVERSE = (0, 2, 1, 3, 4, 6, 5, 7)


def repeat(start, stop, action):
    def body(r, carry):
        action(r)
        return carry

    lax.fori_loop(start, stop, body, 0)


def remote(src, dst, send, recv, target):
    return pltpu.make_async_remote_copy(
        src_ref=src, dst_ref=dst, send_sem=send, recv_sem=recv,
        device_id={"mp": target}, device_id_type=MESH,
    )


def greet(targets):
    barrier = pltpu.get_barrier_semaphore()
    for target in targets:
        pl.semaphore_signal(barrier, inc=1, device_id={"mp": target}, device_id_type=MESH)
    pl.semaphore_wait(barrier, len(targets))


def gather_kernel(x_ref, w_ref, all_ref, qkv_ref, wide, send, recv):
    count, rows, _ = all_ref.shape
    m = lax.axis_index("mp")
    side = m % 2
    sibling = m + 1 - 2 * side
    left = (m + count - 2) % count
    right = (m + 2) % count
    far = (m + 4) % count
    half = OWN - HD
    cut = rows // 2
    greet((left, right, sibling))

    def copy(n, src, dst, target):
        return remote(src, dst, send.at[n], recv.at[n], target)

    def piece(n, which):
        return pl.ds(pl.multiple_of(n * 2 * HD + HD + which * half, half), half)

    def weight_copy(n, which):
        source = w_ref.at[pl.ds(pl.multiple_of(n * OWN + (1 - side) * HD, half), half), :]
        return copy(8 + n, source, wide.at[piece(n, which), :], sibling)

    for n in range(3):
        weight_copy(n, side).start()
    to_right = copy(0, x_ref, all_ref.at[m], right)
    to_left = copy(1, x_ref, all_ref.at[m], left)
    to_sibling = copy(2, x_ref, all_ref.at[m], sibling)
    to_right.start()
    to_left.start()
    to_sibling.start()
    all_ref[m] = x_ref[...]
    for n in range(3):
        solo = pl.ds(pl.multiple_of(n * OWN + side * half, half), HD)
        own = pl.ds(pl.multiple_of(n * OWN + (1 - side) * HD, half), half)
        wide[n * 2 * HD : n * 2 * HD + HD, :] = w_ref[solo, :]
        wide[piece(n, side), :] = w_ref[own, :]
    for n in range(3):
        weight_copy(n, 1 - side).wait_recv()

    def project(block):
        lane = pl.ds(pl.multiple_of(block * rows, rows), rows)
        qkv_ref[:, lane] = nt_dot(wide[...], all_ref[block]).astype(BF16)

    project(m)
    copy(2, x_ref, all_ref.at[sibling], sibling).wait_recv()
    project(sibling)
    copy(0, x_ref, all_ref.at[left], left).wait_recv()
    on_right = copy(3, all_ref.at[left, 0:cut], all_ref.at[left, 0:cut], right)
    on_right.start()
    over_left = copy(5, all_ref.at[left], all_ref.at[left], sibling)
    over_left.start()
    copy(1, x_ref, all_ref.at[right], right).wait_recv()
    on_left = copy(4, all_ref.at[right, cut:rows], all_ref.at[right, cut:rows], left)
    on_left.start()
    over_right = copy(6, all_ref.at[right], all_ref.at[right], sibling)
    over_right.start()
    project(left)
    project(right)
    other_left = (sibling + count - 2) % count
    other_right = (sibling + 2) % count
    other_far = (sibling + 4) % count
    copy(5, x_ref, all_ref.at[other_left], sibling).wait_recv()
    project(other_left)
    copy(6, x_ref, all_ref.at[other_right], sibling).wait_recv()
    project(other_right)
    copy(3, x_ref.at[0:cut], all_ref.at[far, 0:cut], left).wait_recv()
    copy(4, x_ref.at[cut:rows], all_ref.at[far, cut:rows], right).wait_recv()
    over_far = copy(7, all_ref.at[far], all_ref.at[far], sibling)
    over_far.start()
    project(far)
    copy(7, x_ref, all_ref.at[other_far], sibling).wait_recv()
    project(other_far)
    for n in range(3):
        weight_copy(n, side).wait_send()
    for sent in (
        to_right, to_left, to_sibling, on_right, on_left, over_left, over_right, over_far
    ):
        sent.wait_send()


def gather_qkv(x, w_rows, count):
    rows, width = x.shape
    vmem = pl.BlockSpec(memory_space=pltpu.VMEM)
    return pl.pallas_call(
        gather_kernel,
        in_specs=[vmem] * 2,
        out_specs=[vmem] * 2,
        out_shape=(
            jax.ShapeDtypeStruct((count, rows, width), BF16),
            jax.ShapeDtypeStruct((6 * HD, count * rows), BF16),
        ),
        scratch_shapes=[
            pltpu.VMEM((6 * HD, width), BF16),
            pltpu.SemaphoreType.DMA((11,)),
            pltpu.SemaphoreType.DMA((11,)),
        ],
        compiler_params=pltpu.CompilerParams(
            vmem_limit_bytes=VMEM_BYTES, collective_id=2, has_side_effects=True
        ),
        cost_estimate=pl.CostEstimate(
            flops=12 * HD * count * rows * width, bytes_accessed=30_000_000, transcendentals=0
        ),
        name="gather_qkv",
    )(x, w_rows)


def around(m, count):
    sibling = m + 1 - 2 * (m % 2)
    return [(base + count + off) % count for base in (m, sibling) for off in OFFSETS]


def middle_kernel(
    sent_ref, x_ref, cot_ref, own_w, left_w, right_w, far_low, far_high, scale_ref,
    result_ref, lows_ref, one_ref, attn_ref, part_ref,
    wall, out_w, att_in, attn_out, slope, keep, acc,
    load, give_send, give_recv, rest_send, rest_recv, in_send, in_recv, out_send, out_recv,
):
    rows = x_ref.shape[0]
    count = att_in.shape[0]
    units = slope.shape[2]
    both = 2 * units
    m = lax.axis_index("mp")
    devices = around(m, count)
    sibling = devices[4]
    greet(devices[1:])

    def tokens(index):
        return pl.ds(pl.multiple_of(index * rows, rows), rows)

    side = m % 2
    depth = wall.shape[1]
    cut = depth // 2
    blocks = (own_w, left_w, right_w)
    out_rows = slice(both, depth)
    near_rows = slice(cut, both)

    def give(n):
        source = blocks[n].at[out_rows] if n < 3 else far_high.at[both - cut : depth - cut]
        return remote(
            source, wall.at[4 + n, out_rows], give_send.at[n], give_recv.at[n], sibling
        )

    def rest(n, part):
        if part == 0:
            source = blocks[n].at[0:cut] if n < 3 else far_low
            place = wall.at[4 + n, 0:cut]
        else:
            source = blocks[n].at[near_rows] if n < 3 else far_high.at[0 : both - cut]
            place = wall.at[4 + n, near_rows]
        return remote(source, place, rest_send.at[part, n], rest_recv.at[part, n], sibling)

    def loads():
        copies = [pltpu.make_async_copy(blocks[n], wall.at[n], load.at[n]) for n in range(3)]
        copies.append(pltpu.make_async_copy(far_low, wall.at[3, 0:cut], load.at[3]))
        copies.append(pltpu.make_async_copy(far_high, wall.at[3, cut:depth], load.at[4]))
        return copies

    def att_copy(n, slot, sem):
        return remote(
            sent_ref.at[:, tokens(devices[n])], att_in.at[slot], in_send.at[n], in_recv.at[sem],
            devices[n],
        )

    def attn_copy(n, lane, sem):
        return remote(
            attn_out.at[n], attn_ref.at[:, tokens(lane)], out_send.at[n], out_recv.at[sem],
            devices[n],
        )

    for n in range(1, count):
        att_copy(n, INVERSE[n], INVERSE[n]).start()
    for n in range(4):
        give(n).start()
    for copy in loads():
        copy.start()
    for n in range(4):
        rest(n, 0).start()
        rest(n, 1).start()
    att_in[0] = sent_ref[:, tokens(m)]
    for copy in loads():
        copy.wait()
    for n in range(4):
        give(n).wait_recv()
    projected = None
    for n in range(4):
        first, second = n + 4 * side, n + 4 * (1 - side)
        out_w[n, 0:OWN] = wall[first, out_rows]
        out_w[n, OWN : 2 * OWN] = wall[second, out_rows]
        for slot in (n, 4 + n):
            if slot > 0:
                att_copy(slot, slot, slot).wait_recv()
        shared = att_in[first, HD : 2 * HD].astype(F32) + att_in[second, HD : 2 * HD].astype(F32)
        features = jnp.concatenate(
            (att_in[first, 0:HD], shared.astype(BF16), att_in[second, 0:HD]), axis=0
        )
        piece = tn_dot(features, out_w[n])
        projected = piece if projected is None else projected + piece
    unit, inverse = norm_rows(x_ref[...].astype(F32) + projected)
    hidden = unit * scale_ref[0:1] + scale_ref[1:2]
    keep[0] = unit
    keep[1] = hidden
    lows_ref[0] = hidden.astype(BF16)
    acc[...] = jnp.zeros_like(acc)

    def forward(i, carry):
        low = lows_ref[0]
        total = acc[...]
        for n in range(2):
            active, lean = gelu_pair(nt_dot(low, wall[2 * i + n, 0:units]))
            slope[2 * i + n] = lean
            total = total + nn_dot(active.astype(BF16), wall[2 * i + n, units:both])
        acc[...] = total
        return carry

    lax.fori_loop(0, 2, forward, 0)
    for n in range(4):
        rest(n, 0).wait_recv()
        rest(n, 1).wait_recv()
    lax.fori_loop(2, 4, forward, 0)
    unit, inv = norm_rows(keep[1] + acc[...])
    result_ref[...] = (unit * scale_ref[2:3] + scale_ref[3:4]).astype(BF16)
    upstream = cot_ref[...].astype(F32)
    part_ref[2:3] = column_sum(upstream * unit)
    part_ref[3:4] = column_sum(upstream)
    grad = norm_back(upstream, unit, inv, scale_ref[2:3])
    keep[1] = grad
    lows_ref[1] = grad.astype(BF16)
    acc[...] = jnp.zeros_like(acc)

    def backward(i, carry):
        low = lows_ref[1]
        total = acc[...]
        for n in range(2):
            pre_grad = nt_dot(low, wall[2 * i + n, units:both]) * slope[2 * i + n]
            total = total + nn_dot(pre_grad.astype(BF16), wall[2 * i + n, 0:units])
        acc[...] = total
        return carry

    lax.fori_loop(0, 4, backward, 0)
    upstream = keep[1] + acc[...]
    unit = keep[0]
    part_ref[0:1] = column_sum(upstream * unit)
    part_ref[1:2] = column_sum(upstream)
    part_ref[4:8] = jnp.zeros((4, part_ref.shape[1]), F32)
    grad = norm_back(upstream, unit, inverse, scale_ref[0:1])
    one_ref[...] = grad
    low = grad.astype(BF16)
    lows_ref[2] = low
    for n in (3, 1, 2, 0):
        first, second = n + 4 * side, n + 4 * (1 - side)
        back = nt_dot(out_w[n], low).astype(BF16)
        attn_out[first] = back[0 : 2 * HD]
        attn_out[second, 0:HD] = back[2 * HD : 3 * HD]
        attn_out[second, HD : 2 * HD] = back[HD : 2 * HD]
        for slot in (n, 4 + n):
            if slot > 0:
                attn_copy(slot, m, INVERSE[slot]).start()
    attn_ref[:, tokens(m)] = attn_out[0]
    for n in range(1, count):
        attn_copy(n, devices[n], n).wait_recv()
    for n in range(4):
        give(n).wait_send()
        rest(n, 0).wait_send()
        rest(n, 1).wait_send()
    for n in range(1, count):
        att_copy(n, INVERSE[n], INVERSE[n]).wait_send()
        attn_copy(n, m, INVERSE[n]).wait_send()


def middle(sent, x, cot, blocks, scale, count):
    rows, width = x.shape
    depth = sent.shape[0]
    units = (blocks[0].shape[0] - OWN) // 2
    vmem = pl.BlockSpec(memory_space=pltpu.VMEM)
    sems = lambda n: pltpu.SemaphoreType.DMA((n,))
    return pl.pallas_call(
        middle_kernel,
        in_specs=[vmem] * 3 + [pl.BlockSpec(memory_space=pl.ANY)] * 5 + [vmem],
        out_specs=[vmem] * 5,
        out_shape=(
            jax.ShapeDtypeStruct((rows, width), BF16),
            jax.ShapeDtypeStruct((3, rows, width), BF16),
            jax.ShapeDtypeStruct((rows, width), F32),
            jax.ShapeDtypeStruct(sent.shape, BF16),
            jax.ShapeDtypeStruct((8, width), F32),
        ),
        scratch_shapes=[
            pltpu.VMEM((count,) + blocks[0].shape, BF16),
            pltpu.VMEM((count // 2, 2 * OWN, width), BF16),
            pltpu.VMEM((count, depth, rows), BF16),
            pltpu.VMEM((count, depth, rows), BF16),
            pltpu.VMEM((count, rows, units), F32),
            pltpu.VMEM((2, rows, width), F32),
            pltpu.VMEM((rows, width), F32),
            sems(5), sems(4), sems(4),
            pltpu.SemaphoreType.DMA((2, 4)), pltpu.SemaphoreType.DMA((2, 4)),
            sems(count), sems(count), sems(count), sems(count),
        ],
        compiler_params=pltpu.CompilerParams(
            vmem_limit_bytes=VMEM_BYTES, collective_id=1, has_side_effects=True
        ),
        cost_estimate=pl.CostEstimate(
            flops=16 * rows * width * count * units, bytes_accessed=26_000_000,
            transcendentals=0,
        ),
        name="middle",
    )(sent, x, cot, *blocks, scale)


def close_kernel(
    own_x, left_x, right_x, far_low, far_high, solo_ref, shared_ref, conv_ref, sent_ref, all_ref,
    w_rows_ref, w_ref, one_ref, norm_ref, tap_ref,
    inputs_ref, up_ref, down_ref, out_ref, query_ref, key_ref, value_ref, tiny_ref,
    wall, acc, lows, attended, swap_out, swap_in, part_out, part_own, pair_in, stage, line_in,
    a_grads, a_in, a_sums, b_grads, b_in, b_sums, near_in, far_in,
    load, give_send, give_recv, swap_send, swap_recv, pair_send, pair_recv, line_send, line_recv,
    a_send, a_recv, aw_send, aw_recv, b_send, b_recv, bw_send, bw_recv,
    near_send, near_recv, far_send, far_recv,
):
    blocks = a_grads.shape[0]
    count, _, rows, width = wall.shape
    chips = count // 2
    units = down_ref.shape[0]
    d = lax.axis_index("dp")
    m = lax.axis_index("mp")
    side = m % 2
    chip = m // 2
    half = OWN - HD
    devices = around(m, count)
    sibling = devices[4]

    barrier = pltpu.get_barrier_semaphore()
    repeat(
        1, blocks,
        lambda r: pl.semaphore_signal(
            barrier, inc=1, device_id={"dp": (d + r) % blocks}, device_id_type=MESH
        ),
    )
    repeat(
        1, count,
        lambda r: pl.semaphore_signal(
            barrier, inc=1, device_id={"mp": (m + r) % count}, device_id_type=MESH
        ),
    )
    pl.semaphore_wait(barrier, blocks + count - 2)

    def tokens(index):
        return pl.ds(pl.multiple_of(index * rows, rows), rows)

    def across(src, dst, send, recv, r):
        return pltpu.make_async_remote_copy(
            src_ref=src, dst_ref=dst, send_sem=send.at[r], recv_sem=recv.at[r],
            device_id={"dp": (d + r) % blocks}, device_id_type=MESH,
        )

    cut = rows // 2
    sources = (own_x, left_x, right_x)

    def give(n, k):
        return remote(
            sources[n].at[k], wall.at[4 + n, k], give_send.at[n, k], give_recv.at[n, k], sibling
        )

    def give_far(part):
        source = (far_low, far_high)[part]
        place = wall.at[4 + 3, :, part * cut : (part + 1) * cut]
        return remote(source, place, give_send.at[3, part], give_recv.at[3, part], sibling)

    def loads():
        copies = [pltpu.make_async_copy(sources[n], wall.at[n], load.at[n]) for n in range(3)]
        copies.append(pltpu.make_async_copy(far_low, wall.at[3, :, 0:cut], load.at[3]))
        copies.append(pltpu.make_async_copy(far_high, wall.at[3, :, cut:rows], load.at[4]))
        return copies

    for n in range(3):
        start = pl.multiple_of(n * HD + (1 - side) * half, half)
        swap_out[n * half : (n + 1) * half] = shared_ref[pl.ds(start, half), :].astype(BF16)
    swap_out[3 * half : 4 * half] = sent_ref[
        pl.ds(pl.multiple_of(HD + (1 - side) * half, half), half), :
    ]
    swap = remote(swap_out, swap_in, swap_send.at[0], swap_recv.at[0], sibling)
    swap.start()
    for copy in loads():
        copy.start()
    for n in range(3):
        give(n, 2).start()
    for part in range(2):
        give_far(part).start()
    for k in range(2):
        for n in range(3):
            give(n, k).start()
    near_in[m, :, 0:width] = norm_ref[...]
    near_in[m, :, width : width + 2 * LANES] = tap_ref[...]

    def near_copy(r, owner):
        return remote(
            near_in.at[m], near_in.at[owner], near_send.at[r], near_recv.at[r], (m + r) % count
        )

    repeat(1, count, lambda r: near_copy(r, m).start())
    swap.wait_recv()
    solo_at = lambda n: pl.ds(pl.multiple_of(n * OWN + side * half, half), HD)
    half_at = lambda n: pl.ds(pl.multiple_of(n * OWN + (1 - side) * HD, half), half)
    for n in range(3):
        solo = solo_ref[n * HD : (n + 1) * HD, :]
        mine = shared_ref[pl.ds(pl.multiple_of(n * HD + side * half, half), half), :]
        mixed = mine + swap_in[n * half : (n + 1) * half].astype(F32)
        if n == 2:
            solo = solo + conv_ref[0:HD, :]
            mixed = mixed + conv_ref[HD:OWN, :]
        lows[solo_at(n), :] = solo.astype(BF16)
        lows[half_at(n), :] = mixed.astype(BF16)
    sent_half = sent_ref[pl.ds(pl.multiple_of(HD + side * half, half), half), :]
    attended[solo_at(0), :] = sent_ref[0:HD, :]
    attended[half_at(0), :] = (
        sent_half.astype(F32) + swap_in[3 * half : 4 * half].astype(F32)
    ).astype(BF16)

    def pair_copy(target):
        return remote(
            part_out.at[target], pair_in.at[target], pair_send.at[target], pair_recv.at[target],
            sibling,
        )

    def input_part(device):
        return tn_dot(lows[:, tokens(device)], w_rows_ref[...])

    order = [2, 1, 3, 0]
    for k in order:
        target = (chip + k) % chips
        part_out[target] = input_part(2 * target + 1 - side).astype(BF16)
        pair_copy(target).start()
    qkv_grad = nn_dot(lows[...], all_ref[...])
    for copy in loads():
        copy.wait()
    for n in range(3):
        give(n, 2).wait_recv()
    for part in range(2):
        give_far(part).wait_recv()
    out_grad = None
    for slot in range(count):
        piece = nn_dot(attended[:, tokens(devices[slot])], wall[slot, 2])
        out_grad = piece if out_grad is None else out_grad + piece
    depth = a_grads.shape[1]
    a_all = jnp.concatenate((out_grad, qkv_grad), axis=0).astype(BF16)
    for j in range(blocks):
        a_grads[j] = a_all[j * depth : (j + 1) * depth]

    def a_copy(r):
        return across(a_grads.at[(d + r) % blocks], a_in.at[r], a_send, a_recv, r)

    def a_whole(r, owner):
        return across(a_sums.at[d], a_sums.at[owner], aw_send, aw_recv, r)

    def b_copy(r):
        return across(b_grads.at[(d + r) % blocks], b_in.at[r], b_send, b_recv, r)

    def b_whole(r, owner):
        return across(b_sums.at[d], b_sums.at[owner], bw_send, bw_recv, r)

    def far_copy(r, owner):
        return across(far_in.at[d], far_in.at[owner], far_send, far_recv, r)

    repeat(1, blocks, lambda r: a_copy(r).start())

    def line_copy(k):
        return remote(
            stage.at[k], line_in.at[k], line_send.at[k], line_recv.at[k], (m + 2 * k) % count
        )

    for k in order[:3]:
        target = (chip + k) % chips
        mine = input_part(2 * target + side)
        pair_copy(target).wait_recv()
        stage[k] = (mine + pair_in[target].astype(F32)).astype(BF16)
        line_copy(k).start()
    part_own[...] = input_part(m)

    acc[...] = jnp.zeros_like(acc)

    def step(i, carry):
        sums = [None] * 2
        for n in range(2):
            slot = 2 * i + n
            hidden, ffn = wall[slot, 0], wall[slot, 1]
            active, lean = gelu_pair(nt_dot(hidden, w_ref[0:units]))
            pre_grad = (nt_dot(ffn, w_ref[units : 2 * units]) * lean).astype(BF16)
            parts = (tn_dot(pre_grad, hidden), tn_dot(active.astype(BF16), ffn))
            sums = [p if t is None else t + p for t, p in zip(sums, parts)]
        acc[0:units, :] += sums[0]
        acc[units : 2 * units, :] += sums[1]
        return carry

    lax.fori_loop(0, 2, step, 0)
    for k in range(2):
        for n in range(3):
            give(n, k).wait_recv()
    lax.fori_loop(2, 4, step, 0)
    high = b_grads.shape[1]
    for j in range(blocks):
        b_grads[j] = acc[j * high : (j + 1) * high, :].astype(BF16)
    repeat(1, blocks, lambda r: b_copy(r).start())

    repeat(1, count, lambda r: near_copy(r, (m + count - r) % count).wait_recv())
    total = near_in[0]
    for r in range(1, count):
        total = total + near_in[r]
    far_in[d] = total
    repeat(1, blocks, lambda r: far_copy(r, d).start())

    def reduce(grads, inbox, sums):
        size = grads.shape[1]
        for low in range(0, size, 16):
            part = slice(low, min(low + 16, size))
            value = grads[d, part].astype(F32)
            for r in range(1, blocks):
                value = value + inbox[r, part].astype(F32)
            sums[d, part] = value.astype(BF16)

    repeat(1, blocks, lambda r: a_copy(r).wait_recv())
    reduce(a_grads, a_in, a_sums)
    repeat(1, blocks, lambda r: a_whole(r, d).start())
    pair_copy(chip).wait_recv()
    total = part_own[...] + pair_in[chip].astype(F32)
    for k in range(1, chips):
        line_copy(k).wait_recv()
        total = total + line_in[k].astype(F32)
    inputs_ref[...] = one_ref[...] + total
    repeat(1, blocks, lambda r: b_copy(r).wait_recv())
    reduce(b_grads, b_in, b_sums)
    repeat(1, blocks, lambda r: b_whole(r, d).start())

    repeat(1, blocks, lambda r: far_copy(r, (d + blocks - r) % blocks).wait_recv())
    total = far_in[0]
    for r in range(1, blocks):
        total = total + far_in[r]
    tiny_ref[...] = total
    repeat(1, blocks, lambda r: a_whole(r, (d + blocks - r) % blocks).wait_recv())
    whole = jnp.concatenate([a_sums[j].astype(F32) for j in range(blocks)], axis=0)
    out_ref[...] = whole[0:OWN].astype(BF16)
    for n, ref in enumerate((query_ref, key_ref, value_ref)):
        part = jnp.concatenate(
            (whole[(n + 1) * OWN : (n + 2) * OWN], jnp.zeros((LANES - OWN, width), F32)), axis=0
        )
        ref[...] = jnp.transpose(part)[:, 0:OWN].astype(BF16)
    repeat(1, blocks, lambda r: b_whole(r, (d + blocks - r) % blocks).wait_recv())
    split = blocks // 2
    turned = jnp.concatenate([b_sums[j].astype(F32) for j in range(split)], axis=0)
    up_ref[...] = jnp.transpose(turned).astype(BF16)
    for j in range(split):
        down_ref[j * high : (j + 1) * high] = b_sums[split + j]

    swap.wait_send()
    for n in range(3):
        for k in range(3):
            give(n, k).wait_send()
    for part in range(2):
        give_far(part).wait_send()
    for k in range(chips):
        pair_copy((chip + k) % chips).wait_send()
    for k in range(1, chips):
        line_copy(k).wait_send()
    repeat(1, count, lambda r: near_copy(r, m).wait_send())
    repeat(1, blocks, lambda r: a_copy(r).wait_send())
    repeat(1, blocks, lambda r: b_copy(r).wait_send())
    repeat(1, blocks, lambda r: far_copy(r, d).wait_send())
    repeat(1, blocks, lambda r: a_whole(r, d).wait_send())
    repeat(1, blocks, lambda r: b_whole(r, d).wait_send())


def close(blocks_x, solo, shared, conv, sent, gathered, w_rows, block_w, one, norms, taps, blocks):
    _, rows, width = blocks_x[0].shape
    length = sent.shape[1]
    count = length // rows
    chips = count // 2
    units = (block_w.shape[0] - OWN) // 2
    depth = 4 * OWN // blocks
    high = 2 * units // blocks
    lanes = width + 2 * LANES
    vmem = pl.BlockSpec(memory_space=pltpu.VMEM)
    sems = lambda *n: pltpu.SemaphoreType.DMA(n)
    low = lambda *shape: jax.ShapeDtypeStruct(shape, BF16)
    return pl.pallas_call(
        close_kernel,
        in_specs=[pl.BlockSpec(memory_space=pl.ANY)] * 5 + [vmem] * 10,
        out_specs=[vmem] * 8,
        out_shape=(
            jax.ShapeDtypeStruct(one.shape, F32),
            low(width, units), low(units, width), low(OWN, width),
            low(width, OWN), low(width, OWN), low(width, OWN),
            jax.ShapeDtypeStruct((8, lanes), F32),
        ),
        scratch_shapes=[
            pltpu.VMEM((count, 3, rows, width), BF16),
            pltpu.VMEM((2 * units, width), F32),
            pltpu.VMEM((3 * OWN, length), BF16),
            pltpu.VMEM((OWN, length), BF16),
            pltpu.VMEM((2 * HD, length), BF16),
            pltpu.VMEM((2 * HD, length), BF16),
            pltpu.VMEM((chips, rows, width), BF16),
            pltpu.VMEM((rows, width), F32),
            pltpu.VMEM((chips, rows, width), BF16),
            pltpu.VMEM((chips, rows, width), BF16),
            pltpu.VMEM((chips, rows, width), BF16),
            pltpu.VMEM((blocks, depth, width), BF16),
            pltpu.VMEM((blocks, depth, width), BF16),
            pltpu.VMEM((blocks, depth, width), BF16),
            pltpu.VMEM((blocks, high, width), BF16),
            pltpu.VMEM((blocks, high, width), BF16),
            pltpu.VMEM((blocks, high, width), BF16),
            pltpu.VMEM((count, 8, lanes), F32),
            pltpu.VMEM((blocks, 8, lanes), F32),
            sems(5), sems(4, 3), sems(4, 3), sems(1), sems(1), sems(4), sems(4), sems(4), sems(4),
            sems(blocks), sems(blocks), sems(blocks), sems(blocks),
            sems(blocks), sems(blocks), sems(blocks), sems(blocks),
            sems(count), sems(count), sems(blocks), sems(blocks),
        ],
        compiler_params=pltpu.CompilerParams(
            vmem_limit_bytes=VMEM_BYTES, collective_id=0, has_side_effects=True
        ),
        cost_estimate=pl.CostEstimate(flops=0, bytes_accessed=30_000_000, transcendentals=0),
        name="close",
    )(*blocks_x, solo, shared, conv, sent, gathered, w_rows, block_w, one, norms, taps)


def shifted(block, off):
    count = lax.axis_size("mp")
    return lax.ppermute(block, "mp", [(n, (n - off) % count) for n in range(count)])


def far_halves(from_left, from_right, axis):
    cut = from_left.shape[axis] // 2
    low = lax.slice_in_dim(from_left, 0, cut, axis=axis)
    high = lax.slice_in_dim(from_right, cut, 2 * cut, axis=axis)
    return shifted(low, -2), shifted(high, 2)


def on_device(
    inputs, segment, w_query, w_key, w_value, planes, conv_taps, w_out,
    ln1_gain, ln1_bias, w_up, w_down, ln2_gain, ln2_bias, cotangent,
):
    count = lax.axis_size("mp")
    blocks = lax.axis_size("dp")
    rows, width = inputs.shape
    block_w = jnp.concatenate((w_up.T, w_down, w_out), 0)
    left_w, right_w = shifted(block_w, -2), shifted(block_w, 2)
    w_rows = jnp.concatenate((w_query, w_key, w_value), 1).T
    gathered, qkv = gather_qkv(inputs, w_rows, count)
    left_w, right_w, qkv = lax.optimization_barrier((left_w, right_w, qkv))
    far_w = far_halves(left_w, right_w, 0)
    gathered = gathered.reshape(rows * count, width)
    seg_row = segment[None, :]
    taps = jnp.pad(
        jnp.concatenate(
            (
                jnp.pad(conv_taps, ((0, 0), (0, 16 - HEADS))),
                jnp.pad(conv_taps[::-1], ((0, 0), (0, 16 - HEADS))),
            ),
            1,
        ),
        ((0, 2 * LANES - KW), (0, 0)),
    ).T
    conv = segment_conv(qkv, taps, seg_row)
    sent, numer, dens, sign, bucket = attend(qkv, planes, seg_row, conv)
    scale = jnp.stack((ln1_gain, ln1_bias, ln2_gain, ln2_bias) * 2)
    outputs, lows, one_grad, attn_grad, norm_part = middle(
        sent, inputs, cotangent, (block_w, left_w, right_w) + far_w, scale, count
    )
    left_x, right_x = shifted(lows, -2), shifted(lows, 2)
    saved = (numer, dens, sign, bucket)
    value_conv, tap_part = conv_back(qkv, attn_grad, taps, seg_row)
    solo = attend_back(0, qkv, planes, seg_row, attn_grad, *saved)
    solo, value_conv, left_x, right_x, attn_grad = lax.optimization_barrier(
        (solo, value_conv, left_x, right_x, attn_grad)
    )
    far_x = far_halves(left_x, right_x, 1)
    shared = attend_back(1, qkv, planes, seg_row, attn_grad, *saved)
    inputs_grad, up, down, out, query, key, value, tiny = close(
        (lows, left_x, right_x) + far_x, solo, shared, value_conv, sent, gathered, w_rows, block_w,
        one_grad, norm_part, tap_part, blocks,
    )
    conv_rows = jnp.concatenate(
        (tiny[:, width : width + LANES], tiny[: HEADS - 8, width + LANES :]), 0
    )
    return (
        outputs, inputs_grad, query.astype(F32), key.astype(F32), value.astype(F32),
        conv_rows[:, :KW].T, out.astype(F32), tiny[0, :width], tiny[1, :width],
        up.astype(F32), down.astype(F32), tiny[2, :width], tiny[3, :width],
    )


def solution(mesh):
    rows = P(("dp", "mp"), None)
    cols = P(None, "mp")
    return jax.shard_map(
        on_device,
        mesh=mesh,
        in_specs=(
            rows, P("dp"), cols, cols, cols, P(), P(), P("mp", None), P(), P(),
            cols, P("mp", None), P(), P(), rows,
        ),
        out_specs=(
            rows, rows, cols, cols, cols, P(), P("mp", None), P(), P(),
            cols, P("mp", None), P(), P(),
        ),
        check_vma=False,
    )
```

```python
from functools import partial
import math
import jax
import jax.numpy as jnp
from jax import lax
from jax.experimental import pallas as pl
from jax.experimental.pallas import tpu as pltpu
from jax.sharding import PartitionSpec as P

HEADS = 12
HD = 64
TABLES = 4
BITS = 8
KW = 65
MAXSEG = 8
CODES = 256
UNITS = 6
SOLO = 4
SPREAD = MAXSEG * HD
EXT = SPREAD + 128
LANES = 128
TILE = 2048
F32 = jnp.float32
BF16 = jnp.bfloat16
VMEM_BYTES = 56 * 1024 * 1024


def nt_dot(left, right):
    return lax.dot_general(left, right, (((1,), (1,)), ((), ())), preferred_element_type=F32)


def tn_dot(left, right):
    return lax.dot_general(left, right, (((0,), (0,)), ((), ())), preferred_element_type=F32)


def nn_dot(left, right):
    return lax.dot_general(left, right, (((1,), (0,)), ((), ())), preferred_element_type=F32)


def half_sign(bit):
    rows = lax.broadcasted_iota(jnp.int32, (8, LANES), 0)
    return jnp.where((rows >> bit) & 1 == 0, 0.5, -0.5).astype(F32)


def code_factors(signs):
    pos0, neg0 = 0.5 + 0.5 * signs[0:1], 0.5 - 0.5 * signs[0:1]
    pos1, neg1 = 0.5 + 0.5 * signs[1:2], 0.5 - 0.5 * signs[1:2]
    tops = (pos0 * pos1, pos0 * neg1, neg0 * pos1, neg0 * neg1)
    picks = [half_sign(2), half_sign(1), half_sign(0)]
    mids = [0.5 + picks[n] * signs[2 + n : 3 + n] for n in range(3)]
    lows = [0.5 + picks[n] * signs[5 + n : 6 + n] for n in range(3)]
    return tops, mids, lows, picks


def code_probs(signs, out_ref, lane):
    tops, mids, lows, _ = code_factors(signs)
    mid = mids[0] * mids[1] * mids[2]
    low = lows[0] * lows[1] * lows[2]
    for top_index in range(4):
        low_top = low * tops[top_index]
        for pair in range(4):
            rows = jnp.concatenate(
                (
                    low_top * mid[2 * pair : 2 * pair + 1],
                    low_top * mid[2 * pair + 1 : 2 * pair + 2],
                ),
                axis=0,
            )
            first = top_index * 64 + pair * 16
            out_ref[first : first + 16, lane] = rows.astype(BF16)


def signs_back(signs, grads):
    tops, mids, lows, picks = code_factors(signs)
    mid = mids[0] * mids[1] * mids[2]
    low = lows[0] * lows[1] * lows[2]
    mid_rows = [jnp.broadcast_to(mid[m : m + 1], (8, LANES)) for m in range(8)]
    top_rows = [jnp.broadcast_to(tops[t], (8, LANES)) for t in range(4)]
    by_top = [None] * 4
    by_mid = [None] * 8
    for t in range(4):
        for m in range(8):
            piece = grads[t * 64 + m * 8 : t * 64 + m * 8 + 8]
            a = piece * mid_rows[m]
            b = piece * top_rows[t]
            by_top[t] = a if by_top[t] is None else by_top[t] + a
            by_mid[m] = b if by_mid[m] is None else by_mid[m] + b
    low_grad = by_top[0] * top_rows[0]
    for t in range(1, 4):
        low_grad = low_grad + by_top[t] * top_rows[t]
    top_grad = [jnp.sum(low * by_top[t], axis=0, keepdims=True) for t in range(4)]
    mid_grad = jnp.concatenate(
        [jnp.sum(low * by_mid[m], axis=0, keepdims=True) for m in range(8)], axis=0
    )
    pos0, neg0 = 0.5 + 0.5 * signs[0:1], 0.5 - 0.5 * signs[0:1]
    pos1, neg1 = 0.5 + 0.5 * signs[1:2], 0.5 - 0.5 * signs[1:2]
    out = [
        0.5 * ((top_grad[0] - top_grad[2]) * pos1 + (top_grad[1] - top_grad[3]) * neg1),
        0.5 * ((top_grad[0] - top_grad[1]) * pos0 + (top_grad[2] - top_grad[3]) * neg0),
    ]
    for grad, parts in ((mid_grad, mids), (low_grad, lows)):
        for n in range(3):
            others = parts[(n + 1) % 3] * parts[(n + 2) % 3] * picks[n]
            out.append(jnp.sum(grad * others, axis=0, keepdims=True))
    return jnp.concatenate(out, axis=0)


def split_two(value):
    high = value.astype(BF16).astype(F32)
    return high, value - high


def unit_planes(planes):
    return planes * lax.rsqrt(jnp.sum(planes * planes, axis=1, keepdims=True) + 1e-06)


def fill_spread(values, seg_row, spread_ref, lane):
    for s in range(MAXSEG):
        spread_ref[s * HD : (s + 1) * HD, lane] = jnp.where(
            seg_row == s, values, jnp.zeros_like(values)
        )


def fill_member(seg_row, spread_ref, lane):
    width = seg_row.shape[1]
    rows = lax.broadcasted_iota(jnp.int32, (128, width), 0)
    hit = jnp.logical_and(rows < 16, (rows & 7) == seg_row)
    spread_ref[SPREAD:EXT, lane] = jnp.where(hit, 1.0, 0.0).astype(BF16)


def plane_rows(unit):
    side = lax.axis_index("mp") % 2
    row = jnp.where(unit < SOLO, unit, 2 * side + unit - SOLO)
    return pl.ds(pl.multiple_of(row * BITS, BITS), BITS)


def lanes_of(index, width):
    return pl.ds(pl.multiple_of(index * width, width), width)


def masked_fold(product, seg_row):
    total = None
    for s in range(MAXSEG):
        piece = jnp.where(seg_row == s, product[s * HD : (s + 1) * HD], 0.0)
        total = piece if total is None else total + piece
    return total


def attend_kernel(
    qkv_ref, planes_ref, seg_ref, conv_ref,
    sent_ref, numer_ref, dens_ref, sign_ref, bucket_ref,
    spread, norm, qprob, kprob, total, table, est,
):
    unit = pl.program_id(0)
    slot = unit // SOLO
    length = qkv_ref.shape[1]
    tiles = length // TILE
    q_rows = pl.ds(pl.multiple_of(slot * HD, HD), HD)
    k_rows = pl.ds(pl.multiple_of(2 * HD + slot * HD, HD), HD)
    v_rows = pl.ds(pl.multiple_of(4 * HD + slot * HD, HD), HD)

    @pl.when(jnp.logical_or(unit == 0, unit == SOLO))
    def _():
        def step(i, carry):
            lane = lanes_of(i, TILE)
            seg_row = seg_ref[:, lane]
            fill_spread(qkv_ref[v_rows, lane], seg_row, spread, lane)
            fill_member(seg_row, spread, lane)
            query = qkv_ref[q_rows, lane].astype(F32)
            key = qkv_ref[k_rows, lane].astype(F32)
            scale = math.sqrt(HD)
            norm[0:1, lane] = scale * lax.rsqrt(
                jnp.sum(query * query, axis=0, keepdims=True) + 1e-06
            )
            norm[1:2, lane] = scale * lax.rsqrt(jnp.sum(key * key, axis=0, keepdims=True) + 1e-06)
            est[:, lane] = jnp.zeros((HD, TILE), F32)
            return carry

        lax.fori_loop(0, tiles, step, 0)

    planes = unit_planes(planes_ref[plane_rows(unit), :])
    high, rest = split_two(planes)
    middle, low = split_two(rest)
    stack = jnp.concatenate((high, middle, low), axis=0).astype(BF16)
    total[...] = jnp.zeros_like(total)

    def collect(i, carry):
        lane = lanes_of(i, TILE)
        flat_q = nn_dot(stack, qkv_ref[q_rows, lane])
        flat_k = nn_dot(stack, qkv_ref[k_rows, lane])
        sign_q = jnp.tanh((flat_q[0:8] + flat_q[8:16] + flat_q[16:24]) * norm[0:1, lane])
        sign_k = jnp.tanh((flat_k[0:8] + flat_k[8:16] + flat_k[16:24]) * norm[1:2, lane])
        sign_ref[0, 0:8, lane] = sign_q
        sign_ref[0, 8:16, lane] = sign_k
        for part in range(TILE // LANES):
            inner = slice(part * LANES, (part + 1) * LANES)
            code_probs(sign_k[:, inner], kprob, inner)
            code_probs(
                sign_q[:, inner], qprob, pl.ds(pl.multiple_of(i * TILE + part * LANES, LANES), LANES)
            )
        total[...] += nt_dot(spread[0 : SPREAD + 16, lane], kprob[...])
        return carry

    lax.fori_loop(0, tiles, collect, 0)
    mass = total[SPREAD : SPREAD + 8, :]
    mass_high, mass_low = split_two(mass)
    extra = jnp.concatenate(
        (mass_high, mass_high, mass_low, jnp.zeros((104, CODES), F32)), axis=0
    )
    table[0:SPREAD, :] = total[0:SPREAD, :].astype(BF16)
    table[SPREAD:EXT, :] = extra.astype(BF16)
    bucket_ref[0, :, 0:SPREAD] = jnp.transpose(total[0:SPREAD, :]).astype(BF16)
    bucket_ref[0, :, SPREAD:EXT] = jnp.transpose(extra).astype(BF16)

    def spend(i, carry):
        lane = lanes_of(i, TILE)
        seg_row = seg_ref[:, lane]
        product = nn_dot(table[0 : SPREAD + 32, :], qprob[:, lane])
        numer = masked_fold(product, seg_row)
        both = product[SPREAD : SPREAD + 8] + product[SPREAD + 16 : SPREAD + 24]
        which = lax.broadcasted_iota(jnp.int32, (8, TILE), 0)
        density = jnp.sum(jnp.where(which == seg_row, both, 0.0), axis=0, keepdims=True)
        numer_ref[0, :, lane] = numer
        dens_ref[0, :, lane] = density
        est[:, lane] += numer * (1.0 / jnp.maximum(density, 1.0))
        return carry

    lax.fori_loop(0, tiles, spend, 0)

    @pl.when(jnp.logical_or(unit == SOLO - 1, unit == UNITS - 1))
    def _():
        sent_ref[q_rows, :] = (est[...] * (1.0 / TABLES) + conv_ref[q_rows, :]).astype(BF16)


def attend(qkv, planes, seg_row, conv):
    length = qkv.shape[1]
    per_unit = lambda u: (u, 0, 0)
    fixed = lambda u: (0, 0)
    return pl.pallas_call(
        attend_kernel,
        grid=(UNITS,),
        in_specs=[
            pl.BlockSpec(qkv.shape, fixed),
            pl.BlockSpec(planes.shape, fixed),
            pl.BlockSpec(seg_row.shape, fixed),
            pl.BlockSpec(conv.shape, fixed),
        ],
        out_specs=[
            pl.BlockSpec((2 * HD, length), fixed),
            pl.BlockSpec((1, HD, length), per_unit),
            pl.BlockSpec((1, 1, length), per_unit),
            pl.BlockSpec((1, 16, length), per_unit),
            pl.BlockSpec((1, CODES, EXT), per_unit),
        ],
        out_shape=[
            jax.ShapeDtypeStruct((2 * HD, length), BF16),
            jax.ShapeDtypeStruct((UNITS, HD, length), F32),
            jax.ShapeDtypeStruct((UNITS, 1, length), F32),
            jax.ShapeDtypeStruct((UNITS, 16, length), F32),
            jax.ShapeDtypeStruct((UNITS, CODES, EXT), BF16),
        ],
        scratch_shapes=[
            pltpu.VMEM((EXT, length), BF16),
            pltpu.VMEM((8, length), F32),
            pltpu.VMEM((CODES, length), BF16),
            pltpu.VMEM((CODES, TILE), BF16),
            pltpu.VMEM((SPREAD + 16, CODES), F32),
            pltpu.VMEM((EXT, CODES), BF16),
            pltpu.VMEM((HD, length), F32),
        ],
        compiler_params=pltpu.CompilerParams(vmem_limit_bytes=VMEM_BYTES),
        cost_estimate=pl.CostEstimate(flops=0, bytes_accessed=1_000_000, transcendentals=0),
        name="attend",
    )(qkv, planes, seg_row, conv)


def attend_back_kernel(
    slot, first_unit, units,
    qkv_ref, planes_ref, seg_ref, grad_ref, numer_ref, dens_ref, sign_ref, bucket_ref,
    out_ref,
    spread, qprob, kprob, gspread, total, table, turned, gsign, proj,
):
    step_unit = pl.program_id(0)
    unit = first_unit + step_unit
    length = qkv_ref.shape[1]
    tiles = length // TILE
    q_rows = slice(slot * HD, slot * HD + HD)
    k_rows = slice(2 * HD + slot * HD, 3 * HD + slot * HD)
    v_rows = slice(4 * HD + slot * HD, 5 * HD + slot * HD)
    v_out = slice(2 * HD, 3 * HD)

    @pl.when(step_unit == 0)
    def _():
        def step(i, carry):
            lane = lanes_of(i, TILE)
            seg_row = seg_ref[:, lane]
            fill_spread(qkv_ref[v_rows, lane], seg_row, spread, lane)
            fill_member(seg_row, spread, lane)
            proj[:, lane] = jnp.zeros((2 * HD, TILE), F32)
            out_ref[v_out, lane] = jnp.zeros((HD, TILE), F32)
            return carry

        lax.fori_loop(0, tiles, step, 0)
        gspread[SPREAD:EXT, :] = jnp.zeros((128, TILE), BF16)

    total[...] = jnp.zeros_like(total)

    def first(i, carry):
        lane = lanes_of(i, TILE)
        seg_row = seg_ref[:, lane]
        density = dens_ref[0, :, lane]
        inverse = 1.0 / jnp.maximum(density, 1.0)
        est_grad = grad_ref[q_rows, lane].astype(F32) * (1.0 / TABLES)
        num_grad = (est_grad * inverse).astype(BF16)
        fill_spread(num_grad, seg_row, gspread, slice(0, TILE))
        inner_sum = jnp.sum(est_grad * numer_ref[0, :, lane], axis=0, keepdims=True)
        dens_grad = jnp.where(density > 1.0, -inner_sum * inverse * inverse, 0.0)
        which = lax.broadcasted_iota(jnp.int32, (8, TILE), 0)
        high, low = split_two(jnp.where(which == seg_row, dens_grad, 0.0))
        gspread[SPREAD : SPREAD + 32, :] = jnp.concatenate(
            (high, low, high, jnp.zeros_like(high)), axis=0
        ).astype(BF16)
        collected = nn_dot(bucket_ref[0], gspread[...])
        for part in range(TILE // LANES):
            inner = slice(part * LANES, (part + 1) * LANES)
            outer = pl.ds(pl.multiple_of(i * TILE + part * LANES, LANES), LANES)
            sign_q = sign_ref[0, 0:8, outer]
            code_probs(sign_q, qprob, inner)
            gsign[0:8, outer] = signs_back(sign_q, collected[:, inner])
        total[...] += nt_dot(gspread[0 : SPREAD + 16, :], qprob[...])
        return carry

    lax.fori_loop(0, tiles, first, 0)
    mass_grad = total[SPREAD : SPREAD + 8, :] + total[SPREAD + 8 : SPREAD + 16, :]
    high, low = split_two(mass_grad)
    extra = jnp.concatenate((high, low, jnp.zeros((112, CODES), F32)), axis=0)
    table[...] = total[0:SPREAD, :].astype(BF16)
    turned[:, 0:SPREAD] = jnp.transpose(total[0:SPREAD, :]).astype(BF16)
    turned[:, SPREAD:EXT] = jnp.transpose(extra).astype(BF16)

    planes = unit_planes(planes_ref[plane_rows(unit), :])
    plane_high, plane_low = split_two(planes)
    stack = jnp.concatenate((plane_high, plane_low, plane_high, jnp.zeros_like(plane_high)), axis=0)
    stack = stack.astype(BF16)

    def second(i, carry):
        lane = lanes_of(i, TILE)
        seg_row = seg_ref[:, lane]
        for part in range(TILE // LANES):
            inner = slice(part * LANES, (part + 1) * LANES)
            outer = pl.ds(pl.multiple_of(i * TILE + part * LANES, LANES), LANES)
            code_probs(sign_ref[0, 8:16, outer], kprob, inner)
        out_ref[v_out, lane] += masked_fold(nn_dot(table[...], kprob[...]), seg_row)
        collected = nn_dot(turned[...], spread[:, lane])
        for part in range(TILE // LANES):
            inner = slice(part * LANES, (part + 1) * LANES)
            outer = pl.ds(pl.multiple_of(i * TILE + part * LANES, LANES), LANES)
            gsign[8:16, outer] = signs_back(sign_ref[0, 8:16, outer], collected[:, inner])
        signs = sign_ref[0, :, lane]
        flat = gsign[:, lane] * (1.0 - signs * signs)
        high, low = split_two(flat)
        for side in range(2):
            rows = slice(8 * side, 8 * side + 8)
            pieces = jnp.concatenate(
                (high[rows], high[rows], low[rows], jnp.zeros((8, TILE), F32)), axis=0
            ).astype(BF16)
            proj[side * HD : (side + 1) * HD, lane] += tn_dot(stack, pieces)
        return carry

    lax.fori_loop(0, tiles, second, 0)

    @pl.when(step_unit == units - 1)
    def _():
        def step(i, carry):
            lane = lanes_of(i, TILE)
            for side, rows in ((0, q_rows), (1, k_rows)):
                vec = qkv_ref[rows, lane].astype(F32)
                inverse = lax.rsqrt(jnp.sum(vec * vec, axis=0, keepdims=True) + 1e-06)
                unit_vec = vec * inverse
                grad = proj[side * HD : (side + 1) * HD, lane]
                along = jnp.sum(unit_vec * grad, axis=0, keepdims=True)
                out_ref[side * HD : (side + 1) * HD, lane] = math.sqrt(HD) * inverse * (grad - unit_vec * along)
            return carry

        lax.fori_loop(0, tiles, step, 0)


def attend_back(slot, qkv, planes, seg_row, grad, numer, dens, sign, bucket):
    length = qkv.shape[1]
    first_unit = slot * SOLO
    units = SOLO if slot == 0 else UNITS - SOLO
    per_unit = lambda u: (u + first_unit, 0, 0)
    fixed = lambda u: (0, 0)
    return pl.pallas_call(
        partial(attend_back_kernel, slot, first_unit, units),
        grid=(units,),
        in_specs=[
            pl.BlockSpec(qkv.shape, fixed),
            pl.BlockSpec(planes.shape, fixed),
            pl.BlockSpec(seg_row.shape, fixed),
            pl.BlockSpec(grad.shape, fixed),
            pl.BlockSpec((1, HD, length), per_unit),
            pl.BlockSpec((1, 1, length), per_unit),
            pl.BlockSpec((1, 16, length), per_unit),
            pl.BlockSpec((1, CODES, EXT), per_unit),
        ],
        out_specs=pl.BlockSpec((3 * HD, length), fixed),
        out_shape=jax.ShapeDtypeStruct((3 * HD, length), F32),
        scratch_shapes=[
            pltpu.VMEM((EXT, length), BF16),
            pltpu.VMEM((CODES, TILE), BF16),
            pltpu.VMEM((CODES, TILE), BF16),
            pltpu.VMEM((EXT, TILE), BF16),
            pltpu.VMEM((SPREAD + 16, CODES), F32),
            pltpu.VMEM((SPREAD, CODES), BF16),
            pltpu.VMEM((CODES, EXT), BF16),
            pltpu.VMEM((16, length), F32),
            pltpu.VMEM((2 * HD, length), F32),
        ],
        compiler_params=pltpu.CompilerParams(vmem_limit_bytes=VMEM_BYTES),
        cost_estimate=pl.CostEstimate(flops=0, bytes_accessed=1_000_000, transcendentals=0),
        name="attend_back",
    )(qkv, planes, seg_row, grad, numer, dens, sign, bucket)


SPAN = 192
SHIFT = (KW - 1) // 2
OWN = 96
BLOCKS = ((0, HD), (HD, OWN))


def own_heads():
    m = lax.axis_index("mp")
    group = m // 2
    return (3 * group + 2 * (m % 2), 3 * group + 1)


def own_half():
    side = lax.axis_index("mp") % 2
    half = OWN - HD
    return side, half


def band_of(row):
    turned = jnp.broadcast_to(row, (LANES, 2 * LANES))
    index = lax.broadcasted_iota(jnp.int32, turned.shape, 0)
    for bit in range(7):
        moved = pltpu.roll(turned, 1 << bit, 1)
        turned = jnp.where((index >> bit) & 1 == 1, moved, turned)
    return jnp.transpose(turned)[0:SPAN]


def fill_hot(seg_ref, hot, hot_pad):
    length = seg_ref.shape[1]
    rows = lax.broadcasted_iota(jnp.int32, (16, length), 0)
    value = jnp.where(rows == seg_ref[...], 1.0, 0.0)
    value = jnp.where(rows < MAXSEG, value, 0.0).astype(BF16)
    hot[...] = value
    hot_pad[...] = jnp.zeros_like(hot_pad)
    hot_pad[:, SHIFT : SHIFT + length] = value


def band_product(rows, band):
    high, low = split_two(band)
    return nn_dot(rows, high.astype(BF16)) + nn_dot(rows, low.astype(BF16))


def conv_kernel(qkv_ref, taps_ref, seg_ref, out_ref, hot, hot_pad, pad, band):
    length = out_ref.shape[1]
    side, half = own_half()
    own = pl.ds(pl.multiple_of(HD + side * half, half), half)
    other = pl.ds(pl.multiple_of(HD + (1 - side) * half, half), half)
    fill_hot(seg_ref, hot, hot_pad)
    pad[...] = jnp.zeros_like(pad)
    pad[0:HD, SHIFT : SHIFT + length] = qkv_ref[4 * HD : 5 * HD, :]
    value_half = pl.ds(pl.multiple_of(5 * HD + side * half, half), half)
    pad[HD:OWN, SHIFT : SHIFT + length] = qkv_ref[value_half, :]
    for h, head in enumerate(own_heads()):
        band[h] = band_of(taps_ref[pl.ds(head, 1), :])
    out_ref[other, :] = jnp.zeros((half, length), F32)
    for i in range(length // LANES):
        lane = slice(i * LANES, (i + 1) * LANES)
        wide = slice(i * LANES, i * LANES + SPAN)
        mask = tn_dot(hot_pad[:, wide], hot[:, lane])
        out_ref[0:HD, lane] = band_product(pad[0:HD, wide], band[0] * mask)
        out_ref[own, lane] = band_product(pad[HD:OWN, wide], band[1] * mask)


def segment_conv(qkv, taps, seg_row):
    length = seg_row.shape[1]
    return pl.pallas_call(
        conv_kernel,
        out_shape=jax.ShapeDtypeStruct((2 * HD, length), F32),
        scratch_shapes=[
            pltpu.VMEM((16, length), BF16),
            pltpu.VMEM((16, length + LANES), BF16),
            pltpu.VMEM((OWN, length + LANES), BF16),
            pltpu.VMEM((2, SPAN, LANES), F32),
        ],
        compiler_params=pltpu.CompilerParams(vmem_limit_bytes=VMEM_BYTES),
        cost_estimate=pl.CostEstimate(flops=0, bytes_accessed=1_000_000, transcendentals=0),
        name="segment_conv",
    )(qkv, taps, seg_row)


def conv_back_kernel(
    qkv_ref, grad_ref, taps_ref, seg_ref, out_ref, tap_ref, hot, hot_pad, pad, gpad, band, corr
):
    length = seg_ref.shape[1]
    side, half = own_half()
    fill_hot(seg_ref, hot, hot_pad)
    pad[...] = jnp.zeros_like(pad)
    gpad[...] = jnp.zeros_like(gpad)
    inside = slice(SHIFT, SHIFT + length)
    value_half = pl.ds(pl.multiple_of(5 * HD + side * half, half), half)
    grad_half = pl.ds(pl.multiple_of(HD + side * half, half), half)
    pad[0:HD, inside] = qkv_ref[4 * HD : 5 * HD, :]
    pad[HD:OWN, inside] = qkv_ref[value_half, :]
    gpad[0:HD, inside] = grad_ref[0:HD, :]
    gpad[HD:OWN, inside] = grad_ref[grad_half, :]
    heads = own_heads()
    for h, head in enumerate(heads):
        band[h] = band_of(taps_ref[pl.ds(16 + head, 1), :])
    corr[...] = jnp.zeros_like(corr)
    for i in range(length // LANES):
        lane = slice(i * LANES, (i + 1) * LANES)
        wide = slice(i * LANES, i * LANES + SPAN)
        twice = slice(i * LANES, (i + 2) * LANES)
        mask = tn_dot(hot_pad[:, wide], hot[:, lane])
        turned = tn_dot(hot[:, lane], hot_pad[:, twice])
        grads = (grad_ref[0:HD, lane], grad_ref[grad_half, lane])
        for h, (low_row, high_row) in enumerate(BLOCKS):
            out_ref[low_row:high_row, lane] = band_product(
                gpad[low_row:high_row, wide], band[h] * mask
            )
            corr[h] += turned * tn_dot(grads[h], pad[low_row:high_row, twice])
    row = lax.broadcasted_iota(jnp.int32, (LANES, 2 * LANES), 0)
    place = lax.broadcasted_iota(jnp.int32, (8, LANES), 0)
    low_heads = jnp.zeros((8, LANES), F32)
    high_heads = jnp.zeros((8, LANES), F32)
    for h, head in enumerate(heads):
        skew = corr[h]
        for bit in range(7):
            moved = pltpu.roll(skew, 2 * LANES - (1 << bit), 1)
            skew = jnp.where((row >> bit) & 1 == 1, moved, skew)
        taps = jnp.sum(skew, axis=0, keepdims=True)[:, 0:LANES]
        low_heads = low_heads + jnp.where(place == head, taps, 0.0)
        high_heads = high_heads + jnp.where(place + 8 == head, taps, 0.0)
    tap_ref[:, 0:LANES] = low_heads
    tap_ref[:, LANES : 2 * LANES] = high_heads


def conv_back(qkv, grad, taps, seg_row):
    length = seg_row.shape[1]
    return pl.pallas_call(
        conv_back_kernel,
        out_shape=(
            jax.ShapeDtypeStruct((OWN, length), F32),
            jax.ShapeDtypeStruct((8, 2 * LANES), F32),
        ),
        scratch_shapes=[
            pltpu.VMEM((16, length), BF16),
            pltpu.VMEM((16, length + LANES), BF16),
            pltpu.VMEM((OWN, length + LANES), BF16),
            pltpu.VMEM((OWN, length + LANES), BF16),
            pltpu.VMEM((2, SPAN, LANES), F32),
            pltpu.VMEM((2, LANES, 2 * LANES), F32),
        ],
        compiler_params=pltpu.CompilerParams(vmem_limit_bytes=VMEM_BYTES),
        cost_estimate=pl.CostEstimate(flops=0, bytes_accessed=1_000_000, transcendentals=0),
        name="conv_back",
    )(qkv, grad, taps, seg_row)


def norm_rows(values):
    center = values - jnp.mean(values, axis=1, keepdims=True)
    inverse = lax.rsqrt(jnp.mean(center * center, axis=1, keepdims=True) + 1e-05)
    return center * inverse, inverse


def norm_back(upstream, normed, inverse, gain):
    scaled = upstream * gain
    inner = (
        scaled
        - jnp.mean(scaled, axis=1, keepdims=True)
        - normed * jnp.mean(scaled * normed, axis=1, keepdims=True)
    )
    return inner * inverse


def gelu_pair(value):
    cdf = 0.5 + 0.5 * lax.erf(value * math.sqrt(0.5))
    pdf = jnp.exp(-0.5 * value * value) * (1.0 / math.sqrt(2.0 * math.pi))
    return value * cdf, cdf + value * pdf


def column_sum(values):
    return jnp.sum(values, axis=0, keepdims=True)


MESH = pl.DeviceIdType.MESH
OFFSETS = (0, -2, 2, 4)
INVERSE = (0, 2, 1, 3, 4, 6, 5, 7)


def repeat(start, stop, action):
    def body(r, carry):
        action(r)
        return carry

    lax.fori_loop(start, stop, body, 0)


def remote(src, dst, send, recv, target):
    return pltpu.make_async_remote_copy(
        src_ref=src, dst_ref=dst, send_sem=send, recv_sem=recv,
        device_id={"mp": target}, device_id_type=MESH,
    )


def greet(targets):
    barrier = pltpu.get_barrier_semaphore()
    for target in targets:
        pl.semaphore_signal(barrier, inc=1, device_id={"mp": target}, device_id_type=MESH)
    pl.semaphore_wait(barrier, len(targets))


def gather_kernel(x_ref, w_ref, all_ref, qkv_ref, wide, send, recv):
    count, rows, _ = all_ref.shape
    m = lax.axis_index("mp")
    side = m % 2
    sibling = m + 1 - 2 * side
    left = (m + count - 2) % count
    right = (m + 2) % count
    far = (m + 4) % count
    half = OWN - HD
    cut = rows // 2
    greet((left, right, sibling))

    def copy(n, src, dst, target):
        return remote(src, dst, send.at[n], recv.at[n], target)

    def piece(n, which):
        return pl.ds(pl.multiple_of(n * 2 * HD + HD + which * half, half), half)

    def weight_copy(n, which):
        source = w_ref.at[pl.ds(pl.multiple_of(n * OWN + (1 - side) * HD, half), half), :]
        return copy(11 + n, source, wide.at[piece(n, which), :], sibling)

    low, high = slice(0, cut), slice(cut, rows)

    def own_copy(n, owner):
        part, target = ((low, right), (high, right), (high, left), (low, left))[n]
        return copy(n, x_ref.at[part], all_ref.at[owner, part], target)

    for n in range(3):
        weight_copy(n, side).start()
    for n in (0, 2, 1, 3):
        own_copy(n, m).start()
    to_sibling = copy(4, x_ref, all_ref.at[m], sibling)
    to_sibling.start()
    all_ref[m] = x_ref[...]
    for n in range(3):
        solo = pl.ds(pl.multiple_of(n * OWN + side * half, half), HD)
        own = pl.ds(pl.multiple_of(n * OWN + (1 - side) * HD, half), half)
        wide[n * 2 * HD : n * 2 * HD + HD, :] = w_ref[solo, :]
        wide[piece(n, side), :] = w_ref[own, :]
    for n in range(3):
        weight_copy(n, 1 - side).wait_recv()

    def project(block):
        lane = pl.ds(pl.multiple_of(block * rows, rows), rows)
        qkv_ref[:, lane] = nt_dot(wide[...], all_ref[block]).astype(BF16)

    def pass_on(n, owner, part, target):
        return copy(n, all_ref.at[owner, part], all_ref.at[owner, part], target)

    project(m)
    own_copy(0, left).wait_recv()
    on_right = pass_on(5, left, low, right)
    on_right.start()
    own_copy(2, right).wait_recv()
    on_left = pass_on(6, right, high, left)
    on_left.start()
    copy(4, x_ref, all_ref.at[sibling], sibling).wait_recv()
    project(sibling)
    own_copy(1, left).wait_recv()
    over_left = copy(7, all_ref.at[left], all_ref.at[left], sibling)
    over_left.start()
    own_copy(3, right).wait_recv()
    over_right = copy(8, all_ref.at[right], all_ref.at[right], sibling)
    over_right.start()
    project(left)
    project(right)
    other_left = (sibling + count - 2) % count
    other_right = (sibling + 2) % count
    other_far = (sibling + 4) % count
    copy(7, x_ref, all_ref.at[other_left], sibling).wait_recv()
    project(other_left)
    copy(8, x_ref, all_ref.at[other_right], sibling).wait_recv()
    project(other_right)
    pass_on(5, far, low, left).wait_recv()
    over_low = pass_on(9, far, low, sibling)
    over_low.start()
    pass_on(6, far, high, right).wait_recv()
    over_high = pass_on(10, far, high, sibling)
    over_high.start()
    project(far)
    pass_on(9, other_far, low, sibling).wait_recv()
    pass_on(10, other_far, high, sibling).wait_recv()
    project(other_far)
    for n in range(3):
        weight_copy(n, side).wait_send()
    for n in range(4):
        own_copy(n, m).wait_send()
    for sent in (to_sibling, on_right, on_left, over_left, over_right, over_low, over_high):
        sent.wait_send()


def gather_qkv(x, w_rows, count):
    rows, width = x.shape
    vmem = pl.BlockSpec(memory_space=pltpu.VMEM)
    return pl.pallas_call(
        gather_kernel,
        in_specs=[vmem] * 2,
        out_specs=[vmem] * 2,
        out_shape=(
            jax.ShapeDtypeStruct((count, rows, width), BF16),
            jax.ShapeDtypeStruct((6 * HD, count * rows), BF16),
        ),
        scratch_shapes=[
            pltpu.VMEM((6 * HD, width), BF16),
            pltpu.SemaphoreType.DMA((14,)),
            pltpu.SemaphoreType.DMA((14,)),
        ],
        compiler_params=pltpu.CompilerParams(
            vmem_limit_bytes=VMEM_BYTES, collective_id=2, has_side_effects=True
        ),
        cost_estimate=pl.CostEstimate(
            flops=12 * HD * count * rows * width, bytes_accessed=30_000_000, transcendentals=0
        ),
        name="gather_qkv",
    )(x, w_rows)


def around(m, count):
    sibling = m + 1 - 2 * (m % 2)
    return [(base + count + off) % count for base in (m, sibling) for off in OFFSETS]


def middle_kernel(
    sent_ref, x_ref, cot_ref, own_w, left_w, right_w, scale_ref,
    result_ref, lows_ref, one_ref, attn_ref, part_ref,
    wall, out_w, att_in, attn_out, slope, keep, acc,
    load, give_send, give_recv, rest_send, rest_recv, line_send, line_recv, far_send, far_recv,
    in_send, in_recv, out_send, out_recv,
):
    rows = x_ref.shape[0]
    count = att_in.shape[0]
    units = slope.shape[2]
    both = 2 * units
    m = lax.axis_index("mp")
    devices = around(m, count)
    sibling = devices[4]
    greet(devices[1:])

    def tokens(index):
        return pl.ds(pl.multiple_of(index * rows, rows), rows)

    side = m % 2
    depth = wall.shape[1]
    blocks = (own_w, left_w, right_w)
    out_rows = slice(both, depth)
    ffn_rows = slice(0, both)
    parts = (slice(0, units), slice(units, both))

    middle_row = both + OWN // 2
    out_parts = (slice(both, middle_row), slice(middle_row, depth))

    def give(n):
        return remote(
            blocks[n].at[out_rows], wall.at[4 + n, out_rows], give_send.at[n], give_recv.at[n],
            sibling,
        )

    def out_along(n):
        return remote(
            blocks[1 + n].at[out_parts[n]], wall.at[3, out_parts[n]], give_send.at[3 + n],
            give_recv.at[3 + n], devices[2 - n],
        )

    def out_far(n):
        return remote(
            wall.at[3, out_parts[n]], wall.at[7, out_parts[n]], give_send.at[5 + n],
            give_recv.at[5 + n], sibling,
        )

    def rest(n):
        return remote(
            blocks[n].at[ffn_rows], wall.at[4 + n, ffn_rows], rest_send.at[n], rest_recv.at[n],
            sibling,
        )

    def along(n):
        return remote(
            blocks[1 + n].at[parts[n]], wall.at[3, parts[n]], line_send.at[n], line_recv.at[n],
            devices[2 - n],
        )

    def far_copy(n):
        return remote(
            wall.at[3, parts[n]], wall.at[7, parts[n]], far_send.at[n], far_recv.at[n], sibling
        )

    def loads():
        return [pltpu.make_async_copy(blocks[n], wall.at[n], load.at[n]) for n in range(3)]

    def att_copy(n, slot, sem):
        return remote(
            sent_ref.at[:, tokens(devices[n])], att_in.at[slot], in_send.at[n], in_recv.at[sem],
            devices[n],
        )

    def attn_copy(n, lane, sem):
        return remote(
            attn_out.at[n], attn_ref.at[:, tokens(lane)], out_send.at[n], out_recv.at[sem],
            devices[n],
        )

    for n in range(2):
        out_along(n).start()
    for n in range(1, count):
        att_copy(n, INVERSE[n], INVERSE[n]).start()
    for n in range(3):
        give(n).start()
    for copy in loads():
        copy.start()
    for n in range(3):
        rest(n).start()
    att_in[0] = sent_ref[:, tokens(m)]
    for copy in loads():
        copy.wait()
    for n in range(2):
        out_along(n).wait_recv()
        out_far(n).start()
    for n in range(3):
        give(n).wait_recv()
    for n in range(1, count):
        att_copy(n, n, n).wait_recv()
    for n in range(2):
        along(n).start()
    projected = None
    for n in range(4):
        if n == 3:
            for part in range(2):
                out_far(part).wait_recv()
        first, second = n + 4 * side, n + 4 * (1 - side)
        out_w[n, 0:OWN] = wall[first, out_rows]
        out_w[n, OWN : 2 * OWN] = wall[second, out_rows]
        shared = att_in[first, HD : 2 * HD].astype(F32) + att_in[second, HD : 2 * HD].astype(F32)
        features = jnp.concatenate(
            (att_in[first, 0:HD], shared.astype(BF16), att_in[second, 0:HD]), axis=0
        )
        piece = tn_dot(features, out_w[n])
        projected = piece if projected is None else projected + piece
    unit, inverse = norm_rows(x_ref[...].astype(F32) + projected)
    hidden = unit * scale_ref[0:1] + scale_ref[1:2]
    keep[0] = unit
    keep[1] = hidden
    lows_ref[0] = hidden.astype(BF16)
    acc[...] = jnp.zeros_like(acc)

    def forward(slots):
        low = lows_ref[0]
        total = acc[...]
        for slot in slots:
            active, lean = gelu_pair(nt_dot(low, wall[slot, 0:units]))
            slope[slot] = lean
            total = total + nn_dot(active.astype(BF16), wall[slot, units:both])
        acc[...] = total

    for n in range(3):
        rest(n).wait_recv()
    repeat(0, 3, lambda n: forward((n, 4 + n)))
    for n in range(2):
        along(n).wait_recv()
        far_copy(n).start()
    forward((3,))
    for n in range(2):
        far_copy(n).wait_recv()
    forward((7,))
    unit, inv = norm_rows(keep[1] + acc[...])
    result_ref[...] = (unit * scale_ref[2:3] + scale_ref[3:4]).astype(BF16)
    upstream = cot_ref[...].astype(F32)
    part_ref[2:3] = column_sum(upstream * unit)
    part_ref[3:4] = column_sum(upstream)
    grad = norm_back(upstream, unit, inv, scale_ref[2:3])
    keep[1] = grad
    lows_ref[1] = grad.astype(BF16)
    acc[...] = jnp.zeros_like(acc)

    def backward(i, carry):
        low = lows_ref[1]
        total = acc[...]
        for n in range(2):
            pre_grad = nt_dot(low, wall[2 * i + n, units:both]) * slope[2 * i + n]
            total = total + nn_dot(pre_grad.astype(BF16), wall[2 * i + n, 0:units])
        acc[...] = total
        return carry

    lax.fori_loop(0, 4, backward, 0)
    upstream = keep[1] + acc[...]
    unit = keep[0]
    part_ref[0:1] = column_sum(upstream * unit)
    part_ref[1:2] = column_sum(upstream)
    part_ref[4:8] = jnp.zeros((4, part_ref.shape[1]), F32)
    grad = norm_back(upstream, unit, inverse, scale_ref[0:1])
    one_ref[...] = grad
    low = grad.astype(BF16)
    lows_ref[2] = low
    for n in (3, 1, 2, 0):
        first, second = n + 4 * side, n + 4 * (1 - side)
        back = nt_dot(out_w[n], low).astype(BF16)
        attn_out[first] = back[0 : 2 * HD]
        attn_out[second, 0:HD] = back[2 * HD : 3 * HD]
        attn_out[second, HD : 2 * HD] = back[HD : 2 * HD]
        for slot in (n, 4 + n):
            if slot > 0:
                attn_copy(slot, m, INVERSE[slot]).start()
    attn_ref[:, tokens(m)] = attn_out[0]
    for n in range(1, count):
        attn_copy(n, devices[n], n).wait_recv()
    for n in range(2):
        out_along(n).wait_send()
        out_far(n).wait_send()
    for n in range(3):
        give(n).wait_send()
        rest(n).wait_send()
    for n in range(2):
        along(n).wait_send()
        far_copy(n).wait_send()
    for n in range(1, count):
        att_copy(n, INVERSE[n], INVERSE[n]).wait_send()
        attn_copy(n, m, INVERSE[n]).wait_send()


def middle(sent, x, cot, blocks, scale, count):
    rows, width = x.shape
    depth = sent.shape[0]
    units = (blocks[0].shape[0] - OWN) // 2
    vmem = pl.BlockSpec(memory_space=pltpu.VMEM)
    sems = lambda n: pltpu.SemaphoreType.DMA((n,))
    return pl.pallas_call(
        middle_kernel,
        in_specs=[vmem] * 3 + [pl.BlockSpec(memory_space=pl.ANY)] * 3 + [vmem],
        out_specs=[vmem] * 5,
        out_shape=(
            jax.ShapeDtypeStruct((rows, width), BF16),
            jax.ShapeDtypeStruct((3, rows, width), BF16),
            jax.ShapeDtypeStruct((rows, width), F32),
            jax.ShapeDtypeStruct(sent.shape, BF16),
            jax.ShapeDtypeStruct((8, width), F32),
        ),
        scratch_shapes=[
            pltpu.VMEM((count,) + blocks[0].shape, BF16),
            pltpu.VMEM((count // 2, 2 * OWN, width), BF16),
            pltpu.VMEM((count, depth, rows), BF16),
            pltpu.VMEM((count, depth, rows), BF16),
            pltpu.VMEM((count, rows, units), F32),
            pltpu.VMEM((2, rows, width), F32),
            pltpu.VMEM((rows, width), F32),
            sems(3), sems(7), sems(7), sems(3), sems(3), sems(2), sems(2), sems(2), sems(2),
            sems(count), sems(count), sems(count), sems(count),
        ],
        compiler_params=pltpu.CompilerParams(
            vmem_limit_bytes=VMEM_BYTES, collective_id=1, has_side_effects=True
        ),
        cost_estimate=pl.CostEstimate(
            flops=16 * rows * width * count * units, bytes_accessed=26_000_000,
            transcendentals=0,
        ),
        name="middle",
    )(sent, x, cot, *blocks, scale)


def close_kernel(
    own_x, left_x, right_x, far_low, far_high, solo_ref, shared_ref, conv_ref, sent_ref, all_ref,
    w_rows_ref, w_ref, one_ref, norm_ref, tap_ref,
    inputs_ref, up_ref, down_ref, out_ref, query_ref, key_ref, value_ref, tiny_ref,
    wall, acc, lows, attended, swap_out, swap_in, part_out, part_own, pair_in, stage, line_in,
    a_grads, a_in, a_sums, b_grads, b_in, b_sums, c_grads, c_in, c_sums, near_in, far_in,
    load, give_send, give_recv, swap_send, swap_recv, pair_send, pair_recv, line_send, line_recv,
    a_send, a_recv, aw_send, aw_recv, b_send, b_recv, bw_send, bw_recv,
    c_send, c_recv, cw_send, cw_recv,
    near_send, near_recv, far_send, far_recv,
):
    blocks = a_grads.shape[0]
    count, _, rows, width = wall.shape
    chips = count // 2
    units = down_ref.shape[0]
    d = lax.axis_index("dp")
    m = lax.axis_index("mp")
    side = m % 2
    chip = m // 2
    half = OWN - HD
    devices = around(m, count)
    sibling = devices[4]

    barrier = pltpu.get_barrier_semaphore()
    repeat(
        1, blocks,
        lambda r: pl.semaphore_signal(
            barrier, inc=1, device_id={"dp": (d + r) % blocks}, device_id_type=MESH
        ),
    )
    repeat(
        1, count,
        lambda r: pl.semaphore_signal(
            barrier, inc=1, device_id={"mp": (m + r) % count}, device_id_type=MESH
        ),
    )
    pl.semaphore_wait(barrier, blocks + count - 2)

    def tokens(index):
        return pl.ds(pl.multiple_of(index * rows, rows), rows)

    def across(src, dst, send, recv, r):
        return pltpu.make_async_remote_copy(
            src_ref=src, dst_ref=dst, send_sem=send.at[r], recv_sem=recv.at[r],
            device_id={"dp": (d + r) % blocks}, device_id_type=MESH,
        )

    cut = rows // 2
    sources = (own_x, left_x, right_x)

    def give(n, k):
        return remote(
            sources[n].at[k], wall.at[4 + n, k], give_send.at[n, k], give_recv.at[n, k], sibling
        )

    def give_far(part):
        source = (far_low, far_high)[part]
        place = wall.at[4 + 3, :, part * cut : (part + 1) * cut]
        return remote(source, place, give_send.at[3, part], give_recv.at[3, part], sibling)

    def loads():
        copies = [pltpu.make_async_copy(sources[n], wall.at[n], load.at[n]) for n in range(3)]
        copies.append(pltpu.make_async_copy(far_low, wall.at[3, :, 0:cut], load.at[3]))
        copies.append(pltpu.make_async_copy(far_high, wall.at[3, :, cut:rows], load.at[4]))
        return copies

    for n in range(3):
        start = pl.multiple_of(n * HD + (1 - side) * half, half)
        swap_out[n * half : (n + 1) * half] = shared_ref[pl.ds(start, half), :].astype(BF16)
    swap_out[3 * half : 4 * half] = sent_ref[
        pl.ds(pl.multiple_of(HD + (1 - side) * half, half), half), :
    ]
    swap = remote(swap_out, swap_in, swap_send.at[0], swap_recv.at[0], sibling)
    swap.start()
    for copy in loads():
        copy.start()
    for n in range(3):
        give(n, 2).start()
    for part in range(2):
        give_far(part).start()
    for k in range(2):
        for n in range(3):
            give(n, k).start()
    near_in[m, :, 0:width] = norm_ref[...]
    near_in[m, :, width : width + 2 * LANES] = tap_ref[...]

    def near_copy(r, owner):
        return remote(
            near_in.at[m], near_in.at[owner], near_send.at[r], near_recv.at[r], (m + r) % count
        )

    repeat(1, count, lambda r: near_copy(r, m).start())
    swap.wait_recv()
    solo_at = lambda n: pl.ds(pl.multiple_of(n * OWN + side * half, half), HD)
    half_at = lambda n: pl.ds(pl.multiple_of(n * OWN + (1 - side) * HD, half), half)
    for n in range(3):
        solo = solo_ref[n * HD : (n + 1) * HD, :]
        mine = shared_ref[pl.ds(pl.multiple_of(n * HD + side * half, half), half), :]
        mixed = mine + swap_in[n * half : (n + 1) * half].astype(F32)
        if n == 2:
            solo = solo + conv_ref[0:HD, :]
            mixed = mixed + conv_ref[HD:OWN, :]
        lows[solo_at(n), :] = solo.astype(BF16)
        lows[half_at(n), :] = mixed.astype(BF16)
    sent_half = sent_ref[pl.ds(pl.multiple_of(HD + side * half, half), half), :]
    attended[solo_at(0), :] = sent_ref[0:HD, :]
    attended[half_at(0), :] = (
        sent_half.astype(F32) + swap_in[3 * half : 4 * half].astype(F32)
    ).astype(BF16)

    def pair_copy(target):
        return remote(
            part_out.at[target], pair_in.at[target], pair_send.at[target], pair_recv.at[target],
            sibling,
        )

    def input_part(device):
        return tn_dot(lows[:, tokens(device)], w_rows_ref[...])

    order = [2, 1, 3, 0]
    for k in order:
        target = (chip + k) % chips
        part_out[target] = input_part(2 * target + 1 - side).astype(BF16)
        pair_copy(target).start()
    qkv_grad = nn_dot(lows[...], all_ref[...])
    for copy in loads():
        copy.wait()
    for n in range(3):
        give(n, 2).wait_recv()
    for part in range(2):
        give_far(part).wait_recv()
    out_grad = None
    for slot in range(count):
        piece = nn_dot(attended[:, tokens(devices[slot])], wall[slot, 2])
        out_grad = piece if out_grad is None else out_grad + piece
    depth = a_grads.shape[1]
    a_all = jnp.concatenate((out_grad, qkv_grad), axis=0).astype(BF16)
    for j in range(blocks):
        a_grads[j] = a_all[j * depth : (j + 1) * depth]

    def shares(grads, inbox, sums, send, recv, whole_send, whole_recv):
        def copy(r):
            return across(grads.at[(d + r) % blocks], inbox.at[r], send, recv, r)

        def whole(r, owner):
            return across(sums.at[d], sums.at[owner], whole_send, whole_recv, r)

        def reduce():
            size = grads.shape[1]
            repeat(1, blocks, lambda r: copy(r).wait_recv())
            for low in range(0, size, 16):
                part = slice(low, min(low + 16, size))
                value = grads[d, part].astype(F32)
                for r in range(1, blocks):
                    value = value + inbox[r, part].astype(F32)
                sums[d, part] = value.astype(BF16)
            repeat(1, blocks, lambda r: whole(r, d).start())

        def finish():
            repeat(1, blocks, lambda r: whole(r, (d + blocks - r) % blocks).wait_recv())

        def drain():
            repeat(1, blocks, lambda r: copy(r).wait_send())
            repeat(1, blocks, lambda r: whole(r, d).wait_send())

        def start():
            repeat(1, blocks, lambda r: copy(r).start())

        return start, reduce, finish, drain

    a_start, a_reduce, a_finish, a_drain = shares(
        a_grads, a_in, a_sums, a_send, a_recv, aw_send, aw_recv
    )
    b_start, b_reduce, b_finish, b_drain = shares(
        b_grads, b_in, b_sums, b_send, b_recv, bw_send, bw_recv
    )
    c_start, c_reduce, c_finish, c_drain = shares(
        c_grads, c_in, c_sums, c_send, c_recv, cw_send, cw_recv
    )

    def far_copy(r, owner):
        return across(far_in.at[d], far_in.at[owner], far_send, far_recv, r)

    a_start()

    def line_copy(k):
        return remote(
            stage.at[k], line_in.at[k], line_send.at[k], line_recv.at[k], (m + 2 * k) % count
        )

    for k in order[:3]:
        target = (chip + k) % chips
        mine = input_part(2 * target + side)
        pair_copy(target).wait_recv()
        stage[k] = (mine + pair_in[target].astype(F32)).astype(BF16)
        line_copy(k).start()
    part_own[...] = input_part(m)

    def step(i, first, size):
        sums = [None] * 2
        for n in range(2):
            slot = 2 * i + n
            hidden, ffn = wall[slot, 0], wall[slot, 1]
            active, lean = gelu_pair(nt_dot(hidden, w_ref[first : first + size]))
            grad = nt_dot(ffn, w_ref[units + first : units + first + size]) * lean
            parts = (tn_dot(grad.astype(BF16), hidden), tn_dot(active.astype(BF16), ffn))
            sums = [p if t is None else t + p for t, p in zip(sums, parts)]
        acc[0:size, :] += sums[0]
        acc[size : 2 * size, :] += sums[1]

    def put(grads):
        size = grads.shape[1]
        for j in range(blocks):
            grads[j] = acc[j * size : (j + 1) * size, :].astype(BF16)

    first_units = b_grads.shape[1] * blocks // 2
    last_units = units - first_units
    acc[...] = jnp.zeros_like(acc)
    repeat(0, 2, lambda i: step(i, 0, first_units))
    for k in range(2):
        for n in range(3):
            give(n, k).wait_recv()
    repeat(2, 4, lambda i: step(i, 0, first_units))
    put(b_grads)
    b_start()
    a_reduce()
    acc[...] = jnp.zeros_like(acc)
    repeat(0, 4, lambda i: step(i, first_units, last_units))
    put(c_grads)
    c_start()

    repeat(1, count, lambda r: near_copy(r, (m + count - r) % count).wait_recv())
    total = near_in[0]
    for r in range(1, count):
        total = total + near_in[r]
    far_in[d] = total
    repeat(1, blocks, lambda r: far_copy(r, d).start())
    b_reduce()
    pair_copy(chip).wait_recv()
    total = part_own[...] + pair_in[chip].astype(F32)
    for k in range(1, chips):
        line_copy(k).wait_recv()
        total = total + line_in[k].astype(F32)
    inputs_ref[...] = one_ref[...] + total
    c_reduce()

    a_finish()
    whole = jnp.concatenate([a_sums[j].astype(F32) for j in range(blocks)], axis=0).astype(BF16)
    for n, ref in enumerate((out_ref, query_ref, key_ref, value_ref)):
        ref[...] = whole[n * OWN : (n + 1) * OWN]
    repeat(1, blocks, lambda r: far_copy(r, (d + blocks - r) % blocks).wait_recv())
    total = far_in[0]
    for r in range(1, blocks):
        total = total + far_in[r]
    tiny_ref[...] = total
    split = blocks // 2

    def unpack(sums, first, size):
        turned = jnp.concatenate([sums[j].astype(F32) for j in range(split)], axis=0)
        up_ref[:, first : first + size] = jnp.transpose(turned).astype(BF16)
        high = sums.shape[1]
        for j in range(split):
            down_ref[first + j * high : first + (j + 1) * high] = sums[split + j]

    b_finish()
    unpack(b_sums, 0, first_units)
    c_finish()
    unpack(c_sums, first_units, last_units)

    swap.wait_send()
    for n in range(3):
        for k in range(3):
            give(n, k).wait_send()
    for part in range(2):
        give_far(part).wait_send()
    for k in range(chips):
        pair_copy((chip + k) % chips).wait_send()
    for k in range(1, chips):
        line_copy(k).wait_send()
    repeat(1, count, lambda r: near_copy(r, m).wait_send())
    repeat(1, blocks, lambda r: far_copy(r, d).wait_send())
    a_drain()
    b_drain()
    c_drain()


def close(blocks_x, solo, shared, conv, sent, gathered, w_rows, block_w, one, norms, taps, blocks):
    _, rows, width = blocks_x[0].shape
    length = sent.shape[1]
    count = length // rows
    chips = count // 2
    units = (block_w.shape[0] - OWN) // 2
    depth = 4 * OWN // blocks
    wide_units = units // 3 * 2
    high = 2 * wide_units // blocks
    rest = 2 * (units - wide_units) // blocks
    lanes = width + 2 * LANES
    vmem = pl.BlockSpec(memory_space=pltpu.VMEM)
    sems = lambda *n: pltpu.SemaphoreType.DMA(n)
    low = lambda *shape: jax.ShapeDtypeStruct(shape, BF16)
    return pl.pallas_call(
        close_kernel,
        in_specs=[pl.BlockSpec(memory_space=pl.ANY)] * 5 + [vmem] * 10,
        out_specs=[vmem] * 8,
        out_shape=(
            jax.ShapeDtypeStruct(one.shape, F32),
            low(width, units), low(units, width), low(OWN, width),
            low(OWN, width), low(OWN, width), low(OWN, width),
            jax.ShapeDtypeStruct((8, lanes), F32),
        ),
        scratch_shapes=[
            pltpu.VMEM((count, 3, rows, width), BF16),
            pltpu.VMEM((2 * wide_units, width), F32),
            pltpu.VMEM((3 * OWN, length), BF16),
            pltpu.VMEM((OWN, length), BF16),
            pltpu.VMEM((2 * HD, length), BF16),
            pltpu.VMEM((2 * HD, length), BF16),
            pltpu.VMEM((chips, rows, width), BF16),
            pltpu.VMEM((rows, width), F32),
            pltpu.VMEM((chips, rows, width), BF16),
            pltpu.VMEM((chips, rows, width), BF16),
            pltpu.VMEM((chips, rows, width), BF16),
            pltpu.VMEM((blocks, depth, width), BF16),
            pltpu.VMEM((blocks, depth, width), BF16),
            pltpu.VMEM((blocks, depth, width), BF16),
            pltpu.VMEM((blocks, high, width), BF16),
            pltpu.VMEM((blocks, high, width), BF16),
            pltpu.VMEM((blocks, high, width), BF16),
            pltpu.VMEM((blocks, rest, width), BF16),
            pltpu.VMEM((blocks, rest, width), BF16),
            pltpu.VMEM((blocks, rest, width), BF16),
            pltpu.VMEM((count, 8, lanes), F32),
            pltpu.VMEM((blocks, 8, lanes), F32),
            sems(5), sems(4, 3), sems(4, 3), sems(1), sems(1), sems(4), sems(4), sems(4), sems(4),
            sems(blocks), sems(blocks), sems(blocks), sems(blocks),
            sems(blocks), sems(blocks), sems(blocks), sems(blocks),
            sems(blocks), sems(blocks), sems(blocks), sems(blocks),
            sems(count), sems(count), sems(blocks), sems(blocks),
        ],
        compiler_params=pltpu.CompilerParams(
            vmem_limit_bytes=VMEM_BYTES, collective_id=0, has_side_effects=True
        ),
        cost_estimate=pl.CostEstimate(flops=0, bytes_accessed=30_000_000, transcendentals=0),
        name="close",
    )(*blocks_x, solo, shared, conv, sent, gathered, w_rows, block_w, one, norms, taps)


def shifted(block, off):
    count = lax.axis_size("mp")
    return lax.ppermute(block, "mp", [(n, (n - off) % count) for n in range(count)])


def far_halves(from_left, from_right, axis):
    cut = from_left.shape[axis] // 2
    low = lax.slice_in_dim(from_left, 0, cut, axis=axis)
    high = lax.slice_in_dim(from_right, cut, 2 * cut, axis=axis)
    return shifted(low, -2), shifted(high, 2)


def on_device(
    inputs, segment, w_query, w_key, w_value, planes, conv_taps, w_out,
    ln1_gain, ln1_bias, w_up, w_down, ln2_gain, ln2_bias, cotangent,
):
    count = lax.axis_size("mp")
    blocks = lax.axis_size("dp")
    rows, width = inputs.shape
    block_w = jnp.concatenate((w_up.T, w_down, w_out), 0)
    w_rows = jnp.concatenate((w_query, w_key, w_value), 1).T
    gathered, qkv = gather_qkv(inputs, w_rows, count)
    block_w, qkv = lax.optimization_barrier((block_w, qkv))
    left_w, right_w = shifted(block_w, -2), shifted(block_w, 2)
    gathered = gathered.reshape(rows * count, width)
    seg_row = segment[None, :]
    taps = jnp.pad(
        jnp.concatenate(
            (
                jnp.pad(conv_taps, ((0, 0), (0, 16 - HEADS))),
                jnp.pad(conv_taps[::-1], ((0, 0), (0, 16 - HEADS))),
            ),
            1,
        ),
        ((0, 2 * LANES - KW), (0, 0)),
    ).T
    conv = segment_conv(qkv, taps, seg_row)
    sent, numer, dens, sign, bucket = attend(qkv, planes, seg_row, conv)
    scale = jnp.stack((ln1_gain, ln1_bias, ln2_gain, ln2_bias) * 2)
    outputs, lows, one_grad, attn_grad, norm_part = middle(
        sent, inputs, cotangent, (block_w, left_w, right_w), scale, count
    )
    left_x, right_x = shifted(lows, -2), shifted(lows, 2)
    saved = (numer, dens, sign, bucket)
    value_conv, tap_part = conv_back(qkv, attn_grad, taps, seg_row)
    solo = attend_back(0, qkv, planes, seg_row, attn_grad, *saved)
    solo, value_conv, left_x, right_x, attn_grad = lax.optimization_barrier(
        (solo, value_conv, left_x, right_x, attn_grad)
    )
    far_x = far_halves(left_x, right_x, 1)
    shared = attend_back(1, qkv, planes, seg_row, attn_grad, *saved)
    inputs_grad, up, down, out, query, key, value, tiny = close(
        (lows, left_x, right_x) + far_x, solo, shared, value_conv, sent, gathered, w_rows, block_w,
        one_grad, norm_part, tap_part, blocks,
    )
    conv_rows = jnp.concatenate(
        (tiny[:, width : width + LANES], tiny[: HEADS - 8, width + LANES :]), 0
    )
    return (
        outputs, inputs_grad, query.astype(F32).T, key.astype(F32).T, value.astype(F32).T,
        conv_rows[:, :KW].T, out.astype(F32), tiny[0, :width], tiny[1, :width],
        up.astype(F32), down.astype(F32), tiny[2, :width], tiny[3, :width],
    )


def solution(mesh):
    rows = P(("dp", "mp"), None)
    cols = P(None, "mp")
    return jax.shard_map(
        on_device,
        mesh=mesh,
        in_specs=(
            rows, P("dp"), cols, cols, cols, P(), P(), P("mp", None), P(), P(),
            cols, P("mp", None), P(), P(), rows,
        ),
        out_specs=(
            rows, rows, cols, cols, cols, P(), P("mp", None), P(), P(),
            cols, P("mp", None), P(), P(),
        ),
        check_vma=False,
    )
```

```python
import math
import jax
import jax.numpy as jnp
from jax import lax
from jax.experimental import pallas as pl
from jax.experimental.pallas import tpu as pltpu
from jax.sharding import PartitionSpec as P

HEADS = 12
HD = 64
TABLES = 4
BITS = 8
KW = 65
MAXSEG = 8
CODES = 256
UNITS = 6
SOLO = 4
SPREAD = MAXSEG * HD
EXT = SPREAD + 128
LANES = 128
TILE = 2048
F32 = jnp.float32
BF16 = jnp.bfloat16
VMEM_BYTES = 56 * 1024 * 1024
CLOSE_BYTES = 60 * 1024 * 1024


def nt_dot(left, right):
    return lax.dot_general(left, right, (((1,), (1,)), ((), ())), preferred_element_type=F32)


def tn_dot(left, right):
    return lax.dot_general(left, right, (((0,), (0,)), ((), ())), preferred_element_type=F32)


def nn_dot(left, right):
    return lax.dot_general(left, right, (((1,), (0,)), ((), ())), preferred_element_type=F32)


def half_sign(bit):
    rows = lax.broadcasted_iota(jnp.int32, (8, LANES), 0)
    return jnp.where((rows >> bit) & 1 == 0, 0.5, -0.5).astype(F32)


def code_factors(signs):
    pos0, neg0 = 0.5 + 0.5 * signs[0:1], 0.5 - 0.5 * signs[0:1]
    pos1, neg1 = 0.5 + 0.5 * signs[1:2], 0.5 - 0.5 * signs[1:2]
    tops = (pos0 * pos1, pos0 * neg1, neg0 * pos1, neg0 * neg1)
    picks = [half_sign(2), half_sign(1), half_sign(0)]
    mids = [0.5 + picks[n] * signs[2 + n : 3 + n] for n in range(3)]
    lows = [0.5 + picks[n] * signs[5 + n : 6 + n] for n in range(3)]
    return tops, mids, lows, picks


def code_probs(signs, out_ref, lane):
    tops, mids, lows, _ = code_factors(signs)
    mid = mids[0] * mids[1] * mids[2]
    low = lows[0] * lows[1] * lows[2]
    for top_index in range(4):
        low_top = low * tops[top_index]
        for pair in range(4):
            rows = jnp.concatenate(
                (
                    low_top * mid[2 * pair : 2 * pair + 1],
                    low_top * mid[2 * pair + 1 : 2 * pair + 2],
                ),
                axis=0,
            )
            first = top_index * 64 + pair * 16
            out_ref[first : first + 16, lane] = rows.astype(BF16)


def signs_back(signs, grads):
    tops, mids, lows, picks = code_factors(signs)
    mid = mids[0] * mids[1] * mids[2]
    low = lows[0] * lows[1] * lows[2]
    mid_rows = [jnp.broadcast_to(mid[m : m + 1], (8, LANES)) for m in range(8)]
    top_rows = [jnp.broadcast_to(tops[t], (8, LANES)) for t in range(4)]
    by_top = [None] * 4
    by_mid = [None] * 8
    for t in range(4):
        for m in range(8):
            piece = grads[t * 64 + m * 8 : t * 64 + m * 8 + 8]
            a = piece * mid_rows[m]
            b = piece * top_rows[t]
            by_top[t] = a if by_top[t] is None else by_top[t] + a
            by_mid[m] = b if by_mid[m] is None else by_mid[m] + b
    low_grad = by_top[0] * top_rows[0]
    for t in range(1, 4):
        low_grad = low_grad + by_top[t] * top_rows[t]
    top_grad = [jnp.sum(low * by_top[t], axis=0, keepdims=True) for t in range(4)]
    mid_grad = jnp.concatenate(
        [jnp.sum(low * by_mid[m], axis=0, keepdims=True) for m in range(8)], axis=0
    )
    pos0, neg0 = 0.5 + 0.5 * signs[0:1], 0.5 - 0.5 * signs[0:1]
    pos1, neg1 = 0.5 + 0.5 * signs[1:2], 0.5 - 0.5 * signs[1:2]
    out = [
        0.5 * ((top_grad[0] - top_grad[2]) * pos1 + (top_grad[1] - top_grad[3]) * neg1),
        0.5 * ((top_grad[0] - top_grad[1]) * pos0 + (top_grad[2] - top_grad[3]) * neg0),
    ]
    for grad, parts in ((mid_grad, mids), (low_grad, lows)):
        for n in range(3):
            others = parts[(n + 1) % 3] * parts[(n + 2) % 3] * picks[n]
            out.append(jnp.sum(grad * others, axis=0, keepdims=True))
    return jnp.concatenate(out, axis=0)


def split_two(value):
    high = value.astype(BF16).astype(F32)
    return high, value - high


def unit_planes(planes):
    return planes * lax.rsqrt(jnp.sum(planes * planes, axis=1, keepdims=True) + 1e-06)


def fill_spread(values, seg_row, spread_ref, lane):
    for s in range(MAXSEG):
        spread_ref[s * HD : (s + 1) * HD, lane] = jnp.where(
            seg_row == s, values, jnp.zeros_like(values)
        )


def fill_member(seg_row, spread_ref, lane):
    width = seg_row.shape[1]
    rows = lax.broadcasted_iota(jnp.int32, (128, width), 0)
    hit = jnp.logical_and(rows < 16, (rows & 7) == seg_row)
    spread_ref[SPREAD:EXT, lane] = jnp.where(hit, 1.0, 0.0).astype(BF16)


def plane_rows(unit):
    side = lax.axis_index("mp") % 2
    row = jnp.where(unit < SOLO, unit, 2 * side + unit - SOLO)
    return pl.ds(pl.multiple_of(row * BITS, BITS), BITS)


def lanes_of(index, width):
    return pl.ds(pl.multiple_of(index * width, width), width)


def masked_fold(product, seg_row):
    total = None
    for s in range(MAXSEG):
        piece = jnp.where(seg_row == s, product[s * HD : (s + 1) * HD], 0.0)
        total = piece if total is None else total + piece
    return total


def attend_kernel(
    qkv_ref, planes_ref, seg_ref, conv_ref,
    sent_ref, numer_ref, dens_ref, sign_ref, bucket_ref,
    spread, norm, qprob, kprob, total, table, est,
):
    unit = pl.program_id(0)
    slot = unit // SOLO
    length = qkv_ref.shape[1]
    tiles = length // TILE
    q_rows = pl.ds(pl.multiple_of(slot * HD, HD), HD)
    k_rows = pl.ds(pl.multiple_of(2 * HD + slot * HD, HD), HD)
    v_rows = pl.ds(pl.multiple_of(4 * HD + slot * HD, HD), HD)

    @pl.when(jnp.logical_or(unit == 0, unit == SOLO))
    def _():
        def step(i, carry):
            lane = lanes_of(i, TILE)
            seg_row = seg_ref[:, lane]
            fill_spread(qkv_ref[v_rows, lane], seg_row, spread, lane)
            fill_member(seg_row, spread, lane)
            query = qkv_ref[q_rows, lane].astype(F32)
            key = qkv_ref[k_rows, lane].astype(F32)
            scale = math.sqrt(HD)
            norm[0:1, lane] = scale * lax.rsqrt(
                jnp.sum(query * query, axis=0, keepdims=True) + 1e-06
            )
            norm[1:2, lane] = scale * lax.rsqrt(jnp.sum(key * key, axis=0, keepdims=True) + 1e-06)
            est[:, lane] = jnp.zeros((HD, TILE), F32)
            return carry

        lax.fori_loop(0, tiles, step, 0)

    planes = unit_planes(planes_ref[plane_rows(unit), :])
    high, rest = split_two(planes)
    middle, low = split_two(rest)
    stack = jnp.concatenate((high, middle, low), axis=0).astype(BF16)
    total[...] = jnp.zeros_like(total)

    def collect(i, carry):
        lane = lanes_of(i, TILE)
        flat_q = nn_dot(stack, qkv_ref[q_rows, lane])
        flat_k = nn_dot(stack, qkv_ref[k_rows, lane])
        sign_q = jnp.tanh((flat_q[0:8] + flat_q[8:16] + flat_q[16:24]) * norm[0:1, lane])
        sign_k = jnp.tanh((flat_k[0:8] + flat_k[8:16] + flat_k[16:24]) * norm[1:2, lane])
        sign_ref[0, 0:8, lane] = sign_q
        sign_ref[0, 8:16, lane] = sign_k
        for part in range(TILE // LANES):
            inner = slice(part * LANES, (part + 1) * LANES)
            code_probs(sign_k[:, inner], kprob, inner)
            code_probs(
                sign_q[:, inner], qprob, pl.ds(pl.multiple_of(i * TILE + part * LANES, LANES), LANES)
            )
        total[...] += nt_dot(spread[0 : SPREAD + 16, lane], kprob[...])
        return carry

    lax.fori_loop(0, tiles, collect, 0)
    mass = total[SPREAD : SPREAD + 8, :]
    mass_high, mass_low = split_two(mass)
    extra = jnp.concatenate(
        (mass_high, mass_high, mass_low, jnp.zeros((104, CODES), F32)), axis=0
    )
    table[0:SPREAD, :] = total[0:SPREAD, :].astype(BF16)
    table[SPREAD:EXT, :] = extra.astype(BF16)
    bucket_ref[0, :, 0:SPREAD] = jnp.transpose(total[0:SPREAD, :]).astype(BF16)
    bucket_ref[0, :, SPREAD:EXT] = jnp.transpose(extra).astype(BF16)

    def spend(i, carry):
        lane = lanes_of(i, TILE)
        seg_row = seg_ref[:, lane]
        product = nn_dot(table[0 : SPREAD + 32, :], qprob[:, lane])
        numer = masked_fold(product, seg_row)
        both = product[SPREAD : SPREAD + 8] + product[SPREAD + 16 : SPREAD + 24]
        which = lax.broadcasted_iota(jnp.int32, (8, TILE), 0)
        density = jnp.sum(jnp.where(which == seg_row, both, 0.0), axis=0, keepdims=True)
        numer_ref[0, :, lane] = numer
        dens_ref[0, :, lane] = density
        est[:, lane] += numer * (1.0 / jnp.maximum(density, 1.0))
        return carry

    lax.fori_loop(0, tiles, spend, 0)

    @pl.when(jnp.logical_or(unit == SOLO - 1, unit == UNITS - 1))
    def _():
        sent_ref[q_rows, :] = (est[...] * (1.0 / TABLES) + conv_ref[q_rows, :]).astype(BF16)


def attend(qkv, planes, seg_row, conv):
    length = qkv.shape[1]
    per_unit = lambda u: (u, 0, 0)
    fixed = lambda u: (0, 0)
    return pl.pallas_call(
        attend_kernel,
        grid=(UNITS,),
        in_specs=[
            pl.BlockSpec(qkv.shape, fixed),
            pl.BlockSpec(planes.shape, fixed),
            pl.BlockSpec(seg_row.shape, fixed),
            pl.BlockSpec(conv.shape, fixed),
        ],
        out_specs=[
            pl.BlockSpec((2 * HD, length), fixed),
            pl.BlockSpec((1, HD, length), per_unit),
            pl.BlockSpec((1, 1, length), per_unit),
            pl.BlockSpec((1, 16, length), per_unit),
            pl.BlockSpec((1, CODES, EXT), per_unit),
        ],
        out_shape=[
            jax.ShapeDtypeStruct((2 * HD, length), BF16),
            jax.ShapeDtypeStruct((UNITS, HD, length), F32),
            jax.ShapeDtypeStruct((UNITS, 1, length), F32),
            jax.ShapeDtypeStruct((UNITS, 16, length), F32),
            jax.ShapeDtypeStruct((UNITS, CODES, EXT), BF16),
        ],
        scratch_shapes=[
            pltpu.VMEM((EXT, length), BF16),
            pltpu.VMEM((8, length), F32),
            pltpu.VMEM((CODES, length), BF16),
            pltpu.VMEM((CODES, TILE), BF16),
            pltpu.VMEM((SPREAD + 16, CODES), F32),
            pltpu.VMEM((EXT, CODES), BF16),
            pltpu.VMEM((HD, length), F32),
        ],
        compiler_params=pltpu.CompilerParams(vmem_limit_bytes=VMEM_BYTES),
        cost_estimate=pl.CostEstimate(flops=0, bytes_accessed=1_000_000, transcendentals=0),
        name="attend",
    )(qkv, planes, seg_row, conv)


def back_setup(slot, qkv_ref, seg_ref, out_ref, spread, gspread, proj):
    tiles = qkv_ref.shape[1] // TILE
    v_rows = slice(4 * HD + slot * HD, 5 * HD + slot * HD)
    v_out = slice(2 * HD, 3 * HD)

    def step(i, carry):
        lane = lanes_of(i, TILE)
        seg_row = seg_ref[:, lane]
        fill_spread(qkv_ref[v_rows, lane], seg_row, spread, lane)
        fill_member(seg_row, spread, lane)
        proj[:, lane] = jnp.zeros((2 * HD, TILE), F32)
        out_ref[v_out, lane] = jnp.zeros((HD, TILE), F32)
        return carry

    lax.fori_loop(0, tiles, step, 0)
    gspread[SPREAD:EXT, :] = jnp.zeros((128, TILE), BF16)


def back_unit(
    slot, unit, qkv_ref, planes_ref, seg_ref, grad_ref, numer_ref, dens_ref, sign_ref, bucket_ref,
    out_ref, spread, qprob, kprob, gspread, total, table, turned, gsign, proj,
):
    tiles = qkv_ref.shape[1] // TILE
    q_rows = slice(slot * HD, slot * HD + HD)
    k_rows = slice(2 * HD + slot * HD, 3 * HD + slot * HD)
    v_rows = slice(4 * HD + slot * HD, 5 * HD + slot * HD)
    v_out = slice(2 * HD, 3 * HD)
    total[...] = jnp.zeros_like(total)

    def first(i, carry):
        lane = lanes_of(i, TILE)
        seg_row = seg_ref[:, lane]
        density = dens_ref[:, lane]
        inverse = 1.0 / jnp.maximum(density, 1.0)
        est_grad = grad_ref[q_rows, lane].astype(F32) * (1.0 / TABLES)
        num_grad = (est_grad * inverse).astype(BF16)
        fill_spread(num_grad, seg_row, gspread, slice(0, TILE))
        inner_sum = jnp.sum(est_grad * numer_ref[:, lane], axis=0, keepdims=True)
        dens_grad = jnp.where(density > 1.0, -inner_sum * inverse * inverse, 0.0)
        which = lax.broadcasted_iota(jnp.int32, (8, TILE), 0)
        high, low = split_two(jnp.where(which == seg_row, dens_grad, 0.0))
        gspread[SPREAD : SPREAD + 32, :] = jnp.concatenate(
            (high, low, high, jnp.zeros_like(high)), axis=0
        ).astype(BF16)
        collected = nn_dot(bucket_ref[...], gspread[...])
        for part in range(TILE // LANES):
            inner = slice(part * LANES, (part + 1) * LANES)
            outer = pl.ds(pl.multiple_of(i * TILE + part * LANES, LANES), LANES)
            sign_q = sign_ref[0:8, outer]
            code_probs(sign_q, qprob, inner)
            gsign[0:8, outer] = signs_back(sign_q, collected[:, inner])
        total[...] += nt_dot(gspread[0 : SPREAD + 16, :], qprob[...])
        return carry

    lax.fori_loop(0, tiles, first, 0)
    mass_grad = total[SPREAD : SPREAD + 8, :] + total[SPREAD + 8 : SPREAD + 16, :]
    high, low = split_two(mass_grad)
    extra = jnp.concatenate((high, low, jnp.zeros((112, CODES), F32)), axis=0)
    table[...] = total[0:SPREAD, :].astype(BF16)
    turned[:, 0:SPREAD] = jnp.transpose(total[0:SPREAD, :]).astype(BF16)
    turned[:, SPREAD:EXT] = jnp.transpose(extra).astype(BF16)

    planes = unit_planes(planes_ref[plane_rows(unit), :])
    plane_high, plane_low = split_two(planes)
    stack = jnp.concatenate((plane_high, plane_low, plane_high, jnp.zeros_like(plane_high)), axis=0)
    stack = stack.astype(BF16)

    def second(i, carry):
        lane = lanes_of(i, TILE)
        seg_row = seg_ref[:, lane]
        for part in range(TILE // LANES):
            inner = slice(part * LANES, (part + 1) * LANES)
            outer = pl.ds(pl.multiple_of(i * TILE + part * LANES, LANES), LANES)
            code_probs(sign_ref[8:16, outer], kprob, inner)
        out_ref[v_out, lane] += masked_fold(nn_dot(table[...], kprob[...]), seg_row)
        collected = nn_dot(turned[...], spread[:, lane])
        for part in range(TILE // LANES):
            inner = slice(part * LANES, (part + 1) * LANES)
            outer = pl.ds(pl.multiple_of(i * TILE + part * LANES, LANES), LANES)
            gsign[8:16, outer] = signs_back(sign_ref[8:16, outer], collected[:, inner])
        signs = sign_ref[:, lane]
        flat = gsign[:, lane] * (1.0 - signs * signs)
        high, low = split_two(flat)
        for side in range(2):
            rows = slice(8 * side, 8 * side + 8)
            pieces = jnp.concatenate(
                (high[rows], high[rows], low[rows], jnp.zeros((8, TILE), F32)), axis=0
            ).astype(BF16)
            proj[side * HD : (side + 1) * HD, lane] += tn_dot(stack, pieces)
        return carry

    lax.fori_loop(0, tiles, second, 0)


def back_finish(slot, qkv_ref, out_ref, proj):
    tiles = qkv_ref.shape[1] // TILE
    q_rows = slice(slot * HD, slot * HD + HD)
    k_rows = slice(2 * HD + slot * HD, 3 * HD + slot * HD)

    def step(i, carry):
        lane = lanes_of(i, TILE)
        for side, rows in ((0, q_rows), (1, k_rows)):
            vec = qkv_ref[rows, lane].astype(F32)
            inverse = lax.rsqrt(jnp.sum(vec * vec, axis=0, keepdims=True) + 1e-06)
            unit_vec = vec * inverse
            grad = proj[side * HD : (side + 1) * HD, lane]
            along = jnp.sum(unit_vec * grad, axis=0, keepdims=True)
            out_ref[side * HD : (side + 1) * HD, lane] = math.sqrt(HD) * inverse * (grad - unit_vec * along)
        return carry

    lax.fori_loop(0, tiles, step, 0)


SPAN = 192
SHIFT = (KW - 1) // 2
OWN = 96
BLOCKS = ((0, HD), (HD, OWN))


def own_heads():
    m = lax.axis_index("mp")
    group = m // 2
    return (3 * group + 2 * (m % 2), 3 * group + 1)


def own_half():
    side = lax.axis_index("mp") % 2
    half = OWN - HD
    return side, half


def band_of(row):
    turned = jnp.broadcast_to(row, (LANES, 2 * LANES))
    index = lax.broadcasted_iota(jnp.int32, turned.shape, 0)
    for bit in range(7):
        moved = pltpu.roll(turned, 1 << bit, 1)
        turned = jnp.where((index >> bit) & 1 == 1, moved, turned)
    return jnp.transpose(turned)[0:SPAN]


def fill_hot(seg_ref, hot, hot_pad):
    length = seg_ref.shape[1]
    rows = lax.broadcasted_iota(jnp.int32, (16, length), 0)
    value = jnp.where(rows == seg_ref[...], 1.0, 0.0)
    value = jnp.where(rows < MAXSEG, value, 0.0).astype(BF16)
    hot[...] = value
    hot_pad[...] = jnp.zeros_like(hot_pad)
    hot_pad[:, SHIFT : SHIFT + length] = value


def band_product(rows, band):
    high, low = split_two(band)
    return nn_dot(rows, high.astype(BF16)) + nn_dot(rows, low.astype(BF16))


def conv_kernel(qkv_ref, taps_ref, seg_ref, out_ref, hot, hot_pad, pad, band):
    length = out_ref.shape[1]
    side, half = own_half()
    own = pl.ds(pl.multiple_of(HD + side * half, half), half)
    other = pl.ds(pl.multiple_of(HD + (1 - side) * half, half), half)
    fill_hot(seg_ref, hot, hot_pad)
    pad[...] = jnp.zeros_like(pad)
    pad[0:HD, SHIFT : SHIFT + length] = qkv_ref[4 * HD : 5 * HD, :]
    value_half = pl.ds(pl.multiple_of(5 * HD + side * half, half), half)
    pad[HD:OWN, SHIFT : SHIFT + length] = qkv_ref[value_half, :]
    for h, head in enumerate(own_heads()):
        band[h] = band_of(taps_ref[pl.ds(head, 1), :])
    out_ref[other, :] = jnp.zeros((half, length), F32)
    for i in range(length // LANES):
        lane = slice(i * LANES, (i + 1) * LANES)
        wide = slice(i * LANES, i * LANES + SPAN)
        mask = tn_dot(hot_pad[:, wide], hot[:, lane])
        out_ref[0:HD, lane] = band_product(pad[0:HD, wide], band[0] * mask)
        out_ref[own, lane] = band_product(pad[HD:OWN, wide], band[1] * mask)


def segment_conv(qkv, taps, seg_row):
    length = seg_row.shape[1]
    return pl.pallas_call(
        conv_kernel,
        out_shape=jax.ShapeDtypeStruct((2 * HD, length), F32),
        scratch_shapes=[
            pltpu.VMEM((16, length), BF16),
            pltpu.VMEM((16, length + LANES), BF16),
            pltpu.VMEM((OWN, length + LANES), BF16),
            pltpu.VMEM((2, SPAN, LANES), F32),
        ],
        compiler_params=pltpu.CompilerParams(vmem_limit_bytes=VMEM_BYTES),
        cost_estimate=pl.CostEstimate(flops=0, bytes_accessed=1_000_000, transcendentals=0),
        name="segment_conv",
    )(qkv, taps, seg_row)


def conv_back_kernel(
    qkv_ref, grad_ref, taps_ref, seg_ref, out_ref, tap_ref, hot, hot_pad, pad, gpad, band, corr
):
    length = seg_ref.shape[1]
    side, half = own_half()
    fill_hot(seg_ref, hot, hot_pad)
    pad[...] = jnp.zeros_like(pad)
    gpad[...] = jnp.zeros_like(gpad)
    inside = slice(SHIFT, SHIFT + length)
    value_half = pl.ds(pl.multiple_of(5 * HD + side * half, half), half)
    grad_half = pl.ds(pl.multiple_of(HD + side * half, half), half)
    pad[0:HD, inside] = qkv_ref[4 * HD : 5 * HD, :]
    pad[HD:OWN, inside] = qkv_ref[value_half, :]
    gpad[0:HD, inside] = grad_ref[0:HD, :]
    gpad[HD:OWN, inside] = grad_ref[grad_half, :]
    heads = own_heads()
    for h, head in enumerate(heads):
        band[h] = band_of(taps_ref[pl.ds(16 + head, 1), :])
    corr[...] = jnp.zeros_like(corr)
    for i in range(length // LANES):
        lane = slice(i * LANES, (i + 1) * LANES)
        wide = slice(i * LANES, i * LANES + SPAN)
        twice = slice(i * LANES, (i + 2) * LANES)
        mask = tn_dot(hot_pad[:, wide], hot[:, lane])
        turned = tn_dot(hot[:, lane], hot_pad[:, twice])
        grads = (grad_ref[0:HD, lane], grad_ref[grad_half, lane])
        for h, (low_row, high_row) in enumerate(BLOCKS):
            out_ref[low_row:high_row, lane] = band_product(
                gpad[low_row:high_row, wide], band[h] * mask
            )
            corr[h] += turned * tn_dot(grads[h], pad[low_row:high_row, twice])
    row = lax.broadcasted_iota(jnp.int32, (LANES, 2 * LANES), 0)
    place = lax.broadcasted_iota(jnp.int32, (8, LANES), 0)
    low_heads = jnp.zeros((8, LANES), F32)
    high_heads = jnp.zeros((8, LANES), F32)
    for h, head in enumerate(heads):
        skew = corr[h]
        for bit in range(7):
            moved = pltpu.roll(skew, 2 * LANES - (1 << bit), 1)
            skew = jnp.where((row >> bit) & 1 == 1, moved, skew)
        taps = jnp.sum(skew, axis=0, keepdims=True)[:, 0:LANES]
        low_heads = low_heads + jnp.where(place == head, taps, 0.0)
        high_heads = high_heads + jnp.where(place + 8 == head, taps, 0.0)
    tap_ref[:, 0:LANES] = low_heads
    tap_ref[:, LANES : 2 * LANES] = high_heads


def conv_back(qkv, grad, taps, seg_row):
    length = seg_row.shape[1]
    return pl.pallas_call(
        conv_back_kernel,
        out_shape=(
            jax.ShapeDtypeStruct((OWN, length), F32),
            jax.ShapeDtypeStruct((8, 2 * LANES), F32),
        ),
        scratch_shapes=[
            pltpu.VMEM((16, length), BF16),
            pltpu.VMEM((16, length + LANES), BF16),
            pltpu.VMEM((OWN, length + LANES), BF16),
            pltpu.VMEM((OWN, length + LANES), BF16),
            pltpu.VMEM((2, SPAN, LANES), F32),
            pltpu.VMEM((2, LANES, 2 * LANES), F32),
        ],
        compiler_params=pltpu.CompilerParams(vmem_limit_bytes=VMEM_BYTES),
        cost_estimate=pl.CostEstimate(flops=0, bytes_accessed=1_000_000, transcendentals=0),
        name="conv_back",
    )(qkv, grad, taps, seg_row)


def norm_rows(values):
    center = values - jnp.mean(values, axis=1, keepdims=True)
    inverse = lax.rsqrt(jnp.mean(center * center, axis=1, keepdims=True) + 1e-05)
    return center * inverse, inverse


def norm_back(upstream, normed, inverse, gain):
    scaled = upstream * gain
    inner = (
        scaled
        - jnp.mean(scaled, axis=1, keepdims=True)
        - normed * jnp.mean(scaled * normed, axis=1, keepdims=True)
    )
    return inner * inverse


def gelu_pair(value):
    cdf = 0.5 + 0.5 * lax.erf(value * math.sqrt(0.5))
    pdf = jnp.exp(-0.5 * value * value) * (1.0 / math.sqrt(2.0 * math.pi))
    return value * cdf, cdf + value * pdf


def column_sum(values):
    return jnp.sum(values, axis=0, keepdims=True)


MESH = pl.DeviceIdType.MESH
OFFSETS = (0, -2, 2, 4)
INVERSE = (0, 2, 1, 3, 4, 6, 5, 7)


def repeat(start, stop, action):
    def body(r, carry):
        action(r)
        return carry

    lax.fori_loop(start, stop, body, 0)


def remote(src, dst, send, recv, target):
    return pltpu.make_async_remote_copy(
        src_ref=src, dst_ref=dst, send_sem=send, recv_sem=recv,
        device_id={"mp": target}, device_id_type=MESH,
    )


def greet(targets):
    barrier = pltpu.get_barrier_semaphore()
    for target in targets:
        pl.semaphore_signal(barrier, inc=1, device_id={"mp": target}, device_id_type=MESH)
    pl.semaphore_wait(barrier, len(targets))


def gather_kernel(x_ref, w_ref, all_ref, qkv_ref, wide, send, recv):
    count, rows, _ = all_ref.shape
    m = lax.axis_index("mp")
    side = m % 2
    sibling = m + 1 - 2 * side
    left = (m + count - 2) % count
    right = (m + 2) % count
    far = (m + 4) % count
    half = OWN - HD
    cut = rows // 2
    greet((left, right, sibling))

    def copy(n, src, dst, target):
        return remote(src, dst, send.at[n], recv.at[n], target)

    def piece(n, which):
        return pl.ds(pl.multiple_of(n * 2 * HD + HD + which * half, half), half)

    def weight_copy(n, which):
        source = w_ref.at[pl.ds(pl.multiple_of(n * OWN + (1 - side) * HD, half), half), :]
        return copy(11 + n, source, wide.at[piece(n, which), :], sibling)

    low, high = slice(0, cut), slice(cut, rows)

    def own_copy(n, owner):
        part, target = ((low, right), (high, right), (high, left), (low, left))[n]
        return copy(n, x_ref.at[part], all_ref.at[owner, part], target)

    for n in range(3):
        weight_copy(n, side).start()
    for n in (0, 2, 1, 3):
        own_copy(n, m).start()
    to_sibling = copy(4, x_ref, all_ref.at[m], sibling)
    to_sibling.start()
    all_ref[m] = x_ref[...]
    for n in range(3):
        solo = pl.ds(pl.multiple_of(n * OWN + side * half, half), HD)
        own = pl.ds(pl.multiple_of(n * OWN + (1 - side) * HD, half), half)
        wide[n * 2 * HD : n * 2 * HD + HD, :] = w_ref[solo, :]
        wide[piece(n, side), :] = w_ref[own, :]
    for n in range(3):
        weight_copy(n, 1 - side).wait_recv()

    def project(block):
        lane = pl.ds(pl.multiple_of(block * rows, rows), rows)
        qkv_ref[:, lane] = nt_dot(wide[...], all_ref[block]).astype(BF16)

    def pass_on(n, owner, part, target):
        return copy(n, all_ref.at[owner, part], all_ref.at[owner, part], target)

    project(m)
    own_copy(0, left).wait_recv()
    on_right = pass_on(5, left, low, right)
    on_right.start()
    own_copy(2, right).wait_recv()
    on_left = pass_on(6, right, high, left)
    on_left.start()
    copy(4, x_ref, all_ref.at[sibling], sibling).wait_recv()
    project(sibling)
    own_copy(1, left).wait_recv()
    over_left = copy(7, all_ref.at[left], all_ref.at[left], sibling)
    over_left.start()
    own_copy(3, right).wait_recv()
    over_right = copy(8, all_ref.at[right], all_ref.at[right], sibling)
    over_right.start()
    project(left)
    project(right)
    other_left = (sibling + count - 2) % count
    other_right = (sibling + 2) % count
    other_far = (sibling + 4) % count
    copy(7, x_ref, all_ref.at[other_left], sibling).wait_recv()
    project(other_left)
    copy(8, x_ref, all_ref.at[other_right], sibling).wait_recv()
    project(other_right)
    pass_on(5, far, low, left).wait_recv()
    over_low = pass_on(9, far, low, sibling)
    over_low.start()
    pass_on(6, far, high, right).wait_recv()
    over_high = pass_on(10, far, high, sibling)
    over_high.start()
    project(far)
    pass_on(9, other_far, low, sibling).wait_recv()
    pass_on(10, other_far, high, sibling).wait_recv()
    project(other_far)
    for n in range(3):
        weight_copy(n, side).wait_send()
    for n in range(4):
        own_copy(n, m).wait_send()
    for sent in (to_sibling, on_right, on_left, over_left, over_right, over_low, over_high):
        sent.wait_send()


def gather_qkv(x, w_rows, count):
    rows, width = x.shape
    vmem = pl.BlockSpec(memory_space=pltpu.VMEM)
    return pl.pallas_call(
        gather_kernel,
        in_specs=[vmem] * 2,
        out_specs=[vmem] * 2,
        out_shape=(
            jax.ShapeDtypeStruct((count, rows, width), BF16),
            jax.ShapeDtypeStruct((6 * HD, count * rows), BF16),
        ),
        scratch_shapes=[
            pltpu.VMEM((6 * HD, width), BF16),
            pltpu.SemaphoreType.DMA((14,)),
            pltpu.SemaphoreType.DMA((14,)),
        ],
        compiler_params=pltpu.CompilerParams(
            vmem_limit_bytes=VMEM_BYTES, collective_id=2, has_side_effects=True
        ),
        cost_estimate=pl.CostEstimate(
            flops=12 * HD * count * rows * width, bytes_accessed=30_000_000, transcendentals=0
        ),
        name="gather_qkv",
    )(x, w_rows)


def around(m, count):
    sibling = m + 1 - 2 * (m % 2)
    return [(base + count + off) % count for base in (m, sibling) for off in OFFSETS]


def middle_kernel(
    sent_ref, x_ref, cot_ref, own_w, left_w, right_w, scale_ref,
    result_ref, lows_ref, left_ref, right_ref, one_ref, attn_ref, part_ref,
    wall, out_w, att_in, attn_out, slope, keep, acc,
    load, give_send, give_recv, rest_send, rest_recv, line_send, line_recv, far_send, far_recv,
    in_send, in_recv, out_send, out_recv, row_send, row_recv,
):
    rows = x_ref.shape[0]
    count = att_in.shape[0]
    units = slope.shape[2]
    both = 2 * units
    m = lax.axis_index("mp")
    devices = around(m, count)
    sibling = devices[4]
    greet(devices[1:])

    def tokens(index):
        return pl.ds(pl.multiple_of(index * rows, rows), rows)

    side = m % 2
    depth = wall.shape[1]
    blocks = (own_w, left_w, right_w)
    out_rows = slice(both, depth)
    ffn_rows = slice(0, both)
    parts = (slice(0, units), slice(units, both))

    middle_row = both + OWN // 2
    out_parts = (slice(both, middle_row), slice(middle_row, depth))

    def give(n):
        return remote(
            blocks[n].at[out_rows], wall.at[4 + n, out_rows], give_send.at[n], give_recv.at[n],
            sibling,
        )

    def out_along(n):
        return remote(
            blocks[1 + n].at[out_parts[n]], wall.at[3, out_parts[n]], give_send.at[3 + n],
            give_recv.at[3 + n], devices[2 - n],
        )

    def out_far(n):
        return remote(
            wall.at[3, out_parts[n]], wall.at[7, out_parts[n]], give_send.at[5 + n],
            give_recv.at[5 + n], sibling,
        )

    def rest(n):
        return remote(
            blocks[n].at[ffn_rows], wall.at[4 + n, ffn_rows], rest_send.at[n], rest_recv.at[n],
            sibling,
        )

    def along(n):
        return remote(
            blocks[1 + n].at[parts[n]], wall.at[3, parts[n]], line_send.at[n], line_recv.at[n],
            devices[2 - n],
        )

    def row_copy(k, n):
        place = (left_ref, right_ref)[n].at[k]
        return remote(
            lows_ref.at[k], place, row_send.at[k, n], row_recv.at[k, n], devices[2 - n]
        )

    def far_copy(n):
        return remote(
            wall.at[3, parts[n]], wall.at[7, parts[n]], far_send.at[n], far_recv.at[n], sibling
        )

    def loads():
        return [pltpu.make_async_copy(blocks[n], wall.at[n], load.at[n]) for n in range(3)]

    def att_copy(n, slot, sem):
        return remote(
            sent_ref.at[:, tokens(devices[n])], att_in.at[slot], in_send.at[n], in_recv.at[sem],
            devices[n],
        )

    def attn_copy(n, lane, sem):
        return remote(
            attn_out.at[n], attn_ref.at[:, tokens(lane)], out_send.at[n], out_recv.at[sem],
            devices[n],
        )

    for n in range(2):
        out_along(n).start()
    for n in range(1, count):
        att_copy(n, INVERSE[n], INVERSE[n]).start()
    for n in range(3):
        give(n).start()
    for copy in loads():
        copy.start()
    for n in range(3):
        rest(n).start()
    att_in[0] = sent_ref[:, tokens(m)]
    for copy in loads():
        copy.wait()
    for n in range(2):
        out_along(n).wait_recv()
        out_far(n).start()
    for n in range(3):
        give(n).wait_recv()
    for n in range(1, count):
        att_copy(n, n, n).wait_recv()
    for n in range(2):
        along(n).start()
    projected = None
    for n in range(4):
        if n == 3:
            for part in range(2):
                out_far(part).wait_recv()
        first, second = n + 4 * side, n + 4 * (1 - side)
        out_w[n, 0:OWN] = wall[first, out_rows]
        out_w[n, OWN : 2 * OWN] = wall[second, out_rows]
        shared = att_in[first, HD : 2 * HD].astype(F32) + att_in[second, HD : 2 * HD].astype(F32)
        features = jnp.concatenate(
            (att_in[first, 0:HD], shared.astype(BF16), att_in[second, 0:HD]), axis=0
        )
        piece = tn_dot(features, out_w[n])
        projected = piece if projected is None else projected + piece
    unit, inverse = norm_rows(x_ref[...].astype(F32) + projected)
    hidden = unit * scale_ref[0:1] + scale_ref[1:2]
    keep[0] = unit
    keep[1] = hidden
    lows_ref[0] = hidden.astype(BF16)
    acc[...] = jnp.zeros_like(acc)

    def forward(slots):
        low = lows_ref[0]
        total = acc[...]
        for slot in slots:
            active, lean = gelu_pair(nt_dot(low, wall[slot, 0:units]))
            slope[slot] = lean
            total = total + nn_dot(active.astype(BF16), wall[slot, units:both])
        acc[...] = total

    for n in range(3):
        rest(n).wait_recv()
    repeat(0, 3, lambda n: forward((n, 4 + n)))
    for n in range(2):
        along(n).wait_recv()
        far_copy(n).start()
    for n in range(2):
        row_copy(0, n).start()
    forward((3,))
    for n in range(2):
        far_copy(n).wait_recv()
    forward((7,))
    unit, inv = norm_rows(keep[1] + acc[...])
    result_ref[...] = (unit * scale_ref[2:3] + scale_ref[3:4]).astype(BF16)
    upstream = cot_ref[...].astype(F32)
    part_ref[2:3] = column_sum(upstream * unit)
    part_ref[3:4] = column_sum(upstream)
    grad = norm_back(upstream, unit, inv, scale_ref[2:3])
    keep[1] = grad
    lows_ref[1] = grad.astype(BF16)
    for n in range(2):
        row_copy(1, n).start()
    acc[...] = jnp.zeros_like(acc)

    def backward(i, carry):
        low = lows_ref[1]
        total = acc[...]
        for n in range(2):
            pre_grad = nt_dot(low, wall[2 * i + n, units:both]) * slope[2 * i + n]
            total = total + nn_dot(pre_grad.astype(BF16), wall[2 * i + n, 0:units])
        acc[...] = total
        return carry

    lax.fori_loop(0, 4, backward, 0)
    upstream = keep[1] + acc[...]
    unit = keep[0]
    part_ref[0:1] = column_sum(upstream * unit)
    part_ref[1:2] = column_sum(upstream)
    part_ref[4:8] = jnp.zeros((4, part_ref.shape[1]), F32)
    grad = norm_back(upstream, unit, inverse, scale_ref[0:1])
    one_ref[...] = grad
    low = grad.astype(BF16)
    lows_ref[2] = low
    for n in (3, 1, 2, 0):
        first, second = n + 4 * side, n + 4 * (1 - side)
        back = nt_dot(out_w[n], low).astype(BF16)
        attn_out[first] = back[0 : 2 * HD]
        attn_out[second, 0:HD] = back[2 * HD : 3 * HD]
        attn_out[second, HD : 2 * HD] = back[HD : 2 * HD]
        for slot in (n, 4 + n):
            if slot > 0:
                attn_copy(slot, m, INVERSE[slot]).start()
    attn_ref[:, tokens(m)] = attn_out[0]
    for n in range(1, count):
        attn_copy(n, devices[n], n).wait_recv()
    for k in range(2):
        for n in range(2):
            row_copy(k, n).wait_recv()
            row_copy(k, n).wait_send()
    for n in range(2):
        out_along(n).wait_send()
        out_far(n).wait_send()
    for n in range(3):
        give(n).wait_send()
        rest(n).wait_send()
    for n in range(2):
        along(n).wait_send()
        far_copy(n).wait_send()
    for n in range(1, count):
        att_copy(n, INVERSE[n], INVERSE[n]).wait_send()
        attn_copy(n, m, INVERSE[n]).wait_send()


def middle(sent, x, cot, blocks, scale, count):
    rows, width = x.shape
    depth = sent.shape[0]
    units = (blocks[0].shape[0] - OWN) // 2
    vmem = pl.BlockSpec(memory_space=pltpu.VMEM)
    sems = lambda n: pltpu.SemaphoreType.DMA((n,))
    return pl.pallas_call(
        middle_kernel,
        in_specs=[vmem] * 3 + [pl.BlockSpec(memory_space=pl.ANY)] * 3 + [vmem],
        out_specs=[vmem] * 7,
        out_shape=(
            jax.ShapeDtypeStruct((rows, width), BF16),
            jax.ShapeDtypeStruct((3, rows, width), BF16),
            jax.ShapeDtypeStruct((2, rows, width), BF16),
            jax.ShapeDtypeStruct((2, rows, width), BF16),
            jax.ShapeDtypeStruct((rows, width), F32),
            jax.ShapeDtypeStruct(sent.shape, BF16),
            jax.ShapeDtypeStruct((8, width), F32),
        ),
        scratch_shapes=[
            pltpu.VMEM((count,) + blocks[0].shape, BF16),
            pltpu.VMEM((count // 2, 2 * OWN, width), BF16),
            pltpu.VMEM((count, depth, rows), BF16),
            pltpu.VMEM((count, depth, rows), BF16),
            pltpu.VMEM((count, rows, units), F32),
            pltpu.VMEM((2, rows, width), F32),
            pltpu.VMEM((rows, width), F32),
            sems(3), sems(7), sems(7), sems(3), sems(3), sems(2), sems(2), sems(2), sems(2),
            sems(count), sems(count), sems(count), sems(count),
            pltpu.SemaphoreType.DMA((2, 2)), pltpu.SemaphoreType.DMA((2, 2)),
        ],
        compiler_params=pltpu.CompilerParams(
            vmem_limit_bytes=VMEM_BYTES, collective_id=1, has_side_effects=True
        ),
        cost_estimate=pl.CostEstimate(
            flops=16 * rows * width * count * units, bytes_accessed=26_000_000,
            transcendentals=0,
        ),
        name="middle",
    )(sent, x, cot, *blocks, scale)


def close_kernel(
    own_x, left_x, right_x, numer_any, dens_any, sign_any, bucket_any,
    conv_any, all_any, w_any, one_any,
    sent_ref, w_rows_ref, norm_ref, tap_ref, qkv_ref, planes_ref, seg_ref, grad_ref,
    inputs_ref, up_ref, down_ref, out_ref, query_ref, key_ref, value_ref, tiny_ref, taps_ref,
    conv_ref, all_ref, w_ref, one_ref, w_all, half_in,
    wall, acc, solo_low, half_low, w_solo, w_half, attended, swap_out, swap_in, part_out, part_own, pair_in, stage,
    line_in, a_refs, b_refs, d_refs, l_refs, near_in, far_in,
    back_out, numer, dens, sign, bucket,
    spread, qprob, gspread, total_ref, table, turned, gsign, proj,
    load, fetch_sem, give_send, give_recv, along_send, along_recv, over_send, over_recv,
    row_send, row_recv, wa_send, wa_recv, half_send, half_recv,
    swap_send, swap_recv, pair_send, pair_recv, line_send, line_recv,
    a_sems, b_sems, d_sems,
    l_sems,
    near_send, near_recv, far_sems,
):
    edge = far_in.shape[1]
    count, _, rows, width = wall.shape
    chips = count // 2
    units = down_ref.shape[0]
    d = lax.axis_index("dp")
    m = lax.axis_index("mp")
    side = m % 2
    chip = m // 2
    half = OWN - HD
    cut = rows // 2
    devices = around(m, count)
    sibling = devices[4]

    barrier = pltpu.get_barrier_semaphore()
    place_x, place_y = d % edge, d // edge
    for k in range(1, edge):
        for peer in (
            place_y * edge + (place_x + k) % edge, (place_y + k) % edge * edge + place_x
        ):
            pl.semaphore_signal(barrier, inc=1, device_id={"dp": peer}, device_id_type=MESH)
    repeat(
        1, count,
        lambda r: pl.semaphore_signal(
            barrier, inc=1, device_id={"mp": (m + r) % count}, device_id_type=MESH
        ),
    )
    pl.semaphore_wait(barrier, 2 * (edge - 1) + count - 1)

    def tokens(index):
        return pl.ds(pl.multiple_of(index * rows, rows), rows)

    parts = (slice(0, cut), slice(cut, rows))
    pair = slice(0, 2)
    sources = (own_x.at[pair], left_x, right_x)

    def give(n):
        return remote(
            sources[n], wall.at[4 + n, pair], give_send.at[n], give_recv.at[n], sibling
        )

    def along(n):
        return remote(
            sources[1 + n].at[:, parts[n]], wall.at[3, pair, parts[n]], along_send.at[n],
            along_recv.at[n], devices[2 - n],
        )

    def over(n):
        return remote(
            wall.at[3, pair, parts[n]], wall.at[7, pair, parts[n]], over_send.at[n],
            over_recv.at[n], sibling,
        )

    def row_copy(n):
        if n < 3:
            source, slot, target = own_x.at[2], n + 1, devices[2 - n]
            if n == 2:
                slot, target = 4, sibling
            place = wall.at[slot, 2]
        elif n < 5:
            source, place, target = wall.at[n - 2, 2], wall.at[n + 2, 2], sibling
        elif n < 7:
            piece = parts[n - 5]
            source, place = wall.at[n - 4, 2, piece], wall.at[3, 2, piece]
            target = devices[7 - n]
        else:
            piece = parts[n - 7]
            source, place, target = wall.at[3, 2, piece], wall.at[7, 2, piece], sibling
        return remote(source, place, row_send.at[n], row_recv.at[n], target)

    def loads():
        copies = [pltpu.make_async_copy(own_x, wall.at[0], load.at[0])]
        for n in range(1, 3):
            copies.append(pltpu.make_async_copy(sources[n], wall.at[n, pair], load.at[n]))
        pairs = ((w_any, w_ref), (conv_any, conv_ref), (all_any, all_ref), (one_any, one_ref))
        for n, (source, target) in enumerate(pairs):
            copies.append(pltpu.make_async_copy(source, target, load.at[3 + n]))
        return copies

    def w_copy(n, slot):
        return remote(w_half, w_all.at[slot], wa_send.at[n], wa_recv.at[slot], devices[n])

    def half_copy(n, slot):
        return remote(
            half_low.at[:, tokens(devices[n])], half_in.at[slot], half_send.at[n],
            half_recv.at[slot], devices[n],
        )

    def fetch(unit):
        place = unit % 2
        return [
            pltpu.make_async_copy(source.at[unit], target.at[place], fetch_sem.at[place, n])
            for n, (source, target) in enumerate(
                ((numer_any, numer), (dens_any, dens), (sign_any, sign), (bucket_any, bucket))
            )
        ]

    def near_copy(r, owner):
        return remote(
            near_in.at[m], near_in.at[owner], near_send.at[r], near_recv.at[r], (m + r) % count
        )

    def swap(n):
        piece = slice(0, half) if n == 0 else slice(half, 4 * half)
        return remote(
            swap_out.at[piece], swap_in.at[piece], swap_send.at[n], swap_recv.at[n], sibling
        )

    for n in range(2):
        along(n).start()
    swap_out[0:half] = sent_ref[pl.ds(pl.multiple_of(HD + (1 - side) * half, half), half), :]
    swap(0).start()
    for n in range(3):
        give(n).start()
    for copy in fetch(0) + loads():
        copy.start()
    for n in range(3):
        row_copy(n).start()
    near_in[m, :, 0:width] = norm_ref[...]
    near_in[m, :, width : width + 2 * LANES] = tap_ref[...]
    repeat(1, count, lambda r: near_copy(r, m).start())
    solo_at = lambda n: pl.ds(pl.multiple_of(n * OWN + side * half, half), HD)
    half_at = lambda n: pl.ds(pl.multiple_of(n * OWN + (1 - side) * HD, half), half)
    sent_half = sent_ref[pl.ds(pl.multiple_of(HD + side * half, half), half), :]
    attended[solo_at(0), :] = sent_ref[0:HD, :]
    acc[...] = jnp.zeros_like(acc)
    swap(0).wait_recv()
    attended[half_at(0), :] = (
        sent_half.astype(F32) + swap_in[0:half].astype(F32)
    ).astype(BF16)
    def step(slots):
        sums = [None] * 2
        for slot in slots:
            hidden, ffn = wall[slot, 0], wall[slot, 1]
            active, lean = gelu_pair(nt_dot(hidden, w_ref[0:units]))
            grad = nt_dot(ffn, w_ref[units : 2 * units]) * lean
            terms = (
                tn_dot(grad.astype(BF16), hidden),
                tn_dot(active.astype(BF16), ffn),
            )
            sums = [p if t is None else t + p for t, p in zip(sums, terms)]
        acc[0:units, :] += sums[0]
        acc[units : 2 * units, :] += sums[1]

    def staged(along_x, refs, sems):
        grads, first_in, mid, second_in, sums = refs
        u, v = (d % edge, d // edge) if along_x else (d // edge, d % edge)

        def copy(n, src, dst, k):
            du, dv = ((u + k) % edge, v) if n in (0, 3) else (u, (v + k) % edge)
            target = dv * edge + du if along_x else du * edge + dv
            return pltpu.make_async_remote_copy(
                src_ref=src, dst_ref=dst, send_sem=sems.at[2 * n, k], recv_sem=sems.at[2 * n + 1, k],
                device_id={"dp": target}, device_id_type=MESH,
            )

        around_edge = range(1, edge)
        out_copy = lambda k: copy(0, grads.at[(u + k) % edge], first_in.at[k], k)
        mid_copy = lambda k: copy(1, mid.at[(v + k) % edge], second_in.at[k], k)
        back_copy = lambda k, owner: copy(2, sums.at[u, v], sums.at[u, owner], k)
        wide_copy = lambda k, owner: copy(3, sums.at[u], sums.at[owner], k)

        def start():
            for k in around_edge:
                out_copy(k).start()

        def half_reduce():
            for k in around_edge:
                out_copy(k).wait_recv()
            for n in range(edge):
                value = grads[u, n].astype(F32)
                for k in around_edge:
                    value = value + first_in[k, n].astype(F32)
                mid[n] = value.astype(BF16)
            for k in around_edge:
                mid_copy(k).start()

        def reduce():
            for k in around_edge:
                mid_copy(k).wait_recv()
            value = mid[v].astype(F32)
            for k in around_edge:
                value = value + second_in[k].astype(F32)
            sums[u, v] = value.astype(BF16)
            for k in around_edge:
                back_copy(k, v).start()

        def spread():
            for k in around_edge:
                back_copy(k, (v + edge - k) % edge).wait_recv()
            for k in around_edge:
                wide_copy(k, u).start()

        def finish():
            for k in around_edge:
                wide_copy(k, (u + edge - k) % edge).wait_recv()
            for k in around_edge:
                out_copy(k).wait_send()
                mid_copy(k).wait_send()
                back_copy(k, v).wait_send()
                wide_copy(k, u).wait_send()

        def put(value):
            size = grads.shape[2]
            for n in range(edge * edge):
                grads[n // edge, n % edge] = value[n * size : (n + 1) * size].astype(BF16)

        def whole():
            return jnp.concatenate(
                [sums[n // edge, n % edge].astype(F32) for n in range(edge * edge)], axis=0
            )

        return start, half_reduce, reduce, spread, finish, put, whole

    a_start, a_half, a_reduce, a_spread, a_finish, a_put, a_whole = staged(True, a_refs, a_sems)
    b_start, b_half, b_reduce, b_spread, b_finish, b_put, b_whole = staged(True, b_refs, b_sems)
    d_start, d_half, d_reduce, d_spread, d_finish, d_put, d_whole = staged(False, d_refs, d_sems)
    l_start, l_half, l_reduce, l_spread, l_finish, l_put, l_whole = staged(False, l_refs, l_sems)

    def far_copy(n, k, owner):
        target = (
            place_y * edge + (place_x + k) % edge if n == 0
            else (place_y + k) % edge * edge + place_x
        )
        mine = (place_x, place_y)[n]
        return pltpu.make_async_remote_copy(
            src_ref=far_in.at[n, mine], dst_ref=far_in.at[n, owner],
            send_sem=far_sems.at[2 * n, k], recv_sem=far_sems.at[2 * n + 1, k],
            device_id={"dp": target}, device_id_type=MESH,
        )

    def far_start(n, value):
        mine = (place_x, place_y)[n]
        far_in[n, mine] = value
        for k in range(1, edge):
            far_copy(n, k, mine).start()

    def far_sum(n):
        mine = (place_x, place_y)[n]
        for k in range(1, edge):
            far_copy(n, k, (mine + edge - k) % edge).wait_recv()
        value = far_in[n, 0]
        for k in range(1, edge):
            value = value + far_in[n, k]
        for k in range(1, edge):
            far_copy(n, k, mine).wait_send()
        return value

    def attention(slot, low, high):
        back_setup(slot, qkv_ref, seg_ref, back_out, spread, gspread, proj)

        def one_unit(unit):
            for copy in fetch(unit):
                copy.wait()

            @pl.when(unit < UNITS - 1)
            def _():
                for copy in fetch(unit + 1):
                    copy.start()

            if slot == 0:
                @pl.when(unit == 2)
                def _():
                    for n in range(3):
                        row_copy(n).wait_recv()
                    for n in range(3, 7):
                        row_copy(n).start()
                    for n in range(2):
                        along(n).wait_recv()
                        over(n).start()

                @pl.when(unit == 3)
                def _():
                    for n in range(5, 7):
                        row_copy(n).wait_recv()
                    for n in range(7, 9):
                        row_copy(n).start()
            else:
                @pl.when(unit == UNITS - 1)
                def _():
                    b_reduce()
                    d_reduce()
                    a_half()

            place = unit % 2
            back_unit(
                slot, unit, qkv_ref, planes_ref, seg_ref, grad_ref,
                numer.at[place], dens.at[place], sign.at[place], bucket.at[place], back_out,
                spread, qprob, qprob, gspread, total_ref, table, turned, gsign, proj,
            )

        repeat(low, high, one_unit)
        back_finish(slot, qkv_ref, back_out, proj)

    for n in range(3):
        w_solo[n * HD : (n + 1) * HD] = w_rows_ref[solo_at(n), :]
        w_half[n * half : (n + 1) * half] = w_rows_ref[half_at(n), :]
    w_all[0] = w_half[...]
    attention(0, 0, SOLO)
    for n in range(1, count):
        w_copy(n, INVERSE[n]).start()
    for copy in loads():
        copy.wait()
    for n in range(3):
        solo = back_out[n * HD : (n + 1) * HD, :]
        if n == 2:
            solo = solo + conv_ref[0:HD, :]
        solo_low[n * HD : (n + 1) * HD, :] = solo.astype(BF16)

    def pair_copy(target):
        return remote(
            part_out.at[target], pair_in.at[target], pair_send.at[target], pair_recv.at[target],
            sibling,
        )

    def input_part(device):
        lane = tokens(device)
        return tn_dot(solo_low[:, lane], w_solo[...])

    def line_copy(k):
        return remote(
            stage.at[k], line_in.at[k], line_send.at[k], line_recv.at[k], (m + 2 * k) % count
        )

    order = [2, 1, 3, 0]
    for k in order:
        target = (chip + k) % chips
        part_out[target] = input_part(2 * target + 1 - side).astype(BF16)
        pair_copy(target).start()
    for n in range(3):
        give(n).wait_recv()
    for n in range(2):
        over(n).wait_recv()
    repeat(0, 4, lambda i: step((2 * i, 2 * i + 1)))
    b_put(acc[0:units])
    d_put(acc[units : 2 * units])
    b_start()
    d_start()
    for k in order[:3]:
        target = (chip + k) % chips
        mine = input_part(2 * target + side)
        pair_copy(target).wait_recv()
        stage[k] = (mine + pair_in[target].astype(F32)).astype(BF16)
        line_copy(k).start()
    part_own[...] = input_part(m)
    solo_grad = nn_dot(solo_low[...], all_ref[...])
    for n in (3, 4, 7, 8):
        row_copy(n).wait_recv()
    out_grad = None
    for slot in range(count):
        term = nn_dot(attended[:, tokens(devices[slot])], wall[slot, 2])
        out_grad = term if out_grad is None else out_grad + term
    a_put(jnp.concatenate((out_grad, solo_grad), axis=0))
    b_half()
    d_half()
    a_start()
    repeat(1, count, lambda r: near_copy(r, (m + count - r) % count).wait_recv())
    total = near_in[0]
    for r in range(1, count):
        total = total + near_in[r]
    far_start(0, total)
    attention(1, SOLO, UNITS)

    for n in range(3):
        start = pl.multiple_of(n * HD + (1 - side) * half, half)
        swap_out[(n + 1) * half : (n + 2) * half] = back_out[pl.ds(start, half), :].astype(BF16)
    swap(1).start()
    b_spread()
    d_spread()
    a_reduce()
    swap(1).wait_recv()
    for n in range(3):
        mine = back_out[pl.ds(pl.multiple_of(n * HD + side * half, half), half), :]
        mixed = mine + swap_in[(n + 1) * half : (n + 2) * half].astype(F32)
        if n == 2:
            mixed = mixed + conv_ref[HD:OWN, :]
        half_low[n * half : (n + 1) * half] = mixed.astype(BF16)
    for n in range(1, count):
        half_copy(n, INVERSE[n]).start()
    half_in[0] = half_low[:, tokens(m)]
    half_grad = nn_dot(half_low[...], all_ref[...])
    l_put(half_grad)
    l_start()
    a_spread()
    far_start(1, far_sum(0))
    l_half()
    pair_copy(chip).wait_recv()
    total = one_ref[...] + part_own[...] + pair_in[chip].astype(F32)
    for k in range(1, chips):
        line_copy(k).wait_recv()
        total = total + line_in[k].astype(F32)
    for n in range(1, count):
        w_copy(n, n).wait_recv()
        half_copy(n, n).wait_recv()
    late = tn_dot(
        half_in[...].reshape(count * OWN, rows), w_all[...].reshape(count * OWN, width)
    )
    inputs_ref[...] = total + late
    l_reduce()
    total = far_sum(1)
    tiny_ref[...] = total[:, 0:width]
    taps_ref[0:8] = total[:, width : width + LANES]
    taps_ref[8:16] = total[:, width + LANES : width + 2 * LANES]
    b_finish()
    up_ref[...] = jnp.transpose(b_whole()).astype(BF16)
    l_spread()
    d_finish()
    down_ref[...] = d_whole().astype(BF16)
    a_finish()
    whole = a_whole().astype(BF16)
    out_ref[...] = whole[0:OWN]
    outs = (query_ref, key_ref, value_ref)
    for n, ref in enumerate(outs):
        ref[solo_at(0), :] = whole[OWN + n * HD : OWN + (n + 1) * HD]
    l_finish()
    whole = l_whole().astype(BF16)
    for n, ref in enumerate(outs):
        ref[half_at(0), :] = whole[n * half : (n + 1) * half]

    for n in range(1, count):
        w_copy(n, INVERSE[n]).wait_send()
        half_copy(n, INVERSE[n]).wait_send()
    for n in range(2):
        swap(n).wait_send()
        along(n).wait_send()
        over(n).wait_send()
    for n in range(3):
        give(n).wait_send()
    for n in range(9):
        row_copy(n).wait_send()
    for k in range(chips):
        pair_copy((chip + k) % chips).wait_send()
    for k in range(1, chips):
        line_copy(k).wait_send()
    repeat(1, count, lambda r: near_copy(r, m).wait_send())


def close(blocks_x, saved, conv, sent, gathered, w_rows, block_w, one, norms, taps,
          qkv, planes, seg_row, grad, blocks):
    rows, width = one.shape
    length = sent.shape[1]
    count = length // rows
    chips = count // 2
    units = (block_w.shape[0] - OWN) // 2
    depth = (OWN + 3 * HD) // blocks
    thin = OWN // blocks
    high = units // blocks
    edge = 4
    lanes = width + 2 * LANES
    vmem = pl.BlockSpec(memory_space=pltpu.VMEM)
    sems = lambda *n: pltpu.SemaphoreType.DMA(n)
    low = lambda *shape: jax.ShapeDtypeStruct(shape, BF16)
    by_edge = lambda n: (
        pltpu.VMEM((edge, edge, n, width), BF16),
        pltpu.VMEM((edge, edge, n, width), BF16),
        pltpu.VMEM((edge, n, width), BF16),
        pltpu.VMEM((edge, n, width), BF16),
        pltpu.VMEM((edge, edge, n, width), BF16),
    )
    by_chip = pltpu.VMEM((chips, rows, width), BF16)
    return pl.pallas_call(
        close_kernel,
        in_specs=[pl.BlockSpec(memory_space=pl.ANY)] * 11 + [vmem] * 8,
        out_specs=[vmem] * 9,
        out_shape=(
            jax.ShapeDtypeStruct(one.shape, F32),
            low(width, units), low(units, width), low(OWN, width),
            low(OWN, width), low(OWN, width), low(OWN, width),
            jax.ShapeDtypeStruct((8, width), F32),
            jax.ShapeDtypeStruct((16, LANES), F32),
        ),
        scratch_shapes=[
            pltpu.VMEM(conv.shape, F32),
            pltpu.VMEM(gathered.shape, BF16),
            pltpu.VMEM(block_w.shape, BF16),
            pltpu.VMEM(one.shape, F32),
            pltpu.VMEM((count, OWN, width), BF16),
            pltpu.VMEM((count, OWN, rows), BF16),
            pltpu.VMEM((count, 3, rows, width), BF16),
            pltpu.VMEM((2 * units, width), F32),
            pltpu.VMEM((3 * HD, length), BF16),
            pltpu.VMEM((OWN, length), BF16),
            pltpu.VMEM((3 * HD, width), BF16),
            pltpu.VMEM((OWN, width), BF16),
            pltpu.VMEM((OWN, length), BF16),
            pltpu.VMEM((2 * HD, length), BF16),
            pltpu.VMEM((2 * HD, length), BF16),
            by_chip,
            pltpu.VMEM((rows, width), F32),
            by_chip, by_chip, by_chip,
            by_edge(depth), by_edge(high), by_edge(high),
            by_edge(thin),
            pltpu.VMEM((count, 8, lanes), F32),
            pltpu.VMEM((2, edge, 8, lanes), F32),
            pltpu.VMEM((3 * HD, length), F32),
            pltpu.VMEM((2, HD, length), F32),
            pltpu.VMEM((2, 1, length), F32),
            pltpu.VMEM((2, 16, length), F32),
            pltpu.VMEM((2, CODES, EXT), BF16),
            pltpu.VMEM((EXT, length), BF16),
            pltpu.VMEM((CODES, TILE), BF16),
            pltpu.VMEM((EXT, TILE), BF16),
            pltpu.VMEM((SPREAD + 16, CODES), F32),
            pltpu.VMEM((SPREAD, CODES), BF16),
            pltpu.VMEM((CODES, EXT), BF16),
            pltpu.VMEM((16, length), F32),
            pltpu.VMEM((2 * HD, length), F32),
            sems(7), sems(2, 4), sems(3), sems(3), sems(2), sems(2), sems(2), sems(2),
            sems(9), sems(9), sems(count), sems(count), sems(count), sems(count),
            sems(2), sems(2), sems(4), sems(4), sems(4), sems(4),
            sems(8, edge), sems(8, edge), sems(8, edge), sems(8, edge),
            sems(count), sems(count), sems(4, edge),
        ],
        compiler_params=pltpu.CompilerParams(
            vmem_limit_bytes=CLOSE_BYTES, collective_id=0, has_side_effects=True
        ),
        cost_estimate=pl.CostEstimate(flops=0, bytes_accessed=30_000_000, transcendentals=0),
        name="close",
    )(*blocks_x, *saved, conv, gathered, block_w, one, sent, w_rows, norms, taps,
      qkv, planes, seg_row, grad)


def shifted(block, off):
    count = lax.axis_size("mp")
    return lax.ppermute(block, "mp", [(n, (n - off) % count) for n in range(count)])


def on_device(
    inputs, segment, w_query, w_key, w_value, planes, conv_taps, w_out,
    ln1_gain, ln1_bias, w_up, w_down, ln2_gain, ln2_bias, cotangent,
):
    count = lax.axis_size("mp")
    blocks = lax.axis_size("dp")
    rows, width = inputs.shape
    block_w = jnp.concatenate((w_up.T, w_down, w_out), 0)
    w_rows = jnp.concatenate((w_query, w_key, w_value), 1).T
    gathered, qkv = gather_qkv(inputs, w_rows, count)
    block_w, qkv = lax.optimization_barrier((block_w, qkv))
    left_w, right_w = shifted(block_w, -2), shifted(block_w, 2)
    gathered = gathered.reshape(rows * count, width)
    seg_row = segment[None, :]
    taps = jnp.pad(
        jnp.concatenate(
            (
                jnp.pad(conv_taps, ((0, 0), (0, 16 - HEADS))),
                jnp.pad(conv_taps[::-1], ((0, 0), (0, 16 - HEADS))),
            ),
            1,
        ),
        ((0, 2 * LANES - KW), (0, 0)),
    ).T
    conv = segment_conv(qkv, taps, seg_row)
    sent, numer, dens, sign, bucket = attend(qkv, planes, seg_row, conv)
    scale = jnp.stack((ln1_gain, ln1_bias, ln2_gain, ln2_bias) * 2)
    outputs, lows, left_x, right_x, one_grad, attn_grad, norm_part = middle(
        sent, inputs, cotangent, (block_w, left_w, right_w), scale, count
    )
    value_conv, tap_part = conv_back(qkv, attn_grad, taps, seg_row)
    inputs_grad, up, down, out, query, key, value, tiny, conv_rows = close(
        (lows, left_x, right_x), (numer, dens, sign, bucket), value_conv, sent, gathered, w_rows,
        block_w, one_grad, norm_part, tap_part, qkv, planes, seg_row, attn_grad, blocks,
    )
    return (
        outputs, inputs_grad, query.astype(F32).T, key.astype(F32).T, value.astype(F32).T,
        conv_rows[:HEADS, :KW].T, out.astype(F32), tiny[0], tiny[1],
        up.astype(F32), down.astype(F32), tiny[2], tiny[3],
    )


def solution(mesh):
    rows = P(("dp", "mp"), None)
    cols = P(None, "mp")
    return jax.shard_map(
        on_device,
        mesh=mesh,
        in_specs=(
            rows, P("dp"), cols, cols, cols, P(), P(), P("mp", None), P(), P(),
            cols, P("mp", None), P(), P(), rows,
        ),
        out_specs=(
            rows, rows, cols, cols, cols, P(), P("mp", None), P(), P(),
            cols, P("mp", None), P(), P(),
        ),
        check_vma=False,
    )
```

```python
import math
import jax
import jax.numpy as jnp
from jax import lax
from jax.experimental import pallas as pl
from jax.experimental.pallas import tpu as pltpu
from jax.sharding import PartitionSpec as P

HEADS = 12
HD = 64
TABLES = 4
BITS = 8
KW = 65
MAXSEG = 8
CODES = 256
UNITS = 6
SOLO = 4
SPREAD = MAXSEG * HD
EXT = SPREAD + 128
LANES = 128
TILE = 2048
F32 = jnp.float32
BF16 = jnp.bfloat16
VMEM_BYTES = 56 * 1024 * 1024
CLOSE_BYTES = 60 * 1024 * 1024


def nt_dot(left, right):
    return lax.dot_general(left, right, (((1,), (1,)), ((), ())), preferred_element_type=F32)


def tn_dot(left, right):
    return lax.dot_general(left, right, (((0,), (0,)), ((), ())), preferred_element_type=F32)


def nn_dot(left, right):
    return lax.dot_general(left, right, (((1,), (0,)), ((), ())), preferred_element_type=F32)


def half_sign(bit):
    rows = lax.broadcasted_iota(jnp.int32, (8, LANES), 0)
    return jnp.where((rows >> bit) & 1 == 0, 0.5, -0.5).astype(F32)


def code_factors(signs):
    pos0, neg0 = 0.5 + 0.5 * signs[0:1], 0.5 - 0.5 * signs[0:1]
    pos1, neg1 = 0.5 + 0.5 * signs[1:2], 0.5 - 0.5 * signs[1:2]
    tops = (pos0 * pos1, pos0 * neg1, neg0 * pos1, neg0 * neg1)
    picks = [half_sign(2), half_sign(1), half_sign(0)]
    mids = [0.5 + picks[n] * signs[2 + n : 3 + n] for n in range(3)]
    lows = [0.5 + picks[n] * signs[5 + n : 6 + n] for n in range(3)]
    return tops, mids, lows, picks


def code_probs(signs, out_ref, lane):
    tops, mids, lows, _ = code_factors(signs)
    mid = mids[0] * mids[1] * mids[2]
    low = lows[0] * lows[1] * lows[2]
    for top_index in range(4):
        low_top = low * tops[top_index]
        for pair in range(4):
            rows = jnp.concatenate(
                (
                    low_top * mid[2 * pair : 2 * pair + 1],
                    low_top * mid[2 * pair + 1 : 2 * pair + 2],
                ),
                axis=0,
            )
            first = top_index * 64 + pair * 16
            out_ref[first : first + 16, lane] = rows.astype(BF16)


def signs_back(signs, grads):
    tops, mids, lows, picks = code_factors(signs)
    mid = mids[0] * mids[1] * mids[2]
    low = lows[0] * lows[1] * lows[2]
    mid_rows = [jnp.broadcast_to(mid[m : m + 1], (8, LANES)) for m in range(8)]
    top_rows = [jnp.broadcast_to(tops[t], (8, LANES)) for t in range(4)]
    by_top = [None] * 4
    by_mid = [None] * 8
    for t in range(4):
        for m in range(8):
            piece = grads[t * 64 + m * 8 : t * 64 + m * 8 + 8]
            a = piece * mid_rows[m]
            b = piece * top_rows[t]
            by_top[t] = a if by_top[t] is None else by_top[t] + a
            by_mid[m] = b if by_mid[m] is None else by_mid[m] + b
    low_grad = by_top[0] * top_rows[0]
    for t in range(1, 4):
        low_grad = low_grad + by_top[t] * top_rows[t]
    top_grad = [jnp.sum(low * by_top[t], axis=0, keepdims=True) for t in range(4)]
    mid_grad = jnp.concatenate(
        [jnp.sum(low * by_mid[m], axis=0, keepdims=True) for m in range(8)], axis=0
    )
    pos0, neg0 = 0.5 + 0.5 * signs[0:1], 0.5 - 0.5 * signs[0:1]
    pos1, neg1 = 0.5 + 0.5 * signs[1:2], 0.5 - 0.5 * signs[1:2]
    out = [
        0.5 * ((top_grad[0] - top_grad[2]) * pos1 + (top_grad[1] - top_grad[3]) * neg1),
        0.5 * ((top_grad[0] - top_grad[1]) * pos0 + (top_grad[2] - top_grad[3]) * neg0),
    ]
    for grad, parts in ((mid_grad, mids), (low_grad, lows)):
        for n in range(3):
            others = parts[(n + 1) % 3] * parts[(n + 2) % 3] * picks[n]
            out.append(jnp.sum(grad * others, axis=0, keepdims=True))
    return jnp.concatenate(out, axis=0)


def split_two(value):
    high = value.astype(BF16).astype(F32)
    return high, value - high


def unit_planes(planes):
    return planes * lax.rsqrt(jnp.sum(planes * planes, axis=1, keepdims=True) + 1e-06)


def fill_spread(values, seg_row, spread_ref, lane):
    for s in range(MAXSEG):
        spread_ref[s * HD : (s + 1) * HD, lane] = jnp.where(
            seg_row == s, values, jnp.zeros_like(values)
        )


def fill_member(seg_row, spread_ref, lane):
    width = seg_row.shape[1]
    rows = lax.broadcasted_iota(jnp.int32, (128, width), 0)
    hit = jnp.logical_and(rows < 16, (rows & 7) == seg_row)
    spread_ref[SPREAD:EXT, lane] = jnp.where(hit, 1.0, 0.0).astype(BF16)


def plane_rows(unit):
    side = lax.axis_index("mp") % 2
    row = jnp.where(unit < SOLO, unit, 2 * side + unit - SOLO)
    return pl.ds(pl.multiple_of(row * BITS, BITS), BITS)


def lanes_of(index, width):
    return pl.ds(pl.multiple_of(index * width, width), width)


def masked_fold(product, seg_row):
    total = None
    for s in range(MAXSEG):
        piece = jnp.where(seg_row == s, product[s * HD : (s + 1) * HD], 0.0)
        total = piece if total is None else total + piece
    return total


def attend_kernel(
    qkv_ref, planes_ref, seg_ref, conv_ref,
    sent_ref, numer_ref, dens_ref, sign_ref, bucket_ref, query_ref, key_ref,
    spread, norm, total, table, est,
):
    qprob, kprob = query_ref.at[0], key_ref.at[0]
    unit = pl.program_id(0)
    slot = unit // SOLO
    length = qkv_ref.shape[1]
    tiles = length // TILE
    q_rows = pl.ds(pl.multiple_of(slot * HD, HD), HD)
    k_rows = pl.ds(pl.multiple_of(2 * HD + slot * HD, HD), HD)
    v_rows = pl.ds(pl.multiple_of(4 * HD + slot * HD, HD), HD)

    @pl.when(jnp.logical_or(unit == 0, unit == SOLO))
    def _():
        def step(i, carry):
            lane = lanes_of(i, TILE)
            seg_row = seg_ref[:, lane]
            fill_spread(qkv_ref[v_rows, lane], seg_row, spread, lane)
            fill_member(seg_row, spread, lane)
            query = qkv_ref[q_rows, lane].astype(F32)
            key = qkv_ref[k_rows, lane].astype(F32)
            scale = math.sqrt(HD)
            norm[0:1, lane] = scale * lax.rsqrt(
                jnp.sum(query * query, axis=0, keepdims=True) + 1e-06
            )
            norm[1:2, lane] = scale * lax.rsqrt(jnp.sum(key * key, axis=0, keepdims=True) + 1e-06)
            est[:, lane] = jnp.zeros((HD, TILE), F32)
            return carry

        lax.fori_loop(0, tiles, step, 0)

    planes = unit_planes(planes_ref[plane_rows(unit), :])
    high, rest = split_two(planes)
    middle, low = split_two(rest)
    stack = jnp.concatenate((high, middle, low), axis=0).astype(BF16)
    total[...] = jnp.zeros_like(total)

    def collect(i, carry):
        lane = lanes_of(i, TILE)
        flat_q = nn_dot(stack, qkv_ref[q_rows, lane])
        flat_k = nn_dot(stack, qkv_ref[k_rows, lane])
        sign_q = jnp.tanh((flat_q[0:8] + flat_q[8:16] + flat_q[16:24]) * norm[0:1, lane])
        sign_k = jnp.tanh((flat_k[0:8] + flat_k[8:16] + flat_k[16:24]) * norm[1:2, lane])
        sign_ref[0, 0:8, lane] = sign_q
        sign_ref[0, 8:16, lane] = sign_k
        for part in range(TILE // LANES):
            inner = slice(part * LANES, (part + 1) * LANES)
            code_probs(sign_k[:, inner], kprob, inner)
            code_probs(
                sign_q[:, inner], qprob, pl.ds(pl.multiple_of(i * TILE + part * LANES, LANES), LANES)
            )
        total[...] += nt_dot(spread[0 : SPREAD + 16, lane], kprob[...])
        return carry

    lax.fori_loop(0, tiles, collect, 0)
    mass = total[SPREAD : SPREAD + 8, :]
    mass_high, mass_low = split_two(mass)
    extra = jnp.concatenate(
        (mass_high, mass_high, mass_low, jnp.zeros((104, CODES), F32)), axis=0
    )
    table[0:SPREAD, :] = total[0:SPREAD, :].astype(BF16)
    table[SPREAD:EXT, :] = extra.astype(BF16)
    bucket_ref[0, :, 0:SPREAD] = jnp.transpose(total[0:SPREAD, :]).astype(BF16)
    bucket_ref[0, :, SPREAD:EXT] = jnp.transpose(extra).astype(BF16)

    def spend(i, carry):
        lane = lanes_of(i, TILE)
        seg_row = seg_ref[:, lane]
        product = nn_dot(table[0 : SPREAD + 32, :], qprob[:, lane])
        numer = masked_fold(product, seg_row)
        both = product[SPREAD : SPREAD + 8] + product[SPREAD + 16 : SPREAD + 24]
        which = lax.broadcasted_iota(jnp.int32, (8, TILE), 0)
        density = jnp.sum(jnp.where(which == seg_row, both, 0.0), axis=0, keepdims=True)
        numer_ref[0, :, lane] = numer
        dens_ref[0, :, lane] = density
        est[:, lane] += numer * (1.0 / jnp.maximum(density, 1.0))
        return carry

    lax.fori_loop(0, tiles, spend, 0)

    @pl.when(jnp.logical_or(unit == SOLO - 1, unit == UNITS - 1))
    def _():
        sent_ref[q_rows, :] = (est[...] * (1.0 / TABLES) + conv_ref[q_rows, :]).astype(BF16)


def attend(qkv, planes, seg_row, conv):
    length = qkv.shape[1]
    per_unit = lambda u: (u, 0, 0)
    fixed = lambda u: (0, 0)
    return pl.pallas_call(
        attend_kernel,
        grid=(UNITS,),
        in_specs=[
            pl.BlockSpec(qkv.shape, fixed),
            pl.BlockSpec(planes.shape, fixed),
            pl.BlockSpec(seg_row.shape, fixed),
            pl.BlockSpec(conv.shape, fixed),
        ],
        out_specs=[
            pl.BlockSpec((2 * HD, length), fixed),
            pl.BlockSpec((1, HD, length), per_unit),
            pl.BlockSpec((1, 1, length), per_unit),
            pl.BlockSpec((1, 16, length), per_unit),
            pl.BlockSpec((1, CODES, EXT), per_unit),
            pl.BlockSpec((1, CODES, length), per_unit),
            pl.BlockSpec((1, CODES, length), per_unit),
        ],
        out_shape=[
            jax.ShapeDtypeStruct((2 * HD, length), BF16),
            jax.ShapeDtypeStruct((UNITS, HD, length), F32),
            jax.ShapeDtypeStruct((UNITS, 1, length), F32),
            jax.ShapeDtypeStruct((UNITS, 16, length), F32),
            jax.ShapeDtypeStruct((UNITS, CODES, EXT), BF16),
            jax.ShapeDtypeStruct((UNITS, CODES, length), BF16),
            jax.ShapeDtypeStruct((UNITS, CODES, length), BF16),
        ],
        scratch_shapes=[
            pltpu.VMEM((EXT, length), BF16),
            pltpu.VMEM((8, length), F32),
            pltpu.VMEM((SPREAD + 16, CODES), F32),
            pltpu.VMEM((EXT, CODES), BF16),
            pltpu.VMEM((HD, length), F32),
        ],
        compiler_params=pltpu.CompilerParams(vmem_limit_bytes=VMEM_BYTES),
        cost_estimate=pl.CostEstimate(flops=0, bytes_accessed=1_000_000, transcendentals=0),
        name="attend",
    )(qkv, planes, seg_row, conv)


def back_setup(slot, qkv_ref, seg_ref, out_ref, spread, gspread, proj):
    tiles = qkv_ref.shape[1] // TILE
    v_rows = slice(4 * HD + slot * HD, 5 * HD + slot * HD)
    v_out = slice(2 * HD, 3 * HD)

    def step(i, carry):
        lane = lanes_of(i, TILE)
        seg_row = seg_ref[:, lane]
        fill_spread(qkv_ref[v_rows, lane], seg_row, spread, lane)
        fill_member(seg_row, spread, lane)
        proj[:, lane] = jnp.zeros((2 * HD, TILE), F32)
        out_ref[v_out, lane] = jnp.zeros((HD, TILE), F32)
        return carry

    lax.fori_loop(0, tiles, step, 0)
    gspread[SPREAD:EXT, :] = jnp.zeros((128, TILE), BF16)


def back_unit(
    slot, unit, qkv_ref, planes_ref, seg_ref, grad_ref, numer_ref, dens_ref, sign_ref, bucket_ref,
    out_ref, spread, qprob, kprob, gspread, total, table, turned, gsign, proj,
):
    tiles = qkv_ref.shape[1] // TILE
    q_rows = slice(slot * HD, slot * HD + HD)
    k_rows = slice(2 * HD + slot * HD, 3 * HD + slot * HD)
    v_rows = slice(4 * HD + slot * HD, 5 * HD + slot * HD)
    v_out = slice(2 * HD, 3 * HD)
    total[...] = jnp.zeros_like(total)

    def first(i, carry):
        lane = lanes_of(i, TILE)
        seg_row = seg_ref[:, lane]
        density = dens_ref[:, lane]
        inverse = 1.0 / jnp.maximum(density, 1.0)
        est_grad = grad_ref[q_rows, lane].astype(F32) * (1.0 / TABLES)
        num_grad = (est_grad * inverse).astype(BF16)
        fill_spread(num_grad, seg_row, gspread, slice(0, TILE))
        inner_sum = jnp.sum(est_grad * numer_ref[:, lane], axis=0, keepdims=True)
        dens_grad = jnp.where(density > 1.0, -inner_sum * inverse * inverse, 0.0)
        which = lax.broadcasted_iota(jnp.int32, (8, TILE), 0)
        high, low = split_two(jnp.where(which == seg_row, dens_grad, 0.0))
        gspread[SPREAD : SPREAD + 32, :] = jnp.concatenate(
            (high, low, high, jnp.zeros_like(high)), axis=0
        ).astype(BF16)
        collected = nn_dot(bucket_ref[...], gspread[...])
        for part in range(TILE // LANES):
            inner = slice(part * LANES, (part + 1) * LANES)
            outer = pl.ds(pl.multiple_of(i * TILE + part * LANES, LANES), LANES)
            sign_q = sign_ref[0:8, outer]
            gsign[0:8, outer] = signs_back(sign_q, collected[:, inner])
        total[...] += nt_dot(gspread[0 : SPREAD + 16, :], qprob[...])
        return carry

    lax.fori_loop(0, tiles, first, 0)
    mass_grad = total[SPREAD : SPREAD + 8, :] + total[SPREAD + 8 : SPREAD + 16, :]
    high, low = split_two(mass_grad)
    extra = jnp.concatenate((high, low, jnp.zeros((112, CODES), F32)), axis=0)
    table[...] = total[0:SPREAD, :].astype(BF16)
    turned[:, 0:SPREAD] = jnp.transpose(total[0:SPREAD, :]).astype(BF16)
    turned[:, SPREAD:EXT] = jnp.transpose(extra).astype(BF16)

    planes = unit_planes(planes_ref[plane_rows(unit), :])
    plane_high, plane_low = split_two(planes)
    stack = jnp.concatenate((plane_high, plane_low, plane_high, jnp.zeros_like(plane_high)), axis=0)
    stack = stack.astype(BF16)

    def second(i, carry):
        lane = lanes_of(i, TILE)
        seg_row = seg_ref[:, lane]
        out_ref[v_out, lane] += masked_fold(nn_dot(table[...], kprob[...]), seg_row)
        collected = nn_dot(turned[...], spread[:, lane])
        for part in range(TILE // LANES):
            inner = slice(part * LANES, (part + 1) * LANES)
            outer = pl.ds(pl.multiple_of(i * TILE + part * LANES, LANES), LANES)
            gsign[8:16, outer] = signs_back(sign_ref[8:16, outer], collected[:, inner])
        signs = sign_ref[:, lane]
        flat = gsign[:, lane] * (1.0 - signs * signs)
        high, low = split_two(flat)
        for side in range(2):
            rows = slice(8 * side, 8 * side + 8)
            pieces = jnp.concatenate(
                (high[rows], high[rows], low[rows], jnp.zeros((8, TILE), F32)), axis=0
            ).astype(BF16)
            proj[side * HD : (side + 1) * HD, lane] += tn_dot(stack, pieces)
        return carry

    lax.fori_loop(0, tiles, second, 0)


def back_finish(slot, qkv_ref, out_ref, proj):
    tiles = qkv_ref.shape[1] // TILE
    q_rows = slice(slot * HD, slot * HD + HD)
    k_rows = slice(2 * HD + slot * HD, 3 * HD + slot * HD)

    def step(i, carry):
        lane = lanes_of(i, TILE)
        for side, rows in ((0, q_rows), (1, k_rows)):
            vec = qkv_ref[rows, lane].astype(F32)
            inverse = lax.rsqrt(jnp.sum(vec * vec, axis=0, keepdims=True) + 1e-06)
            unit_vec = vec * inverse
            grad = proj[side * HD : (side + 1) * HD, lane]
            along = jnp.sum(unit_vec * grad, axis=0, keepdims=True)
            out_ref[side * HD : (side + 1) * HD, lane] = math.sqrt(HD) * inverse * (grad - unit_vec * along)
        return carry

    lax.fori_loop(0, tiles, step, 0)


SPAN = 192
SHIFT = (KW - 1) // 2
OWN = 96
BLOCKS = ((0, HD), (HD, OWN))


def own_heads():
    m = lax.axis_index("mp")
    group = m // 2
    return (3 * group + 2 * (m % 2), 3 * group + 1)


def own_half():
    side = lax.axis_index("mp") % 2
    half = OWN - HD
    return side, half


def band_of(row):
    turned = jnp.broadcast_to(row, (LANES, 2 * LANES))
    index = lax.broadcasted_iota(jnp.int32, turned.shape, 0)
    for bit in range(7):
        moved = pltpu.roll(turned, 1 << bit, 1)
        turned = jnp.where((index >> bit) & 1 == 1, moved, turned)
    return jnp.transpose(turned)[0:SPAN]


def fill_hot(seg_ref, hot, hot_pad):
    length = seg_ref.shape[1]
    rows = lax.broadcasted_iota(jnp.int32, (16, length), 0)
    value = jnp.where(rows == seg_ref[...], 1.0, 0.0)
    value = jnp.where(rows < MAXSEG, value, 0.0).astype(BF16)
    hot[...] = value
    hot_pad[...] = jnp.zeros_like(hot_pad)
    hot_pad[:, SHIFT : SHIFT + length] = value


def band_product(rows, band):
    return nn_dot(rows, band.astype(BF16))


def conv_kernel(qkv_ref, taps_ref, seg_ref, out_ref, hot, hot_pad, pad, band):
    length = out_ref.shape[1]
    side, half = own_half()
    own = pl.ds(pl.multiple_of(HD + side * half, half), half)
    other = pl.ds(pl.multiple_of(HD + (1 - side) * half, half), half)
    fill_hot(seg_ref, hot, hot_pad)
    pad[...] = jnp.zeros_like(pad)
    pad[0:HD, SHIFT : SHIFT + length] = qkv_ref[4 * HD : 5 * HD, :]
    value_half = pl.ds(pl.multiple_of(5 * HD + side * half, half), half)
    pad[HD:OWN, SHIFT : SHIFT + length] = qkv_ref[value_half, :]
    for h, head in enumerate(own_heads()):
        band[h] = band_of(taps_ref[pl.ds(head, 1), :])
    out_ref[other, :] = jnp.zeros((half, length), F32)
    for i in range(length // LANES):
        lane = slice(i * LANES, (i + 1) * LANES)
        wide = slice(i * LANES, i * LANES + SPAN)
        mask = tn_dot(hot_pad[:, wide], hot[:, lane])
        out_ref[0:HD, lane] = band_product(pad[0:HD, wide], band[0] * mask)
        out_ref[own, lane] = band_product(pad[HD:OWN, wide], band[1] * mask)


def segment_conv(qkv, taps, seg_row):
    length = seg_row.shape[1]
    return pl.pallas_call(
        conv_kernel,
        out_shape=jax.ShapeDtypeStruct((2 * HD, length), F32),
        scratch_shapes=[
            pltpu.VMEM((16, length), BF16),
            pltpu.VMEM((16, length + LANES), BF16),
            pltpu.VMEM((OWN, length + LANES), BF16),
            pltpu.VMEM((2, SPAN, LANES), F32),
        ],
        compiler_params=pltpu.CompilerParams(vmem_limit_bytes=VMEM_BYTES),
        cost_estimate=pl.CostEstimate(flops=0, bytes_accessed=1_000_000, transcendentals=0),
        name="segment_conv",
    )(qkv, taps, seg_row)


def conv_back_kernel(
    qkv_ref, grad_ref, taps_ref, seg_ref, out_ref, tap_ref, hot, hot_pad, pad, gpad, band, corr
):
    length = seg_ref.shape[1]
    side, half = own_half()
    fill_hot(seg_ref, hot, hot_pad)
    pad[...] = jnp.zeros_like(pad)
    gpad[...] = jnp.zeros_like(gpad)
    inside = slice(SHIFT, SHIFT + length)
    value_half = pl.ds(pl.multiple_of(5 * HD + side * half, half), half)
    grad_half = pl.ds(pl.multiple_of(HD + side * half, half), half)
    pad[0:HD, inside] = qkv_ref[4 * HD : 5 * HD, :]
    pad[HD:OWN, inside] = qkv_ref[value_half, :]
    gpad[0:HD, inside] = grad_ref[0:HD, :]
    gpad[HD:OWN, inside] = grad_ref[grad_half, :]
    heads = own_heads()
    for h, head in enumerate(heads):
        band[h] = band_of(taps_ref[pl.ds(16 + head, 1), :])
    corr[...] = jnp.zeros_like(corr)
    for i in range(length // LANES):
        lane = slice(i * LANES, (i + 1) * LANES)
        wide = slice(i * LANES, i * LANES + SPAN)
        twice = slice(i * LANES, (i + 2) * LANES)
        mask = tn_dot(hot_pad[:, wide], hot[:, lane])
        turned = tn_dot(hot[:, lane], hot_pad[:, twice])
        grads = (grad_ref[0:HD, lane], grad_ref[grad_half, lane])
        for h, (low_row, high_row) in enumerate(BLOCKS):
            out_ref[low_row:high_row, lane] = band_product(
                gpad[low_row:high_row, wide], band[h] * mask
            )
            corr[h] += turned * tn_dot(grads[h], pad[low_row:high_row, twice])
    row = lax.broadcasted_iota(jnp.int32, (LANES, 2 * LANES), 0)
    place = lax.broadcasted_iota(jnp.int32, (8, LANES), 0)
    low_heads = jnp.zeros((8, LANES), F32)
    high_heads = jnp.zeros((8, LANES), F32)
    for h, head in enumerate(heads):
        skew = corr[h]
        for bit in range(7):
            moved = pltpu.roll(skew, 2 * LANES - (1 << bit), 1)
            skew = jnp.where((row >> bit) & 1 == 1, moved, skew)
        taps = jnp.sum(skew, axis=0, keepdims=True)[:, 0:LANES]
        low_heads = low_heads + jnp.where(place == head, taps, 0.0)
        high_heads = high_heads + jnp.where(place + 8 == head, taps, 0.0)
    tap_ref[:, 0:LANES] = low_heads
    tap_ref[:, LANES : 2 * LANES] = high_heads


def conv_back(qkv, grad, taps, seg_row):
    length = seg_row.shape[1]
    return pl.pallas_call(
        conv_back_kernel,
        out_shape=(
            jax.ShapeDtypeStruct((OWN, length), F32),
            jax.ShapeDtypeStruct((8, 2 * LANES), F32),
        ),
        scratch_shapes=[
            pltpu.VMEM((16, length), BF16),
            pltpu.VMEM((16, length + LANES), BF16),
            pltpu.VMEM((OWN, length + LANES), BF16),
            pltpu.VMEM((OWN, length + LANES), BF16),
            pltpu.VMEM((2, SPAN, LANES), F32),
            pltpu.VMEM((2, LANES, 2 * LANES), F32),
        ],
        compiler_params=pltpu.CompilerParams(vmem_limit_bytes=VMEM_BYTES),
        cost_estimate=pl.CostEstimate(flops=0, bytes_accessed=1_000_000, transcendentals=0),
        name="conv_back",
    )(qkv, grad, taps, seg_row)


def norm_rows(values):
    center = values - jnp.mean(values, axis=1, keepdims=True)
    inverse = lax.rsqrt(jnp.mean(center * center, axis=1, keepdims=True) + 1e-05)
    return center * inverse, inverse


def norm_back(upstream, normed, inverse, gain):
    scaled = upstream * gain
    inner = (
        scaled
        - jnp.mean(scaled, axis=1, keepdims=True)
        - normed * jnp.mean(scaled * normed, axis=1, keepdims=True)
    )
    return inner * inverse


def gelu_pair(value):
    cdf = 0.5 + 0.5 * lax.erf(value * math.sqrt(0.5))
    pdf = jnp.exp(-0.5 * value * value) * (1.0 / math.sqrt(2.0 * math.pi))
    return value * cdf, cdf + value * pdf


def column_sum(values):
    return jnp.sum(values, axis=0, keepdims=True)


MESH = pl.DeviceIdType.MESH
OFFSETS = (0, -2, 2, 4)
INVERSE = (0, 2, 1, 3, 4, 6, 5, 7)


def repeat(start, stop, action):
    def body(r, carry):
        action(r)
        return carry

    lax.fori_loop(start, stop, body, 0)


def remote(src, dst, send, recv, target):
    return pltpu.make_async_remote_copy(
        src_ref=src, dst_ref=dst, send_sem=send, recv_sem=recv,
        device_id={"mp": target}, device_id_type=MESH,
    )


def greet(targets):
    barrier = pltpu.get_barrier_semaphore()
    for target in targets:
        pl.semaphore_signal(barrier, inc=1, device_id={"mp": target}, device_id_type=MESH)
    pl.semaphore_wait(barrier, len(targets))


def gather_kernel(
    x_ref, query_ref, key_ref, value_ref, up_ref, down_ref, out_w_ref,
    all_ref, qkv_ref, block_ref, wide, send, recv,
):
    w_refs = (query_ref, key_ref, value_ref)
    count, rows, _ = all_ref.shape
    m = lax.axis_index("mp")
    side = m % 2
    sibling = m + 1 - 2 * side
    left = (m + count - 2) % count
    right = (m + 2) % count
    far = (m + 4) % count
    half = OWN - HD
    cut = rows // 2
    greet((left, right, sibling))

    def copy(n, src, dst, target):
        return remote(src, dst, send.at[n], recv.at[n], target)

    def piece(n, which):
        return pl.ds(pl.multiple_of(n * 2 * HD + HD + which * half, half), half)

    def weight_copy(n, which):
        source = w_refs[n].at[pl.ds(pl.multiple_of((1 - side) * HD, half), half), :]
        return copy(11 + n, source, wide.at[piece(n, which), :], sibling)

    low, high = slice(0, cut), slice(cut, rows)

    def own_copy(n, owner):
        part, target = ((low, right), (high, right), (high, left), (low, left))[n]
        return copy(n, x_ref.at[part], all_ref.at[owner, part], target)

    for n in range(3):
        weight_copy(n, side).start()
    for n in (0, 2, 1, 3):
        own_copy(n, m).start()
    to_sibling = copy(4, x_ref, all_ref.at[m], sibling)
    to_sibling.start()
    all_ref[m] = x_ref[...]
    for n in range(3):
        solo = pl.ds(pl.multiple_of(side * half, half), HD)
        own = pl.ds(pl.multiple_of((1 - side) * HD, half), half)
        wide[n * 2 * HD : n * 2 * HD + HD, :] = w_refs[n][solo, :]
        wide[piece(n, side), :] = w_refs[n][own, :]
    units = down_ref.shape[0]
    block_ref[0:units] = jnp.transpose(up_ref[...].astype(F32)).astype(BF16)
    block_ref[units : 2 * units] = down_ref[...]
    block_ref[2 * units : 2 * units + OWN] = out_w_ref[...]
    for n in range(3):
        weight_copy(n, 1 - side).wait_recv()

    def project(block):
        lane = pl.ds(pl.multiple_of(block * rows, rows), rows)
        qkv_ref[:, lane] = nt_dot(wide[...], all_ref[block]).astype(BF16)

    def pass_on(n, owner, part, target):
        return copy(n, all_ref.at[owner, part], all_ref.at[owner, part], target)

    project(m)
    own_copy(0, left).wait_recv()
    on_right = pass_on(5, left, low, right)
    on_right.start()
    own_copy(2, right).wait_recv()
    on_left = pass_on(6, right, high, left)
    on_left.start()
    copy(4, x_ref, all_ref.at[sibling], sibling).wait_recv()
    project(sibling)
    own_copy(1, left).wait_recv()
    over_left = copy(7, all_ref.at[left], all_ref.at[left], sibling)
    over_left.start()
    own_copy(3, right).wait_recv()
    over_right = copy(8, all_ref.at[right], all_ref.at[right], sibling)
    over_right.start()
    project(left)
    project(right)
    other_left = (sibling + count - 2) % count
    other_right = (sibling + 2) % count
    other_far = (sibling + 4) % count
    copy(7, x_ref, all_ref.at[other_left], sibling).wait_recv()
    project(other_left)
    copy(8, x_ref, all_ref.at[other_right], sibling).wait_recv()
    project(other_right)
    pass_on(5, far, low, left).wait_recv()
    over_low = pass_on(9, far, low, sibling)
    over_low.start()
    pass_on(6, far, high, right).wait_recv()
    over_high = pass_on(10, far, high, sibling)
    over_high.start()
    project(far)
    pass_on(9, other_far, low, sibling).wait_recv()
    pass_on(10, other_far, high, sibling).wait_recv()
    project(other_far)
    for n in range(3):
        weight_copy(n, side).wait_send()
    for n in range(4):
        own_copy(n, m).wait_send()
    for sent in (to_sibling, on_right, on_left, over_left, over_right, over_low, over_high):
        sent.wait_send()


def gather_qkv(x, w_rows, w_up, w_down, w_out, count):
    rows, width = x.shape
    vmem = pl.BlockSpec(memory_space=pltpu.VMEM)
    return pl.pallas_call(
        gather_kernel,
        in_specs=[vmem] * 7,
        out_specs=[vmem] * 3,
        out_shape=(
            jax.ShapeDtypeStruct((count, rows, width), BF16),
            jax.ShapeDtypeStruct((6 * HD, count * rows), BF16),
            jax.ShapeDtypeStruct((2 * w_down.shape[0] + OWN, width), BF16),
        ),
        scratch_shapes=[
            pltpu.VMEM((6 * HD, width), BF16),
            pltpu.SemaphoreType.DMA((14,)),
            pltpu.SemaphoreType.DMA((14,)),
        ],
        compiler_params=pltpu.CompilerParams(
            vmem_limit_bytes=VMEM_BYTES, collective_id=2, has_side_effects=True
        ),
        cost_estimate=pl.CostEstimate(
            flops=12 * HD * count * rows * width, bytes_accessed=30_000_000, transcendentals=0
        ),
        name="gather_qkv",
    )(x, *w_rows, w_up, w_down, w_out)


def around(m, count):
    sibling = m + 1 - 2 * (m % 2)
    return [(base + count + off) % count for base in (m, sibling) for off in OFFSETS]


def middle_kernel(
    sent_ref, x_ref, cot_ref, own_w, left_w, right_w, scale_ref,
    result_ref, lows_ref, left_ref, right_ref, one_ref, attn_ref, part_ref,
    wall, out_w, att_in, attn_out, slope, keep, acc,
    load, give_send, give_recv, rest_send, rest_recv, line_send, line_recv, far_send, far_recv,
    in_send, in_recv, out_send, out_recv, row_send, row_recv,
):
    rows = x_ref.shape[0]
    count = att_in.shape[0]
    units = slope.shape[2]
    both = 2 * units
    m = lax.axis_index("mp")
    devices = around(m, count)
    sibling = devices[4]
    greet(devices[1:])

    def tokens(index):
        return pl.ds(pl.multiple_of(index * rows, rows), rows)

    side = m % 2
    depth = wall.shape[1]
    blocks = (own_w, left_w, right_w)
    out_rows = slice(both, depth)
    ffn_rows = slice(0, both)
    parts = (slice(0, units), slice(units, both))

    middle_row = both + OWN // 2
    out_parts = (slice(both, middle_row), slice(middle_row, depth))

    def give(n):
        return remote(
            blocks[n].at[out_rows], wall.at[4 + n, out_rows], give_send.at[n], give_recv.at[n],
            sibling,
        )

    def out_along(n):
        return remote(
            blocks[1 + n].at[out_parts[n]], wall.at[3, out_parts[n]], give_send.at[3 + n],
            give_recv.at[3 + n], devices[2 - n],
        )

    def out_far(n):
        return remote(
            wall.at[3, out_parts[n]], wall.at[7, out_parts[n]], give_send.at[5 + n],
            give_recv.at[5 + n], sibling,
        )

    def rest(n):
        return remote(
            blocks[n].at[ffn_rows], wall.at[4 + n, ffn_rows], rest_send.at[n], rest_recv.at[n],
            sibling,
        )

    def along(n):
        return remote(
            blocks[1 + n].at[parts[n]], wall.at[3, parts[n]], line_send.at[n], line_recv.at[n],
            devices[2 - n],
        )

    def row_copy(k, n):
        place = (left_ref, right_ref)[n].at[k]
        return remote(
            lows_ref.at[k], place, row_send.at[k, n], row_recv.at[k, n], devices[2 - n]
        )

    def far_copy(n):
        return remote(
            wall.at[3, parts[n]], wall.at[7, parts[n]], far_send.at[n], far_recv.at[n], sibling
        )

    def loads():
        return [pltpu.make_async_copy(blocks[n], wall.at[n], load.at[n]) for n in range(3)]

    def att_copy(n, slot, sem):
        return remote(
            sent_ref.at[:, tokens(devices[n])], att_in.at[slot], in_send.at[n], in_recv.at[sem],
            devices[n],
        )

    def attn_copy(n, lane, sem):
        return remote(
            attn_out.at[n], attn_ref.at[:, tokens(lane)], out_send.at[n], out_recv.at[sem],
            devices[n],
        )

    for n in range(2):
        out_along(n).start()
    for n in range(1, count):
        att_copy(n, INVERSE[n], INVERSE[n]).start()
    for n in range(3):
        give(n).start()
    for copy in loads():
        copy.start()
    for n in range(3):
        rest(n).start()
    att_in[0] = sent_ref[:, tokens(m)]
    for copy in loads():
        copy.wait()
    for n in range(2):
        out_along(n).wait_recv()
        out_far(n).start()
    for n in range(3):
        give(n).wait_recv()
    for n in range(1, count):
        att_copy(n, n, n).wait_recv()
    for n in range(2):
        along(n).start()
    projected = None
    for n in range(4):
        if n == 3:
            for part in range(2):
                out_far(part).wait_recv()
        first, second = n + 4 * side, n + 4 * (1 - side)
        out_w[n, 0:OWN] = wall[first, out_rows]
        out_w[n, OWN : 2 * OWN] = wall[second, out_rows]
        shared = att_in[first, HD : 2 * HD].astype(F32) + att_in[second, HD : 2 * HD].astype(F32)
        features = jnp.concatenate(
            (att_in[first, 0:HD], shared.astype(BF16), att_in[second, 0:HD]), axis=0
        )
        piece = tn_dot(features, out_w[n])
        projected = piece if projected is None else projected + piece
    unit, inverse = norm_rows(x_ref[...].astype(F32) + projected)
    hidden = unit * scale_ref[0:1] + scale_ref[1:2]
    keep[0] = unit
    keep[1] = hidden
    lows_ref[0] = hidden.astype(BF16)
    acc[...] = jnp.zeros_like(acc)

    def forward(slots):
        low = lows_ref[0]
        total = acc[...]
        for slot in slots:
            active, lean = gelu_pair(nt_dot(low, wall[slot, 0:units]))
            slope[slot] = lean
            total = total + nn_dot(active.astype(BF16), wall[slot, units:both])
        acc[...] = total

    for n in range(3):
        rest(n).wait_recv()
    repeat(0, 3, lambda n: forward((n, 4 + n)))
    for n in range(2):
        along(n).wait_recv()
        far_copy(n).start()
    for n in range(2):
        row_copy(0, n).start()
    forward((3,))
    for n in range(2):
        far_copy(n).wait_recv()
    forward((7,))
    unit, inv = norm_rows(keep[1] + acc[...])
    result_ref[...] = (unit * scale_ref[2:3] + scale_ref[3:4]).astype(BF16)
    upstream = cot_ref[...].astype(F32)
    part_ref[2:3] = column_sum(upstream * unit)
    part_ref[3:4] = column_sum(upstream)
    grad = norm_back(upstream, unit, inv, scale_ref[2:3])
    keep[1] = grad
    lows_ref[1] = grad.astype(BF16)
    for n in range(2):
        row_copy(1, n).start()
    acc[...] = jnp.zeros_like(acc)

    def backward(i, carry):
        low = lows_ref[1]
        total = acc[...]
        for n in range(2):
            pre_grad = nt_dot(low, wall[2 * i + n, units:both]) * slope[2 * i + n]
            total = total + nn_dot(pre_grad.astype(BF16), wall[2 * i + n, 0:units])
        acc[...] = total
        return carry

    lax.fori_loop(0, 4, backward, 0)
    upstream = keep[1] + acc[...]
    unit = keep[0]
    part_ref[0:1] = column_sum(upstream * unit)
    part_ref[1:2] = column_sum(upstream)
    part_ref[4:8] = jnp.zeros((4, part_ref.shape[1]), F32)
    grad = norm_back(upstream, unit, inverse, scale_ref[0:1])
    one_ref[...] = grad
    low = grad.astype(BF16)
    lows_ref[2] = low
    for n in (3, 1, 2, 0):
        first, second = n + 4 * side, n + 4 * (1 - side)
        back = nt_dot(out_w[n], low).astype(BF16)
        attn_out[first] = back[0 : 2 * HD]
        attn_out[second, 0:HD] = back[2 * HD : 3 * HD]
        attn_out[second, HD : 2 * HD] = back[HD : 2 * HD]
        for slot in (n, 4 + n):
            if slot > 0:
                attn_copy(slot, m, INVERSE[slot]).start()
    attn_ref[:, tokens(m)] = attn_out[0]
    for n in range(1, count):
        attn_copy(n, devices[n], n).wait_recv()
    for k in range(2):
        for n in range(2):
            row_copy(k, n).wait_recv()
            row_copy(k, n).wait_send()
    for n in range(2):
        out_along(n).wait_send()
        out_far(n).wait_send()
    for n in range(3):
        give(n).wait_send()
        rest(n).wait_send()
    for n in range(2):
        along(n).wait_send()
        far_copy(n).wait_send()
    for n in range(1, count):
        att_copy(n, INVERSE[n], INVERSE[n]).wait_send()
        attn_copy(n, m, INVERSE[n]).wait_send()


def middle(sent, x, cot, blocks, scale, count):
    rows, width = x.shape
    depth = sent.shape[0]
    units = (blocks[0].shape[0] - OWN) // 2
    vmem = pl.BlockSpec(memory_space=pltpu.VMEM)
    sems = lambda n: pltpu.SemaphoreType.DMA((n,))
    return pl.pallas_call(
        middle_kernel,
        in_specs=[vmem] * 3 + [pl.BlockSpec(memory_space=pl.ANY)] * 3 + [vmem],
        out_specs=[vmem] * 7,
        out_shape=(
            jax.ShapeDtypeStruct((rows, width), BF16),
            jax.ShapeDtypeStruct((3, rows, width), BF16),
            jax.ShapeDtypeStruct((2, rows, width), BF16),
            jax.ShapeDtypeStruct((2, rows, width), BF16),
            jax.ShapeDtypeStruct((rows, width), F32),
            jax.ShapeDtypeStruct(sent.shape, BF16),
            jax.ShapeDtypeStruct((8, width), F32),
        ),
        scratch_shapes=[
            pltpu.VMEM((count,) + blocks[0].shape, BF16),
            pltpu.VMEM((count // 2, 2 * OWN, width), BF16),
            pltpu.VMEM((count, depth, rows), BF16),
            pltpu.VMEM((count, depth, rows), BF16),
            pltpu.VMEM((count, rows, units), F32),
            pltpu.VMEM((2, rows, width), F32),
            pltpu.VMEM((rows, width), F32),
            sems(3), sems(7), sems(7), sems(3), sems(3), sems(2), sems(2), sems(2), sems(2),
            sems(count), sems(count), sems(count), sems(count),
            pltpu.SemaphoreType.DMA((2, 2)), pltpu.SemaphoreType.DMA((2, 2)),
        ],
        compiler_params=pltpu.CompilerParams(
            vmem_limit_bytes=VMEM_BYTES, collective_id=1, has_side_effects=True
        ),
        cost_estimate=pl.CostEstimate(
            flops=16 * rows * width * count * units, bytes_accessed=26_000_000,
            transcendentals=0,
        ),
        name="middle",
    )(sent, x, cot, *blocks, scale)


def close_kernel(
    own_x, left_x, right_x, numer_any, dens_any, sign_any, bucket_any, query_any, key_any,
    conv_any, all_any, w_any, one_any,
    sent_ref, wq_ref, wk_ref, wv_ref, norm_ref, tap_ref, qkv_ref, planes_ref, seg_ref, grad_ref,
    inputs_ref, up_ref, down_ref, out_ref, query_ref, key_ref, value_ref, tiny_ref, taps_ref,
    conv_ref, all_ref, w_ref, one_ref, w_all, half_in,
    wall, acc, solo_low, half_low, w_solo, w_half, attended, swap_out, swap_in, part_out, part_own, pair_in, stage,
    line_in, a_refs, b_refs, d_refs, l_refs, near_in, far_in,
    back_out, numer, dens, sign, bucket, qprob, kprob,
    spread, gspread, total_ref, table, turned, gsign, proj,
    load, fetch_sem, give_send, give_recv, along_send, along_recv, over_send, over_recv,
    row_send, row_recv, wa_send, wa_recv, half_send, half_recv,
    swap_send, swap_recv, pair_send, pair_recv, line_send, line_recv,
    a_sems, b_sems, d_sems,
    l_sems,
    near_send, near_recv, far_sems,
):
    edge = far_in.shape[1]
    count, _, rows, width = wall.shape
    chips = count // 2
    units = down_ref.shape[0]
    d = lax.axis_index("dp")
    m = lax.axis_index("mp")
    side = m % 2
    chip = m // 2
    half = OWN - HD
    cut = rows // 2
    devices = around(m, count)
    sibling = devices[4]

    barrier = pltpu.get_barrier_semaphore()
    place_x, place_y = d % edge, d // edge
    for k in range(1, edge):
        for peer in (
            place_y * edge + (place_x + k) % edge, (place_y + k) % edge * edge + place_x
        ):
            pl.semaphore_signal(barrier, inc=1, device_id={"dp": peer}, device_id_type=MESH)
    repeat(
        1, count,
        lambda r: pl.semaphore_signal(
            barrier, inc=1, device_id={"mp": (m + r) % count}, device_id_type=MESH
        ),
    )
    pl.semaphore_wait(barrier, 2 * (edge - 1) + count - 1)

    def tokens(index):
        return pl.ds(pl.multiple_of(index * rows, rows), rows)

    parts = (slice(0, cut), slice(cut, rows))
    pair = slice(0, 2)
    sources = (own_x.at[pair], left_x, right_x)

    def give(n):
        return remote(
            sources[n], wall.at[4 + n, pair], give_send.at[n], give_recv.at[n], sibling
        )

    def along(n):
        return remote(
            sources[1 + n].at[:, parts[n]], wall.at[3, pair, parts[n]], along_send.at[n],
            along_recv.at[n], devices[2 - n],
        )

    def over(n):
        return remote(
            wall.at[3, pair, parts[n]], wall.at[7, pair, parts[n]], over_send.at[n],
            over_recv.at[n], sibling,
        )

    def row_copy(n):
        if n < 3:
            source, slot, target = own_x.at[2], n + 1, devices[2 - n]
            if n == 2:
                slot, target = 4, sibling
            place = wall.at[slot, 2]
        elif n < 5:
            source, place, target = wall.at[n - 2, 2], wall.at[n + 2, 2], sibling
        elif n < 7:
            piece = parts[n - 5]
            source, place = wall.at[n - 4, 2, piece], wall.at[3, 2, piece]
            target = devices[7 - n]
        else:
            piece = parts[n - 7]
            source, place, target = wall.at[3, 2, piece], wall.at[7, 2, piece], sibling
        return remote(source, place, row_send.at[n], row_recv.at[n], target)

    def loads():
        copies = [pltpu.make_async_copy(own_x, wall.at[0], load.at[0])]
        for n in range(1, 3):
            copies.append(pltpu.make_async_copy(sources[n], wall.at[n, pair], load.at[n]))
        pairs = ((w_any, w_ref), (conv_any, conv_ref), (all_any, all_ref), (one_any, one_ref))
        for n, (source, target) in enumerate(pairs):
            copies.append(pltpu.make_async_copy(source, target, load.at[3 + n]))
        return copies

    def w_copy(n, slot):
        return remote(w_half, w_all.at[slot], wa_send.at[n], wa_recv.at[slot], devices[n])

    def half_copy(n, slot):
        return remote(
            half_low.at[:, tokens(devices[n])], half_in.at[slot], half_send.at[n],
            half_recv.at[slot], devices[n],
        )

    def fetch(unit):
        place = unit % 2
        return [
            pltpu.make_async_copy(source.at[unit], target.at[place], fetch_sem.at[place, n])
            for n, (source, target) in enumerate(
                (
                    (numer_any, numer), (dens_any, dens), (sign_any, sign), (bucket_any, bucket),
                    (query_any, qprob), (key_any, kprob),
                )
            )
        ]

    def near_copy(r, owner):
        return remote(
            near_in.at[m], near_in.at[owner], near_send.at[r], near_recv.at[r], (m + r) % count
        )

    def swap(n):
        piece = slice(0, half) if n == 0 else slice(half, 4 * half)
        return remote(
            swap_out.at[piece], swap_in.at[piece], swap_send.at[n], swap_recv.at[n], sibling
        )

    for n in range(2):
        along(n).start()
    swap_out[0:half] = sent_ref[pl.ds(pl.multiple_of(HD + (1 - side) * half, half), half), :]
    swap(0).start()
    for n in range(3):
        give(n).start()
    for copy in fetch(0) + loads():
        copy.start()
    for n in range(3):
        row_copy(n).start()
    near_in[m, :, 0:width] = norm_ref[...]
    near_in[m, :, width : width + 2 * LANES] = tap_ref[...]
    repeat(1, count, lambda r: near_copy(r, m).start())
    solo_at = lambda n: pl.ds(pl.multiple_of(n * OWN + side * half, half), HD)
    half_at = lambda n: pl.ds(pl.multiple_of(n * OWN + (1 - side) * HD, half), half)
    sent_half = sent_ref[pl.ds(pl.multiple_of(HD + side * half, half), half), :]
    attended[solo_at(0), :] = sent_ref[0:HD, :]
    acc[...] = jnp.zeros_like(acc)
    swap(0).wait_recv()
    attended[half_at(0), :] = (
        sent_half.astype(F32) + swap_in[0:half].astype(F32)
    ).astype(BF16)
    def step(slots):
        sums = [None] * 2
        for slot in slots:
            hidden, ffn = wall[slot, 0], wall[slot, 1]
            active, lean = gelu_pair(nt_dot(hidden, w_ref[0:units]))
            grad = nt_dot(ffn, w_ref[units : 2 * units]) * lean
            terms = (
                tn_dot(grad.astype(BF16), hidden),
                tn_dot(active.astype(BF16), ffn),
            )
            sums = [p if t is None else t + p for t, p in zip(sums, terms)]
        acc[0:units, :] += sums[0]
        acc[units : 2 * units, :] += sums[1]

    def staged(along_x, refs, sems):
        grads, first_in, mid, second_in, sums = refs
        u, v = (d % edge, d // edge) if along_x else (d // edge, d % edge)

        def copy(n, src, dst, k):
            du, dv = ((u + k) % edge, v) if n in (0, 3) else (u, (v + k) % edge)
            target = dv * edge + du if along_x else du * edge + dv
            return pltpu.make_async_remote_copy(
                src_ref=src, dst_ref=dst, send_sem=sems.at[2 * n, k], recv_sem=sems.at[2 * n + 1, k],
                device_id={"dp": target}, device_id_type=MESH,
            )

        around_edge = range(1, edge)
        out_copy = lambda k: copy(0, grads.at[(u + k) % edge], first_in.at[k], k)
        mid_copy = lambda k: copy(1, mid.at[(v + k) % edge], second_in.at[k], k)
        back_copy = lambda k, owner: copy(2, sums.at[u, v], sums.at[u, owner], k)
        wide_copy = lambda k, owner: copy(3, sums.at[u], sums.at[owner], k)

        def start():
            for k in around_edge:
                out_copy(k).start()

        def half_reduce():
            for k in around_edge:
                out_copy(k).wait_recv()
            for n in range(edge):
                value = grads[u, n].astype(F32)
                for k in around_edge:
                    value = value + first_in[k, n].astype(F32)
                mid[n] = value.astype(BF16)
            for k in around_edge:
                mid_copy(k).start()

        def reduce():
            for k in around_edge:
                mid_copy(k).wait_recv()
            value = mid[v].astype(F32)
            for k in around_edge:
                value = value + second_in[k].astype(F32)
            sums[u, v] = value.astype(BF16)
            for k in around_edge:
                back_copy(k, v).start()

        def spread():
            for k in around_edge:
                back_copy(k, (v + edge - k) % edge).wait_recv()
            for k in around_edge:
                wide_copy(k, u).start()

        def finish():
            for k in around_edge:
                wide_copy(k, (u + edge - k) % edge).wait_recv()
            for k in around_edge:
                out_copy(k).wait_send()
                mid_copy(k).wait_send()
                back_copy(k, v).wait_send()
                wide_copy(k, u).wait_send()

        def put(value):
            size = grads.shape[2]
            for n in range(edge * edge):
                grads[n // edge, n % edge] = value[n * size : (n + 1) * size].astype(BF16)

        def whole():
            return jnp.concatenate(
                [sums[n // edge, n % edge].astype(F32) for n in range(edge * edge)], axis=0
            )

        return start, half_reduce, reduce, spread, finish, put, whole

    a_start, a_half, a_reduce, a_spread, a_finish, a_put, a_whole = staged(True, a_refs, a_sems)
    b_start, b_half, b_reduce, b_spread, b_finish, b_put, b_whole = staged(True, b_refs, b_sems)
    d_start, d_half, d_reduce, d_spread, d_finish, d_put, d_whole = staged(False, d_refs, d_sems)
    l_start, l_half, l_reduce, l_spread, l_finish, l_put, l_whole = staged(False, l_refs, l_sems)

    def far_copy(n, k, owner):
        target = (
            place_y * edge + (place_x + k) % edge if n == 0
            else (place_y + k) % edge * edge + place_x
        )
        mine = (place_x, place_y)[n]
        return pltpu.make_async_remote_copy(
            src_ref=far_in.at[n, mine], dst_ref=far_in.at[n, owner],
            send_sem=far_sems.at[2 * n, k], recv_sem=far_sems.at[2 * n + 1, k],
            device_id={"dp": target}, device_id_type=MESH,
        )

    def far_start(n, value):
        mine = (place_x, place_y)[n]
        far_in[n, mine] = value
        for k in range(1, edge):
            far_copy(n, k, mine).start()

    def far_sum(n):
        mine = (place_x, place_y)[n]
        for k in range(1, edge):
            far_copy(n, k, (mine + edge - k) % edge).wait_recv()
        value = far_in[n, 0]
        for k in range(1, edge):
            value = value + far_in[n, k]
        for k in range(1, edge):
            far_copy(n, k, mine).wait_send()
        return value

    def attention(slot, low, high):
        back_setup(slot, qkv_ref, seg_ref, back_out, spread, gspread, proj)

        def one_unit(unit):
            for copy in fetch(unit):
                copy.wait()

            @pl.when(unit < UNITS - 1)
            def _():
                for copy in fetch(unit + 1):
                    copy.start()

            if slot == 0:
                @pl.when(unit == 2)
                def _():
                    for n in range(3):
                        row_copy(n).wait_recv()
                    for n in range(3, 7):
                        row_copy(n).start()
                    for n in range(2):
                        along(n).wait_recv()
                        over(n).start()

                @pl.when(unit == 3)
                def _():
                    for n in range(5, 7):
                        row_copy(n).wait_recv()
                    for n in range(7, 9):
                        row_copy(n).start()
            else:
                @pl.when(unit == UNITS - 1)
                def _():
                    b_reduce()
                    d_reduce()
                    a_half()

            place = unit % 2
            back_unit(
                slot, unit, qkv_ref, planes_ref, seg_ref, grad_ref,
                numer.at[place], dens.at[place], sign.at[place], bucket.at[place], back_out,
                spread, qprob.at[place], kprob.at[place], gspread, total_ref, table, turned, gsign, proj,
            )

        repeat(low, high, one_unit)
        back_finish(slot, qkv_ref, back_out, proj)

    for n in range(3):
        w_ref_n = (wq_ref, wk_ref, wv_ref)[n]
        w_solo[n * HD : (n + 1) * HD] = w_ref_n[solo_at(0), :]
        w_half[n * half : (n + 1) * half] = w_ref_n[half_at(0), :]
    w_all[0] = w_half[...]
    attention(0, 0, SOLO)
    for n in range(1, count):
        w_copy(n, INVERSE[n]).start()
    for copy in loads():
        copy.wait()
    for n in range(3):
        solo = back_out[n * HD : (n + 1) * HD, :]
        if n == 2:
            solo = solo + conv_ref[0:HD, :]
        solo_low[n * HD : (n + 1) * HD, :] = solo.astype(BF16)

    def pair_copy(target):
        return remote(
            part_out.at[target], pair_in.at[target], pair_send.at[target], pair_recv.at[target],
            sibling,
        )

    def input_part(device):
        lane = tokens(device)
        return tn_dot(solo_low[:, lane], w_solo[...])

    def line_copy(k):
        return remote(
            stage.at[k], line_in.at[k], line_send.at[k], line_recv.at[k], (m + 2 * k) % count
        )

    order = [2, 1, 3, 0]
    for k in order:
        target = (chip + k) % chips
        part_out[target] = input_part(2 * target + 1 - side).astype(BF16)
        pair_copy(target).start()
    for n in range(3):
        give(n).wait_recv()
    for n in range(2):
        over(n).wait_recv()
    repeat(0, 4, lambda i: step((2 * i, 2 * i + 1)))
    b_put(acc[0:units])
    d_put(acc[units : 2 * units])
    b_start()
    d_start()
    for k in order[:3]:
        target = (chip + k) % chips
        mine = input_part(2 * target + side)
        pair_copy(target).wait_recv()
        stage[k] = (mine + pair_in[target].astype(F32)).astype(BF16)
        line_copy(k).start()
    part_own[...] = input_part(m)
    solo_grad = nn_dot(solo_low[...], all_ref[...])
    for n in (3, 4, 7, 8):
        row_copy(n).wait_recv()
    out_grad = None
    for slot in range(count):
        term = nn_dot(attended[:, tokens(devices[slot])], wall[slot, 2])
        out_grad = term if out_grad is None else out_grad + term
    a_put(jnp.concatenate((out_grad, solo_grad), axis=0))
    b_half()
    d_half()
    a_start()
    repeat(1, count, lambda r: near_copy(r, (m + count - r) % count).wait_recv())
    total = near_in[0]
    for r in range(1, count):
        total = total + near_in[r]
    far_start(0, total)
    attention(1, SOLO, UNITS)

    for n in range(3):
        start = pl.multiple_of(n * HD + (1 - side) * half, half)
        swap_out[(n + 1) * half : (n + 2) * half] = back_out[pl.ds(start, half), :].astype(BF16)
    swap(1).start()
    b_spread()
    d_spread()
    a_reduce()
    swap(1).wait_recv()
    for n in range(3):
        mine = back_out[pl.ds(pl.multiple_of(n * HD + side * half, half), half), :]
        mixed = mine + swap_in[(n + 1) * half : (n + 2) * half].astype(F32)
        if n == 2:
            mixed = mixed + conv_ref[HD:OWN, :]
        half_low[n * half : (n + 1) * half] = mixed.astype(BF16)
    for n in range(1, count):
        half_copy(n, INVERSE[n]).start()
    half_in[0] = half_low[:, tokens(m)]
    half_grad = nn_dot(half_low[...], all_ref[...])
    l_put(half_grad)
    l_start()
    a_spread()
    far_start(1, far_sum(0))
    l_half()
    pair_copy(chip).wait_recv()
    total = one_ref[...] + part_own[...] + pair_in[chip].astype(F32)
    for k in range(1, chips):
        line_copy(k).wait_recv()
        total = total + line_in[k].astype(F32)
    for n in range(1, count):
        w_copy(n, n).wait_recv()
        half_copy(n, n).wait_recv()
    late = tn_dot(
        half_in[...].reshape(count * OWN, rows), w_all[...].reshape(count * OWN, width)
    )
    inputs_ref[...] = total + late
    l_reduce()
    total = far_sum(1)
    tiny_ref[...] = total[:, 0:width]
    taps_ref[0:8] = total[:, width : width + LANES]
    taps_ref[8:16] = total[:, width + LANES : width + 2 * LANES]
    b_finish()
    up_ref[...] = jnp.transpose(b_whole()).astype(BF16)
    l_spread()
    d_finish()
    down_ref[...] = d_whole().astype(BF16)
    a_finish()
    whole = a_whole().astype(BF16)
    out_ref[...] = whole[0:OWN]
    outs = (query_ref, key_ref, value_ref)
    for n, ref in enumerate(outs):
        ref[solo_at(0), :] = whole[OWN + n * HD : OWN + (n + 1) * HD]
    l_finish()
    whole = l_whole().astype(BF16)
    for n, ref in enumerate(outs):
        ref[half_at(0), :] = whole[n * half : (n + 1) * half]

    for n in range(1, count):
        w_copy(n, INVERSE[n]).wait_send()
        half_copy(n, INVERSE[n]).wait_send()
    for n in range(2):
        swap(n).wait_send()
        along(n).wait_send()
        over(n).wait_send()
    for n in range(3):
        give(n).wait_send()
    for n in range(9):
        row_copy(n).wait_send()
    for k in range(chips):
        pair_copy((chip + k) % chips).wait_send()
    for k in range(1, chips):
        line_copy(k).wait_send()
    repeat(1, count, lambda r: near_copy(r, m).wait_send())


def close(blocks_x, saved, conv, sent, gathered, w_rows, block_w, one, norms, taps,
          qkv, planes, seg_row, grad, blocks):
    rows, width = one.shape
    length = sent.shape[1]
    count = length // rows
    chips = count // 2
    units = (block_w.shape[0] - OWN) // 2
    depth = (OWN + 3 * HD) // blocks
    thin = OWN // blocks
    high = units // blocks
    edge = 4
    lanes = width + 2 * LANES
    vmem = pl.BlockSpec(memory_space=pltpu.VMEM)
    sems = lambda *n: pltpu.SemaphoreType.DMA(n)
    low = lambda *shape: jax.ShapeDtypeStruct(shape, BF16)
    by_edge = lambda n: (
        pltpu.VMEM((edge, edge, n, width), BF16),
        pltpu.VMEM((edge, edge, n, width), BF16),
        pltpu.VMEM((edge, n, width), BF16),
        pltpu.VMEM((edge, n, width), BF16),
        pltpu.VMEM((edge, edge, n, width), BF16),
    )
    by_chip = pltpu.VMEM((chips, rows, width), BF16)
    return pl.pallas_call(
        close_kernel,
        in_specs=[pl.BlockSpec(memory_space=pl.ANY)] * 13 + [vmem] * 10,
        out_specs=[vmem] * 9,
        out_shape=(
            jax.ShapeDtypeStruct(one.shape, F32),
            low(width, units), low(units, width), low(OWN, width),
            low(OWN, width), low(OWN, width), low(OWN, width),
            jax.ShapeDtypeStruct((8, width), F32),
            jax.ShapeDtypeStruct((16, LANES), F32),
        ),
        scratch_shapes=[
            pltpu.VMEM(conv.shape, F32),
            pltpu.VMEM(gathered.shape, BF16),
            pltpu.VMEM(block_w.shape, BF16),
            pltpu.VMEM(one.shape, F32),
            pltpu.VMEM((count, OWN, width), BF16),
            pltpu.VMEM((count, OWN, rows), BF16),
            pltpu.VMEM((count, 3, rows, width), BF16),
            pltpu.VMEM((2 * units, width), F32),
            pltpu.VMEM((3 * HD, length), BF16),
            pltpu.VMEM((OWN, length), BF16),
            pltpu.VMEM((3 * HD, width), BF16),
            pltpu.VMEM((OWN, width), BF16),
            pltpu.VMEM((OWN, length), BF16),
            pltpu.VMEM((2 * HD, length), BF16),
            pltpu.VMEM((2 * HD, length), BF16),
            by_chip,
            pltpu.VMEM((rows, width), F32),
            by_chip, by_chip, by_chip,
            by_edge(depth), by_edge(high), by_edge(high),
            by_edge(thin),
            pltpu.VMEM((count, 8, lanes), F32),
            pltpu.VMEM((2, edge, 8, lanes), F32),
            pltpu.VMEM((3 * HD, length), F32),
            pltpu.VMEM((2, HD, length), F32),
            pltpu.VMEM((2, 1, length), F32),
            pltpu.VMEM((2, 16, length), F32),
            pltpu.VMEM((2, CODES, EXT), BF16),
            pltpu.VMEM((2, CODES, length), BF16),
            pltpu.VMEM((2, CODES, length), BF16),
            pltpu.VMEM((EXT, length), BF16),
            pltpu.VMEM((EXT, TILE), BF16),
            pltpu.VMEM((SPREAD + 16, CODES), F32),
            pltpu.VMEM((SPREAD, CODES), BF16),
            pltpu.VMEM((CODES, EXT), BF16),
            pltpu.VMEM((16, length), F32),
            pltpu.VMEM((2 * HD, length), F32),
            sems(7), sems(2, 6), sems(3), sems(3), sems(2), sems(2), sems(2), sems(2),
            sems(9), sems(9), sems(count), sems(count), sems(count), sems(count),
            sems(2), sems(2), sems(4), sems(4), sems(4), sems(4),
            sems(8, edge), sems(8, edge), sems(8, edge), sems(8, edge),
            sems(count), sems(count), sems(4, edge),
        ],
        compiler_params=pltpu.CompilerParams(
            vmem_limit_bytes=CLOSE_BYTES, collective_id=0, has_side_effects=True
        ),
        cost_estimate=pl.CostEstimate(flops=0, bytes_accessed=30_000_000, transcendentals=0),
        name="close",
    )(*blocks_x, *saved, conv, gathered, block_w, one, sent, *w_rows, norms, taps,
      qkv, planes, seg_row, grad)


def shifted(block, off):
    count = lax.axis_size("mp")
    return lax.ppermute(block, "mp", [(n, (n - off) % count) for n in range(count)])


def on_device(
    inputs, segment, w_query, w_key, w_value, planes, conv_taps, w_out,
    ln1_gain, ln1_bias, w_up, w_down, ln2_gain, ln2_bias, cotangent,
):
    count = lax.axis_size("mp")
    blocks = lax.axis_size("dp")
    rows, width = inputs.shape
    w_rows = (w_query.T, w_key.T, w_value.T)
    gathered, qkv, block_w = gather_qkv(inputs, w_rows, w_up, w_down, w_out, count)
    left_w, right_w = shifted(block_w, -2), shifted(block_w, 2)
    gathered = gathered.reshape(rows * count, width)
    seg_row = segment[None, :]
    taps = jnp.pad(
        jnp.concatenate(
            (
                jnp.pad(conv_taps, ((0, 0), (0, 16 - HEADS))),
                jnp.pad(conv_taps[::-1], ((0, 0), (0, 16 - HEADS))),
            ),
            1,
        ),
        ((0, 2 * LANES - KW), (0, 0)),
    ).T
    conv = segment_conv(qkv, taps, seg_row)
    sent, *saved = attend(qkv, planes, seg_row, conv)
    scale = jnp.stack((ln1_gain, ln1_bias, ln2_gain, ln2_bias) * 2)
    outputs, lows, left_x, right_x, one_grad, attn_grad, norm_part = middle(
        sent, inputs, cotangent, (block_w, left_w, right_w), scale, count
    )
    value_conv, tap_part = conv_back(qkv, attn_grad, taps, seg_row)
    inputs_grad, up, down, out, query, key, value, tiny, conv_rows = close(
        (lows, left_x, right_x), saved, value_conv, sent, gathered, w_rows,
        block_w, one_grad, norm_part, tap_part, qkv, planes, seg_row, attn_grad, blocks,
    )
    return (
        outputs, inputs_grad, query.astype(F32).T, key.astype(F32).T, value.astype(F32).T,
        conv_rows[:HEADS, :KW].T, out.astype(F32), tiny[0], tiny[1],
        up.astype(F32), down.astype(F32), tiny[2], tiny[3],
    )


def solution(mesh):
    rows = P(("dp", "mp"), None)
    cols = P(None, "mp")
    return jax.shard_map(
        on_device,
        mesh=mesh,
        in_specs=(
            rows, P("dp"), cols, cols, cols, P(), P(), P("mp", None), P(), P(),
            cols, P("mp", None), P(), P(), rows,
        ),
        out_specs=(
            rows, rows, cols, cols, cols, P(), P("mp", None), P(), P(),
            cols, P("mp", None), P(), P(),
        ),
        check_vma=False,
    )
```

```python
import math
import jax
import jax.numpy as jnp
from jax import lax
from jax.experimental import pallas as pl
from jax.experimental.pallas import tpu as pltpu
from jax.sharding import PartitionSpec as P

HEADS = 12
HD = 64
TABLES = 4
BITS = 8
KW = 65
MAXSEG = 8
CODES = 256
UNITS = 6
SOLO = 4
SPREAD = MAXSEG * HD
EXT = SPREAD + 128
LANES = 128
TILE = 2048
F32 = jnp.float32
BF16 = jnp.bfloat16
VMEM_BYTES = 56 * 1024 * 1024
CLOSE_BYTES = 60 * 1024 * 1024


def nt_dot(left, right):
    return lax.dot_general(left, right, (((1,), (1,)), ((), ())), preferred_element_type=F32)


def tn_dot(left, right):
    return lax.dot_general(left, right, (((0,), (0,)), ((), ())), preferred_element_type=F32)


def nn_dot(left, right):
    return lax.dot_general(left, right, (((1,), (0,)), ((), ())), preferred_element_type=F32)


def half_sign(bit):
    rows = lax.broadcasted_iota(jnp.int32, (8, LANES), 0)
    return jnp.where((rows >> bit) & 1 == 0, 0.5, -0.5).astype(F32)


def code_factors(signs):
    pos0, neg0 = 0.5 + 0.5 * signs[0:1], 0.5 - 0.5 * signs[0:1]
    pos1, neg1 = 0.5 + 0.5 * signs[1:2], 0.5 - 0.5 * signs[1:2]
    tops = (pos0 * pos1, pos0 * neg1, neg0 * pos1, neg0 * neg1)
    picks = [half_sign(2), half_sign(1), half_sign(0)]
    mids = [0.5 + picks[n] * signs[2 + n : 3 + n] for n in range(3)]
    lows = [0.5 + picks[n] * signs[5 + n : 6 + n] for n in range(3)]
    return tops, mids, lows, picks


def code_probs(signs, out_ref, lane):
    tops, mids, lows, _ = code_factors(signs)
    mid = mids[0] * mids[1] * mids[2]
    low = lows[0] * lows[1] * lows[2]
    for top_index in range(4):
        low_top = low * tops[top_index]
        for pair in range(4):
            rows = jnp.concatenate(
                (
                    low_top * mid[2 * pair : 2 * pair + 1],
                    low_top * mid[2 * pair + 1 : 2 * pair + 2],
                ),
                axis=0,
            )
            first = top_index * 64 + pair * 16
            out_ref[first : first + 16, lane] = rows.astype(BF16)


def signs_back(signs, grads):
    tops, mids, lows, picks = code_factors(signs)
    mid = mids[0] * mids[1] * mids[2]
    low = lows[0] * lows[1] * lows[2]
    mid_rows = [jnp.broadcast_to(mid[m : m + 1], (8, LANES)) for m in range(8)]
    top_rows = [jnp.broadcast_to(tops[t], (8, LANES)) for t in range(4)]
    by_top = [None] * 4
    by_mid = [None] * 8
    for t in range(4):
        for m in range(8):
            piece = grads[t * 64 + m * 8 : t * 64 + m * 8 + 8]
            a = piece * mid_rows[m]
            b = piece * top_rows[t]
            by_top[t] = a if by_top[t] is None else by_top[t] + a
            by_mid[m] = b if by_mid[m] is None else by_mid[m] + b
    low_grad = by_top[0] * top_rows[0]
    for t in range(1, 4):
        low_grad = low_grad + by_top[t] * top_rows[t]
    top_grad = [jnp.sum(low * by_top[t], axis=0, keepdims=True) for t in range(4)]
    mid_grad = jnp.concatenate(
        [jnp.sum(low * by_mid[m], axis=0, keepdims=True) for m in range(8)], axis=0
    )
    pos0, neg0 = 0.5 + 0.5 * signs[0:1], 0.5 - 0.5 * signs[0:1]
    pos1, neg1 = 0.5 + 0.5 * signs[1:2], 0.5 - 0.5 * signs[1:2]
    out = [
        0.5 * ((top_grad[0] - top_grad[2]) * pos1 + (top_grad[1] - top_grad[3]) * neg1),
        0.5 * ((top_grad[0] - top_grad[1]) * pos0 + (top_grad[2] - top_grad[3]) * neg0),
    ]
    for grad, parts in ((mid_grad, mids), (low_grad, lows)):
        for n in range(3):
            others = parts[(n + 1) % 3] * parts[(n + 2) % 3] * picks[n]
            out.append(jnp.sum(grad * others, axis=0, keepdims=True))
    return jnp.concatenate(out, axis=0)


def split_two(value):
    high = value.astype(BF16).astype(F32)
    return high, value - high


def unit_planes(planes):
    return planes * lax.rsqrt(jnp.sum(planes * planes, axis=1, keepdims=True) + 1e-06)


def fill_spread(values, seg_row, spread_ref, lane):
    for s in range(MAXSEG):
        spread_ref[s * HD : (s + 1) * HD, lane] = jnp.where(
            seg_row == s, values, jnp.zeros_like(values)
        )


def fill_member(seg_row, spread_ref, lane):
    width = seg_row.shape[1]
    rows = lax.broadcasted_iota(jnp.int32, (128, width), 0)
    hit = jnp.logical_and(rows < 16, (rows & 7) == seg_row)
    spread_ref[SPREAD:EXT, lane] = jnp.where(hit, 1.0, 0.0).astype(BF16)


def plane_rows(unit):
    side = lax.axis_index("mp") % 2
    row = jnp.where(unit < SOLO, unit, 2 * side + unit - SOLO)
    return pl.ds(pl.multiple_of(row * BITS, BITS), BITS)


def lanes_of(index, width):
    return pl.ds(pl.multiple_of(index * width, width), width)


def masked_fold(product, seg_row):
    total = None
    for s in range(MAXSEG):
        piece = jnp.where(seg_row == s, product[s * HD : (s + 1) * HD], 0.0)
        total = piece if total is None else total + piece
    return total


def attend_kernel(
    qkv_ref, planes_ref, seg_ref, conv_ref,
    sent_ref, numer_ref, dens_ref, sign_ref, bucket_ref, query_ref, key_ref,
    spread, norm, total, table, est,
):
    qprob, kprob = query_ref.at[0], key_ref.at[0]
    unit = pl.program_id(0)
    slot = unit // SOLO
    length = qkv_ref.shape[1]
    tiles = length // TILE
    q_rows = pl.ds(pl.multiple_of(slot * HD, HD), HD)
    k_rows = pl.ds(pl.multiple_of(2 * HD + slot * HD, HD), HD)
    v_rows = pl.ds(pl.multiple_of(4 * HD + slot * HD, HD), HD)

    @pl.when(jnp.logical_or(unit == 0, unit == SOLO))
    def _():
        def step(i, carry):
            lane = lanes_of(i, TILE)
            seg_row = seg_ref[:, lane]
            fill_spread(qkv_ref[v_rows, lane], seg_row, spread, lane)
            fill_member(seg_row, spread, lane)
            query = qkv_ref[q_rows, lane].astype(F32)
            key = qkv_ref[k_rows, lane].astype(F32)
            scale = math.sqrt(HD)
            norm[0:1, lane] = scale * lax.rsqrt(
                jnp.sum(query * query, axis=0, keepdims=True) + 1e-06
            )
            norm[1:2, lane] = scale * lax.rsqrt(jnp.sum(key * key, axis=0, keepdims=True) + 1e-06)
            est[:, lane] = jnp.zeros((HD, TILE), F32)
            return carry

        lax.fori_loop(0, tiles, step, 0)

    planes = unit_planes(planes_ref[plane_rows(unit), :])
    high, rest = split_two(planes)
    middle, low = split_two(rest)
    stack = jnp.concatenate((high, middle, low), axis=0).astype(BF16)
    total[...] = jnp.zeros_like(total)

    def collect(i, carry):
        lane = lanes_of(i, TILE)
        flat_q = nn_dot(stack, qkv_ref[q_rows, lane])
        flat_k = nn_dot(stack, qkv_ref[k_rows, lane])
        sign_q = jnp.tanh((flat_q[0:8] + flat_q[8:16] + flat_q[16:24]) * norm[0:1, lane])
        sign_k = jnp.tanh((flat_k[0:8] + flat_k[8:16] + flat_k[16:24]) * norm[1:2, lane])
        sign_ref[0, 0:8, lane] = sign_q
        sign_ref[0, 8:16, lane] = sign_k
        for part in range(TILE // LANES):
            inner = slice(part * LANES, (part + 1) * LANES)
            code_probs(sign_k[:, inner], kprob, inner)
            code_probs(
                sign_q[:, inner], qprob, pl.ds(pl.multiple_of(i * TILE + part * LANES, LANES), LANES)
            )
        total[...] += nt_dot(spread[0 : SPREAD + 16, lane], kprob[...])
        return carry

    lax.fori_loop(0, tiles, collect, 0)
    mass = total[SPREAD : SPREAD + 8, :]
    mass_high, mass_low = split_two(mass)
    extra = jnp.concatenate(
        (mass_high, mass_high, mass_low, jnp.zeros((104, CODES), F32)), axis=0
    )
    table[0:SPREAD, :] = total[0:SPREAD, :].astype(BF16)
    table[SPREAD:EXT, :] = extra.astype(BF16)
    bucket_ref[0, :, 0:SPREAD] = jnp.transpose(total[0:SPREAD, :]).astype(BF16)
    bucket_ref[0, :, SPREAD:EXT] = jnp.transpose(extra).astype(BF16)

    def spend(i, carry):
        lane = lanes_of(i, TILE)
        seg_row = seg_ref[:, lane]
        product = nn_dot(table[0 : SPREAD + 32, :], qprob[:, lane])
        numer = masked_fold(product, seg_row)
        both = product[SPREAD : SPREAD + 8] + product[SPREAD + 16 : SPREAD + 24]
        which = lax.broadcasted_iota(jnp.int32, (8, TILE), 0)
        density = jnp.sum(jnp.where(which == seg_row, both, 0.0), axis=0, keepdims=True)
        numer_ref[0, :, lane] = numer
        dens_ref[0, :, lane] = density
        est[:, lane] += numer * (1.0 / jnp.maximum(density, 1.0))
        return carry

    lax.fori_loop(0, tiles, spend, 0)

    @pl.when(jnp.logical_or(unit == SOLO - 1, unit == UNITS - 1))
    def _():
        sent_ref[q_rows, :] = (est[...] * (1.0 / TABLES) + conv_ref[q_rows, :]).astype(BF16)


def attend(qkv, planes, seg_row, conv):
    length = qkv.shape[1]
    per_unit = lambda u: (u, 0, 0)
    fixed = lambda u: (0, 0)
    return pl.pallas_call(
        attend_kernel,
        grid=(UNITS,),
        in_specs=[
            pl.BlockSpec(qkv.shape, fixed),
            pl.BlockSpec(planes.shape, fixed),
            pl.BlockSpec(seg_row.shape, fixed),
            pl.BlockSpec(conv.shape, fixed),
        ],
        out_specs=[
            pl.BlockSpec((2 * HD, length), fixed),
            pl.BlockSpec((1, HD, length), per_unit),
            pl.BlockSpec((1, 1, length), per_unit),
            pl.BlockSpec((1, 16, length), per_unit),
            pl.BlockSpec((1, CODES, EXT), per_unit),
            pl.BlockSpec((1, CODES, length), per_unit),
            pl.BlockSpec((1, CODES, length), per_unit),
        ],
        out_shape=[
            jax.ShapeDtypeStruct((2 * HD, length), BF16),
            jax.ShapeDtypeStruct((UNITS, HD, length), F32),
            jax.ShapeDtypeStruct((UNITS, 1, length), F32),
            jax.ShapeDtypeStruct((UNITS, 16, length), F32),
            jax.ShapeDtypeStruct((UNITS, CODES, EXT), BF16),
            jax.ShapeDtypeStruct((UNITS, CODES, length), BF16),
            jax.ShapeDtypeStruct((UNITS, CODES, length), BF16),
        ],
        scratch_shapes=[
            pltpu.VMEM((EXT, length), BF16),
            pltpu.VMEM((8, length), F32),
            pltpu.VMEM((SPREAD + 16, CODES), F32),
            pltpu.VMEM((EXT, CODES), BF16),
            pltpu.VMEM((HD, length), F32),
        ],
        compiler_params=pltpu.CompilerParams(vmem_limit_bytes=VMEM_BYTES),
        cost_estimate=pl.CostEstimate(flops=0, bytes_accessed=1_000_000, transcendentals=0),
        name="attend",
    )(qkv, planes, seg_row, conv)


def back_setup(slot, qkv_ref, seg_ref, out_ref, spread, gspread, proj):
    tiles = qkv_ref.shape[1] // TILE
    v_rows = slice(4 * HD + slot * HD, 5 * HD + slot * HD)
    v_out = slice(2 * HD, 3 * HD)

    def step(i, carry):
        lane = lanes_of(i, TILE)
        seg_row = seg_ref[:, lane]
        fill_spread(qkv_ref[v_rows, lane], seg_row, spread, lane)
        fill_member(seg_row, spread, lane)
        proj[:, lane] = jnp.zeros((2 * HD, TILE), F32)
        out_ref[v_out, lane] = jnp.zeros((HD, TILE), F32)
        return carry

    lax.fori_loop(0, tiles, step, 0)
    gspread[SPREAD:EXT, :] = jnp.zeros((128, TILE), BF16)


def back_unit(
    slot, unit, qkv_ref, planes_ref, seg_ref, grad_ref, numer_ref, dens_ref, sign_ref, bucket_ref,
    out_ref, spread, qprob, kprob, gspread, total, table, turned, gsign, proj,
):
    tiles = qkv_ref.shape[1] // TILE
    q_rows = slice(slot * HD, slot * HD + HD)
    k_rows = slice(2 * HD + slot * HD, 3 * HD + slot * HD)
    v_rows = slice(4 * HD + slot * HD, 5 * HD + slot * HD)
    v_out = slice(2 * HD, 3 * HD)
    total[...] = jnp.zeros_like(total)

    def first(i, carry):
        lane = lanes_of(i, TILE)
        seg_row = seg_ref[:, lane]
        density = dens_ref[:, lane]
        inverse = 1.0 / jnp.maximum(density, 1.0)
        est_grad = grad_ref[q_rows, lane].astype(F32) * (1.0 / TABLES)
        num_grad = (est_grad * inverse).astype(BF16)
        fill_spread(num_grad, seg_row, gspread, slice(0, TILE))
        inner_sum = jnp.sum(est_grad * numer_ref[:, lane], axis=0, keepdims=True)
        dens_grad = jnp.where(density > 1.0, -inner_sum * inverse * inverse, 0.0)
        which = lax.broadcasted_iota(jnp.int32, (8, TILE), 0)
        high, low = split_two(jnp.where(which == seg_row, dens_grad, 0.0))
        gspread[SPREAD : SPREAD + 32, :] = jnp.concatenate(
            (high, low, high, jnp.zeros_like(high)), axis=0
        ).astype(BF16)
        collected = nn_dot(bucket_ref[...], gspread[...])
        for part in range(TILE // LANES):
            inner = slice(part * LANES, (part + 1) * LANES)
            outer = pl.ds(pl.multiple_of(i * TILE + part * LANES, LANES), LANES)
            sign_q = sign_ref[0:8, outer]
            gsign[0:8, outer] = signs_back(sign_q, collected[:, inner])
        total[...] += nt_dot(gspread[0 : SPREAD + 16, :], qprob[...])
        return carry

    lax.fori_loop(0, tiles, first, 0)
    mass_grad = total[SPREAD : SPREAD + 8, :] + total[SPREAD + 8 : SPREAD + 16, :]
    high, low = split_two(mass_grad)
    extra = jnp.concatenate((high, low, jnp.zeros((112, CODES), F32)), axis=0)
    table[...] = total[0:SPREAD, :].astype(BF16)
    turned[:, 0:SPREAD] = jnp.transpose(total[0:SPREAD, :]).astype(BF16)
    turned[:, SPREAD:EXT] = jnp.transpose(extra).astype(BF16)

    planes = unit_planes(planes_ref[plane_rows(unit), :])
    plane_high, plane_low = split_two(planes)
    stack = jnp.concatenate((plane_high, plane_low, plane_high, jnp.zeros_like(plane_high)), axis=0)
    stack = stack.astype(BF16)

    def second(i, carry):
        lane = lanes_of(i, TILE)
        seg_row = seg_ref[:, lane]
        out_ref[v_out, lane] += masked_fold(nn_dot(table[...], kprob[...]), seg_row)
        collected = nn_dot(turned[...], spread[:, lane])
        for part in range(TILE // LANES):
            inner = slice(part * LANES, (part + 1) * LANES)
            outer = pl.ds(pl.multiple_of(i * TILE + part * LANES, LANES), LANES)
            gsign[8:16, outer] = signs_back(sign_ref[8:16, outer], collected[:, inner])
        signs = sign_ref[:, lane]
        flat = gsign[:, lane] * (1.0 - signs * signs)
        high, low = split_two(flat)
        for side in range(2):
            rows = slice(8 * side, 8 * side + 8)
            pieces = jnp.concatenate(
                (high[rows], high[rows], low[rows], jnp.zeros((8, TILE), F32)), axis=0
            ).astype(BF16)
            proj[side * HD : (side + 1) * HD, lane] += tn_dot(stack, pieces)
        return carry

    lax.fori_loop(0, tiles, second, 0)


def back_finish(slot, qkv_ref, out_ref, proj):
    tiles = qkv_ref.shape[1] // TILE
    q_rows = slice(slot * HD, slot * HD + HD)
    k_rows = slice(2 * HD + slot * HD, 3 * HD + slot * HD)

    def step(i, carry):
        lane = lanes_of(i, TILE)
        for side, rows in ((0, q_rows), (1, k_rows)):
            vec = qkv_ref[rows, lane].astype(F32)
            inverse = lax.rsqrt(jnp.sum(vec * vec, axis=0, keepdims=True) + 1e-06)
            unit_vec = vec * inverse
            grad = proj[side * HD : (side + 1) * HD, lane]
            along = jnp.sum(unit_vec * grad, axis=0, keepdims=True)
            out_ref[side * HD : (side + 1) * HD, lane] = math.sqrt(HD) * inverse * (grad - unit_vec * along)
        return carry

    lax.fori_loop(0, tiles, step, 0)


SPAN = 192
SHIFT = (KW - 1) // 2
OWN = 96
BLOCKS = ((0, HD), (HD, OWN))


def own_heads():
    m = lax.axis_index("mp")
    group = m // 2
    return (3 * group + 2 * (m % 2), 3 * group + 1)


def own_half():
    side = lax.axis_index("mp") % 2
    half = OWN - HD
    return side, half


def band_of(row):
    turned = jnp.broadcast_to(row, (LANES, 2 * LANES))
    index = lax.broadcasted_iota(jnp.int32, turned.shape, 0)
    for bit in range(7):
        moved = pltpu.roll(turned, 1 << bit, 1)
        turned = jnp.where((index >> bit) & 1 == 1, moved, turned)
    return jnp.transpose(turned)[0:SPAN]


def fill_hot(seg_ref, hot, hot_pad):
    length = seg_ref.shape[1]
    rows = lax.broadcasted_iota(jnp.int32, (16, length), 0)
    value = jnp.where(rows == seg_ref[...], 1.0, 0.0)
    value = jnp.where(rows < MAXSEG, value, 0.0).astype(BF16)
    hot[...] = value
    hot_pad[...] = jnp.zeros_like(hot_pad)
    hot_pad[:, SHIFT : SHIFT + length] = value


def band_product(rows, band):
    return nn_dot(rows, band.astype(BF16))


def conv_kernel(qkv_ref, taps_ref, seg_ref, out_ref, hot, hot_pad, pad, band):
    length = out_ref.shape[1]
    side, half = own_half()
    own = pl.ds(pl.multiple_of(HD + side * half, half), half)
    other = pl.ds(pl.multiple_of(HD + (1 - side) * half, half), half)
    fill_hot(seg_ref, hot, hot_pad)
    pad[...] = jnp.zeros_like(pad)
    pad[0:HD, SHIFT : SHIFT + length] = qkv_ref[4 * HD : 5 * HD, :]
    value_half = pl.ds(pl.multiple_of(5 * HD + side * half, half), half)
    pad[HD:OWN, SHIFT : SHIFT + length] = qkv_ref[value_half, :]
    for h, head in enumerate(own_heads()):
        band[h] = band_of(taps_ref[pl.ds(head, 1), :])
    out_ref[other, :] = jnp.zeros((half, length), F32)
    for i in range(length // LANES):
        lane = slice(i * LANES, (i + 1) * LANES)
        wide = slice(i * LANES, i * LANES + SPAN)
        mask = tn_dot(hot_pad[:, wide], hot[:, lane])
        out_ref[0:HD, lane] = band_product(pad[0:HD, wide], band[0] * mask)
        out_ref[own, lane] = band_product(pad[HD:OWN, wide], band[1] * mask)


def segment_conv(qkv, taps, seg_row):
    length = seg_row.shape[1]
    return pl.pallas_call(
        conv_kernel,
        out_shape=jax.ShapeDtypeStruct((2 * HD, length), F32),
        scratch_shapes=[
            pltpu.VMEM((16, length), BF16),
            pltpu.VMEM((16, length + LANES), BF16),
            pltpu.VMEM((OWN, length + LANES), BF16),
            pltpu.VMEM((2, SPAN, LANES), F32),
        ],
        compiler_params=pltpu.CompilerParams(vmem_limit_bytes=VMEM_BYTES),
        cost_estimate=pl.CostEstimate(flops=0, bytes_accessed=1_000_000, transcendentals=0),
        name="segment_conv",
    )(qkv, taps, seg_row)


def conv_back_kernel(
    qkv_ref, grad_ref, taps_ref, seg_ref, out_ref, tap_ref, hot, hot_pad, pad, gpad, band, corr
):
    length = seg_ref.shape[1]
    side, half = own_half()
    fill_hot(seg_ref, hot, hot_pad)
    pad[...] = jnp.zeros_like(pad)
    gpad[...] = jnp.zeros_like(gpad)
    inside = slice(SHIFT, SHIFT + length)
    value_half = pl.ds(pl.multiple_of(5 * HD + side * half, half), half)
    grad_half = pl.ds(pl.multiple_of(HD + side * half, half), half)
    pad[0:HD, inside] = qkv_ref[4 * HD : 5 * HD, :]
    pad[HD:OWN, inside] = qkv_ref[value_half, :]
    gpad[0:HD, inside] = grad_ref[0:HD, :]
    gpad[HD:OWN, inside] = grad_ref[grad_half, :]
    heads = own_heads()
    for h, head in enumerate(heads):
        band[h] = band_of(taps_ref[pl.ds(16 + head, 1), :])
    corr[...] = jnp.zeros_like(corr)
    for i in range(length // LANES):
        lane = slice(i * LANES, (i + 1) * LANES)
        wide = slice(i * LANES, i * LANES + SPAN)
        twice = slice(i * LANES, (i + 2) * LANES)
        mask = tn_dot(hot_pad[:, wide], hot[:, lane])
        turned = tn_dot(hot[:, lane], hot_pad[:, twice])
        grads = (grad_ref[0:HD, lane], grad_ref[grad_half, lane])
        for h, (low_row, high_row) in enumerate(BLOCKS):
            out_ref[low_row:high_row, lane] = band_product(
                gpad[low_row:high_row, wide], band[h] * mask
            )
            corr[h] += turned * tn_dot(grads[h], pad[low_row:high_row, twice])
    row = lax.broadcasted_iota(jnp.int32, (LANES, 2 * LANES), 0)
    place = lax.broadcasted_iota(jnp.int32, (8, LANES), 0)
    low_heads = jnp.zeros((8, LANES), F32)
    high_heads = jnp.zeros((8, LANES), F32)
    for h, head in enumerate(heads):
        skew = corr[h]
        for bit in range(7):
            moved = pltpu.roll(skew, 2 * LANES - (1 << bit), 1)
            skew = jnp.where((row >> bit) & 1 == 1, moved, skew)
        taps = jnp.sum(skew, axis=0, keepdims=True)[:, 0:LANES]
        low_heads = low_heads + jnp.where(place == head, taps, 0.0)
        high_heads = high_heads + jnp.where(place + 8 == head, taps, 0.0)
    tap_ref[:, 0:LANES] = low_heads
    tap_ref[:, LANES : 2 * LANES] = high_heads


def conv_back(qkv, grad, taps, seg_row):
    length = seg_row.shape[1]
    return pl.pallas_call(
        conv_back_kernel,
        out_shape=(
            jax.ShapeDtypeStruct((OWN, length), F32),
            jax.ShapeDtypeStruct((8, 2 * LANES), F32),
        ),
        scratch_shapes=[
            pltpu.VMEM((16, length), BF16),
            pltpu.VMEM((16, length + LANES), BF16),
            pltpu.VMEM((OWN, length + LANES), BF16),
            pltpu.VMEM((OWN, length + LANES), BF16),
            pltpu.VMEM((2, SPAN, LANES), F32),
            pltpu.VMEM((2, LANES, 2 * LANES), F32),
        ],
        compiler_params=pltpu.CompilerParams(vmem_limit_bytes=VMEM_BYTES),
        cost_estimate=pl.CostEstimate(flops=0, bytes_accessed=1_000_000, transcendentals=0),
        name="conv_back",
    )(qkv, grad, taps, seg_row)


def norm_rows(values):
    center = values - jnp.mean(values, axis=1, keepdims=True)
    inverse = lax.rsqrt(jnp.mean(center * center, axis=1, keepdims=True) + 1e-05)
    return center * inverse, inverse


def norm_back(upstream, normed, inverse, gain):
    scaled = upstream * gain
    inner = (
        scaled
        - jnp.mean(scaled, axis=1, keepdims=True)
        - normed * jnp.mean(scaled * normed, axis=1, keepdims=True)
    )
    return inner * inverse


def gelu_pair(value):
    cdf = 0.5 + 0.5 * lax.erf(value * math.sqrt(0.5))
    pdf = jnp.exp(-0.5 * value * value) * (1.0 / math.sqrt(2.0 * math.pi))
    return value * cdf, cdf + value * pdf


def column_sum(values):
    return jnp.sum(values, axis=0, keepdims=True)


MESH = pl.DeviceIdType.MESH
OFFSETS = (0, -2, 2, 4)
INVERSE = (0, 2, 1, 3, 4, 6, 5, 7)


def repeat(start, stop, action):
    def body(r, carry):
        action(r)
        return carry

    lax.fori_loop(start, stop, body, 0)


def remote(src, dst, send, recv, target):
    return pltpu.make_async_remote_copy(
        src_ref=src, dst_ref=dst, send_sem=send, recv_sem=recv,
        device_id={"mp": target}, device_id_type=MESH,
    )


def greet(targets):
    barrier = pltpu.get_barrier_semaphore()
    for target in targets:
        pl.semaphore_signal(barrier, inc=1, device_id={"mp": target}, device_id_type=MESH)
    pl.semaphore_wait(barrier, len(targets))


def gather_kernel(
    x_ref, query_ref, key_ref, value_ref, up_ref, down_ref, out_w_ref,
    all_ref, qkv_ref, block_ref, wide, send, recv,
):
    w_refs = (query_ref, key_ref, value_ref)
    count, rows, _ = all_ref.shape
    m = lax.axis_index("mp")
    side = m % 2
    sibling = m + 1 - 2 * side
    left = (m + count - 2) % count
    right = (m + 2) % count
    far = (m + 4) % count
    half = OWN - HD
    cut = rows // 2
    greet((left, right, sibling))

    def copy(n, src, dst, target):
        return remote(src, dst, send.at[n], recv.at[n], target)

    def piece(n, which):
        return pl.ds(pl.multiple_of(n * 2 * HD + HD + which * half, half), half)

    def weight_copy(n, which):
        source = w_refs[n].at[pl.ds(pl.multiple_of((1 - side) * HD, half), half), :]
        return copy(11 + n, source, wide.at[piece(n, which), :], sibling)

    low, high = slice(0, cut), slice(cut, rows)

    def own_copy(n, owner):
        part, target = ((low, right), (high, right), (high, left), (low, left))[n]
        return copy(n, x_ref.at[part], all_ref.at[owner, part], target)

    for n in range(3):
        weight_copy(n, side).start()
    for n in (0, 2, 1, 3):
        own_copy(n, m).start()
    to_sibling = copy(4, x_ref, all_ref.at[m], sibling)
    to_sibling.start()
    all_ref[m] = x_ref[...]
    for n in range(3):
        solo = pl.ds(pl.multiple_of(side * half, half), HD)
        own = pl.ds(pl.multiple_of((1 - side) * HD, half), half)
        wide[n * 2 * HD : n * 2 * HD + HD, :] = w_refs[n][solo, :]
        wide[piece(n, side), :] = w_refs[n][own, :]
    units = down_ref.shape[0]
    block_ref[0:units] = jnp.transpose(up_ref[...].astype(F32)).astype(BF16)
    block_ref[units : 2 * units] = down_ref[...]
    block_ref[2 * units : 2 * units + OWN] = out_w_ref[...]
    for n in range(3):
        weight_copy(n, 1 - side).wait_recv()

    def project(block):
        lane = pl.ds(pl.multiple_of(block * rows, rows), rows)
        qkv_ref[:, lane] = nt_dot(wide[...], all_ref[block]).astype(BF16)

    def pass_on(n, owner, part, target):
        return copy(n, all_ref.at[owner, part], all_ref.at[owner, part], target)

    project(m)
    own_copy(0, left).wait_recv()
    on_right = pass_on(5, left, low, right)
    on_right.start()
    own_copy(2, right).wait_recv()
    on_left = pass_on(6, right, high, left)
    on_left.start()
    copy(4, x_ref, all_ref.at[sibling], sibling).wait_recv()
    project(sibling)
    own_copy(1, left).wait_recv()
    over_left = copy(7, all_ref.at[left], all_ref.at[left], sibling)
    over_left.start()
    own_copy(3, right).wait_recv()
    over_right = copy(8, all_ref.at[right], all_ref.at[right], sibling)
    over_right.start()
    project(left)
    project(right)
    other_left = (sibling + count - 2) % count
    other_right = (sibling + 2) % count
    other_far = (sibling + 4) % count
    copy(7, x_ref, all_ref.at[other_left], sibling).wait_recv()
    project(other_left)
    copy(8, x_ref, all_ref.at[other_right], sibling).wait_recv()
    project(other_right)
    pass_on(5, far, low, left).wait_recv()
    over_low = pass_on(9, far, low, sibling)
    over_low.start()
    pass_on(6, far, high, right).wait_recv()
    over_high = pass_on(10, far, high, sibling)
    over_high.start()
    project(far)
    pass_on(9, other_far, low, sibling).wait_recv()
    pass_on(10, other_far, high, sibling).wait_recv()
    project(other_far)
    for n in range(3):
        weight_copy(n, side).wait_send()
    for n in range(4):
        own_copy(n, m).wait_send()
    for sent in (to_sibling, on_right, on_left, over_left, over_right, over_low, over_high):
        sent.wait_send()


def gather_qkv(x, w_rows, w_up, w_down, w_out, count):
    rows, width = x.shape
    vmem = pl.BlockSpec(memory_space=pltpu.VMEM)
    return pl.pallas_call(
        gather_kernel,
        in_specs=[vmem] * 7,
        out_specs=[vmem] * 3,
        out_shape=(
            jax.ShapeDtypeStruct((count, rows, width), BF16),
            jax.ShapeDtypeStruct((6 * HD, count * rows), BF16),
            jax.ShapeDtypeStruct((2 * w_down.shape[0] + OWN, width), BF16),
        ),
        scratch_shapes=[
            pltpu.VMEM((6 * HD, width), BF16),
            pltpu.SemaphoreType.DMA((14,)),
            pltpu.SemaphoreType.DMA((14,)),
        ],
        compiler_params=pltpu.CompilerParams(
            vmem_limit_bytes=VMEM_BYTES, collective_id=2, has_side_effects=True
        ),
        cost_estimate=pl.CostEstimate(
            flops=12 * HD * count * rows * width, bytes_accessed=30_000_000, transcendentals=0
        ),
        name="gather_qkv",
    )(x, *w_rows, w_up, w_down, w_out)


def around(m, count):
    sibling = m + 1 - 2 * (m % 2)
    return [(base + count + off) % count for base in (m, sibling) for off in OFFSETS]


def middle_kernel(
    sent_ref, x_ref, cot_ref, own_w, left_w, right_w, scale_ref,
    result_ref, lows_ref, left_ref, right_ref, one_ref, attn_ref, part_ref,
    wall, out_w, att_in, attn_out, slope, keep, acc,
    load, give_send, give_recv, rest_send, rest_recv, line_send, line_recv, far_send, far_recv,
    in_send, in_recv, out_send, out_recv, row_send, row_recv,
):
    rows = x_ref.shape[0]
    count = att_in.shape[0]
    units = slope.shape[2]
    both = 2 * units
    m = lax.axis_index("mp")
    devices = around(m, count)
    sibling = devices[4]
    greet(devices[1:])

    def tokens(index):
        return pl.ds(pl.multiple_of(index * rows, rows), rows)

    side = m % 2
    depth = wall.shape[1]
    blocks = (own_w, left_w, right_w)
    out_rows = slice(both, depth)
    ffn_rows = slice(0, both)
    parts = (slice(0, units), slice(units, both))

    middle_row = both + OWN // 2
    out_parts = (slice(both, middle_row), slice(middle_row, depth))

    def give(n):
        return remote(
            blocks[n].at[out_rows], wall.at[4 + n, out_rows], give_send.at[n], give_recv.at[n],
            sibling,
        )

    def out_along(n):
        return remote(
            blocks[1 + n].at[out_parts[n]], wall.at[3, out_parts[n]], give_send.at[3 + n],
            give_recv.at[3 + n], devices[2 - n],
        )

    def out_far(n):
        return remote(
            wall.at[3, out_parts[n]], wall.at[7, out_parts[n]], give_send.at[5 + n],
            give_recv.at[5 + n], sibling,
        )

    def rest(n):
        return remote(
            blocks[n].at[ffn_rows], wall.at[4 + n, ffn_rows], rest_send.at[n], rest_recv.at[n],
            sibling,
        )

    def along(n):
        return remote(
            blocks[1 + n].at[parts[n]], wall.at[3, parts[n]], line_send.at[n], line_recv.at[n],
            devices[2 - n],
        )

    def row_copy(k, n):
        place = (left_ref, right_ref)[n].at[k]
        return remote(
            lows_ref.at[k], place, row_send.at[k, n], row_recv.at[k, n], devices[2 - n]
        )

    def far_copy(n):
        return remote(
            wall.at[3, parts[n]], wall.at[7, parts[n]], far_send.at[n], far_recv.at[n], sibling
        )

    def loads():
        return [pltpu.make_async_copy(blocks[n], wall.at[n], load.at[n]) for n in range(3)]

    def att_copy(n, slot, sem):
        return remote(
            sent_ref.at[:, tokens(devices[n])], att_in.at[slot], in_send.at[n], in_recv.at[sem],
            devices[n],
        )

    def attn_copy(n, lane, sem):
        return remote(
            attn_out.at[n], attn_ref.at[:, tokens(lane)], out_send.at[n], out_recv.at[sem],
            devices[n],
        )

    for n in range(2):
        out_along(n).start()
    for n in range(1, count):
        att_copy(n, INVERSE[n], INVERSE[n]).start()
    for n in range(3):
        give(n).start()
    for copy in loads():
        copy.start()
    for n in range(3):
        rest(n).start()
    att_in[0] = sent_ref[:, tokens(m)]
    for copy in loads():
        copy.wait()
    for n in range(2):
        out_along(n).wait_recv()
        out_far(n).start()
    for n in range(3):
        give(n).wait_recv()
    for n in range(1, count):
        att_copy(n, n, n).wait_recv()
    for n in range(2):
        along(n).start()
    projected = None
    for n in range(4):
        if n == 3:
            for part in range(2):
                out_far(part).wait_recv()
        first, second = n + 4 * side, n + 4 * (1 - side)
        out_w[n, 0:OWN] = wall[first, out_rows]
        out_w[n, OWN : 2 * OWN] = wall[second, out_rows]
        shared = att_in[first, HD : 2 * HD].astype(F32) + att_in[second, HD : 2 * HD].astype(F32)
        features = jnp.concatenate(
            (att_in[first, 0:HD], shared.astype(BF16), att_in[second, 0:HD]), axis=0
        )
        piece = tn_dot(features, out_w[n])
        projected = piece if projected is None else projected + piece
    unit, inverse = norm_rows(x_ref[...].astype(F32) + projected)
    hidden = unit * scale_ref[0:1] + scale_ref[1:2]
    keep[0] = unit
    keep[1] = hidden
    lows_ref[0] = hidden.astype(BF16)
    acc[...] = jnp.zeros_like(acc)

    def forward(slots):
        low = lows_ref[0]
        total = acc[...]
        for slot in slots:
            active, lean = gelu_pair(nt_dot(low, wall[slot, 0:units]))
            slope[slot] = lean
            total = total + nn_dot(active.astype(BF16), wall[slot, units:both])
        acc[...] = total

    for n in range(3):
        rest(n).wait_recv()
    repeat(0, 3, lambda n: forward((n, 4 + n)))
    for n in range(2):
        along(n).wait_recv()
        far_copy(n).start()
    for n in range(2):
        row_copy(0, n).start()
    forward((3,))
    for n in range(2):
        far_copy(n).wait_recv()
    forward((7,))
    unit, inv = norm_rows(keep[1] + acc[...])
    result_ref[...] = (unit * scale_ref[2:3] + scale_ref[3:4]).astype(BF16)
    upstream = cot_ref[...].astype(F32)
    part_ref[2:3] = column_sum(upstream * unit)
    part_ref[3:4] = column_sum(upstream)
    grad = norm_back(upstream, unit, inv, scale_ref[2:3])
    keep[1] = grad
    lows_ref[1] = grad.astype(BF16)
    for n in range(2):
        row_copy(1, n).start()
    acc[...] = jnp.zeros_like(acc)

    def backward(i, carry):
        low = lows_ref[1]
        total = acc[...]
        for n in range(2):
            pre_grad = nt_dot(low, wall[2 * i + n, units:both]) * slope[2 * i + n]
            total = total + nn_dot(pre_grad.astype(BF16), wall[2 * i + n, 0:units])
        acc[...] = total
        return carry

    lax.fori_loop(0, 4, backward, 0)
    upstream = keep[1] + acc[...]
    unit = keep[0]
    part_ref[0:1] = column_sum(upstream * unit)
    part_ref[1:2] = column_sum(upstream)
    part_ref[4:8] = jnp.zeros((4, part_ref.shape[1]), F32)
    grad = norm_back(upstream, unit, inverse, scale_ref[0:1])
    one_ref[...] = grad
    low = grad.astype(BF16)
    lows_ref[2] = low
    for n in (3, 1, 2, 0):
        first, second = n + 4 * side, n + 4 * (1 - side)
        back = nt_dot(out_w[n], low).astype(BF16)
        attn_out[first] = back[0 : 2 * HD]
        attn_out[second, 0:HD] = back[2 * HD : 3 * HD]
        attn_out[second, HD : 2 * HD] = back[HD : 2 * HD]
        for slot in (n, 4 + n):
            if slot > 0:
                attn_copy(slot, m, INVERSE[slot]).start()
    attn_ref[:, tokens(m)] = attn_out[0]
    for n in range(1, count):
        attn_copy(n, devices[n], n).wait_recv()
    for k in range(2):
        for n in range(2):
            row_copy(k, n).wait_recv()
            row_copy(k, n).wait_send()
    for n in range(2):
        out_along(n).wait_send()
        out_far(n).wait_send()
    for n in range(3):
        give(n).wait_send()
        rest(n).wait_send()
    for n in range(2):
        along(n).wait_send()
        far_copy(n).wait_send()
    for n in range(1, count):
        att_copy(n, INVERSE[n], INVERSE[n]).wait_send()
        attn_copy(n, m, INVERSE[n]).wait_send()


def middle(sent, x, cot, blocks, scale, count):
    rows, width = x.shape
    depth = sent.shape[0]
    units = (blocks[0].shape[0] - OWN) // 2
    vmem = pl.BlockSpec(memory_space=pltpu.VMEM)
    sems = lambda n: pltpu.SemaphoreType.DMA((n,))
    return pl.pallas_call(
        middle_kernel,
        in_specs=[vmem] * 3 + [pl.BlockSpec(memory_space=pl.ANY)] * 3 + [vmem],
        out_specs=[vmem] * 7,
        out_shape=(
            jax.ShapeDtypeStruct((rows, width), BF16),
            jax.ShapeDtypeStruct((3, rows, width), BF16),
            jax.ShapeDtypeStruct((2, rows, width), BF16),
            jax.ShapeDtypeStruct((2, rows, width), BF16),
            jax.ShapeDtypeStruct((rows, width), F32),
            jax.ShapeDtypeStruct(sent.shape, BF16),
            jax.ShapeDtypeStruct((8, width), F32),
        ),
        scratch_shapes=[
            pltpu.VMEM((count,) + blocks[0].shape, BF16),
            pltpu.VMEM((count // 2, 2 * OWN, width), BF16),
            pltpu.VMEM((count, depth, rows), BF16),
            pltpu.VMEM((count, depth, rows), BF16),
            pltpu.VMEM((count, rows, units), F32),
            pltpu.VMEM((2, rows, width), F32),
            pltpu.VMEM((rows, width), F32),
            sems(3), sems(7), sems(7), sems(3), sems(3), sems(2), sems(2), sems(2), sems(2),
            sems(count), sems(count), sems(count), sems(count),
            pltpu.SemaphoreType.DMA((2, 2)), pltpu.SemaphoreType.DMA((2, 2)),
        ],
        compiler_params=pltpu.CompilerParams(
            vmem_limit_bytes=VMEM_BYTES, collective_id=1, has_side_effects=True
        ),
        cost_estimate=pl.CostEstimate(
            flops=16 * rows * width * count * units, bytes_accessed=26_000_000,
            transcendentals=0,
        ),
        name="middle",
    )(sent, x, cot, *blocks, scale)


def close_kernel(
    own_x, left_x, right_x, numer_any, dens_any, sign_any, bucket_any, query_any, key_any,
    conv_any, all_any, w_any, one_any,
    sent_ref, wq_ref, wk_ref, wv_ref, norm_ref, tap_ref, qkv_ref, planes_ref, seg_ref, grad_ref,
    inputs_ref, up_ref, down_ref, out_ref, query_ref, key_ref, value_ref, tiny_ref, taps_ref,
    conv_ref, all_ref, w_ref, one_ref, w_all, half_in,
    wall, acc, solo_low, half_low, w_solo, w_half, attended, swap_out, swap_in, part_out, part_own, pair_in, stage,
    line_in, a_refs, b_refs, d_refs, l_refs, near_in, far_in,
    back_out, numer, dens, sign, bucket, qprob, kprob,
    spread, gspread, total_ref, table, turned, gsign, proj,
    load, fetch_sem, give_send, give_recv, along_send, along_recv, over_send, over_recv,
    row_send, row_recv, wa_send, wa_recv, half_send, half_recv,
    swap_send, swap_recv, pair_send, pair_recv, line_send, line_recv,
    a_sems, b_sems, d_sems,
    l_sems,
    near_send, near_recv, far_sems,
):
    edge = far_in.shape[1]
    count, _, rows, width = wall.shape
    chips = count // 2
    units = down_ref.shape[0]
    d = lax.axis_index("dp")
    m = lax.axis_index("mp")
    side = m % 2
    chip = m // 2
    half = OWN - HD
    cut = rows // 2
    devices = around(m, count)
    sibling = devices[4]

    barrier = pltpu.get_barrier_semaphore()
    place_x, place_y = d % edge, d // edge
    for k in range(1, edge):
        for peer in (
            place_y * edge + (place_x + k) % edge, (place_y + k) % edge * edge + place_x
        ):
            pl.semaphore_signal(barrier, inc=1, device_id={"dp": peer}, device_id_type=MESH)
    repeat(
        1, count,
        lambda r: pl.semaphore_signal(
            barrier, inc=1, device_id={"mp": (m + r) % count}, device_id_type=MESH
        ),
    )
    pl.semaphore_wait(barrier, 2 * (edge - 1) + count - 1)

    def tokens(index):
        return pl.ds(pl.multiple_of(index * rows, rows), rows)

    parts = (slice(0, cut), slice(cut, rows))
    pair = slice(0, 2)
    sources = (own_x.at[pair], left_x, right_x)

    def give(n):
        return remote(
            sources[n], wall.at[4 + n, pair], give_send.at[n], give_recv.at[n], sibling
        )

    def along(n):
        return remote(
            sources[1 + n].at[:, parts[n]], wall.at[3, pair, parts[n]], along_send.at[n],
            along_recv.at[n], devices[2 - n],
        )

    def over(n):
        return remote(
            wall.at[3, pair, parts[n]], wall.at[7, pair, parts[n]], over_send.at[n],
            over_recv.at[n], sibling,
        )

    def row_copy(n):
        if n < 3:
            source, slot, target = own_x.at[2], n + 1, devices[2 - n]
            if n == 2:
                slot, target = 4, sibling
            place = wall.at[slot, 2]
        elif n < 5:
            source, place, target = wall.at[n - 2, 2], wall.at[n + 2, 2], sibling
        elif n < 7:
            piece = parts[n - 5]
            source, place = wall.at[n - 4, 2, piece], wall.at[3, 2, piece]
            target = devices[7 - n]
        else:
            piece = parts[n - 7]
            source, place, target = wall.at[3, 2, piece], wall.at[7, 2, piece], sibling
        return remote(source, place, row_send.at[n], row_recv.at[n], target)

    def loads():
        copies = [pltpu.make_async_copy(own_x, wall.at[0], load.at[0])]
        for n in range(1, 3):
            copies.append(pltpu.make_async_copy(sources[n], wall.at[n, pair], load.at[n]))
        pairs = ((w_any, w_ref), (conv_any, conv_ref), (all_any, all_ref), (one_any, one_ref))
        for n, (source, target) in enumerate(pairs):
            copies.append(pltpu.make_async_copy(source, target, load.at[3 + n]))
        return copies

    def w_copy(n, slot):
        return remote(w_half, w_all.at[slot], wa_send.at[n], wa_recv.at[slot], devices[n])

    def half_copy(n, slot):
        return remote(
            half_low.at[:, tokens(devices[n])], half_in.at[slot], half_send.at[n],
            half_recv.at[slot], devices[n],
        )

    def fetch(unit):
        place = unit % 2
        return [
            pltpu.make_async_copy(source.at[unit], target.at[place], fetch_sem.at[place, n])
            for n, (source, target) in enumerate(
                (
                    (numer_any, numer), (dens_any, dens), (sign_any, sign), (bucket_any, bucket),
                    (query_any, qprob), (key_any, kprob),
                )
            )
        ]

    def near_copy(r, owner):
        return remote(
            near_in.at[m], near_in.at[owner], near_send.at[r], near_recv.at[r], (m + r) % count
        )

    def swap(n):
        piece = slice(0, half) if n == 0 else slice(half, 4 * half)
        return remote(
            swap_out.at[piece], swap_in.at[piece], swap_send.at[n], swap_recv.at[n], sibling
        )

    for n in range(2):
        along(n).start()
    swap_out[0:half] = sent_ref[pl.ds(pl.multiple_of(HD + (1 - side) * half, half), half), :]
    swap(0).start()
    for n in range(3):
        give(n).start()
    for copy in fetch(0) + loads():
        copy.start()
    for n in range(3):
        row_copy(n).start()
    near_in[m, :, 0:width] = norm_ref[...]
    near_in[m, :, width : width + 2 * LANES] = tap_ref[...]
    repeat(1, count, lambda r: near_copy(r, m).start())
    solo_at = lambda n: pl.ds(pl.multiple_of(n * OWN + side * half, half), HD)
    half_at = lambda n: pl.ds(pl.multiple_of(n * OWN + (1 - side) * HD, half), half)
    sent_half = sent_ref[pl.ds(pl.multiple_of(HD + side * half, half), half), :]
    attended[solo_at(0), :] = sent_ref[0:HD, :]
    acc[...] = jnp.zeros_like(acc)
    swap(0).wait_recv()
    attended[half_at(0), :] = (
        sent_half.astype(F32) + swap_in[0:half].astype(F32)
    ).astype(BF16)
    def step(slots):
        sums = [None] * 2
        for slot in slots:
            hidden, ffn = wall[slot, 0], wall[slot, 1]
            active, lean = gelu_pair(nt_dot(hidden, w_ref[0:units]))
            grad = nt_dot(ffn, w_ref[units : 2 * units]) * lean
            terms = (
                tn_dot(grad.astype(BF16), hidden),
                tn_dot(active.astype(BF16), ffn),
            )
            sums = [p if t is None else t + p for t, p in zip(sums, terms)]
        acc[0:units, :] += sums[0]
        acc[units : 2 * units, :] += sums[1]

    def staged(along_x, refs, sems):
        grads, first_in, mid, second_in, sums = refs
        u, v = (d % edge, d // edge) if along_x else (d // edge, d % edge)

        def copy(n, src, dst, k):
            du, dv = ((u + k) % edge, v) if n in (0, 3) else (u, (v + k) % edge)
            target = dv * edge + du if along_x else du * edge + dv
            return pltpu.make_async_remote_copy(
                src_ref=src, dst_ref=dst, send_sem=sems.at[2 * n, k], recv_sem=sems.at[2 * n + 1, k],
                device_id={"dp": target}, device_id_type=MESH,
            )

        around_edge = range(1, edge)
        out_copy = lambda k: copy(0, grads.at[(u + k) % edge], first_in.at[k], k)
        mid_copy = lambda k: copy(1, mid.at[(v + k) % edge], second_in.at[k], k)
        back_copy = lambda k, owner: copy(2, sums.at[u, v], sums.at[u, owner], k)
        wide_copy = lambda k, owner: copy(3, sums.at[u], sums.at[owner], k)

        def start():
            for k in around_edge:
                out_copy(k).start()

        def half_reduce():
            for k in around_edge:
                out_copy(k).wait_recv()
            for n in range(edge):
                value = grads[u, n].astype(F32)
                for k in around_edge:
                    value = value + first_in[k, n].astype(F32)
                mid[n] = value.astype(BF16)
            for k in around_edge:
                mid_copy(k).start()

        def reduce():
            for k in around_edge:
                mid_copy(k).wait_recv()
            value = mid[v].astype(F32)
            for k in around_edge:
                value = value + second_in[k].astype(F32)
            sums[u, v] = value.astype(BF16)
            for k in around_edge:
                back_copy(k, v).start()

        def spread():
            for k in around_edge:
                back_copy(k, (v + edge - k) % edge).wait_recv()
            for k in around_edge:
                wide_copy(k, u).start()

        def finish():
            for k in around_edge:
                wide_copy(k, (u + edge - k) % edge).wait_recv()
            for k in around_edge:
                out_copy(k).wait_send()
                mid_copy(k).wait_send()
                back_copy(k, v).wait_send()
                wide_copy(k, u).wait_send()

        def put(value):
            size = grads.shape[2]
            for n in range(edge * edge):
                grads[n // edge, n % edge] = value[n * size : (n + 1) * size].astype(BF16)

        def whole():
            return jnp.concatenate(
                [sums[n // edge, n % edge].astype(F32) for n in range(edge * edge)], axis=0
            )

        return start, half_reduce, reduce, spread, finish, put, whole

    a_start, a_half, a_reduce, a_spread, a_finish, a_put, a_whole = staged(True, a_refs, a_sems)
    b_start, b_half, b_reduce, b_spread, b_finish, b_put, b_whole = staged(True, b_refs, b_sems)
    d_start, d_half, d_reduce, d_spread, d_finish, d_put, d_whole = staged(False, d_refs, d_sems)
    l_start, l_half, l_reduce, l_spread, l_finish, l_put, l_whole = staged(False, l_refs, l_sems)

    def far_copy(n, k, owner):
        target = (
            place_y * edge + (place_x + k) % edge if n == 0
            else (place_y + k) % edge * edge + place_x
        )
        mine = (place_x, place_y)[n]
        return pltpu.make_async_remote_copy(
            src_ref=far_in.at[n, mine], dst_ref=far_in.at[n, owner],
            send_sem=far_sems.at[2 * n, k], recv_sem=far_sems.at[2 * n + 1, k],
            device_id={"dp": target}, device_id_type=MESH,
        )

    def far_start(n, value):
        mine = (place_x, place_y)[n]
        far_in[n, mine] = value
        for k in range(1, edge):
            far_copy(n, k, mine).start()

    def far_sum(n):
        mine = (place_x, place_y)[n]
        for k in range(1, edge):
            far_copy(n, k, (mine + edge - k) % edge).wait_recv()
        value = far_in[n, 0]
        for k in range(1, edge):
            value = value + far_in[n, k]
        for k in range(1, edge):
            far_copy(n, k, mine).wait_send()
        return value

    def attention(slot, low, high):
        back_setup(slot, qkv_ref, seg_ref, back_out, spread, gspread, proj)

        def one_unit(unit):
            for copy in fetch(unit):
                copy.wait()

            @pl.when(unit < UNITS - 1)
            def _():
                for copy in fetch(unit + 1):
                    copy.start()

            if slot == 0:
                @pl.when(unit == 2)
                def _():
                    for n in range(3):
                        row_copy(n).wait_recv()
                    for n in range(3, 7):
                        row_copy(n).start()
                    for n in range(2):
                        along(n).wait_recv()
                        over(n).start()

                @pl.when(unit == 3)
                def _():
                    for n in range(5, 7):
                        row_copy(n).wait_recv()
                    for n in range(7, 9):
                        row_copy(n).start()
            else:
                @pl.when(unit == UNITS - 1)
                def _():
                    b_reduce()
                    d_reduce()
                    a_half()

            place = unit % 2
            back_unit(
                slot, unit, qkv_ref, planes_ref, seg_ref, grad_ref,
                numer.at[place], dens.at[place], sign.at[place], bucket.at[place], back_out,
                spread, qprob.at[place], kprob.at[place], gspread, total_ref, table, turned, gsign, proj,
            )

        repeat(low, high, one_unit)
        back_finish(slot, qkv_ref, back_out, proj)

    for n in range(3):
        w_ref_n = (wq_ref, wk_ref, wv_ref)[n]
        w_solo[n * HD : (n + 1) * HD] = w_ref_n[solo_at(0), :]
        w_half[n * half : (n + 1) * half] = w_ref_n[half_at(0), :]
    w_all[0] = w_half[...]
    attention(0, 0, SOLO)
    for n in range(1, count):
        w_copy(n, INVERSE[n]).start()
    for copy in loads():
        copy.wait()
    for n in range(3):
        solo = back_out[n * HD : (n + 1) * HD, :]
        if n == 2:
            solo = solo + conv_ref[0:HD, :]
        solo_low[n * HD : (n + 1) * HD, :] = solo.astype(BF16)

    def pair_copy(target):
        return remote(
            part_out.at[target], pair_in.at[target], pair_send.at[target], pair_recv.at[target],
            sibling,
        )

    def input_part(device):
        lane = tokens(device)
        return tn_dot(solo_low[:, lane], w_solo[...])

    def line_copy(k):
        return remote(
            stage.at[k], line_in.at[k], line_send.at[k], line_recv.at[k], (m + 2 * k) % count
        )

    order = [2, 1, 3, 0]
    for k in order:
        target = (chip + k) % chips
        part_out[target] = input_part(2 * target + 1 - side).astype(BF16)
        pair_copy(target).start()
    for n in range(3):
        give(n).wait_recv()
    for n in range(2):
        over(n).wait_recv()
    repeat(0, 4, lambda i: step((2 * i, 2 * i + 1)))
    b_put(acc[0:units])
    d_put(acc[units : 2 * units])
    b_start()
    d_start()
    for k in order[:3]:
        target = (chip + k) % chips
        mine = input_part(2 * target + side)
        pair_copy(target).wait_recv()
        stage[k] = (mine + pair_in[target].astype(F32)).astype(BF16)
        line_copy(k).start()
    part_own[...] = input_part(m)
    solo_grad = nn_dot(solo_low[...], all_ref[...])
    for n in (3, 4, 7, 8):
        row_copy(n).wait_recv()
    out_grad = None
    for slot in range(count):
        term = nn_dot(attended[:, tokens(devices[slot])], wall[slot, 2])
        out_grad = term if out_grad is None else out_grad + term
    a_put(jnp.concatenate((out_grad, solo_grad), axis=0))
    b_half()
    d_half()
    a_start()
    repeat(1, count, lambda r: near_copy(r, (m + count - r) % count).wait_recv())
    total = near_in[0]
    for r in range(1, count):
        total = total + near_in[r]
    far_start(0, total)
    attention(1, SOLO, UNITS)

    for n in range(3):
        start = pl.multiple_of(n * HD + (1 - side) * half, half)
        swap_out[(n + 1) * half : (n + 2) * half] = back_out[pl.ds(start, half), :].astype(BF16)
    swap(1).start()
    b_spread()
    d_spread()
    a_reduce()
    swap(1).wait_recv()
    for n in range(3):
        mine = back_out[pl.ds(pl.multiple_of(n * HD + side * half, half), half), :]
        mixed = mine + swap_in[(n + 1) * half : (n + 2) * half].astype(F32)
        if n == 2:
            mixed = mixed + conv_ref[HD:OWN, :]
        half_low[n * half : (n + 1) * half] = mixed.astype(BF16)
    for n in range(1, count):
        half_copy(n, INVERSE[n]).start()
    half_in[0] = half_low[:, tokens(m)]
    half_grad = nn_dot(half_low[...], all_ref[...])
    l_put(half_grad)
    l_start()
    a_spread()
    far_start(1, far_sum(0))
    l_half()
    b_finish()
    up_ref[...] = jnp.transpose(b_whole()).astype(BF16)
    l_reduce()
    d_finish()
    down_ref[...] = d_whole().astype(BF16)
    l_spread()
    pair_copy(chip).wait_recv()
    total = one_ref[...] + part_own[...] + pair_in[chip].astype(F32)
    for k in range(1, chips):
        line_copy(k).wait_recv()
        total = total + line_in[k].astype(F32)
    for n in range(1, count):
        w_copy(n, n).wait_recv()
        half_copy(n, n).wait_recv()
    late = tn_dot(
        half_in[...].reshape(count * OWN, rows), w_all[...].reshape(count * OWN, width)
    )
    inputs_ref[...] = total + late
    total = far_sum(1)
    tiny_ref[...] = total[:, 0:width]
    taps_ref[0:8] = total[:, width : width + LANES]
    taps_ref[8:16] = total[:, width + LANES : width + 2 * LANES]
    a_finish()
    whole = a_whole().astype(BF16)
    out_ref[...] = whole[0:OWN]
    outs = (query_ref, key_ref, value_ref)
    for n, ref in enumerate(outs):
        ref[solo_at(0), :] = whole[OWN + n * HD : OWN + (n + 1) * HD]
    l_finish()
    whole = l_whole().astype(BF16)
    for n, ref in enumerate(outs):
        ref[half_at(0), :] = whole[n * half : (n + 1) * half]

    for n in range(1, count):
        w_copy(n, INVERSE[n]).wait_send()
        half_copy(n, INVERSE[n]).wait_send()
    for n in range(2):
        swap(n).wait_send()
        along(n).wait_send()
        over(n).wait_send()
    for n in range(3):
        give(n).wait_send()
    for n in range(9):
        row_copy(n).wait_send()
    for k in range(chips):
        pair_copy((chip + k) % chips).wait_send()
    for k in range(1, chips):
        line_copy(k).wait_send()
    repeat(1, count, lambda r: near_copy(r, m).wait_send())


def close(blocks_x, saved, conv, sent, gathered, w_rows, block_w, one, norms, taps,
          qkv, planes, seg_row, grad, blocks):
    rows, width = one.shape
    length = sent.shape[1]
    count = length // rows
    chips = count // 2
    units = (block_w.shape[0] - OWN) // 2
    depth = (OWN + 3 * HD) // blocks
    thin = OWN // blocks
    high = units // blocks
    edge = 4
    lanes = width + 2 * LANES
    vmem = pl.BlockSpec(memory_space=pltpu.VMEM)
    sems = lambda *n: pltpu.SemaphoreType.DMA(n)
    low = lambda *shape: jax.ShapeDtypeStruct(shape, BF16)
    by_edge = lambda n: (
        pltpu.VMEM((edge, edge, n, width), BF16),
        pltpu.VMEM((edge, edge, n, width), BF16),
        pltpu.VMEM((edge, n, width), BF16),
        pltpu.VMEM((edge, n, width), BF16),
        pltpu.VMEM((edge, edge, n, width), BF16),
    )
    by_chip = pltpu.VMEM((chips, rows, width), BF16)
    return pl.pallas_call(
        close_kernel,
        in_specs=[pl.BlockSpec(memory_space=pl.ANY)] * 13 + [vmem] * 10,
        out_specs=[vmem] * 9,
        out_shape=(
            jax.ShapeDtypeStruct(one.shape, F32),
            low(width, units), low(units, width), low(OWN, width),
            low(OWN, width), low(OWN, width), low(OWN, width),
            jax.ShapeDtypeStruct((8, width), F32),
            jax.ShapeDtypeStruct((16, LANES), F32),
        ),
        scratch_shapes=[
            pltpu.VMEM(conv.shape, F32),
            pltpu.VMEM(gathered.shape, BF16),
            pltpu.VMEM(block_w.shape, BF16),
            pltpu.VMEM(one.shape, F32),
            pltpu.VMEM((count, OWN, width), BF16),
            pltpu.VMEM((count, OWN, rows), BF16),
            pltpu.VMEM((count, 3, rows, width), BF16),
            pltpu.VMEM((2 * units, width), F32),
            pltpu.VMEM((3 * HD, length), BF16),
            pltpu.VMEM((OWN, length), BF16),
            pltpu.VMEM((3 * HD, width), BF16),
            pltpu.VMEM((OWN, width), BF16),
            pltpu.VMEM((OWN, length), BF16),
            pltpu.VMEM((2 * HD, length), BF16),
            pltpu.VMEM((2 * HD, length), BF16),
            by_chip,
            pltpu.VMEM((rows, width), F32),
            by_chip, by_chip, by_chip,
            by_edge(depth), by_edge(high), by_edge(high),
            by_edge(thin),
            pltpu.VMEM((count, 8, lanes), F32),
            pltpu.VMEM((2, edge, 8, lanes), F32),
            pltpu.VMEM((3 * HD, length), F32),
            pltpu.VMEM((2, HD, length), F32),
            pltpu.VMEM((2, 1, length), F32),
            pltpu.VMEM((2, 16, length), F32),
            pltpu.VMEM((2, CODES, EXT), BF16),
            pltpu.VMEM((2, CODES, length), BF16),
            pltpu.VMEM((2, CODES, length), BF16),
            pltpu.VMEM((EXT, length), BF16),
            pltpu.VMEM((EXT, TILE), BF16),
            pltpu.VMEM((SPREAD + 16, CODES), F32),
            pltpu.VMEM((SPREAD, CODES), BF16),
            pltpu.VMEM((CODES, EXT), BF16),
            pltpu.VMEM((16, length), F32),
            pltpu.VMEM((2 * HD, length), F32),
            sems(7), sems(2, 6), sems(3), sems(3), sems(2), sems(2), sems(2), sems(2),
            sems(9), sems(9), sems(count), sems(count), sems(count), sems(count),
            sems(2), sems(2), sems(4), sems(4), sems(4), sems(4),
            sems(8, edge), sems(8, edge), sems(8, edge), sems(8, edge),
            sems(count), sems(count), sems(4, edge),
        ],
        compiler_params=pltpu.CompilerParams(
            vmem_limit_bytes=CLOSE_BYTES, collective_id=0, has_side_effects=True
        ),
        cost_estimate=pl.CostEstimate(flops=0, bytes_accessed=30_000_000, transcendentals=0),
        name="close",
    )(*blocks_x, *saved, conv, gathered, block_w, one, sent, *w_rows, norms, taps,
      qkv, planes, seg_row, grad)


def shifted(block, off):
    count = lax.axis_size("mp")
    return lax.ppermute(block, "mp", [(n, (n - off) % count) for n in range(count)])


def on_device(
    inputs, segment, w_query, w_key, w_value, planes, conv_taps, w_out,
    ln1_gain, ln1_bias, w_up, w_down, ln2_gain, ln2_bias, cotangent,
):
    count = lax.axis_size("mp")
    blocks = lax.axis_size("dp")
    rows, width = inputs.shape
    w_rows = (w_query.T, w_key.T, w_value.T)
    gathered, qkv, block_w = gather_qkv(inputs, w_rows, w_up, w_down, w_out, count)
    left_w, right_w = shifted(block_w, -2), shifted(block_w, 2)
    gathered = gathered.reshape(rows * count, width)
    seg_row = segment[None, :]
    taps = jnp.pad(
        jnp.concatenate(
            (
                jnp.pad(conv_taps, ((0, 0), (0, 16 - HEADS))),
                jnp.pad(conv_taps[::-1], ((0, 0), (0, 16 - HEADS))),
            ),
            1,
        ),
        ((0, 2 * LANES - KW), (0, 0)),
    ).T
    conv = segment_conv(qkv, taps, seg_row)
    sent, *saved = attend(qkv, planes, seg_row, conv)
    scale = jnp.stack((ln1_gain, ln1_bias, ln2_gain, ln2_bias) * 2)
    outputs, lows, left_x, right_x, one_grad, attn_grad, norm_part = middle(
        sent, inputs, cotangent, (block_w, left_w, right_w), scale, count
    )
    value_conv, tap_part = conv_back(qkv, attn_grad, taps, seg_row)
    inputs_grad, up, down, out, query, key, value, tiny, conv_rows = close(
        (lows, left_x, right_x), saved, value_conv, sent, gathered, w_rows,
        block_w, one_grad, norm_part, tap_part, qkv, planes, seg_row, attn_grad, blocks,
    )
    return (
        outputs, inputs_grad, query.astype(F32).T, key.astype(F32).T, value.astype(F32).T,
        conv_rows[:HEADS, :KW].T, out.astype(F32), tiny[0], tiny[1],
        up.astype(F32), down.astype(F32), tiny[2], tiny[3],
    )


def solution(mesh):
    rows = P(("dp", "mp"), None)
    cols = P(None, "mp")
    return jax.shard_map(
        on_device,
        mesh=mesh,
        in_specs=(
            rows, P("dp"), cols, cols, cols, P(), P(), P("mp", None), P(), P(),
            cols, P("mp", None), P(), P(), rows,
        ),
        out_specs=(
            rows, rows, cols, cols, cols, P(), P("mp", None), P(), P(),
            cols, P("mp", None), P(), P(),
        ),
        check_vma=False,
    )
```
